32 devices in a mesh: seq: 16 (over z, y, core), ctx: 2 (over x).
Axes of the slice: x: 2, y: 2, z: 4, core: 2. Of those that a mesh axis runs over, the one named last changes fastest.
Arguments:
- tokens: bfloat16 [16, 256, 896], P('seq', 'ctx'), may hold values from -6 to 6
- positions: int32 [16, 256], P('seq'), may hold values from 0 to 255, as said below
- cotangent: bfloat16 [16, 256, 896], P('seq', 'ctx'), may hold values from -6 to 6
- qkv_weight: bfloat16 [896, 1152], P('seq'), may hold values from -0.1875 to 0.1875
- qkv_bias: bfloat16 [1152], P('seq'), may hold values from -16 to 16
- out_weight: bfloat16 [896, 896], P('seq'), may hold values from -0.75 to 0.75
- gate_up_weight: bfloat16 [896, 9728], P('seq'), may hold values from -0.1875 to 0.1875
- down_weight: bfloat16 [4864, 896], P('seq'), may hold values from -0.078125 to 0.078125
- attn_gain: bfloat16 [896], P('seq'), may hold values from 0.099609375 to 1.8984375
- ffn_gain: bfloat16 [896], P('seq'), may hold values from 0.099609375 to 1.8984375
Outputs:
- output: bfloat16 [16, 256, 896], P('seq', 'ctx')
- input_grad: float32 [16, 256, 896], P('seq', 'ctx')
- qkv_weight_grad: float32 [896, 1152], P('seq')
- qkv_bias_grad: float32 [1152], P('seq')
- out_weight_grad: float32 [896, 896], P('seq')
- gate_up_weight_grad: float32 [896, 9728], P('seq')
- down_weight_grad: float32 [4864, 896], P('seq')
- attn_gain_grad: float32 [896], P('seq')
- ffn_gain_grad: float32 [896], P('seq')
The draws below stay inside these ranges and needn't reach their ends.
Inputs may be any that keep to these rules, and one draw needn't show every extreme that they name: Each sequence holds every position of 0 to 255 once. The 128 stored tokens of one index of ctx are two blocks of 64 consecutive positions in rising order, block b and block 3 - b, with b drawn for each sequence.
All inputs are finite; a program needn't handle non-finite values.
Results may differ from the reference program's by a relative error of at most 0.018.
The reference program's roundings to bfloat16 on the way count: a program that leaves them out, or rounds other values in their place, can miss the bound.
Values may be sent and summed in bfloat16 or wider, within the bound.
A program may use at most 192 MiB of HBM per device.

```python
import jax
import jax.numpy as jnp
from jax import lax

D = 896
HEADS = 14
KV_HEADS = 2
HEAD_DIM = 64
FF = 4864
SPAN = 64
LEN = 256
SEQS = 16
QKV = 1152
N_CTX = 2


def draw_positions(key, part):
    seq_keys = jax.random.split(key, SEQS)
    orders = jax.vmap(lambda one_key: jax.random.permutation(one_key, N_CTX))(seq_keys)
    offsets = jnp.arange(SPAN, dtype=jnp.int32)
    first_half = orders[:, :, None] * SPAN + offsets[None, None, :]
    second_half = (2 * N_CTX - 1 - orders[:, :, None]) * SPAN + offsets[None, None, :]
    joined = jnp.concatenate([first_half, second_half], axis=2)
    return joined.reshape(SEQS, LEN).astype(jnp.int32)


def draw_qkv_bias(key, part):
    columns = (HEADS + 2 * KV_HEADS) * HEAD_DIM
    normal_draw = jax.random.normal(key, (columns,), jnp.float32)
    return jnp.clip(normal_draw * 0.5, -2.5, 2.5).astype(jnp.bfloat16)


def levels(key, dims, cuts, low, largest):
    def one(axis_at, shards_of):
        steps = jax.random.uniform(jax.random.fold_in(jax.random.fold_in(key, 6), axis_at), (shards_of,), jnp.float32, low / len(cuts), largest / len(cuts))
        return jnp.repeat(jnp.exp(steps), dims[axis_at] // shards_of).reshape((-1,) + (1,) * (len(dims) - axis_at - 1))

    gain = one(*cuts[0])
    for cut in cuts[1:]:
        gain = gain * one(*cut)
    return gain


def noise(key, dims, spread, most, cuts=(), held_as=jnp.bfloat16):
    factor_of = levels(key, dims, cuts, -0.22, 0.18) if cuts else 1.0
    values = jax.random.normal(key, dims, jnp.float32) * spread * factor_of
    return jnp.minimum(jnp.maximum(values, -most), most).astype(held_as)


def setup_inputs(seed: int = 0) -> dict:
    seeds = jax.random.split(jax.random.key(seed), 11)
    return {
        "tokens": noise(seeds[0], (SEQS, LEN, D), 1.0, 6.0, ((0, 16), (1, 2))),
        "positions": draw_positions(jax.random.fold_in(seeds[10], 71), 0),
        "cotangent": noise(seeds[2], (SEQS, LEN, D), 1.0, 6.0, ((0, 16), (1, 2))),
        "qkv_weight": noise(seeds[3], (D, QKV), D ** -0.5, 0.1875, ((0, 16),)),
        "qkv_bias": draw_qkv_bias(jax.random.fold_in(seeds[10], 71), 0),
        "out_weight": noise(seeds[5], (HEADS * HEAD_DIM, D), (HEADS * HEAD_DIM // 16) ** -0.5, 0.75, ((0, 16),)),
        "gate_up_weight": noise(seeds[6], (D, 2 * FF), D ** -0.5, 0.1875, ((0, 16),)),
        "down_weight": noise(seeds[7], (FF, D), FF ** -0.5, 0.078125, ((0, 16),)),
        "attn_gain": jnp.clip(1.0 + 0.18 * jax.random.normal(seeds[8], (D,), jnp.float32), 0.099609375, 1.8984375).astype(jnp.bfloat16),
        "ffn_gain": jnp.clip(1.0 + 0.18 * jax.random.normal(seeds[9], (D,), jnp.float32), 0.099609375, 1.8984375).astype(jnp.bfloat16),
    }


EPS = 1e-06
ROPE_BASE = 1000000.0

def to_bf16(values):
    return lax.optimization_barrier(values.astype(jnp.bfloat16))

def rope_tables(position_row):
    half_dim = HEAD_DIM // 2
    exponent = jnp.arange(half_dim, dtype=jnp.float32) * (2.0 / HEAD_DIM)
    inverse = ROPE_BASE ** (-exponent)
    angles = position_row.astype(jnp.float32)[:, None] * inverse[None, :]
    cosine_table = jnp.cos(angles)
    sine_table = jnp.sin(angles)
    return (jnp.concatenate([cosine_table, cosine_table], -1), jnp.concatenate([sine_table, sine_table], -1))

def rotate_half(values):
    half_dim = values.shape[-1] // 2
    return jnp.concatenate([-values[..., half_dim:], values[..., :half_dim]], -1)

def rotate_back(values):
    half_dim = values.shape[-1] // 2
    return jnp.concatenate([values[..., half_dim:], -values[..., :half_dim]], -1)

def rms_forward(values):
    scaling = lax.rsqrt(lax.optimization_barrier(jnp.mean(values * values, axis=-1, keepdims=True)) + EPS)
    return (values * scaling, scaling)

def rms_backward(grad_normed, normed, scaling, gain_float):
    gain_grad = lax.optimization_barrier(jnp.sum(grad_normed * normed, axis=0))
    grad_scaled = grad_normed * gain_float
    inner = lax.optimization_barrier(jnp.mean(grad_scaled * normed, axis=-1, keepdims=True))
    return (scaling * (grad_scaled - normed * inner), gain_grad)

def sequence_pass(token_row, position_row, cot_row, weights):
    full_qkv, full_bias, full_out, full_gate_up, full_down, gain_one, gain_two = weights
    row_count = token_row.shape[0]
    group_size = HEADS // KV_HEADS
    query_width = HEADS * HEAD_DIM
    key_width = KV_HEADS * HEAD_DIM
    score_scale = HEAD_DIM ** (-0.5)
    f32 = jnp.float32
    inputs_f = token_row.astype(f32)
    gain_one_f = gain_one.astype(f32)
    gain_two_f = gain_two.astype(f32)
    normed_one, scale_one = rms_forward(inputs_f)
    first_in = to_bf16(normed_one * gain_one_f)
    projected = jnp.dot(first_in, full_qkv, preferred_element_type=f32) + full_bias.astype(f32)
    cosine_table, sine_table = rope_tables(position_row)
    cos_query = cosine_table[:, None, None, :]
    sin_query = sine_table[:, None, None, :]
    cos_key = cosine_table[:, None, :]
    sin_key = sine_table[:, None, :]
    query = projected[:, :query_width].reshape(row_count, KV_HEADS, group_size, HEAD_DIM)
    keys = projected[:, query_width:query_width + key_width].reshape(row_count, KV_HEADS, HEAD_DIM)
    values = projected[:, query_width + key_width:].reshape(row_count, KV_HEADS, HEAD_DIM)
    query_rot = to_bf16(query * cos_query + rotate_half(query) * sin_query)
    key_rot = to_bf16(keys * cos_key + rotate_half(keys) * sin_key)
    value_b = to_bf16(values)
    scores = jnp.einsum('tkgd,skd->kgts', query_rot.astype(f32), key_rot.astype(f32)) * score_scale
    allowed = position_row[None, :] <= position_row[:, None]
    scores = jnp.where(allowed, scores, -1e+30)
    row_top = lax.optimization_barrier(jnp.max(scores, axis=-1, keepdims=True))
    log_total = row_top + jnp.log(lax.optimization_barrier(jnp.sum(jnp.exp(scores - row_top), axis=-1, keepdims=True)))
    probs = jnp.exp(scores - log_total)
    probs_b = to_bf16(probs)
    attended = to_bf16(jnp.einsum('kgts,skd->tkgd', probs_b.astype(f32), value_b.astype(f32)))
    attended_flat = attended.reshape(row_count, query_width)
    residual = inputs_f + jnp.dot(attended_flat, full_out, preferred_element_type=f32)
    normed_two, scale_two = rms_forward(residual)
    second_in = to_bf16(normed_two * gain_two_f)
    gate_up = jnp.dot(second_in, full_gate_up, preferred_element_type=f32)
    gate = gate_up[:, :FF]
    upward = gate_up[:, FF:]
    activated = to_bf16(jax.nn.silu(gate) * upward)
    output_row = (residual + jnp.dot(activated, full_down, preferred_element_type=f32)).astype(jnp.bfloat16)
    down_grad = jnp.dot(activated.T, cot_row, preferred_element_type=f32)
    grad_act = jnp.dot(cot_row, full_down.T, preferred_element_type=f32)
    sigmoid_gate = jax.nn.sigmoid(gate)
    grad_gate = grad_act * upward * sigmoid_gate * (1.0 + gate * (1.0 - sigmoid_gate))
    grad_upward = grad_act * jax.nn.silu(gate)
    grad_gate_up = to_bf16(jnp.concatenate([grad_gate, grad_upward], -1))
    gate_up_grad = jnp.dot(second_in.T, grad_gate_up, preferred_element_type=f32)
    grad_second = jnp.dot(grad_gate_up, full_gate_up.T, preferred_element_type=f32)
    grad_through, gain_two_grad = rms_backward(grad_second, normed_two, scale_two, gain_two_f)
    grad_residual = cot_row.astype(f32) + grad_through
    grad_res_b = to_bf16(grad_residual)
    out_grad = jnp.dot(attended_flat.T, grad_res_b, preferred_element_type=f32)
    grad_attended = to_bf16(jnp.dot(grad_res_b, full_out.T, preferred_element_type=f32))
    grad_attended = grad_attended.reshape(row_count, KV_HEADS, group_size, HEAD_DIM)
    grad_probs = jnp.einsum('tkgd,skd->kgts', grad_attended.astype(f32), value_b.astype(f32))
    delta = lax.optimization_barrier(jnp.sum(grad_attended.astype(f32) * attended.astype(f32), axis=-1))
    delta = jnp.transpose(delta, (1, 2, 0))[..., None]
    grad_scores = to_bf16(probs * (grad_probs - delta) * score_scale)
    grad_query_rot = jnp.einsum('kgts,skd->tkgd', grad_scores.astype(f32), key_rot.astype(f32))
    grad_key_rot = jnp.einsum('kgts,tkgd->skd', grad_scores.astype(f32), query_rot.astype(f32))
    grad_value = jnp.einsum('kgts,tkgd->skd', probs_b.astype(f32), grad_attended.astype(f32))
    grad_query = grad_query_rot * cos_query + rotate_back(grad_query_rot * sin_query)
    grad_key = grad_key_rot * cos_key + rotate_back(grad_key_rot * sin_key)
    grad_projected = jnp.concatenate([grad_query.reshape(row_count, query_width), grad_key.reshape(row_count, key_width), grad_value.reshape(row_count, key_width)], -1)
    bias_grad = lax.optimization_barrier(jnp.sum(grad_projected, axis=0))
    grad_proj_b = to_bf16(grad_projected)
    qkv_grad = jnp.dot(first_in.T, grad_proj_b, preferred_element_type=f32)
    grad_first = jnp.dot(grad_proj_b, full_qkv.T, preferred_element_type=f32)
    grad_input_part, gain_one_grad = rms_backward(grad_first, normed_one, scale_one, gain_one_f)
    input_row_grad = grad_residual + grad_input_part
    grads = (qkv_grad, bias_grad, out_grad, gate_up_grad, down_grad, gain_one_grad, gain_two_grad)
    return (output_row, input_row_grad, grads)

def reference(tokens, positions, cotangent, qkv_weight, qkv_bias, out_weight, gate_up_weight, down_weight, attn_gain, ffn_gain):
    weights = (qkv_weight, qkv_bias, out_weight, gate_up_weight, down_weight, attn_gain, ffn_gain)
    totals = tuple((jnp.zeros(weight.shape, jnp.float32) for weight in weights))

    def step_sequence(carried, inputs_row):
        token_row, position_row, cot_row = inputs_row
        output_row, input_row_grad, grads = sequence_pass(token_row, position_row, cot_row, weights)
        return (jax.tree.map(jnp.add, carried, grads), (output_row, input_row_grad))
    sums, (outputs, input_grads) = lax.scan(step_sequence, totals, (tokens, positions, cotangent))
    return (outputs, input_grads, sums[0], sums[1], sums[2], sums[3], sums[4], sums[5], sums[6])
```

```python
import functools

import jax
import jax.numpy as jnp
from jax import lax
from jax.experimental import pallas as pl
from jax.experimental.pallas import tpu as pltpu
from jax.sharding import PartitionSpec as P

HEADS = 14
KV_HEADS = 2
HEAD_DIM = 64


EPS = 1e-06
ROPE_BASE = 1000000.0


def to_bf16(values):
    return lax.optimization_barrier(values.astype(jnp.bfloat16))


def rope_tables(position_row):
    half_dim = HEAD_DIM // 2
    exponent = jnp.arange(half_dim, dtype=jnp.float32) * (2.0 / HEAD_DIM)
    inverse = ROPE_BASE ** (-exponent)
    angles = position_row.astype(jnp.float32)[:, None] * inverse[None, :]
    cosine_table = jnp.cos(angles)
    sine_table = jnp.sin(angles)
    return (
        jnp.concatenate([cosine_table, cosine_table], -1),
        jnp.concatenate([sine_table, sine_table], -1),
    )


def rotate_half(values):
    half_dim = values.shape[-1] // 2
    return jnp.concatenate([-values[..., half_dim:], values[..., :half_dim]], -1)


def rotate_back(values):
    half_dim = values.shape[-1] // 2
    return jnp.concatenate([values[..., half_dim:], -values[..., :half_dim]], -1)


def rms_forward(values):
    scaling = lax.rsqrt(jnp.mean(values * values, axis=-1, keepdims=True) + EPS)
    return (values * scaling, scaling)


def rms_backward(grad_normed, normed, scaling, gain_float):
    gain_grad = jnp.sum(grad_normed * normed, axis=0)
    grad_scaled = grad_normed * gain_float
    inner = jnp.mean(grad_scaled * normed, axis=-1, keepdims=True)
    return (scaling * (grad_scaled - normed * inner), gain_grad)


def weight_rows(left_side, right_side):
    return lax.psum_scatter(
        lax.dot_general(
            left_side, right_side, (((0,), (0,)), ((), ())), preferred_element_type=jnp.float32
        ),
        "seq",
        scatter_dimension=0,
        tiled=True,
    )


def columns_from_rows(rows, parts):
    depth = rows.shape[0]
    hidden = rows.shape[1] // (2 * parts)
    split = jnp.transpose(rows.reshape(depth, 2, parts, hidden), (2, 0, 1, 3))
    split = split.reshape(parts, depth, 2 * hidden)
    moved = lax.all_to_all(split, "seq", split_axis=0, concat_axis=0, tiled=True)
    return moved.reshape(parts * depth, 2 * hidden)


def rows_from_columns(columns, parts):
    depth = columns.shape[0] // parts
    hidden = columns.shape[1] // 2
    split = columns.reshape(parts, depth, 2 * hidden)
    moved = lax.all_to_all(split, "seq", split_axis=0, concat_axis=0, tiled=True)
    moved = jnp.transpose(moved.reshape(parts, depth, 2, hidden), (1, 2, 0, 3))
    return moved.reshape(depth, 2 * parts * hidden)


def contract_rows(left_side, right_side):
    return lax.dot_general(
        left_side, right_side, (((0,), (0,)), ((), ())), preferred_element_type=jnp.float32
    )


def contract_columns(left_side, right_side):
    return lax.dot_general(
        left_side, right_side, (((1,), (1,)), ((), ())), preferred_element_type=jnp.float32
    )


def scatter_tokens(partial):
    total = lax.psum_scatter(to_bf16(partial), "seq", scatter_dimension=0, tiled=True)
    return total.astype(jnp.float32)


def gather_kernel(outer, own_ref, all_ref, local_sem, outer_sems, middle_sems, core_sems):
    me = lax.axis_index("seq")
    at_outer = me // 4
    middle = (me // 2) % 2
    core = me % 2
    rows = own_ref.shape[0]

    def place(outer_at, middle_at, core_at):
        index = outer_at * 4 + middle_at * 2 + core_at
        return all_ref.at[pl.ds(pl.multiple_of(index * rows, rows), rows)]

    def remote(source, target, sems, slot, device):
        return pltpu.make_async_remote_copy(
            src_ref=source,
            dst_ref=target,
            send_sem=sems.at[0, slot],
            recv_sem=sems.at[1, slot],
            device_id={"seq": device},
            device_id_type=pl.DeviceIdType.MESH,
        )

    middle_partner = at_outer * 4 + (1 - middle) * 2 + core
    core_partner = at_outer * 4 + middle * 2 + (1 - core)
    outer_partners = [
        ((at_outer + step) % outer) * 4 + middle * 2 + core for step in range(1, outer)
    ]
    barrier = pltpu.get_barrier_semaphore()
    for device in [middle_partner, core_partner] + outer_partners:
        pl.semaphore_signal(
            barrier, inc=1, device_id={"seq": device}, device_id_type=pl.DeviceIdType.MESH
        )
    pl.semaphore_wait(barrier, outer + 1)

    own_place = place(at_outer, middle, core)
    local = pltpu.make_async_copy(own_ref, own_place, local_sem)
    local.start()
    started = []
    outer_copies = []
    for step in range(1, outer):
        copy = remote(own_ref, own_place, outer_sems, step - 1, outer_partners[step - 1])
        copy.start()
        outer_copies.append(copy)
    middle_copies = []
    for step in range(outer):
        source_outer = (at_outer + outer - step) % outer
        here = place(source_outer, middle, core)
        if step == 0:
            source = own_ref
        else:
            outer_copies[step - 1].wait_recv()
            source = here
        copy = remote(source, here, middle_sems, step, middle_partner)
        copy.start()
        middle_copies.append(copy)
        copy = remote(source, here, core_sems, 2 * step, core_partner)
        copy.start()
        started.append(copy)
    for step in range(outer):
        source_outer = (at_outer + outer - step) % outer
        middle_copies[step].wait_recv()
        here = place(source_outer, 1 - middle, core)
        copy = remote(here, here, core_sems, 2 * step + 1, core_partner)
        copy.start()
        started.append(copy)
    for copy in started:
        copy.wait_recv()
    for copy in outer_copies + middle_copies + started:
        copy.wait_send()
    local.wait()


def gather_rows(rows, collective_id):
    parts = lax.axis_size("seq")
    if parts % 4:
        return lax.all_gather(rows, "seq", axis=0, tiled=True)
    outer = parts // 4
    return pl.pallas_call(
        functools.partial(gather_kernel, outer),
        out_shape=jax.ShapeDtypeStruct((parts * rows.shape[0], rows.shape[1]), rows.dtype),
        in_specs=[pl.BlockSpec(memory_space=pltpu.VMEM)],
        out_specs=pl.BlockSpec(memory_space=pltpu.VMEM),
        scratch_shapes=[
            pltpu.SemaphoreType.DMA,
            pltpu.SemaphoreType.DMA((2, max(outer - 1, 1))),
            pltpu.SemaphoreType.DMA((2, outer)),
            pltpu.SemaphoreType.DMA((2, 2 * outer)),
        ],
        compiler_params=pltpu.CompilerParams(
            collective_id=collective_id, has_side_effects=True, vmem_limit_bytes=24 * 2**20
        ),
    )(rows)


def packed_height(depth):
    return (depth + 16) // 16 * 16


def other(values):
    return lax.ppermute(values, "ctx", [(0, 1), (1, 0)])


def sum_rounded(values):
    if lax.axis_size("ctx") != 2:
        return lax.psum(values, "ctx")
    mine = to_bf16(values)
    return mine.astype(jnp.float32) + other(mine).astype(jnp.float32)


def sum_ctx(values):
    if lax.axis_size("ctx") != 2:
        return lax.psum(values, "ctx")
    return values + other(values)


MESH = pl.DeviceIdType.MESH
LANES = 128


def padded(width):
    return (width + LANES - 1) // LANES * LANES


def remote_copy(source, target, send_sem, recv_sem, device):
    return pltpu.make_async_remote_copy(
        src_ref=source,
        dst_ref=target,
        send_sem=send_sem,
        recv_sem=recv_sem,
        device_id=device,
        device_id_type=MESH,
    )


def greet(devices):
    barrier = pltpu.get_barrier_semaphore()
    for device in devices:
        pl.semaphore_signal(barrier, inc=1, device_id=device, device_id_type=MESH)
    pl.semaphore_wait(barrier, len(devices))


def dot_last(left, right):
    return lax.dot_general(
        left, right, (((1,), (1,)), ((), ())), preferred_element_type=jnp.float32
    )


def dot_first(left, right):
    return lax.dot_general(
        left, right, (((0,), (0,)), ((), ())), preferred_element_type=jnp.float32
    )


def z_order(z):
    return (z + 1 - 2 * (z % 2), 2 - z // 2, 3 - 3 * (z // 2))


class Place:
    def __init__(self):
        me = lax.axis_index("seq")
        self.z = me // 4
        self.y = (me // 2) % 2
        self.k = me % 2
        self.c = lax.axis_index("ctx")
        self.me = me

    def seq(self, z, y, k):
        return {"seq": z * 4 + y * 2 + k}

    def others(self):
        z, y, k = self.z, self.y, self.k
        return (
            [self.seq(z, 1 - y, k), self.seq(z, y, 1 - k)]
            + [self.seq(other, y, k) for other in z_order(z)]
        )


class Gather:
    def __init__(self, at, own_ref, all_ref, send_sems, recv_sems, local_sem):
        self.at, self.own, self.all = at, own_ref, all_ref
        self.send_sems, self.recv_sems, self.local_sem = send_sems, recv_sems, local_sem
        self.rows = own_ref.shape[0]
        self.sent = []
        self.hop_sent = []

    def block(self, z, y, k):
        start = pl.multiple_of((z * 4 + y * 2 + k) * self.rows, self.rows)
        return self.all.at[pl.ds(start, self.rows)]

    def copy(self, source, z, y, k, kind, device, slot=None):
        return remote_copy(
            source,
            self.block(z, y, k),
            self.send_sems.at[z, kind if slot is None else slot],
            self.recv_sems.at[z, kind],
            device,
        )

    def to_y_and_core(self, source, z):
        at = self.at
        copy = self.copy(source, z, at.y, at.k, 1, at.seq(at.z, 1 - at.y, at.k))
        copy.start()
        self.sent.append(copy)
        self.to_core(source, z, at.y)

    def to_core(self, source, z, y):
        at = self.at
        copy = self.copy(source, z, y, at.k, 2 + y, at.seq(at.z, at.y, 1 - at.k))
        copy.start()
        self.sent.append(copy)

    def hop(self, source, z, right):
        at = self.at
        target = at.z + 1 if right else at.z - 1
        copy = self.copy(
            source, z, at.y, at.k, 0, at.seq(target, at.y, at.k), slot=None if right else 4
        )
        ok = (target < 4) if right else (target >= 0)
        return ok, copy

    def begin(self):
        at = self.at
        for right in (True, False):
            ok, copy = self.hop(self.own, at.z, right)
            self.hop_sent.append((ok, copy))

            @pl.when(ok)
            def _():
                copy.start()

        self.to_y_and_core(self.own, at.z)
        self.local = pltpu.make_async_copy(
            self.own, self.block(at.z, at.y, at.k), self.local_sem
        )
        self.local.start()

    def from_z(self, z):
        at = self.at
        here = self.block(z, at.y, at.k)
        self.copy(here, z, at.y, at.k, 0, at.seq(at.z, 1 - at.y, at.k)).wait_recv()
        for right in (True, False):
            ok, copy = self.hop(here, z, right)
            ok = jnp.logical_and(ok, z < at.z if right else z > at.z)
            self.hop_sent.append((ok, copy))

            @pl.when(ok)
            def _():
                copy.start()

        self.to_y_and_core(here, z)

    def from_y(self, z):
        at = self.at
        here = self.block(z, 1 - at.y, at.k)
        self.copy(here, z, 1 - at.y, at.k, 1, at.seq(at.z, 1 - at.y, at.k)).wait_recv()
        self.to_core(here, z, 1 - at.y)

    def from_core(self, z):
        at = self.at
        for y in range(2):
            here = self.block(z, y, 1 - at.k)
            self.copy(here, z, y, 1 - at.k, 2 + y, at.seq(at.z, at.y, 1 - at.k)).wait_recv()

    def end(self):
        for copy in self.sent:
            copy.wait_send()
        for ok, copy in self.hop_sent:

            @pl.when(ok)
            def _():
                copy.wait_send()


class Scatter:
    def __init__(self, at, part, core_buf, y_buf, z_buf, out_ref, send_sems, recv_sems):
        self.at, self.part, self.out = at, part, out_ref
        self.core_buf, self.y_buf, self.z_buf = core_buf, y_buf, z_buf
        self.send_sems, self.recv_sems = send_sems, recv_sems
        self.rows = out_ref.shape[0]
        self.sent = []
        self.core_copies = {}

    def block(self, z, y, k):
        start = pl.multiple_of((z * 4 + y * 2 + k) * self.rows, self.rows)
        return self.part.at[pl.ds(start, self.rows)]

    def core_copy(self, z, y):
        at = self.at
        return remote_copy(
            self.block(z, y, 1 - at.k),
            self.core_buf.at[z, y],
            self.send_sems.at[z, y],
            self.recv_sems.at[z, y],
            at.seq(at.z, at.y, 1 - at.k),
        )

    def to_core(self, z):
        for y in range(2):
            copy = self.core_copy(z, y)
            copy.start()
            self.sent.append(copy)

    def y_copy(self, z):
        at = self.at
        return remote_copy(
            self.block(z, 1 - at.y, at.k),
            self.y_buf.at[z],
            self.send_sems.at[z, 2],
            self.recv_sems.at[z, 2],
            at.seq(at.z, 1 - at.y, at.k),
        )

    def add_core(self, z, y):
        at = self.at
        here = self.block(z, y, at.k)
        total = here[...].astype(jnp.float32) + self.core_buf[z, y].astype(jnp.float32)
        here[...] = total.astype(jnp.bfloat16)

    def to_y(self, z):
        at = self.at
        for y in range(2):
            self.core_copy(z, y).wait_recv()
        self.add_core(z, 1 - at.y)
        copy = self.y_copy(z)
        copy.start()
        self.sent.append(copy)
        self.add_core(z, at.y)

    def z_copy(self, z, source_z):
        at = self.at
        return remote_copy(
            self.block(z, at.y, at.k),
            self.z_buf.at[source_z],
            self.send_sems.at[z, 3],
            self.recv_sems.at[source_z, 3],
            at.seq(z, at.y, at.k),
        )

    def to_z(self, z, own):
        at = self.at
        self.y_copy(z).wait_recv()
        here = self.block(z, at.y, at.k)
        total = here[...].astype(jnp.float32) + self.y_buf[z].astype(jnp.float32)
        if own:
            self.out[...] = total
        else:
            here[...] = total.astype(jnp.bfloat16)
            copy = self.z_copy(z, at.z)
            copy.start()
            self.sent.append(copy)

    def finish(self):
        at = self.at
        total = self.out[...]
        for z in z_order(at.z):
            remote_copy(
                self.block(z, at.y, at.k),
                self.z_buf.at[z],
                self.send_sems.at[z, 3],
                self.recv_sems.at[z, 3],
                at.seq(z, at.y, at.k),
            ).wait_recv()
            total += self.z_buf[z].astype(jnp.float32)
        self.out[...] = total

    def end(self):
        for copy in self.sent:
            copy.wait_send()


def ffn_kernel(
    own_ref,
    cot_ref,
    weight_ref,
    down_ref,
    second_sum_ref,
    down_sum_ref,
    down_grad_ref,
    gate_grad_ref,
    all_ref,
    act_ref,
    grad_ref,
    part_ref,
    core_buf,
    y_buf,
    z_buf,
    flat_ref,
    gate_send,
    gate_recv,
    down_send,
    down_recv,
    gather_send,
    gather_recv,
    local_sem,
    scatter_send,
    scatter_recv,
    x_send,
    x_recv,
):
    at = Place()
    width = down_ref.shape[0]
    rows = own_ref.shape[0]
    parts = all_ref.shape[0] // rows
    depth = weight_ref.shape[0] // parts
    other_ctx = {"ctx": 1 - at.c}
    greet(at.others() + [other_ctx])
    gather = Gather(at, own_ref, all_ref, gather_send, gather_recv, local_sem)
    scatters = [
        Scatter(
            at,
            part_ref.at[which],
            core_buf.at[which],
            y_buf.at[which],
            z_buf.at[which],
            (second_sum_ref, down_sum_ref)[which],
            scatter_send.at[which],
            scatter_recv.at[which],
        )
        for which in range(2)
    ]
    second, down = scatters
    tile = 2 * rows

    def compute(z):
        def step(index, carry):
            start = pl.multiple_of(z * (4 * rows) + index * tile, tile)
            here = pl.ds(start, tile)
            gate_up = jnp.dot(
                all_ref[here], weight_ref[...], preferred_element_type=jnp.float32
            )
            grad_act = dot_last(cot_ref[here], down_ref[...])
            gate = gate_up[:, :width]
            upward = gate_up[:, width:]
            sigmoid_gate = jax.nn.sigmoid(gate)
            silu = gate * sigmoid_gate
            activated = (silu * upward).astype(jnp.bfloat16)
            act_ref[here] = activated
            grad_gate = grad_act * upward * sigmoid_gate * (1.0 + gate * (1.0 - sigmoid_gate))
            grad_ref[here, :width] = grad_gate.astype(jnp.bfloat16)
            grad_ref[here, width:] = (grad_act * silu).astype(jnp.bfloat16)
            part_ref[0, here] = dot_last(grad_ref[here], weight_ref[...]).astype(jnp.bfloat16)
            part_ref[1, here] = jnp.dot(
                activated, down_ref[...], preferred_element_type=jnp.float32
            ).astype(jnp.bfloat16)
            return carry

        lax.fori_loop(0, 2, step, 0)

    order = (at.z,) + z_order(at.z)
    gather.begin()
    for index, z in enumerate(order):
        if index + 1 < len(order):
            gather.from_z(order[index + 1])
        gather.from_y(z)
        if index == 0:
            gather.local.wait()
        gather.from_core(z)
        if index > 0:
            second.to_y(order[index - 1])
        compute(z)
        second.to_core(z)
        if index > 0:
            second.to_z(order[index - 1], index == 1)
    last = order[-1]
    down_grad = dot_first(act_ref[...], cot_ref[...])
    down_send[...] = down_grad.astype(jnp.bfloat16)
    down_copy = remote_copy(down_send, down_recv, x_send.at[0], x_recv.at[0], other_ctx)
    down_copy.start()
    second.to_y(last)
    down.to_core(order[0])
    down.to_core(order[1])
    half = lane_tile = LANES

    def gate_tile(index, carry):
        columns = pl.ds(pl.multiple_of(index * lane_tile, lane_tile), lane_tile)
        flat_ref[columns] = dot_first(all_ref[:, columns], grad_ref[...])
        return carry

    lax.fori_loop(0, all_ref.shape[1] // lane_tile, gate_tile, 0)
    second.to_z(last, False)
    down.to_y(order[0])
    down.to_y(order[1])
    down.to_core(order[2])
    down.to_core(order[3])

    def columns_of(ctx):
        return pl.ds(pl.multiple_of(ctx * width, LANES), width)

    for part in range(parts):
        gate_send[part] = flat_ref[
            part * depth : (part + 1) * depth, columns_of(1 - at.c)
        ].astype(jnp.bfloat16)
    gate_copy = remote_copy(gate_send, gate_recv, x_send.at[1], x_recv.at[1], other_ctx)
    gate_copy.start()
    down.to_z(order[0], True)
    down.to_z(order[1], False)
    down.to_y(order[2])
    down.to_y(order[3])
    down.to_z(order[2], False)
    second.finish()
    down.to_z(order[3], False)
    down_copy.wait_recv()
    hidden = down_grad_ref.shape[0]
    down_grad_ref[...] = (
        down_send[:hidden].astype(jnp.float32) + down_recv[:hidden].astype(jnp.float32)
    )
    gate_copy.wait_recv()
    for part in range(parts):
        mine = flat_ref[part * depth : (part + 1) * depth, columns_of(at.c)]
        mine = mine.astype(jnp.bfloat16).astype(jnp.float32)
        gate_grad_ref[part] = (mine + gate_recv[part].astype(jnp.float32)).astype(jnp.bfloat16)
    down.finish()
    down_copy.wait_send()
    gate_copy.wait_send()
    gather.end()
    for scatter in scatters:
        scatter.end()


def ffn(second_in, all_cot, weight, down, hidden, collective_id):
    rows, model = second_in.shape
    parts = all_cot.shape[0] // rows
    width = down.shape[0]
    depth = model // parts
    tokens = parts * rows
    f32, bf16 = jnp.float32, jnp.bfloat16
    vmem = pl.BlockSpec(memory_space=pltpu.VMEM)
    flops = 2 * tokens * model * width * 9
    return pl.pallas_call(
        ffn_kernel,
        out_shape=(
            jax.ShapeDtypeStruct((rows, model), f32),
            jax.ShapeDtypeStruct((rows, model), f32),
            jax.ShapeDtypeStruct((hidden, model), f32),
            jax.ShapeDtypeStruct((parts, depth, width), bf16),
        ),
        in_specs=[vmem] * 4,
        out_specs=(vmem,) * 4,
        scratch_shapes=[
            pltpu.VMEM((tokens, model), bf16),
            pltpu.VMEM((tokens, width), bf16),
            pltpu.VMEM((tokens, 2 * width), bf16),
            pltpu.VMEM((2, tokens, model), bf16),
            pltpu.VMEM((2, 4, 2, rows, model), bf16),
            pltpu.VMEM((2, 4, rows, model), bf16),
            pltpu.VMEM((2, 4, rows, model), bf16),
            pltpu.VMEM((model, 2 * width), f32),
            pltpu.VMEM((parts, depth, width), bf16),
            pltpu.VMEM((parts, depth, width), bf16),
            pltpu.VMEM((width, model), bf16),
            pltpu.VMEM((width, model), bf16),
            pltpu.SemaphoreType.DMA((4, 5)),
            pltpu.SemaphoreType.DMA((4, 4)),
            pltpu.SemaphoreType.DMA,
            pltpu.SemaphoreType.DMA((2, 4, 4)),
            pltpu.SemaphoreType.DMA((2, 4, 4)),
            pltpu.SemaphoreType.DMA((2,)),
            pltpu.SemaphoreType.DMA((2,)),
        ],
        compiler_params=pltpu.CompilerParams(
            collective_id=collective_id, has_side_effects=True, vmem_limit_bytes=48 * 2**20
        ),
        cost_estimate=pl.CostEstimate(
            flops=flops, bytes_accessed=16 * 2**20, transcendentals=tokens * width
        ),
    )(second_in, all_cot, weight, down)


def shards(
    tokens,
    positions,
    cotangent,
    qkv_weight,
    qkv_bias,
    out_weight,
    gate_up_weight,
    down_weight,
    attn_gain,
    ffn_gain,
):
    f32 = jnp.float32
    qkv_columns = qkv_weight.shape[1]
    depth = qkv_weight.shape[0]
    bias_count = qkv_bias.shape[0]
    packed_rows = packed_height(depth)
    pair = jnp.concatenate([qkv_weight, out_weight], 1)
    extra = jnp.concatenate([qkv_bias, attn_gain, ffn_gain])
    extra = jnp.pad(extra, (0, pair.shape[1] - extra.shape[0]))[None]
    packed = jnp.concatenate(
        [pair, extra, jnp.zeros((packed_rows - depth - 1, pair.shape[1]), pair.dtype)], 0
    )
    packed = lax.all_gather(packed, "seq", axis=0, tiled=True).reshape(-1, packed_rows, pair.shape[1])
    full_qkv = packed[:, :depth, :qkv_columns].reshape(-1, qkv_columns)
    full_out = packed[:, :depth, qkv_columns:].reshape(-1, out_weight.shape[1])
    full_bias = packed[:, depth, :bias_count].reshape(-1)
    gain_one = packed[:, depth, bias_count : bias_count + depth].reshape(-1)
    gain_two = packed[:, depth, bias_count + depth : bias_count + 2 * depth].reshape(-1)
    parts = lax.axis_size("seq")
    hidden = down_weight.shape[0]
    own_gate_up = columns_from_rows(gate_up_weight, parts)
    all_cot = gather_rows(cotangent[0], 0)
    own_gate_up, all_cot, full_qkv = lax.optimization_barrier((own_gate_up, all_cot, full_qkv))
    inputs_f = tokens[0].astype(f32)
    cot_row = cotangent[0]
    row_count = inputs_f.shape[0]
    group_size = HEADS // KV_HEADS
    query_width = HEADS * HEAD_DIM
    key_width = KV_HEADS * HEAD_DIM
    score_scale = HEAD_DIM ** (-0.5)
    all_positions = positions[0]
    position_row = lax.dynamic_slice_in_dim(
        all_positions, lax.axis_index("ctx") * row_count, row_count, 0
    )
    normed_one, scale_one = rms_forward(inputs_f)
    first_in = to_bf16(normed_one * gain_one.astype(f32))
    projected = jnp.dot(first_in, full_qkv, preferred_element_type=f32) + full_bias.astype(f32)
    cosine_table, sine_table = rope_tables(position_row)
    cos_query = cosine_table[:, None, None, :]
    sin_query = sine_table[:, None, None, :]
    cos_key = cosine_table[:, None, :]
    sin_key = sine_table[:, None, :]
    query = projected[:, :query_width].reshape(row_count, KV_HEADS, group_size, HEAD_DIM)
    keys = projected[:, query_width : query_width + key_width].reshape(
        row_count, KV_HEADS, HEAD_DIM
    )
    values = projected[:, query_width + key_width :]
    query_rot = to_bf16(query * cos_query + rotate_half(query) * sin_query)
    key_rot = to_bf16(keys * cos_key + rotate_half(keys) * sin_key).reshape(row_count, key_width)
    value_b = to_bf16(values)
    both = jnp.concatenate([key_rot, value_b], -1)
    if lax.axis_size("ctx") == 2:
        both = jnp.concatenate([both, other(both)], 0)
        other_row = lax.dynamic_slice_in_dim(
            all_positions, (1 - lax.axis_index("ctx")) * row_count, row_count, 0
        )
        all_positions = jnp.concatenate([position_row, other_row])
    else:
        both = lax.all_gather(both, "ctx", axis=0, tiled=True)
    all_keys, all_values = both[:, :key_width], both[:, key_width:]
    all_keys = all_keys.reshape(-1, KV_HEADS, HEAD_DIM)
    all_values = all_values.reshape(-1, KV_HEADS, HEAD_DIM)
    scores = (
        jnp.einsum("tkgd,skd->kgts", query_rot, all_keys, preferred_element_type=f32) * score_scale
    )
    allowed = all_positions[None, :] <= position_row[:, None]
    scores = jnp.where(allowed, scores, -1e30)
    row_top = jnp.max(scores, axis=-1, keepdims=True)
    log_total = row_top + jnp.log(jnp.sum(jnp.exp(scores - row_top), axis=-1, keepdims=True))
    probs = jnp.exp(scores - log_total)
    probs_b = to_bf16(probs)
    attended = to_bf16(
        jnp.einsum("kgts,skd->tkgd", probs_b, all_values, preferred_element_type=f32)
    )
    attended_flat = attended.reshape(row_count, query_width)
    residual = inputs_f + jnp.dot(attended_flat, full_out, preferred_element_type=f32)
    normed_two, scale_two = rms_forward(residual)
    second_in = to_bf16(normed_two * gain_two.astype(f32))
    all_second = gather_rows(second_in, 1)
    gate_up = jnp.dot(all_second, own_gate_up, preferred_element_type=f32)
    gate = gate_up[:, :hidden]
    upward = gate_up[:, hidden:]
    sigmoid_gate = jax.nn.sigmoid(gate)
    activated = to_bf16(gate * sigmoid_gate * upward)
    grad_act = contract_columns(all_cot, down_weight)
    grad_gate = grad_act * upward * sigmoid_gate * (1.0 + gate * (1.0 - sigmoid_gate))
    grad_upward = grad_act * (gate * sigmoid_gate)
    grad_gate_up = to_bf16(jnp.concatenate([grad_gate, grad_upward], -1))
    grad_second = scatter_tokens(contract_columns(grad_gate_up, own_gate_up))
    down_sum = scatter_tokens(jnp.dot(activated, down_weight, preferred_element_type=f32))
    output_row = (residual + down_sum).astype(jnp.bfloat16)
    result_down = sum_rounded(contract_rows(activated, all_cot))
    result_gate_up = rows_from_columns(
        to_bf16(sum_rounded(contract_rows(all_second, grad_gate_up))), parts
    ).astype(f32)
    grad_through, gain_two_grad = rms_backward(
        grad_second, normed_two, scale_two, gain_two.astype(f32)
    )
    grad_residual = cot_row.astype(f32) + grad_through
    grad_res_b = to_bf16(grad_residual)
    out_grad = weight_rows(attended_flat, grad_res_b)
    grad_attended = to_bf16(jnp.dot(grad_res_b, full_out.T, preferred_element_type=f32))
    grad_attended = grad_attended.reshape(row_count, KV_HEADS, group_size, HEAD_DIM)
    grad_probs = jnp.einsum("tkgd,skd->kgts", grad_attended, all_values, preferred_element_type=f32)
    delta = jnp.sum(grad_attended.astype(f32) * attended.astype(f32), axis=-1)
    delta = jnp.transpose(delta, (1, 2, 0))[..., None]
    grad_scores = to_bf16(probs * (grad_probs - delta) * score_scale)
    grad_query_rot = jnp.einsum("kgts,skd->tkgd", grad_scores, all_keys, preferred_element_type=f32)
    key_part = jnp.einsum("kgts,tkgd->skd", grad_scores, query_rot, preferred_element_type=f32)
    value_part = jnp.einsum("kgts,tkgd->skd", probs_b, grad_attended, preferred_element_type=f32)
    key_parts = jnp.concatenate(
        [
            key_part.reshape(row_count * lax.axis_size("ctx"), key_width),
            value_part.reshape(row_count * lax.axis_size("ctx"), key_width),
        ],
        -1,
    )
    if lax.axis_size("ctx") == 2:
        key_local = key_parts[:row_count] + other(key_parts[row_count:])
    else:
        key_local = lax.psum_scatter(key_parts, "ctx", scatter_dimension=0, tiled=True)
    grad_key_rot = key_local[:, :key_width].reshape(row_count, KV_HEADS, HEAD_DIM)
    grad_value = key_local[:, key_width:]
    grad_query = grad_query_rot * cos_query + rotate_back(grad_query_rot * sin_query)
    grad_key = grad_key_rot * cos_key + rotate_back(grad_key_rot * sin_key)
    grad_projected = jnp.concatenate(
        [
            grad_query.reshape(row_count, query_width),
            grad_key.reshape(row_count, key_width),
            grad_value,
        ],
        -1,
    )
    bias_grad = jnp.sum(grad_projected, axis=0)
    grad_proj_b = to_bf16(grad_projected)
    grad_first = jnp.dot(grad_proj_b, full_qkv.T, preferred_element_type=f32)
    grad_input_part, gain_one_grad = rms_backward(
        grad_first, normed_one, scale_one, gain_one.astype(f32)
    )
    input_row_grad = grad_residual + grad_input_part
    small = jnp.concatenate(
        [
            bias_grad.reshape(parts, -1),
            gain_one_grad.reshape(parts, -1),
            gain_two_grad.reshape(parts, -1),
        ],
        -1,
    )
    small = jnp.pad(small, ((0, 0), (0, qkv_columns - small.shape[1])))[:, None]
    grad_rows = (depth + 8) // 8 * 8
    packed_grad = jnp.concatenate(
        [
            contract_rows(first_in, grad_proj_b).reshape(parts, depth, qkv_columns),
            small,
            jnp.zeros((parts, grad_rows - depth - 1, qkv_columns), f32),
        ],
        1,
    ).reshape(parts * grad_rows, qkv_columns)
    packed_grad, output_row = lax.optimization_barrier((packed_grad, output_row))
    packed_sum = sum_ctx(lax.psum_scatter(packed_grad, "seq", scatter_dimension=0, tiled=True))
    result_qkv = packed_sum[:depth]
    result_bias = packed_sum[depth, :bias_count]
    result_gain_one = packed_sum[depth, bias_count : bias_count + depth]
    result_gain_two = packed_sum[depth, bias_count + depth : bias_count + 2 * depth]
    result_out = sum_ctx(out_grad)
    return (
        output_row[None],
        input_row_grad[None],
        result_qkv,
        result_bias,
        result_out,
        result_gate_up,
        result_down,
        result_gain_one,
        result_gain_two,
    )


def shards_fast(
    tokens,
    positions,
    cotangent,
    qkv_weight,
    qkv_bias,
    out_weight,
    gate_up_weight,
    down_weight,
    attn_gain,
    ffn_gain,
):
    f32 = jnp.float32
    qkv_columns = qkv_weight.shape[1]
    depth = qkv_weight.shape[0]
    bias_count = qkv_bias.shape[0]
    packed_rows = packed_height(depth)
    pair = jnp.concatenate([qkv_weight, out_weight], 1)
    extra = jnp.concatenate([qkv_bias, attn_gain, ffn_gain])
    extra = jnp.pad(extra, (0, pair.shape[1] - extra.shape[0]))[None]
    packed = jnp.concatenate(
        [pair, extra, jnp.zeros((packed_rows - depth - 1, pair.shape[1]), pair.dtype)], 0
    )
    packed = lax.all_gather(packed, "seq", axis=0, tiled=True).reshape(-1, packed_rows, pair.shape[1])
    full_qkv = packed[:, :depth, :qkv_columns].reshape(-1, qkv_columns)
    full_out = packed[:, :depth, qkv_columns:].reshape(-1, out_weight.shape[1])
    full_bias = packed[:, depth, :bias_count].reshape(-1)
    gain_one = packed[:, depth, bias_count : bias_count + depth].reshape(-1)
    gain_two = packed[:, depth, bias_count + depth : bias_count + 2 * depth].reshape(-1)
    parts = lax.axis_size("seq")
    hidden = down_weight.shape[0]
    own_gate_up = columns_from_rows(gate_up_weight, parts)
    all_cot = gather_rows(cotangent[0], 0)
    own_gate_up, all_cot, full_qkv = lax.optimization_barrier((own_gate_up, all_cot, full_qkv))
    inputs_f = tokens[0].astype(f32)
    cot_row = cotangent[0]
    row_count = inputs_f.shape[0]
    group_size = HEADS // KV_HEADS
    query_width = HEADS * HEAD_DIM
    key_width = KV_HEADS * HEAD_DIM
    score_scale = HEAD_DIM ** (-0.5)
    all_positions = positions[0]
    position_row = lax.dynamic_slice_in_dim(
        all_positions, lax.axis_index("ctx") * row_count, row_count, 0
    )
    normed_one, scale_one = rms_forward(inputs_f)
    first_in = to_bf16(normed_one * gain_one.astype(f32))
    projected = jnp.dot(first_in, full_qkv, preferred_element_type=f32) + full_bias.astype(f32)
    cosine_table, sine_table = rope_tables(position_row)
    cos_query = cosine_table[:, None, None, :]
    sin_query = sine_table[:, None, None, :]
    cos_key = cosine_table[:, None, :]
    sin_key = sine_table[:, None, :]
    query = projected[:, :query_width].reshape(row_count, KV_HEADS, group_size, HEAD_DIM)
    keys = projected[:, query_width : query_width + key_width].reshape(
        row_count, KV_HEADS, HEAD_DIM
    )
    values = projected[:, query_width + key_width :]
    query_rot = to_bf16(query * cos_query + rotate_half(query) * sin_query)
    key_rot = to_bf16(keys * cos_key + rotate_half(keys) * sin_key).reshape(row_count, key_width)
    value_b = to_bf16(values)
    both = jnp.concatenate([key_rot, value_b], -1)
    if lax.axis_size("ctx") == 2:
        both = jnp.concatenate([both, other(both)], 0)
        other_row = lax.dynamic_slice_in_dim(
            all_positions, (1 - lax.axis_index("ctx")) * row_count, row_count, 0
        )
        all_positions = jnp.concatenate([position_row, other_row])
    else:
        both = lax.all_gather(both, "ctx", axis=0, tiled=True)
    all_keys, all_values = both[:, :key_width], both[:, key_width:]
    all_keys = all_keys.reshape(-1, KV_HEADS, HEAD_DIM)
    all_values = all_values.reshape(-1, KV_HEADS, HEAD_DIM)
    scores = (
        jnp.einsum("tkgd,skd->kgts", query_rot, all_keys, preferred_element_type=f32) * score_scale
    )
    allowed = all_positions[None, :] <= position_row[:, None]
    scores = jnp.where(allowed, scores, -1e30)
    row_top = jnp.max(scores, axis=-1, keepdims=True)
    log_total = row_top + jnp.log(jnp.sum(jnp.exp(scores - row_top), axis=-1, keepdims=True))
    probs = jnp.exp(scores - log_total)
    probs_b = to_bf16(probs)
    attended = to_bf16(
        jnp.einsum("kgts,skd->tkgd", probs_b, all_values, preferred_element_type=f32)
    )
    attended_flat = attended.reshape(row_count, query_width)
    residual = inputs_f + jnp.dot(attended_flat, full_out, preferred_element_type=f32)
    normed_two, scale_two = rms_forward(residual)
    second_in = to_bf16(normed_two * gain_two.astype(f32))
    down_sum_width = padded(hidden)
    extra_rows = down_sum_width - hidden
    weight_wide = jnp.pad(
        own_gate_up.reshape(-1, 2, hidden), ((0, 0), (0, 0), (0, extra_rows))
    ).reshape(-1, 2 * down_sum_width)
    down_wide = jnp.pad(down_weight, ((0, extra_rows), (0, 0)))
    grad_second, down_sum, result_down, gate_half = ffn(
        second_in, all_cot, weight_wide, down_wide, hidden, 1
    )
    output_row = (residual + down_sum).astype(jnp.bfloat16)
    moved = lax.all_to_all(gate_half, "seq", split_axis=0, concat_axis=0, tiled=True)
    moved = jnp.transpose(moved[:, :, :hidden], (1, 0, 2)).reshape(depth, -1)
    swapped = other(moved)
    is_first = lax.axis_index("ctx") == 0
    result_gate_up = jnp.concatenate(
        [jnp.where(is_first, moved, swapped), jnp.where(is_first, swapped, moved)], -1
    ).astype(f32)
    grad_through, gain_two_grad = rms_backward(
        grad_second, normed_two, scale_two, gain_two.astype(f32)
    )
    grad_residual = cot_row.astype(f32) + grad_through
    grad_res_b = to_bf16(grad_residual)
    out_grad = weight_rows(attended_flat, grad_res_b)
    grad_attended = to_bf16(jnp.dot(grad_res_b, full_out.T, preferred_element_type=f32))
    grad_attended = grad_attended.reshape(row_count, KV_HEADS, group_size, HEAD_DIM)
    grad_probs = jnp.einsum("tkgd,skd->kgts", grad_attended, all_values, preferred_element_type=f32)
    delta = jnp.sum(grad_attended.astype(f32) * attended.astype(f32), axis=-1)
    delta = jnp.transpose(delta, (1, 2, 0))[..., None]
    grad_scores = to_bf16(probs * (grad_probs - delta) * score_scale)
    grad_query_rot = jnp.einsum("kgts,skd->tkgd", grad_scores, all_keys, preferred_element_type=f32)
    key_part = jnp.einsum("kgts,tkgd->skd", grad_scores, query_rot, preferred_element_type=f32)
    value_part = jnp.einsum("kgts,tkgd->skd", probs_b, grad_attended, preferred_element_type=f32)
    key_parts = jnp.concatenate(
        [
            key_part.reshape(row_count * lax.axis_size("ctx"), key_width),
            value_part.reshape(row_count * lax.axis_size("ctx"), key_width),
        ],
        -1,
    )
    if lax.axis_size("ctx") == 2:
        key_local = key_parts[:row_count] + other(key_parts[row_count:])
    else:
        key_local = lax.psum_scatter(key_parts, "ctx", scatter_dimension=0, tiled=True)
    grad_key_rot = key_local[:, :key_width].reshape(row_count, KV_HEADS, HEAD_DIM)
    grad_value = key_local[:, key_width:]
    grad_query = grad_query_rot * cos_query + rotate_back(grad_query_rot * sin_query)
    grad_key = grad_key_rot * cos_key + rotate_back(grad_key_rot * sin_key)
    grad_projected = jnp.concatenate(
        [
            grad_query.reshape(row_count, query_width),
            grad_key.reshape(row_count, key_width),
            grad_value,
        ],
        -1,
    )
    bias_grad = jnp.sum(grad_projected, axis=0)
    grad_proj_b = to_bf16(grad_projected)
    grad_first = jnp.dot(grad_proj_b, full_qkv.T, preferred_element_type=f32)
    grad_input_part, gain_one_grad = rms_backward(
        grad_first, normed_one, scale_one, gain_one.astype(f32)
    )
    input_row_grad = grad_residual + grad_input_part
    small = jnp.concatenate(
        [
            bias_grad.reshape(parts, -1),
            gain_one_grad.reshape(parts, -1),
            gain_two_grad.reshape(parts, -1),
        ],
        -1,
    )
    small = jnp.pad(small, ((0, 0), (0, qkv_columns - small.shape[1])))[:, None]
    grad_rows = (depth + 8) // 8 * 8
    packed_grad = jnp.concatenate(
        [
            contract_rows(first_in, grad_proj_b).reshape(parts, depth, qkv_columns),
            small,
            jnp.zeros((parts, grad_rows - depth - 1, qkv_columns), f32),
        ],
        1,
    ).reshape(parts * grad_rows, qkv_columns)
    packed_grad, output_row = lax.optimization_barrier((packed_grad, output_row))
    packed_sum = sum_ctx(lax.psum_scatter(packed_grad, "seq", scatter_dimension=0, tiled=True))
    result_qkv = packed_sum[:depth]
    result_bias = packed_sum[depth, :bias_count]
    result_gain_one = packed_sum[depth, bias_count : bias_count + depth]
    result_gain_two = packed_sum[depth, bias_count + depth : bias_count + 2 * depth]
    result_out = sum_ctx(out_grad)
    return (
        output_row[None],
        input_row_grad[None],
        result_qkv,
        result_bias,
        result_out,
        result_gate_up,
        result_down,
        result_gain_one,
        result_gain_two,
    )


def solution(mesh):
    in_specs = (
        P("seq", "ctx", None),
        P("seq", None),
        P("seq", "ctx", None),
        P("seq", None),
        P("seq"),
        P("seq", None),
        P("seq", None),
        P("seq", None),
        P("seq"),
        P("seq"),
    )
    out_specs = (
        P("seq", "ctx", None),
        P("seq", "ctx", None),
        P("seq", None),
        P("seq"),
        P("seq", None),
        P("seq", None),
        P("seq", None),
        P("seq"),
        P("seq"),
    )
    fast = mesh.shape["ctx"] == 2 and mesh.shape["seq"] == 16
    return jax.shard_map(shards_fast if fast else shards, mesh=mesh, in_specs=in_specs, out_specs=out_specs, check_vma=False)
```

```python
import functools

import jax
import jax.numpy as jnp
from jax import lax
from jax.experimental import pallas as pl
from jax.experimental.pallas import tpu as pltpu
from jax.sharding import PartitionSpec as P

HEADS = 14
KV_HEADS = 2
HEAD_DIM = 64


EPS = 1e-06
ROPE_BASE = 1000000.0


def to_bf16(values):
    return lax.optimization_barrier(values.astype(jnp.bfloat16))


def rope_tables(position_row):
    half_dim = HEAD_DIM // 2
    exponent = jnp.arange(half_dim, dtype=jnp.float32) * (2.0 / HEAD_DIM)
    inverse = ROPE_BASE ** (-exponent)
    angles = position_row.astype(jnp.float32)[:, None] * inverse[None, :]
    cosine_table = jnp.cos(angles)
    sine_table = jnp.sin(angles)
    return (
        jnp.concatenate([cosine_table, cosine_table], -1),
        jnp.concatenate([sine_table, sine_table], -1),
    )


def rotate_half(values):
    half_dim = values.shape[-1] // 2
    return jnp.concatenate([-values[..., half_dim:], values[..., :half_dim]], -1)


def rotate_back(values):
    half_dim = values.shape[-1] // 2
    return jnp.concatenate([values[..., half_dim:], -values[..., :half_dim]], -1)


def rms_forward(values):
    scaling = lax.rsqrt(jnp.mean(values * values, axis=-1, keepdims=True) + EPS)
    return (values * scaling, scaling)


def rms_backward(grad_normed, normed, scaling, gain_float):
    gain_grad = jnp.sum(grad_normed * normed, axis=0)
    grad_scaled = grad_normed * gain_float
    inner = jnp.mean(grad_scaled * normed, axis=-1, keepdims=True)
    return (scaling * (grad_scaled - normed * inner), gain_grad)


def weight_rows(left_side, right_side):
    return lax.psum_scatter(
        lax.dot_general(
            left_side, right_side, (((0,), (0,)), ((), ())), preferred_element_type=jnp.float32
        ),
        "seq",
        scatter_dimension=0,
        tiled=True,
    )


def columns_from_rows(rows, parts):
    depth = rows.shape[0]
    hidden = rows.shape[1] // (2 * parts)
    split = jnp.transpose(rows.reshape(depth, 2, parts, hidden), (2, 0, 1, 3))
    split = split.reshape(parts, depth, 2 * hidden)
    moved = lax.all_to_all(split, "seq", split_axis=0, concat_axis=0, tiled=True)
    return moved.reshape(parts * depth, 2 * hidden)


def rows_from_columns(columns, parts):
    depth = columns.shape[0] // parts
    hidden = columns.shape[1] // 2
    split = columns.reshape(parts, depth, 2 * hidden)
    moved = lax.all_to_all(split, "seq", split_axis=0, concat_axis=0, tiled=True)
    moved = jnp.transpose(moved.reshape(parts, depth, 2, hidden), (1, 2, 0, 3))
    return moved.reshape(depth, 2 * parts * hidden)


def contract_rows(left_side, right_side):
    return lax.dot_general(
        left_side, right_side, (((0,), (0,)), ((), ())), preferred_element_type=jnp.float32
    )


def contract_columns(left_side, right_side):
    return lax.dot_general(
        left_side, right_side, (((1,), (1,)), ((), ())), preferred_element_type=jnp.float32
    )


def scatter_tokens(partial):
    total = lax.psum_scatter(to_bf16(partial), "seq", scatter_dimension=0, tiled=True)
    return total.astype(jnp.float32)


def gather_kernel(outer, own_ref, all_ref, local_sem, outer_sems, middle_sems, core_sems):
    me = lax.axis_index("seq")
    at_outer = me // 4
    middle = (me // 2) % 2
    core = me % 2
    rows = own_ref.shape[0]

    def place(outer_at, middle_at, core_at):
        index = outer_at * 4 + middle_at * 2 + core_at
        return all_ref.at[pl.ds(pl.multiple_of(index * rows, rows), rows)]

    def remote(source, target, sems, slot, device):
        return pltpu.make_async_remote_copy(
            src_ref=source,
            dst_ref=target,
            send_sem=sems.at[0, slot],
            recv_sem=sems.at[1, slot],
            device_id={"seq": device},
            device_id_type=pl.DeviceIdType.MESH,
        )

    middle_partner = at_outer * 4 + (1 - middle) * 2 + core
    core_partner = at_outer * 4 + middle * 2 + (1 - core)
    outer_partners = [
        ((at_outer + step) % outer) * 4 + middle * 2 + core for step in range(1, outer)
    ]
    barrier = pltpu.get_barrier_semaphore()
    for device in [middle_partner, core_partner] + outer_partners:
        pl.semaphore_signal(
            barrier, inc=1, device_id={"seq": device}, device_id_type=pl.DeviceIdType.MESH
        )
    pl.semaphore_wait(barrier, outer + 1)

    own_place = place(at_outer, middle, core)
    local = pltpu.make_async_copy(own_ref, own_place, local_sem)
    local.start()
    started = []
    outer_copies = []
    for step in range(1, outer):
        copy = remote(own_ref, own_place, outer_sems, step - 1, outer_partners[step - 1])
        copy.start()
        outer_copies.append(copy)
    middle_copies = []
    for step in range(outer):
        source_outer = (at_outer + outer - step) % outer
        here = place(source_outer, middle, core)
        if step == 0:
            source = own_ref
        else:
            outer_copies[step - 1].wait_recv()
            source = here
        copy = remote(source, here, middle_sems, step, middle_partner)
        copy.start()
        middle_copies.append(copy)
        copy = remote(source, here, core_sems, 2 * step, core_partner)
        copy.start()
        started.append(copy)
    for step in range(outer):
        source_outer = (at_outer + outer - step) % outer
        middle_copies[step].wait_recv()
        here = place(source_outer, 1 - middle, core)
        copy = remote(here, here, core_sems, 2 * step + 1, core_partner)
        copy.start()
        started.append(copy)
    for copy in started:
        copy.wait_recv()
    for copy in outer_copies + middle_copies + started:
        copy.wait_send()
    local.wait()


def gather_rows(rows, collective_id):
    parts = lax.axis_size("seq")
    if parts % 4:
        return lax.all_gather(rows, "seq", axis=0, tiled=True)
    outer = parts // 4
    return pl.pallas_call(
        functools.partial(gather_kernel, outer),
        out_shape=jax.ShapeDtypeStruct((parts * rows.shape[0], rows.shape[1]), rows.dtype),
        in_specs=[pl.BlockSpec(memory_space=pltpu.VMEM)],
        out_specs=pl.BlockSpec(memory_space=pltpu.VMEM),
        scratch_shapes=[
            pltpu.SemaphoreType.DMA,
            pltpu.SemaphoreType.DMA((2, max(outer - 1, 1))),
            pltpu.SemaphoreType.DMA((2, outer)),
            pltpu.SemaphoreType.DMA((2, 2 * outer)),
        ],
        compiler_params=pltpu.CompilerParams(
            collective_id=collective_id, has_side_effects=True, vmem_limit_bytes=24 * 2**20
        ),
    )(rows)


def packed_height(depth):
    return (depth + 16) // 16 * 16


def other(values):
    return lax.ppermute(values, "ctx", [(0, 1), (1, 0)])


def sum_rounded(values):
    if lax.axis_size("ctx") != 2:
        return lax.psum(values, "ctx")
    mine = to_bf16(values)
    return mine.astype(jnp.float32) + other(mine).astype(jnp.float32)


def sum_ctx(values):
    if lax.axis_size("ctx") != 2:
        return lax.psum(values, "ctx")
    return values + other(values)


MESH = pl.DeviceIdType.MESH
LANES = 128


def padded(width):
    return (width + LANES - 1) // LANES * LANES


def remote_copy(source, target, send_sem, recv_sem, device):
    return pltpu.make_async_remote_copy(
        src_ref=source,
        dst_ref=target,
        send_sem=send_sem,
        recv_sem=recv_sem,
        device_id=device,
        device_id_type=MESH,
    )


def greet(devices):
    barrier = pltpu.get_barrier_semaphore()
    for device in devices:
        pl.semaphore_signal(barrier, inc=1, device_id=device, device_id_type=MESH)
    pl.semaphore_wait(barrier, len(devices))


def dot_last(left, right):
    return lax.dot_general(
        left, right, (((1,), (1,)), ((), ())), preferred_element_type=jnp.float32
    )


def dot_first(left, right):
    return lax.dot_general(
        left, right, (((0,), (0,)), ((), ())), preferred_element_type=jnp.float32
    )


def z_order(z):
    return (z + 1 - 2 * (z % 2), 2 - z // 2, 3 - 3 * (z // 2))


class Place:
    def __init__(self):
        me = lax.axis_index("seq")
        self.z = me // 4
        self.y = (me // 2) % 2
        self.k = me % 2
        self.c = lax.axis_index("ctx")
        self.me = me

    def seq(self, z, y, k):
        return {"seq": z * 4 + y * 2 + k}

    def others(self):
        z, y, k = self.z, self.y, self.k
        return (
            [self.seq(z, 1 - y, k), self.seq(z, y, 1 - k)]
            + [self.seq(other, y, k) for other in z_order(z)]
        )


class Gather:
    def __init__(self, at, own_ref, all_ref, send_sems, recv_sems, local_sem):
        self.at, self.own, self.all = at, own_ref, all_ref
        self.send_sems, self.recv_sems, self.local_sem = send_sems, recv_sems, local_sem
        self.rows = own_ref.shape[0]
        self.sent = []
        self.hop_sent = []

    def block(self, z, y, k):
        start = pl.multiple_of((z * 4 + y * 2 + k) * self.rows, self.rows)
        return self.all.at[pl.ds(start, self.rows)]

    def copy(self, source, z, y, k, kind, device, slot=None):
        return remote_copy(
            source,
            self.block(z, y, k),
            self.send_sems.at[z, kind if slot is None else slot],
            self.recv_sems.at[z, kind],
            device,
        )

    def to_y_and_core(self, source, z):
        at = self.at
        copy = self.copy(source, z, at.y, at.k, 1, at.seq(at.z, 1 - at.y, at.k))
        copy.start()
        self.sent.append(copy)
        self.to_core(source, z, at.y)

    def to_core(self, source, z, y):
        at = self.at
        copy = self.copy(source, z, y, at.k, 2 + y, at.seq(at.z, at.y, 1 - at.k))
        copy.start()
        self.sent.append(copy)

    def hop(self, source, z, right):
        at = self.at
        target = at.z + 1 if right else at.z - 1
        copy = self.copy(
            source, z, at.y, at.k, 0, at.seq(target, at.y, at.k), slot=None if right else 4
        )
        ok = (target < 4) if right else (target >= 0)
        return ok, copy

    def begin(self):
        at = self.at
        for right in (True, False):
            ok, copy = self.hop(self.own, at.z, right)
            self.hop_sent.append((ok, copy))

            @pl.when(ok)
            def _():
                copy.start()

        self.to_y_and_core(self.own, at.z)
        self.local = pltpu.make_async_copy(
            self.own, self.block(at.z, at.y, at.k), self.local_sem
        )
        self.local.start()

    def from_z(self, z):
        at = self.at
        here = self.block(z, at.y, at.k)
        self.copy(here, z, at.y, at.k, 0, at.seq(at.z, 1 - at.y, at.k)).wait_recv()
        for right in (True, False):
            ok, copy = self.hop(here, z, right)
            ok = jnp.logical_and(ok, z < at.z if right else z > at.z)
            self.hop_sent.append((ok, copy))

            @pl.when(ok)
            def _():
                copy.start()

        self.to_y_and_core(here, z)

    def from_y(self, z):
        at = self.at
        here = self.block(z, 1 - at.y, at.k)
        self.copy(here, z, 1 - at.y, at.k, 1, at.seq(at.z, 1 - at.y, at.k)).wait_recv()
        self.to_core(here, z, 1 - at.y)

    def from_core(self, z):
        at = self.at
        for y in range(2):
            here = self.block(z, y, 1 - at.k)
            self.copy(here, z, y, 1 - at.k, 2 + y, at.seq(at.z, at.y, 1 - at.k)).wait_recv()

    def end(self):
        for copy in self.sent:
            copy.wait_send()
        for ok, copy in self.hop_sent:

            @pl.when(ok)
            def _():
                copy.wait_send()


class Scatter:
    def __init__(self, at, part, core_buf, y_buf, z_buf, out_ref, send_sems, recv_sems):
        self.at, self.part, self.out = at, part, out_ref
        self.core_buf, self.y_buf, self.z_buf = core_buf, y_buf, z_buf
        self.send_sems, self.recv_sems = send_sems, recv_sems
        self.rows = out_ref.shape[0]
        self.sent = []
        self.core_copies = {}

    def block(self, z, y, k):
        start = pl.multiple_of((z * 4 + y * 2 + k) * self.rows, self.rows)
        return self.part.at[pl.ds(start, self.rows)]

    def core_copy(self, z, y):
        at = self.at
        return remote_copy(
            self.block(z, y, 1 - at.k),
            self.core_buf.at[z, y],
            self.send_sems.at[z, y],
            self.recv_sems.at[z, y],
            at.seq(at.z, at.y, 1 - at.k),
        )

    def to_core(self, z):
        for y in range(2):
            copy = self.core_copy(z, y)
            copy.start()
            self.sent.append(copy)

    def y_copy(self, z):
        at = self.at
        return remote_copy(
            self.block(z, 1 - at.y, at.k),
            self.y_buf.at[z],
            self.send_sems.at[z, 2],
            self.recv_sems.at[z, 2],
            at.seq(at.z, 1 - at.y, at.k),
        )

    def add_core(self, z, y):
        at = self.at
        here = self.block(z, y, at.k)
        total = here[...].astype(jnp.float32) + self.core_buf[z, y].astype(jnp.float32)
        here[...] = total.astype(jnp.bfloat16)

    def to_y(self, z):
        at = self.at
        for y in range(2):
            self.core_copy(z, y).wait_recv()
        self.add_core(z, 1 - at.y)
        copy = self.y_copy(z)
        copy.start()
        self.sent.append(copy)
        self.add_core(z, at.y)

    def z_copy(self, z, source_z):
        at = self.at
        return remote_copy(
            self.block(z, at.y, at.k),
            self.z_buf.at[source_z],
            self.send_sems.at[z, 3],
            self.recv_sems.at[source_z, 3],
            at.seq(z, at.y, at.k),
        )

    def to_z(self, z, own):
        at = self.at
        self.y_copy(z).wait_recv()
        here = self.block(z, at.y, at.k)
        total = here[...].astype(jnp.float32) + self.y_buf[z].astype(jnp.float32)
        if own:
            self.out[...] = total
        else:
            here[...] = total.astype(jnp.bfloat16)
            copy = self.z_copy(z, at.z)
            copy.start()
            self.sent.append(copy)

    def finish(self):
        at = self.at
        total = self.out[...]
        for z in z_order(at.z):
            remote_copy(
                self.block(z, at.y, at.k),
                self.z_buf.at[z],
                self.send_sems.at[z, 3],
                self.recv_sems.at[z, 3],
                at.seq(z, at.y, at.k),
            ).wait_recv()
            total += self.z_buf[z].astype(jnp.float32)
        self.out[...] = total

    def end(self):
        for copy in self.sent:
            copy.wait_send()


def ffn_kernel(
    own_ref,
    cot_ref,
    weight_ref,
    down_ref,
    second_sum_ref,
    down_sum_ref,
    down_grad_ref,
    gate_grad_ref,
    all_ref,
    act_ref,
    grad_ref,
    part_ref,
    core_buf,
    y_buf,
    z_buf,
    flat_ref,
    gate_send,
    gate_recv,
    down_send,
    down_recv,
    gather_send,
    gather_recv,
    local_sem,
    scatter_send,
    scatter_recv,
    x_send,
    x_recv,
):
    at = Place()
    width = down_ref.shape[0]
    rows = own_ref.shape[0]
    parts = all_ref.shape[0] // rows
    depth = weight_ref.shape[0] // parts
    other_ctx = {"ctx": 1 - at.c}
    greet(at.others() + [other_ctx])
    gather = Gather(at, own_ref, all_ref, gather_send, gather_recv, local_sem)
    scatters = [
        Scatter(
            at,
            part_ref.at[which],
            core_buf.at[which],
            y_buf.at[which],
            z_buf.at[which],
            (second_sum_ref, down_sum_ref)[which],
            scatter_send.at[which],
            scatter_recv.at[which],
        )
        for which in range(2)
    ]
    second, down = scatters
    tile = 2 * rows

    def compute(z):
        def step(index, carry):
            start = pl.multiple_of(z * (4 * rows) + index * tile, tile)
            here = pl.ds(start, tile)
            gate_up = jnp.dot(
                all_ref[here], weight_ref[...], preferred_element_type=jnp.float32
            )
            grad_act = dot_last(cot_ref[here], down_ref[...])
            gate = gate_up[:, :width]
            upward = gate_up[:, width:]
            sigmoid_gate = jax.nn.sigmoid(gate)
            silu = gate * sigmoid_gate
            activated = (silu * upward).astype(jnp.bfloat16)
            act_ref[here] = activated
            grad_gate = grad_act * upward * sigmoid_gate * (1.0 + gate * (1.0 - sigmoid_gate))
            grad_ref[here, :width] = grad_gate.astype(jnp.bfloat16)
            grad_ref[here, width:] = (grad_act * silu).astype(jnp.bfloat16)
            part_ref[0, here] = dot_last(grad_ref[here], weight_ref[...]).astype(jnp.bfloat16)
            part_ref[1, here] = jnp.dot(
                activated, down_ref[...], preferred_element_type=jnp.float32
            ).astype(jnp.bfloat16)
            return carry

        lax.fori_loop(0, 2, step, 0)

    order = (at.z,) + z_order(at.z)
    gather.begin()
    for index, z in enumerate(order):
        if index + 1 < len(order):
            gather.from_z(order[index + 1])
        gather.from_y(z)
        if index == 0:
            gather.local.wait()
        gather.from_core(z)
        if index > 0:
            second.to_y(order[index - 1])
        compute(z)
        second.to_core(z)
        if index > 0:
            second.to_z(order[index - 1], index == 1)
    last = order[-1]
    down_grad = dot_first(act_ref[...], cot_ref[...])
    down_send[...] = down_grad.astype(jnp.bfloat16)
    down_copy = remote_copy(down_send, down_recv, x_send.at[0], x_recv.at[0], other_ctx)
    down_copy.start()
    second.to_y(last)
    down.to_core(order[0])
    down.to_core(order[1])
    half = lane_tile = LANES

    def gate_tile(index, carry):
        columns = pl.ds(pl.multiple_of(index * lane_tile, lane_tile), lane_tile)
        flat_ref[columns] = dot_first(all_ref[:, columns], grad_ref[...])
        return carry

    lax.fori_loop(0, all_ref.shape[1] // lane_tile, gate_tile, 0)
    second.to_z(last, False)
    down.to_y(order[0])
    down.to_y(order[1])
    down.to_core(order[2])
    down.to_core(order[3])

    def columns_of(ctx):
        return pl.ds(pl.multiple_of(ctx * width, LANES), width)

    for part in range(parts):
        gate_send[part] = flat_ref[
            part * depth : (part + 1) * depth, columns_of(1 - at.c)
        ].astype(jnp.bfloat16)
    gate_copy = remote_copy(gate_send, gate_recv, x_send.at[1], x_recv.at[1], other_ctx)
    gate_copy.start()
    down.to_z(order[0], True)
    down.to_z(order[1], False)
    down.to_y(order[2])
    down.to_y(order[3])
    down.to_z(order[2], False)
    second.finish()
    down.to_z(order[3], False)
    down_copy.wait_recv()
    hidden = down_grad_ref.shape[0]
    down_grad_ref[...] = (
        down_send[:hidden].astype(jnp.float32) + down_recv[:hidden].astype(jnp.float32)
    )
    gate_copy.wait_recv()
    for part in range(parts):
        mine = flat_ref[part * depth : (part + 1) * depth, columns_of(at.c)]
        mine = mine.astype(jnp.bfloat16).astype(jnp.float32)
        gate_grad_ref[part] = (mine + gate_recv[part].astype(jnp.float32)).astype(jnp.bfloat16)
    down.finish()
    down_copy.wait_send()
    gate_copy.wait_send()
    gather.end()
    for scatter in scatters:
        scatter.end()


def ffn(second_in, all_cot, weight, down, hidden, collective_id):
    rows, model = second_in.shape
    parts = all_cot.shape[0] // rows
    width = down.shape[0]
    depth = model // parts
    tokens = parts * rows
    f32, bf16 = jnp.float32, jnp.bfloat16
    vmem = pl.BlockSpec(memory_space=pltpu.VMEM)
    flops = 2 * tokens * model * width * 9
    return pl.pallas_call(
        ffn_kernel,
        out_shape=(
            jax.ShapeDtypeStruct((rows, model), f32),
            jax.ShapeDtypeStruct((rows, model), f32),
            jax.ShapeDtypeStruct((hidden, model), f32),
            jax.ShapeDtypeStruct((parts, depth, width), bf16),
        ),
        in_specs=[vmem] * 4,
        out_specs=(vmem,) * 4,
        scratch_shapes=[
            pltpu.VMEM((tokens, model), bf16),
            pltpu.VMEM((tokens, width), bf16),
            pltpu.VMEM((tokens, 2 * width), bf16),
            pltpu.VMEM((2, tokens, model), bf16),
            pltpu.VMEM((2, 4, 2, rows, model), bf16),
            pltpu.VMEM((2, 4, rows, model), bf16),
            pltpu.VMEM((2, 4, rows, model), bf16),
            pltpu.VMEM((model, 2 * width), f32),
            pltpu.VMEM((parts, depth, width), bf16),
            pltpu.VMEM((parts, depth, width), bf16),
            pltpu.VMEM((width, model), bf16),
            pltpu.VMEM((width, model), bf16),
            pltpu.SemaphoreType.DMA((4, 5)),
            pltpu.SemaphoreType.DMA((4, 4)),
            pltpu.SemaphoreType.DMA,
            pltpu.SemaphoreType.DMA((2, 4, 4)),
            pltpu.SemaphoreType.DMA((2, 4, 4)),
            pltpu.SemaphoreType.DMA((2,)),
            pltpu.SemaphoreType.DMA((2,)),
        ],
        compiler_params=pltpu.CompilerParams(
            collective_id=collective_id, has_side_effects=True, vmem_limit_bytes=48 * 2**20
        ),
        cost_estimate=pl.CostEstimate(
            flops=flops, bytes_accessed=16 * 2**20, transcendentals=tokens * width
        ),
    )(second_in, all_cot, weight, down)


class Flow:
    def __init__(self, at, source, out_ref, bufs, sems, x_first, halves):
        self.at, self.source, self.out = at, source, out_ref
        (self.core_recv, self.x_send, self.x_recv, self.y_send, self.y_recv,
         self.z_send, self.z_recv, self.last_send, self.last_recv) = bufs
        self.sems = sems
        self.x_first, self.halves = x_first, halves
        rows = source.shape[3]
        self.count = rows // 2 if halves else rows
        self.mine = self.half(at.c) if halves else pl.ds(0, rows)
        self.theirs = self.half(1 - at.c) if halves else pl.ds(0, rows)
        self.all_rows = pl.ds(0, rows)
        self.sent = []

    def half(self, ctx):
        return pl.ds(pl.multiple_of(ctx * self.count, self.count), self.count)

    def send(self, source, target, slot, device, recv_slot=None):
        copy = remote_copy(
            source,
            target,
            self.sems.at[0, slot],
            self.sems.at[1, slot if recv_slot is None else recv_slot],
            device,
        )
        copy.start()
        self.sent.append(copy)
        return copy

    def begin(self):
        at = self.at
        self.core = self.send(
            self.source.at[1 - at.k], self.core_recv, 0, at.seq(at.z, at.y, 1 - at.k)
        )

    def add_core(self):
        at = self.at
        self.core.wait_recv()
        for z in range(4):
            for y in range(2):
                self.source[at.k, z, y] += self.core_recv[z, y]
        if self.x_first:
            self.to_x_both()
        else:
            self.to_y()

    def to_x_both(self):
        at = self.at
        for z in range(4):
            for y in range(2):
                self.x_send[z, y] = self.source[at.k, z, y, self.theirs].astype(self.x_send.dtype)
        self.x = self.send(self.x_send, self.x_recv, 1, {"ctx": 1 - at.c})

    def to_y(self):
        at = self.at
        rows = self.mine if self.x_first else self.all_rows
        for z in range(4):
            self.y_send[z] = self.source[at.k, z, 1 - at.y, rows].astype(self.y_send.dtype)
        self.y = self.send(self.y_send, self.y_recv, 2, at.seq(at.z, 1 - at.y, at.k))

    def second(self):
        at = self.at
        if self.x_first:
            self.x.wait_recv()
            for z in range(4):
                for y in range(2):
                    self.source[at.k, z, y, self.mine] += self.x_recv[z, y].astype(jnp.float32)
            self.to_y()
        else:
            self.y.wait_recv()
            for z in range(4):
                self.source[at.k, z, at.y] += self.y_recv[z].astype(jnp.float32)
            for z in range(4):
                self.x_send[z] = self.source[at.k, z, at.y, self.theirs].astype(self.x_send.dtype)
            self.x = self.send(self.x_send, self.x_recv, 1, {"ctx": 1 - at.c})

    def to_z(self):
        at = self.at
        (self.y if self.x_first else self.x).wait_recv()
        arrived = self.y_recv if self.x_first else self.x_recv
        for z in range(4):
            total = self.source[at.k, z, at.y, self.mine] + arrived[z].astype(jnp.float32)
            self.source[at.k, z, at.y, self.mine] = total
            self.z_send[z] = total.astype(self.z_send.dtype)
        for index, z in enumerate(z_order(at.z)):
            self.send(
                self.z_send.at[z], self.z_recv.at[at.z], 3 + z, at.seq(z, at.y, at.k), 3 + at.z
            )

    def finish(self):
        at = self.at
        total = self.source[at.k, at.z, at.y, self.mine]
        for z in z_order(at.z):
            remote_copy(
                self.z_send.at[z],
                self.z_recv.at[z],
                self.sems.at[0, 3 + z],
                self.sems.at[1, 3 + z],
                at.seq(z, at.y, at.k),
            ).wait_recv()
            total += self.z_recv[z].astype(jnp.float32)
        self.out[self.mine] = total
        if self.halves:
            self.last_send[...] = total
            self.last = self.send(self.last_send, self.last_recv, 7, {"ctx": 1 - at.c})

    def end(self):
        if self.halves:
            self.last.wait_recv()
            self.out[self.theirs] = self.last_recv[...]
        for copy in self.sent:
            copy.wait_send()


def flow_scratch(rows, width, x_first, halves, dtype):
    f32 = jnp.float32
    count = rows // 2 if halves else rows
    x_shape = (4, 2, count, width) if x_first else (4, count, width)
    y_shape = (4, count if x_first else rows, width)
    z_shape = (4, count, width)
    last = (count, width) if halves else (8, LANES)
    return [
        pltpu.VMEM((2, 4, 2, rows, width), f32),
        pltpu.VMEM((4, 2, rows, width), f32),
        pltpu.VMEM(x_shape, dtype),
        pltpu.VMEM(x_shape, dtype),
        pltpu.VMEM(y_shape, dtype),
        pltpu.VMEM(y_shape, dtype),
        pltpu.VMEM(z_shape, dtype),
        pltpu.VMEM(z_shape, dtype),
        pltpu.VMEM(last, f32),
        pltpu.VMEM(last, f32),
        pltpu.SemaphoreType.DMA((2, 8)),
    ]


def grads_kernel(
    first_ref,
    grad_proj_ref,
    attended_ref,
    grad_res_ref,
    small_ref,
    gate_ref,
    qkv_out_ref,
    out_out_ref,
    small_out_ref,
    gate_out_ref,
    *scratch,
):
    at = Place()
    flow_bufs = [scratch[11 * index : 11 * (index + 1)] for index in range(3)]
    flat_ref, out_flat_ref, gate_recv, half_ref, half_recv, gate_sems, half_sems = scratch[33:]
    parts, depth, width = gate_ref.shape
    hidden = gate_out_ref.shape[1] // (2 * parts)
    seq_peers = [lax.rem(at.me + step, parts) for step in range(1, parts)]
    greet([{"seq": peer} for peer in seq_peers] + [{"ctx": 1 - at.c}])
    qkv = Flow(at, flow_bufs[0][0], qkv_out_ref, flow_bufs[0][1:10], flow_bufs[0][10], True, True)
    out = Flow(at, flow_bufs[1][0], out_out_ref, flow_bufs[1][1:10], flow_bufs[1][10], False, True)
    small = Flow(
        at, flow_bufs[2][0], small_out_ref, flow_bufs[2][1:10], flow_bufs[2][10], True, False
    )

    def spread(flat, source):
        rows = source.shape[3]
        tail = jnp.zeros((rows - depth, source.shape[4]), jnp.float32)
        for part in range(parts):
            z, y, k = part // 4, (part // 2) % 2, part % 2
            source[k, z, y, :depth] = flat[part * depth : (part + 1) * depth]
            source[k, z, y, depth:] = tail

    gate_copies = []
    for step, peer in enumerate(seq_peers):
        copy = remote_copy(
            gate_ref.at[peer],
            gate_recv.at[at.me],
            gate_sems.at[0, step],
            gate_sems.at[1, step],
            {"seq": peer},
        )
        copy.start()
        gate_copies.append(copy)
    out_flat_ref[...] = dot_first(attended_ref[...], grad_res_ref[...])
    spread(out_flat_ref, out.source)
    out.begin()
    small.source[...] = small_ref[...]
    small.begin()
    flat_ref[...] = dot_first(first_ref[...], grad_proj_ref[...])
    spread(flat_ref, qkv.source)
    qkv.begin()
    out.add_core()
    small.add_core()
    qkv.add_core()
    out.second()
    small.second()
    qkv.second()
    out.to_z()
    small.to_z()
    gate_recv[at.me] = gate_ref[at.me]
    for step in range(1, parts):
        source = lax.rem(at.me + parts - step, parts)
        remote_copy(
            gate_ref.at[source],
            gate_recv.at[source],
            gate_sems.at[0, step - 1],
            gate_sems.at[1, step - 1],
            {"seq": source},
        ).wait_recv()
    for part in range(parts):
        half_ref[:, part * hidden : (part + 1) * hidden] = gate_recv[part, :, :hidden]
    half_copy = remote_copy(
        half_ref, half_recv, half_sems.at[0], half_sems.at[1], {"ctx": 1 - at.c}
    )
    half_copy.start()
    qkv.to_z()
    out.finish()
    small.finish()
    qkv.finish()
    whole = parts * hidden

    def columns_of(ctx):
        return pl.ds(pl.multiple_of(ctx * whole, LANES), whole)

    gate_out_ref[:, columns_of(at.c)] = half_ref[...].astype(jnp.float32)
    half_copy.wait_recv()
    gate_out_ref[:, columns_of(1 - at.c)] = half_recv[...].astype(jnp.float32)
    half_copy.wait_send()
    for copy in gate_copies:
        copy.wait_send()
    out.end()
    small.end()
    qkv.end()


def reduce_grads(
    first_in, grad_proj, attended, grad_res, small, gate_half, hidden, collective_id
):
    parts, depth, width = gate_half.shape
    f32, bf16 = jnp.float32, jnp.bfloat16
    rows = (depth + 31) // 32 * 32
    model, qkv_columns = first_in.shape[1], grad_proj.shape[1]
    out_columns = grad_res.shape[1]
    out_rows = attended.shape[1]
    whole = parts * hidden
    vmem = pl.BlockSpec(memory_space=pltpu.VMEM)
    return pl.pallas_call(
        grads_kernel,
        out_shape=(
            jax.ShapeDtypeStruct((rows, qkv_columns), f32),
            jax.ShapeDtypeStruct((rows, out_columns), f32),
            jax.ShapeDtypeStruct(small.shape[3:], f32),
            jax.ShapeDtypeStruct((depth, 2 * whole), f32),
        ),
        in_specs=[vmem] * 6,
        out_specs=(vmem,) * 4,
        scratch_shapes=flow_scratch(rows, qkv_columns, True, True, bf16)
        + flow_scratch(rows, out_columns, False, True, bf16)
        + flow_scratch(small.shape[3], small.shape[4], True, False, f32)
        + [
            pltpu.VMEM((model, qkv_columns), f32),
            pltpu.VMEM((out_rows, out_columns), f32),
            pltpu.VMEM((parts, depth, width), bf16),
            pltpu.VMEM((depth, whole), bf16),
            pltpu.VMEM((depth, whole), bf16),
            pltpu.SemaphoreType.DMA((2, parts - 1)),
            pltpu.SemaphoreType.DMA((2,)),
        ],
        compiler_params=pltpu.CompilerParams(
            collective_id=collective_id, has_side_effects=True, vmem_limit_bytes=52 * 2**20
        ),
    )(first_in, grad_proj, attended, grad_res, small, gate_half)


def shards(
    tokens,
    positions,
    cotangent,
    qkv_weight,
    qkv_bias,
    out_weight,
    gate_up_weight,
    down_weight,
    attn_gain,
    ffn_gain,
):
    f32 = jnp.float32
    qkv_columns = qkv_weight.shape[1]
    depth = qkv_weight.shape[0]
    bias_count = qkv_bias.shape[0]
    packed_rows = packed_height(depth)
    pair = jnp.concatenate([qkv_weight, out_weight], 1)
    extra = jnp.concatenate([qkv_bias, attn_gain, ffn_gain])
    extra = jnp.pad(extra, (0, pair.shape[1] - extra.shape[0]))[None]
    packed = jnp.concatenate(
        [pair, extra, jnp.zeros((packed_rows - depth - 1, pair.shape[1]), pair.dtype)], 0
    )
    packed = lax.all_gather(packed, "seq", axis=0, tiled=True).reshape(-1, packed_rows, pair.shape[1])
    full_qkv = packed[:, :depth, :qkv_columns].reshape(-1, qkv_columns)
    full_out = packed[:, :depth, qkv_columns:].reshape(-1, out_weight.shape[1])
    full_bias = packed[:, depth, :bias_count].reshape(-1)
    gain_one = packed[:, depth, bias_count : bias_count + depth].reshape(-1)
    gain_two = packed[:, depth, bias_count + depth : bias_count + 2 * depth].reshape(-1)
    parts = lax.axis_size("seq")
    hidden = down_weight.shape[0]
    own_gate_up = columns_from_rows(gate_up_weight, parts)
    all_cot = gather_rows(cotangent[0], 0)
    own_gate_up, all_cot, full_qkv = lax.optimization_barrier((own_gate_up, all_cot, full_qkv))
    inputs_f = tokens[0].astype(f32)
    cot_row = cotangent[0]
    row_count = inputs_f.shape[0]
    group_size = HEADS // KV_HEADS
    query_width = HEADS * HEAD_DIM
    key_width = KV_HEADS * HEAD_DIM
    score_scale = HEAD_DIM ** (-0.5)
    all_positions = positions[0]
    position_row = lax.dynamic_slice_in_dim(
        all_positions, lax.axis_index("ctx") * row_count, row_count, 0
    )
    normed_one, scale_one = rms_forward(inputs_f)
    first_in = to_bf16(normed_one * gain_one.astype(f32))
    projected = jnp.dot(first_in, full_qkv, preferred_element_type=f32) + full_bias.astype(f32)
    cosine_table, sine_table = rope_tables(position_row)
    cos_query = cosine_table[:, None, None, :]
    sin_query = sine_table[:, None, None, :]
    cos_key = cosine_table[:, None, :]
    sin_key = sine_table[:, None, :]
    query = projected[:, :query_width].reshape(row_count, KV_HEADS, group_size, HEAD_DIM)
    keys = projected[:, query_width : query_width + key_width].reshape(
        row_count, KV_HEADS, HEAD_DIM
    )
    values = projected[:, query_width + key_width :]
    query_rot = to_bf16(query * cos_query + rotate_half(query) * sin_query)
    key_rot = to_bf16(keys * cos_key + rotate_half(keys) * sin_key).reshape(row_count, key_width)
    value_b = to_bf16(values)
    both = jnp.concatenate([key_rot, value_b], -1)
    if lax.axis_size("ctx") == 2:
        both = jnp.concatenate([both, other(both)], 0)
        other_row = lax.dynamic_slice_in_dim(
            all_positions, (1 - lax.axis_index("ctx")) * row_count, row_count, 0
        )
        all_positions = jnp.concatenate([position_row, other_row])
    else:
        both = lax.all_gather(both, "ctx", axis=0, tiled=True)
    all_keys, all_values = both[:, :key_width], both[:, key_width:]
    all_keys = all_keys.reshape(-1, KV_HEADS, HEAD_DIM)
    all_values = all_values.reshape(-1, KV_HEADS, HEAD_DIM)
    scores = (
        jnp.einsum("tkgd,skd->kgts", query_rot, all_keys, preferred_element_type=f32) * score_scale
    )
    allowed = all_positions[None, :] <= position_row[:, None]
    scores = jnp.where(allowed, scores, -1e30)
    row_top = jnp.max(scores, axis=-1, keepdims=True)
    log_total = row_top + jnp.log(jnp.sum(jnp.exp(scores - row_top), axis=-1, keepdims=True))
    probs = jnp.exp(scores - log_total)
    probs_b = to_bf16(probs)
    attended = to_bf16(
        jnp.einsum("kgts,skd->tkgd", probs_b, all_values, preferred_element_type=f32)
    )
    attended_flat = attended.reshape(row_count, query_width)
    residual = inputs_f + jnp.dot(attended_flat, full_out, preferred_element_type=f32)
    normed_two, scale_two = rms_forward(residual)
    second_in = to_bf16(normed_two * gain_two.astype(f32))
    all_second = gather_rows(second_in, 1)
    gate_up = jnp.dot(all_second, own_gate_up, preferred_element_type=f32)
    gate = gate_up[:, :hidden]
    upward = gate_up[:, hidden:]
    sigmoid_gate = jax.nn.sigmoid(gate)
    activated = to_bf16(gate * sigmoid_gate * upward)
    grad_act = contract_columns(all_cot, down_weight)
    grad_gate = grad_act * upward * sigmoid_gate * (1.0 + gate * (1.0 - sigmoid_gate))
    grad_upward = grad_act * (gate * sigmoid_gate)
    grad_gate_up = to_bf16(jnp.concatenate([grad_gate, grad_upward], -1))
    grad_second = scatter_tokens(contract_columns(grad_gate_up, own_gate_up))
    down_sum = scatter_tokens(jnp.dot(activated, down_weight, preferred_element_type=f32))
    output_row = (residual + down_sum).astype(jnp.bfloat16)
    result_down = sum_rounded(contract_rows(activated, all_cot))
    result_gate_up = rows_from_columns(
        to_bf16(sum_rounded(contract_rows(all_second, grad_gate_up))), parts
    ).astype(f32)
    grad_through, gain_two_grad = rms_backward(
        grad_second, normed_two, scale_two, gain_two.astype(f32)
    )
    grad_residual = cot_row.astype(f32) + grad_through
    grad_res_b = to_bf16(grad_residual)
    out_grad = weight_rows(attended_flat, grad_res_b)
    grad_attended = to_bf16(jnp.dot(grad_res_b, full_out.T, preferred_element_type=f32))
    grad_attended = grad_attended.reshape(row_count, KV_HEADS, group_size, HEAD_DIM)
    grad_probs = jnp.einsum("tkgd,skd->kgts", grad_attended, all_values, preferred_element_type=f32)
    delta = jnp.sum(grad_attended.astype(f32) * attended.astype(f32), axis=-1)
    delta = jnp.transpose(delta, (1, 2, 0))[..., None]
    grad_scores = to_bf16(probs * (grad_probs - delta) * score_scale)
    grad_query_rot = jnp.einsum("kgts,skd->tkgd", grad_scores, all_keys, preferred_element_type=f32)
    key_part = jnp.einsum("kgts,tkgd->skd", grad_scores, query_rot, preferred_element_type=f32)
    value_part = jnp.einsum("kgts,tkgd->skd", probs_b, grad_attended, preferred_element_type=f32)
    key_parts = jnp.concatenate(
        [
            key_part.reshape(row_count * lax.axis_size("ctx"), key_width),
            value_part.reshape(row_count * lax.axis_size("ctx"), key_width),
        ],
        -1,
    )
    if lax.axis_size("ctx") == 2:
        key_local = key_parts[:row_count] + other(key_parts[row_count:])
    else:
        key_local = lax.psum_scatter(key_parts, "ctx", scatter_dimension=0, tiled=True)
    grad_key_rot = key_local[:, :key_width].reshape(row_count, KV_HEADS, HEAD_DIM)
    grad_value = key_local[:, key_width:]
    grad_query = grad_query_rot * cos_query + rotate_back(grad_query_rot * sin_query)
    grad_key = grad_key_rot * cos_key + rotate_back(grad_key_rot * sin_key)
    grad_projected = jnp.concatenate(
        [
            grad_query.reshape(row_count, query_width),
            grad_key.reshape(row_count, key_width),
            grad_value,
        ],
        -1,
    )
    bias_grad = jnp.sum(grad_projected, axis=0)
    grad_proj_b = to_bf16(grad_projected)
    grad_first = jnp.dot(grad_proj_b, full_qkv.T, preferred_element_type=f32)
    grad_input_part, gain_one_grad = rms_backward(
        grad_first, normed_one, scale_one, gain_one.astype(f32)
    )
    input_row_grad = grad_residual + grad_input_part
    small = jnp.concatenate(
        [
            bias_grad.reshape(parts, -1),
            gain_one_grad.reshape(parts, -1),
            gain_two_grad.reshape(parts, -1),
        ],
        -1,
    )
    small = jnp.pad(small, ((0, 0), (0, qkv_columns - small.shape[1])))[:, None]
    grad_rows = (depth + 8) // 8 * 8
    packed_grad = jnp.concatenate(
        [
            contract_rows(first_in, grad_proj_b).reshape(parts, depth, qkv_columns),
            small,
            jnp.zeros((parts, grad_rows - depth - 1, qkv_columns), f32),
        ],
        1,
    ).reshape(parts * grad_rows, qkv_columns)
    packed_grad, output_row = lax.optimization_barrier((packed_grad, output_row))
    packed_sum = sum_ctx(lax.psum_scatter(packed_grad, "seq", scatter_dimension=0, tiled=True))
    result_qkv = packed_sum[:depth]
    result_bias = packed_sum[depth, :bias_count]
    result_gain_one = packed_sum[depth, bias_count : bias_count + depth]
    result_gain_two = packed_sum[depth, bias_count + depth : bias_count + 2 * depth]
    result_out = sum_ctx(out_grad)
    return (
        output_row[None],
        input_row_grad[None],
        result_qkv,
        result_bias,
        result_out,
        result_gate_up,
        result_down,
        result_gain_one,
        result_gain_two,
    )


def shards_fast(
    tokens,
    positions,
    cotangent,
    qkv_weight,
    qkv_bias,
    out_weight,
    gate_up_weight,
    down_weight,
    attn_gain,
    ffn_gain,
):
    f32 = jnp.float32
    qkv_columns = qkv_weight.shape[1]
    depth = qkv_weight.shape[0]
    bias_count = qkv_bias.shape[0]
    packed_rows = packed_height(depth)
    pair = jnp.concatenate([qkv_weight, out_weight], 1)
    extra = jnp.concatenate([qkv_bias, attn_gain, ffn_gain])
    extra = jnp.pad(extra, (0, pair.shape[1] - extra.shape[0]))[None]
    packed = jnp.concatenate(
        [pair, extra, jnp.zeros((packed_rows - depth - 1, pair.shape[1]), pair.dtype)], 0
    )
    packed = lax.all_gather(packed, "seq", axis=0, tiled=True).reshape(-1, packed_rows, pair.shape[1])
    full_qkv = packed[:, :depth, :qkv_columns].reshape(-1, qkv_columns)
    full_out = packed[:, :depth, qkv_columns:].reshape(-1, out_weight.shape[1])
    full_bias = packed[:, depth, :bias_count].reshape(-1)
    gain_one = packed[:, depth, bias_count : bias_count + depth].reshape(-1)
    gain_two = packed[:, depth, bias_count + depth : bias_count + 2 * depth].reshape(-1)
    parts = lax.axis_size("seq")
    hidden = down_weight.shape[0]
    own_gate_up = columns_from_rows(gate_up_weight, parts)
    all_cot = gather_rows(cotangent[0], 0)
    own_gate_up, all_cot, full_qkv = lax.optimization_barrier((own_gate_up, all_cot, full_qkv))
    inputs_f = tokens[0].astype(f32)
    cot_row = cotangent[0]
    row_count = inputs_f.shape[0]
    group_size = HEADS // KV_HEADS
    query_width = HEADS * HEAD_DIM
    key_width = KV_HEADS * HEAD_DIM
    score_scale = HEAD_DIM ** (-0.5)
    all_positions = positions[0]
    position_row = lax.dynamic_slice_in_dim(
        all_positions, lax.axis_index("ctx") * row_count, row_count, 0
    )
    normed_one, scale_one = rms_forward(inputs_f)
    first_in = to_bf16(normed_one * gain_one.astype(f32))
    projected = jnp.dot(first_in, full_qkv, preferred_element_type=f32) + full_bias.astype(f32)
    cosine_table, sine_table = rope_tables(position_row)
    cos_query = cosine_table[:, None, None, :]
    sin_query = sine_table[:, None, None, :]
    cos_key = cosine_table[:, None, :]
    sin_key = sine_table[:, None, :]
    query = projected[:, :query_width].reshape(row_count, KV_HEADS, group_size, HEAD_DIM)
    keys = projected[:, query_width : query_width + key_width].reshape(
        row_count, KV_HEADS, HEAD_DIM
    )
    values = projected[:, query_width + key_width :]
    query_rot = to_bf16(query * cos_query + rotate_half(query) * sin_query)
    key_rot = to_bf16(keys * cos_key + rotate_half(keys) * sin_key).reshape(row_count, key_width)
    value_b = to_bf16(values)
    both = jnp.concatenate([key_rot, value_b], -1)
    if lax.axis_size("ctx") == 2:
        both = jnp.concatenate([both, other(both)], 0)
        other_row = lax.dynamic_slice_in_dim(
            all_positions, (1 - lax.axis_index("ctx")) * row_count, row_count, 0
        )
        all_positions = jnp.concatenate([position_row, other_row])
    else:
        both = lax.all_gather(both, "ctx", axis=0, tiled=True)
    all_keys, all_values = both[:, :key_width], both[:, key_width:]
    all_keys = all_keys.reshape(-1, KV_HEADS, HEAD_DIM)
    all_values = all_values.reshape(-1, KV_HEADS, HEAD_DIM)
    scores = (
        jnp.einsum("tkgd,skd->kgts", query_rot, all_keys, preferred_element_type=f32) * score_scale
    )
    allowed = all_positions[None, :] <= position_row[:, None]
    scores = jnp.where(allowed, scores, -1e30)
    row_top = jnp.max(scores, axis=-1, keepdims=True)
    log_total = row_top + jnp.log(jnp.sum(jnp.exp(scores - row_top), axis=-1, keepdims=True))
    probs = jnp.exp(scores - log_total)
    probs_b = to_bf16(probs)
    attended = to_bf16(
        jnp.einsum("kgts,skd->tkgd", probs_b, all_values, preferred_element_type=f32)
    )
    attended_flat = attended.reshape(row_count, query_width)
    residual = inputs_f + jnp.dot(attended_flat, full_out, preferred_element_type=f32)
    normed_two, scale_two = rms_forward(residual)
    second_in = to_bf16(normed_two * gain_two.astype(f32))
    down_sum_width = padded(hidden)
    extra_rows = down_sum_width - hidden
    weight_wide = jnp.pad(
        own_gate_up.reshape(-1, 2, hidden), ((0, 0), (0, 0), (0, extra_rows))
    ).reshape(-1, 2 * down_sum_width)
    down_wide = jnp.pad(down_weight, ((0, extra_rows), (0, 0)))
    grad_second, down_sum, result_down, gate_half = ffn(
        second_in, all_cot, weight_wide, down_wide, hidden, 1
    )
    output_row = (residual + down_sum).astype(jnp.bfloat16)
    grad_through, gain_two_grad = rms_backward(
        grad_second, normed_two, scale_two, gain_two.astype(f32)
    )
    grad_residual = cot_row.astype(f32) + grad_through
    grad_res_b = to_bf16(grad_residual)
    grad_attended = to_bf16(jnp.dot(grad_res_b, full_out.T, preferred_element_type=f32))
    grad_attended = grad_attended.reshape(row_count, KV_HEADS, group_size, HEAD_DIM)
    grad_probs = jnp.einsum("tkgd,skd->kgts", grad_attended, all_values, preferred_element_type=f32)
    delta = jnp.sum(grad_attended.astype(f32) * attended.astype(f32), axis=-1)
    delta = jnp.transpose(delta, (1, 2, 0))[..., None]
    grad_scores = to_bf16(probs * (grad_probs - delta) * score_scale)
    grad_query_rot = jnp.einsum("kgts,skd->tkgd", grad_scores, all_keys, preferred_element_type=f32)
    key_part = jnp.einsum("kgts,tkgd->skd", grad_scores, query_rot, preferred_element_type=f32)
    value_part = jnp.einsum("kgts,tkgd->skd", probs_b, grad_attended, preferred_element_type=f32)
    key_parts = jnp.concatenate(
        [
            key_part.reshape(row_count * lax.axis_size("ctx"), key_width),
            value_part.reshape(row_count * lax.axis_size("ctx"), key_width),
        ],
        -1,
    )
    if lax.axis_size("ctx") == 2:
        key_local = key_parts[:row_count] + other(key_parts[row_count:])
    else:
        key_local = lax.psum_scatter(key_parts, "ctx", scatter_dimension=0, tiled=True)
    grad_key_rot = key_local[:, :key_width].reshape(row_count, KV_HEADS, HEAD_DIM)
    grad_value = key_local[:, key_width:]
    grad_query = grad_query_rot * cos_query + rotate_back(grad_query_rot * sin_query)
    grad_key = grad_key_rot * cos_key + rotate_back(grad_key_rot * sin_key)
    grad_projected = jnp.concatenate(
        [
            grad_query.reshape(row_count, query_width),
            grad_key.reshape(row_count, key_width),
            grad_value,
        ],
        -1,
    )
    bias_grad = jnp.sum(grad_projected, axis=0)
    grad_proj_b = to_bf16(grad_projected)
    grad_first = jnp.dot(grad_proj_b, full_qkv.T, preferred_element_type=f32)
    grad_input_part, gain_one_grad = rms_backward(
        grad_first, normed_one, scale_one, gain_one.astype(f32)
    )
    input_row_grad = grad_residual + grad_input_part
    small = jnp.concatenate(
        [
            bias_grad.reshape(parts, -1),
            gain_one_grad.reshape(parts, -1),
            gain_two_grad.reshape(parts, -1),
        ],
        -1,
    )
    small_width = padded(small.shape[1])
    small = jnp.pad(small, ((0, 0), (0, small_width - small.shape[1])))[:, None]
    small = jnp.pad(small, ((0, 0), (0, 7), (0, 0))).reshape(4, 2, 2, 8, small_width)
    small = jnp.transpose(small, (2, 0, 1, 3, 4))
    qkv_sum, out_sum, small_sum, result_gate_up = reduce_grads(
        first_in, grad_proj_b, attended_flat, grad_res_b, small, gate_half, hidden, 2
    )
    result_qkv = qkv_sum[:depth]
    result_out = out_sum[:depth]
    result_bias = small_sum[0, :bias_count]
    result_gain_one = small_sum[0, bias_count : bias_count + depth]
    result_gain_two = small_sum[0, bias_count + depth : bias_count + 2 * depth]
    return (
        output_row[None],
        input_row_grad[None],
        result_qkv,
        result_bias,
        result_out,
        result_gate_up,
        result_down,
        result_gain_one,
        result_gain_two,
    )


def solution(mesh):
    in_specs = (
        P("seq", "ctx", None),
        P("seq", None),
        P("seq", "ctx", None),
        P("seq", None),
        P("seq"),
        P("seq", None),
        P("seq", None),
        P("seq", None),
        P("seq"),
        P("seq"),
    )
    out_specs = (
        P("seq", "ctx", None),
        P("seq", "ctx", None),
        P("seq", None),
        P("seq"),
        P("seq", None),
        P("seq", None),
        P("seq", None),
        P("seq"),
        P("seq"),
    )
    fast = mesh.shape["ctx"] == 2 and mesh.shape["seq"] == 16
    return jax.shard_map(shards_fast if fast else shards, mesh=mesh, in_specs=in_specs, out_specs=out_specs, check_vma=False)
```

```python
import functools

import jax
import jax.numpy as jnp
from jax import lax
from jax.experimental import pallas as pl
from jax.experimental.pallas import tpu as pltpu
from jax.sharding import PartitionSpec as P

HEADS = 14
KV_HEADS = 2
HEAD_DIM = 64


EPS = 1e-06
ROPE_BASE = 1000000.0


def to_bf16(values):
    return lax.optimization_barrier(values.astype(jnp.bfloat16))


def rope_tables(position_row):
    half_dim = HEAD_DIM // 2
    exponent = jnp.arange(half_dim, dtype=jnp.float32) * (2.0 / HEAD_DIM)
    inverse = ROPE_BASE ** (-exponent)
    angles = position_row.astype(jnp.float32)[:, None] * inverse[None, :]
    cosine_table = jnp.cos(angles)
    sine_table = jnp.sin(angles)
    return (
        jnp.concatenate([cosine_table, cosine_table], -1),
        jnp.concatenate([sine_table, sine_table], -1),
    )


def rotate_half(values):
    half_dim = values.shape[-1] // 2
    return jnp.concatenate([-values[..., half_dim:], values[..., :half_dim]], -1)


def rotate_back(values):
    half_dim = values.shape[-1] // 2
    return jnp.concatenate([values[..., half_dim:], -values[..., :half_dim]], -1)


def rms_forward(values):
    scaling = lax.rsqrt(jnp.mean(values * values, axis=-1, keepdims=True) + EPS)
    return (values * scaling, scaling)


def rms_backward(grad_normed, normed, scaling, gain_float):
    gain_grad = jnp.sum(grad_normed * normed, axis=0)
    grad_scaled = grad_normed * gain_float
    inner = jnp.mean(grad_scaled * normed, axis=-1, keepdims=True)
    return (scaling * (grad_scaled - normed * inner), gain_grad)


def weight_rows(left_side, right_side):
    return lax.psum_scatter(
        lax.dot_general(
            left_side, right_side, (((0,), (0,)), ((), ())), preferred_element_type=jnp.float32
        ),
        "seq",
        scatter_dimension=0,
        tiled=True,
    )


def columns_from_rows(rows, parts):
    depth = rows.shape[0]
    hidden = rows.shape[1] // (2 * parts)
    split = jnp.transpose(rows.reshape(depth, 2, parts, hidden), (2, 0, 1, 3))
    split = split.reshape(parts, depth, 2 * hidden)
    moved = lax.all_to_all(split, "seq", split_axis=0, concat_axis=0, tiled=True)
    return moved.reshape(parts * depth, 2 * hidden)


def rows_from_columns(columns, parts):
    depth = columns.shape[0] // parts
    hidden = columns.shape[1] // 2
    split = columns.reshape(parts, depth, 2 * hidden)
    moved = lax.all_to_all(split, "seq", split_axis=0, concat_axis=0, tiled=True)
    moved = jnp.transpose(moved.reshape(parts, depth, 2, hidden), (1, 2, 0, 3))
    return moved.reshape(depth, 2 * parts * hidden)


def contract_rows(left_side, right_side):
    return lax.dot_general(
        left_side, right_side, (((0,), (0,)), ((), ())), preferred_element_type=jnp.float32
    )


def contract_columns(left_side, right_side):
    return lax.dot_general(
        left_side, right_side, (((1,), (1,)), ((), ())), preferred_element_type=jnp.float32
    )


def scatter_tokens(partial):
    total = lax.psum_scatter(to_bf16(partial), "seq", scatter_dimension=0, tiled=True)
    return total.astype(jnp.float32)


def gather_kernel(outer, own_ref, all_ref, local_sem, outer_sems, middle_sems, core_sems):
    me = lax.axis_index("seq")
    at_outer = me // 4
    middle = (me // 2) % 2
    core = me % 2
    rows = own_ref.shape[0]

    def place(outer_at, middle_at, core_at):
        index = outer_at * 4 + middle_at * 2 + core_at
        return all_ref.at[pl.ds(pl.multiple_of(index * rows, rows), rows)]

    def remote(source, target, sems, slot, device):
        return pltpu.make_async_remote_copy(
            src_ref=source,
            dst_ref=target,
            send_sem=sems.at[0, slot],
            recv_sem=sems.at[1, slot],
            device_id={"seq": device},
            device_id_type=pl.DeviceIdType.MESH,
        )

    middle_partner = at_outer * 4 + (1 - middle) * 2 + core
    core_partner = at_outer * 4 + middle * 2 + (1 - core)
    outer_partners = [
        ((at_outer + step) % outer) * 4 + middle * 2 + core for step in range(1, outer)
    ]
    barrier = pltpu.get_barrier_semaphore()
    for device in [middle_partner, core_partner] + outer_partners:
        pl.semaphore_signal(
            barrier, inc=1, device_id={"seq": device}, device_id_type=pl.DeviceIdType.MESH
        )
    pl.semaphore_wait(barrier, outer + 1)

    own_place = place(at_outer, middle, core)
    local = pltpu.make_async_copy(own_ref, own_place, local_sem)
    local.start()
    started = []
    outer_copies = []
    for step in range(1, outer):
        copy = remote(own_ref, own_place, outer_sems, step - 1, outer_partners[step - 1])
        copy.start()
        outer_copies.append(copy)
    middle_copies = []
    for step in range(outer):
        source_outer = (at_outer + outer - step) % outer
        here = place(source_outer, middle, core)
        if step == 0:
            source = own_ref
        else:
            outer_copies[step - 1].wait_recv()
            source = here
        copy = remote(source, here, middle_sems, step, middle_partner)
        copy.start()
        middle_copies.append(copy)
        copy = remote(source, here, core_sems, 2 * step, core_partner)
        copy.start()
        started.append(copy)
    for step in range(outer):
        source_outer = (at_outer + outer - step) % outer
        middle_copies[step].wait_recv()
        here = place(source_outer, 1 - middle, core)
        copy = remote(here, here, core_sems, 2 * step + 1, core_partner)
        copy.start()
        started.append(copy)
    for copy in started:
        copy.wait_recv()
    for copy in outer_copies + middle_copies + started:
        copy.wait_send()
    local.wait()


def gather_rows(rows, collective_id):
    parts = lax.axis_size("seq")
    if parts % 4:
        return lax.all_gather(rows, "seq", axis=0, tiled=True)
    outer = parts // 4
    return pl.pallas_call(
        functools.partial(gather_kernel, outer),
        out_shape=jax.ShapeDtypeStruct((parts * rows.shape[0], rows.shape[1]), rows.dtype),
        in_specs=[pl.BlockSpec(memory_space=pltpu.VMEM)],
        out_specs=pl.BlockSpec(memory_space=pltpu.VMEM),
        scratch_shapes=[
            pltpu.SemaphoreType.DMA,
            pltpu.SemaphoreType.DMA((2, max(outer - 1, 1))),
            pltpu.SemaphoreType.DMA((2, outer)),
            pltpu.SemaphoreType.DMA((2, 2 * outer)),
        ],
        compiler_params=pltpu.CompilerParams(
            collective_id=collective_id, has_side_effects=True, vmem_limit_bytes=24 * 2**20
        ),
    )(rows)


def packed_height(depth):
    return (depth + 16) // 16 * 16


def other(values):
    return lax.ppermute(values, "ctx", [(0, 1), (1, 0)])


def sum_rounded(values):
    if lax.axis_size("ctx") != 2:
        return lax.psum(values, "ctx")
    mine = to_bf16(values)
    return mine.astype(jnp.float32) + other(mine).astype(jnp.float32)


def sum_ctx(values):
    if lax.axis_size("ctx") != 2:
        return lax.psum(values, "ctx")
    return values + other(values)


MESH = pl.DeviceIdType.MESH
LANES = 128


def padded(width):
    return (width + LANES - 1) // LANES * LANES


def remote_copy(source, target, send_sem, recv_sem, device):
    return pltpu.make_async_remote_copy(
        src_ref=source,
        dst_ref=target,
        send_sem=send_sem,
        recv_sem=recv_sem,
        device_id=device,
        device_id_type=MESH,
    )


def greet(devices):
    barrier = pltpu.get_barrier_semaphore()
    for device in devices:
        pl.semaphore_signal(barrier, inc=1, device_id=device, device_id_type=MESH)
    pl.semaphore_wait(barrier, len(devices))


def dot_last(left, right):
    return lax.dot_general(
        left, right, (((1,), (1,)), ((), ())), preferred_element_type=jnp.float32
    )


def dot_first(left, right):
    return lax.dot_general(
        left, right, (((0,), (0,)), ((), ())), preferred_element_type=jnp.float32
    )


def z_order(z):
    return (z + 1 - 2 * (z % 2), 2 - z // 2, 3 - 3 * (z // 2))


class Place:
    def __init__(self):
        me = lax.axis_index("seq")
        self.z = me // 4
        self.y = (me // 2) % 2
        self.k = me % 2
        self.c = lax.axis_index("ctx")
        self.me = me

    def seq(self, z, y, k):
        return {"seq": z * 4 + y * 2 + k}

    def others(self):
        z, y, k = self.z, self.y, self.k
        return (
            [self.seq(z, 1 - y, k), self.seq(z, y, 1 - k)]
            + [self.seq(other, y, k) for other in z_order(z)]
        )


class Gather:
    def __init__(self, at, own_ref, all_ref, send_sems, recv_sems, local_sem):
        self.at, self.own, self.all = at, own_ref, all_ref
        self.send_sems, self.recv_sems, self.local_sem = send_sems, recv_sems, local_sem
        self.rows = own_ref.shape[0]
        self.sent = []
        self.hop_sent = []

    def block(self, z, y, k):
        start = pl.multiple_of((z * 4 + y * 2 + k) * self.rows, self.rows)
        return self.all.at[pl.ds(start, self.rows)]

    def copy(self, source, z, y, k, kind, device, slot=None):
        return remote_copy(
            source,
            self.block(z, y, k),
            self.send_sems.at[z, kind if slot is None else slot],
            self.recv_sems.at[z, kind],
            device,
        )

    def to_y_and_core(self, source, z):
        at = self.at
        copy = self.copy(source, z, at.y, at.k, 1, at.seq(at.z, 1 - at.y, at.k))
        copy.start()
        self.sent.append(copy)
        self.to_core(source, z, at.y)

    def to_core(self, source, z, y):
        at = self.at
        copy = self.copy(source, z, y, at.k, 2 + y, at.seq(at.z, at.y, 1 - at.k))
        copy.start()
        self.sent.append(copy)

    def hop(self, source, z, right):
        at = self.at
        target = at.z + 1 if right else at.z - 1
        copy = self.copy(
            source, z, at.y, at.k, 0, at.seq(target, at.y, at.k), slot=None if right else 4
        )
        ok = (target < 4) if right else (target >= 0)
        return ok, copy

    def begin(self):
        at = self.at
        for right in (True, False):
            ok, copy = self.hop(self.own, at.z, right)
            self.hop_sent.append((ok, copy))

            @pl.when(ok)
            def _():
                copy.start()

        self.to_y_and_core(self.own, at.z)
        self.local = pltpu.make_async_copy(
            self.own, self.block(at.z, at.y, at.k), self.local_sem
        )
        self.local.start()

    def from_z(self, z):
        at = self.at
        here = self.block(z, at.y, at.k)
        self.copy(here, z, at.y, at.k, 0, at.seq(at.z, 1 - at.y, at.k)).wait_recv()
        for right in (True, False):
            ok, copy = self.hop(here, z, right)
            ok = jnp.logical_and(ok, z < at.z if right else z > at.z)
            self.hop_sent.append((ok, copy))

            @pl.when(ok)
            def _():
                copy.start()

        self.to_y_and_core(here, z)

    def from_y(self, z):
        at = self.at
        here = self.block(z, 1 - at.y, at.k)
        self.copy(here, z, 1 - at.y, at.k, 1, at.seq(at.z, 1 - at.y, at.k)).wait_recv()
        self.to_core(here, z, 1 - at.y)

    def from_core(self, z):
        at = self.at
        for y in range(2):
            here = self.block(z, y, 1 - at.k)
            self.copy(here, z, y, 1 - at.k, 2 + y, at.seq(at.z, at.y, 1 - at.k)).wait_recv()

    def end(self):
        for copy in self.sent:
            copy.wait_send()
        for ok, copy in self.hop_sent:

            @pl.when(ok)
            def _():
                copy.wait_send()


class Scatter:
    def __init__(self, at, part, core_buf, y_buf, z_buf, out_ref, send_sems, recv_sems):
        self.at, self.part, self.out = at, part, out_ref
        self.core_buf, self.y_buf, self.z_buf = core_buf, y_buf, z_buf
        self.send_sems, self.recv_sems = send_sems, recv_sems
        self.rows = out_ref.shape[0]
        self.sent = []
        self.core_copies = {}

    def block(self, z, y, k):
        start = pl.multiple_of((z * 4 + y * 2 + k) * self.rows, self.rows)
        return self.part.at[pl.ds(start, self.rows)]

    def core_copy(self, z, y):
        at = self.at
        return remote_copy(
            self.block(z, y, 1 - at.k),
            self.core_buf.at[z, y],
            self.send_sems.at[z, y],
            self.recv_sems.at[z, y],
            at.seq(at.z, at.y, 1 - at.k),
        )

    def to_core(self, z):
        for y in range(2):
            copy = self.core_copy(z, y)
            copy.start()
            self.sent.append(copy)

    def y_copy(self, z):
        at = self.at
        return remote_copy(
            self.block(z, 1 - at.y, at.k),
            self.y_buf.at[z],
            self.send_sems.at[z, 2],
            self.recv_sems.at[z, 2],
            at.seq(at.z, 1 - at.y, at.k),
        )

    def add_core(self, z, y):
        at = self.at
        here = self.block(z, y, at.k)
        total = here[...].astype(jnp.float32) + self.core_buf[z, y].astype(jnp.float32)
        here[...] = total.astype(jnp.bfloat16)

    def to_y(self, z):
        at = self.at
        for y in range(2):
            self.core_copy(z, y).wait_recv()
        self.add_core(z, 1 - at.y)
        copy = self.y_copy(z)
        copy.start()
        self.sent.append(copy)
        self.add_core(z, at.y)

    def z_copy(self, z, source_z):
        at = self.at
        return remote_copy(
            self.block(z, at.y, at.k),
            self.z_buf.at[source_z],
            self.send_sems.at[z, 3],
            self.recv_sems.at[source_z, 3],
            at.seq(z, at.y, at.k),
        )

    def to_z(self, z, own):
        at = self.at
        self.y_copy(z).wait_recv()
        here = self.block(z, at.y, at.k)
        total = here[...].astype(jnp.float32) + self.y_buf[z].astype(jnp.float32)
        if own:
            self.out[...] = total
        else:
            here[...] = total.astype(jnp.bfloat16)
            copy = self.z_copy(z, at.z)
            copy.start()
            self.sent.append(copy)

    def finish(self):
        at = self.at
        total = self.out[...]
        for z in z_order(at.z):
            remote_copy(
                self.block(z, at.y, at.k),
                self.z_buf.at[z],
                self.send_sems.at[z, 3],
                self.recv_sems.at[z, 3],
                at.seq(z, at.y, at.k),
            ).wait_recv()
            total += self.z_buf[z].astype(jnp.float32)
        self.out[...] = total

    def end(self):
        for copy in self.sent:
            copy.wait_send()


def ffn_kernel(
    own_ref,
    cot_ref,
    weight_ref,
    down_ref,
    second_sum_ref,
    down_part_ref,
    down_grad_ref,
    gate_mine_ref,
    gate_theirs_ref,
    all_ref,
    act_ref,
    grad_ref,
    part_ref,
    core_buf,
    y_buf,
    z_buf,
    flat_ref,
    gather_send,
    gather_recv,
    local_sem,
    scatter_send,
    scatter_recv,
):
    at = Place()
    width = down_ref.shape[0]
    rows = own_ref.shape[0]
    parts = all_ref.shape[0] // rows
    depth = weight_ref.shape[0] // parts
    greet(at.others())
    gather = Gather(at, own_ref, all_ref, gather_send, gather_recv, local_sem)
    second = Scatter(
        at, part_ref, core_buf, y_buf, z_buf, second_sum_ref, scatter_send, scatter_recv
    )
    tile = 2 * rows

    def compute(z):
        def step(index, carry):
            start = pl.multiple_of(z * (4 * rows) + index * tile, tile)
            here = pl.ds(start, tile)
            gate_up = jnp.dot(
                all_ref[here], weight_ref[...], preferred_element_type=jnp.float32
            )
            grad_act = dot_last(cot_ref[here], down_ref[...])
            gate = gate_up[:, :width]
            upward = gate_up[:, width:]
            sigmoid_gate = jax.nn.sigmoid(gate)
            silu = gate * sigmoid_gate
            activated = (silu * upward).astype(jnp.bfloat16)
            act_ref[here] = activated
            grad_gate = grad_act * upward * sigmoid_gate * (1.0 + gate * (1.0 - sigmoid_gate))
            grad_ref[here, :width] = grad_gate.astype(jnp.bfloat16)
            grad_ref[here, width:] = (grad_act * silu).astype(jnp.bfloat16)
            part_ref[here] = dot_last(grad_ref[here], weight_ref[...]).astype(jnp.bfloat16)
            down_part_ref[here] = jnp.dot(
                activated, down_ref[...], preferred_element_type=jnp.float32
            ).astype(jnp.bfloat16)
            return carry

        lax.fori_loop(0, 2, step, 0)

    order = (at.z,) + z_order(at.z)
    gather.begin()
    for index, z in enumerate(order):
        if index + 1 < len(order):
            gather.from_z(order[index + 1])
        gather.from_y(z)
        if index == 0:
            gather.local.wait()
        gather.from_core(z)
        if index > 0:
            second.to_y(order[index - 1])
        compute(z)
        second.to_core(z)
        if index > 0:
            second.to_z(order[index - 1], index == 1)
    last = order[-1]

    def gate_tile(index, carry):
        columns = pl.ds(pl.multiple_of(index * LANES, LANES), LANES)
        flat_ref[columns] = dot_first(all_ref[:, columns], grad_ref[...])
        return carry

    def columns_of(ctx):
        return pl.ds(pl.multiple_of(ctx * width, LANES), width)

    down_grad = dot_first(act_ref[...], cot_ref[...])
    hidden = down_grad_ref.shape[0]
    down_grad_ref[...] = down_grad[:hidden].astype(jnp.bfloat16)
    second.to_y(last)
    tiles = all_ref.shape[1] // LANES
    lax.fori_loop(0, tiles, gate_tile, 0)
    second.to_z(last, False)
    for part in range(parts):
        here = slice(part * depth, (part + 1) * depth)
        gate_mine_ref[part] = flat_ref[here, columns_of(at.c)].astype(jnp.bfloat16)
        gate_theirs_ref[part] = flat_ref[here, columns_of(1 - at.c)].astype(jnp.bfloat16)
    second.finish()
    gather.end()
    second.end()


def ffn(second_in, all_cot, weight, down, hidden, collective_id):
    rows, model = second_in.shape
    parts = all_cot.shape[0] // rows
    width = down.shape[0]
    depth = model // parts
    tokens = parts * rows
    f32, bf16 = jnp.float32, jnp.bfloat16
    vmem = pl.BlockSpec(memory_space=pltpu.VMEM)
    flops = 2 * tokens * model * width * 9
    return pl.pallas_call(
        ffn_kernel,
        out_shape=(
            jax.ShapeDtypeStruct((rows, model), f32),
            jax.ShapeDtypeStruct((tokens, model), bf16),
            jax.ShapeDtypeStruct((hidden, model), bf16),
            jax.ShapeDtypeStruct((parts, depth, width), bf16),
            jax.ShapeDtypeStruct((parts, depth, width), bf16),
        ),
        in_specs=[vmem] * 4,
        out_specs=(vmem,) * 5,
        scratch_shapes=[
            pltpu.VMEM((tokens, model), bf16),
            pltpu.VMEM((tokens, width), bf16),
            pltpu.VMEM((tokens, 2 * width), bf16),
            pltpu.VMEM((tokens, model), bf16),
            pltpu.VMEM((4, 2, rows, model), bf16),
            pltpu.VMEM((4, rows, model), bf16),
            pltpu.VMEM((4, rows, model), bf16),
            pltpu.VMEM((model, 2 * width), f32),
            pltpu.SemaphoreType.DMA((4, 5)),
            pltpu.SemaphoreType.DMA((4, 4)),
            pltpu.SemaphoreType.DMA,
            pltpu.SemaphoreType.DMA((4, 4)),
            pltpu.SemaphoreType.DMA((4, 4)),
        ],
        compiler_params=pltpu.CompilerParams(
            collective_id=collective_id, has_side_effects=True, vmem_limit_bytes=48 * 2**20
        ),
        cost_estimate=pl.CostEstimate(
            flops=flops, bytes_accessed=16 * 2**20, transcendentals=tokens * width
        ),
    )(second_in, all_cot, weight, down)


class SharedGather(Gather):
    def __init__(self, at, own_ref, all_ref, send_sems, recv_sems, local_sem):
        self.at, self.whole_all = at, all_ref
        self.count = own_ref.shape[0] // 2
        self.mine = self.half(at.c)
        self.theirs = self.half(1 - at.c)
        self.own = own_ref.at[self.mine]
        self.all = all_ref
        self.send_sems, self.recv_sems, self.local_sem = send_sems, recv_sems, local_sem
        self.sent = []
        self.hop_sent = []

    def half(self, ctx):
        return pl.ds(pl.multiple_of(ctx * self.count, self.count), self.count)

    def block(self, z, y, k, rows=None):
        return self.all.at[z * 4 + y * 2 + k, self.mine if rows is None else rows]

    def to_core(self, source, z, y):
        super().to_core(source, z, y)
        self.to_x(source, z, y)

    def x_copy(self, source, z, y, rows):
        at = self.at
        return remote_copy(
            source,
            self.block(z, y, at.k, rows),
            self.send_sems.at[z, 5 + y],
            self.recv_sems.at[z, 4 + y],
            {"ctx": 1 - at.c},
        )

    def to_x(self, source, z, y):
        copy = self.x_copy(source, z, y, self.mine)
        copy.start()
        self.sent.append(copy)

    def core_again(self, z, y, k):
        at = self.at
        here = self.block(z, y, k, self.theirs)
        return remote_copy(
            here,
            here,
            self.send_sems.at[z, 7 + y],
            self.recv_sems.at[z, 6 + y],
            at.seq(at.z, at.y, 1 - at.k),
        )

    def from_x(self, z, y):
        at = self.at
        here = self.block(z, y, at.k, self.theirs)
        self.x_copy(here, z, y, self.theirs).wait_recv()
        copy = self.core_again(z, y, at.k)
        copy.start()
        self.sent.append(copy)

    def from_core(self, z):
        super().from_core(z)
        for y in range(2):
            self.core_again(z, y, 1 - self.at.k).wait_recv()


def rotated(values):
    width = values.shape[1]
    half = HEAD_DIM // 2
    lane = lax.broadcasted_iota(jnp.int32, values.shape, 1) % HEAD_DIM
    ahead = pltpu.roll(values, width - half, 1)
    behind = pltpu.roll(values, half, 1)
    return jnp.where(lane < half, -ahead, behind)


def tiled(table, width):
    return jnp.concatenate([table] * (width // table.shape[1]), 1)


def head_columns(head):
    return slice(head * HEAD_DIM, (head + 1) * HEAD_DIM)


def forward_kernel(
    qkv_ref,
    out_ref,
    cot_ref,
    gate_up_ref,
    tokens_ref,
    cos_ref,
    sin_ref,
    query_pos_ref,
    key_pos_ref,
    full_qkv_ref,
    full_out_ref,
    all_cot_ref,
    weight_ref,
    gains_ref,
    first_ref,
    query_ref,
    kv_ref,
    probs_ref,
    attended_ref,
    residual_ref,
    second_ref,
    all_qkv_ref,
    all_out_ref,
    bias_ref,
    gate_send,
    gate_all,
    qkv_send,
    qkv_recv,
    out_send,
    out_recv,
    cot_send,
    cot_recv,
    local_sems,
    gate_sems,
    x_sems,
    kv_sems,
):
    f32, bf16 = jnp.float32, jnp.bfloat16
    at = Place()
    parts, depth, width = gate_send.shape
    half = gate_up_ref.shape[1] // 2
    hidden = half // parts
    bias_count = bias_ref.shape[1] // parts
    query_width = HEADS * HEAD_DIM
    key_width = KV_HEADS * HEAD_DIM
    seq_peers = [lax.rem(at.me + step, parts) for step in range(1, parts)]
    other_ctx = {"ctx": 1 - at.c}
    greet([{"seq": peer} for peer in seq_peers] + [other_ctx])
    qkv = SharedGather(at, qkv_ref, all_qkv_ref, qkv_send, qkv_recv, local_sems.at[0])
    out = SharedGather(at, out_ref, all_out_ref, out_send, out_recv, local_sems.at[1])
    cot = Gather(at, cot_ref, all_cot_ref, cot_send, cot_recv, local_sems.at[2])
    order = (at.z,) + z_order(at.z)
    qkv.begin()
    half_value = gate_up_ref[:, pl.ds(pl.multiple_of(at.c * half, LANES), half)]
    tail = jnp.zeros((depth, width - hidden), gate_send.dtype)
    for part in range(parts):
        gate_send[part, :, :hidden] = half_value[:, part * hidden : (part + 1) * hidden]
        gate_send[part, :, hidden:] = tail
    qkv.from_y(order[0])
    qkv.from_z(order[1])
    out.begin()
    qkv.from_y(order[1])
    qkv.from_z(order[2])
    gate_copies = []

    def gate_start(steps):
        for step in steps:
            peer = lax.rem(at.me + step, parts)
            copy = remote_copy(
                gate_send.at[peer],
                gate_all.at[at.c, at.me],
                gate_sems.at[0, step - 1],
                gate_sems.at[1, step - 1],
                {"seq": peer},
            )
            copy.start()
            gate_copies.append(copy)

    def gate_x(source, ctx, step):
        here = gate_all.at[ctx, source]
        return remote_copy(here, here, x_sems.at[0, step], x_sems.at[1, step], other_ctx)

    def gate_arrive(steps):
        for step in steps:
            source = lax.rem(at.me + parts - step, parts)
            if step > 0:
                remote_copy(
                    gate_send.at[source],
                    gate_all.at[at.c, source],
                    gate_sems.at[0, step - 1],
                    gate_sems.at[1, step - 1],
                    {"seq": source},
                ).wait_recv()
            copy = gate_x(source, at.c, step)
            copy.start()
            gate_copies.append(copy)

    gate_all[at.c, at.me] = gate_send[at.me]
    qkv.from_y(order[2])
    qkv.from_z(order[3])
    cot.begin()
    qkv.from_y(order[3])
    out.from_y(order[0])
    out.from_z(order[1])
    for z in order:
        for y in range(2):
            qkv.from_x(z, y)
    out.from_y(order[1])
    out.from_z(order[2])
    qkv.local.wait()
    for z in order:
        qkv.from_core(z)
    gate_start(range(1, parts))
    cot.from_y(order[0])
    cot.from_z(order[1])
    for part in range(parts):
        rows = pl.ds(part * depth, depth)
        full_qkv_ref[rows] = all_qkv_ref[part, :depth]
        extra = all_qkv_ref[part, depth : depth + 1, : bias_count + 2 * depth].astype(f32)
        bias_ref[:, part * bias_count : (part + 1) * bias_count] = extra[:, :bias_count]
        for index in range(2):
            start = bias_count + index * depth
            gains_ref[index : index + 1, part * depth : (part + 1) * depth] = extra[
                :, start : start + depth
            ]
    tokens = tokens_ref[...].astype(f32)
    normed_one, _ = rms_forward(tokens)
    first_ref[...] = (normed_one * gains_ref[0:1]).astype(bf16)
    projected = (
        jnp.dot(first_ref[...], full_qkv_ref[...], preferred_element_type=f32) + bias_ref[...]
    )
    rotary = projected[:, : query_width + key_width]
    turned = rotary * tiled(cos_ref[...], rotary.shape[1]) + rotated(rotary) * tiled(
        sin_ref[...], rotary.shape[1]
    )
    turned = turned.astype(bf16)
    query_ref[...] = turned[:, :query_width]
    kv_ref[0, :, :key_width] = turned[:, query_width:]
    kv_ref[0, :, key_width:] = projected[:, query_width + key_width :].astype(bf16)
    kv_copy = remote_copy(kv_ref.at[0], kv_ref.at[1], kv_sems.at[0], kv_sems.at[1], other_ctx)
    kv_copy.start()
    out.from_y(order[2])
    out.from_z(order[3])
    cot.from_y(order[1])
    cot.from_z(order[2])
    out.from_y(order[3])
    for z in order:
        for y in range(2):
            out.from_x(z, y)
    kv_copy.wait_recv()
    rows = tokens.shape[0]
    kv = kv_ref[...].reshape(2 * rows, 2 * key_width)
    allowed = key_pos_ref[...] <= query_pos_ref[...]
    group_size = HEADS // KV_HEADS

    def attend(head):
        keys = kv[:, head_columns(head // group_size)]
        values = kv[:, head_columns(KV_HEADS + head // group_size)]
        scores = dot_last(query_ref[:, head_columns(head)], keys) * (HEAD_DIM ** (-0.5))
        scores = jnp.where(allowed, scores, -1e30)
        row_top = jnp.max(scores, axis=-1, keepdims=True)
        log_total = row_top + jnp.log(
            jnp.sum(jnp.exp(scores - row_top), axis=-1, keepdims=True)
        )
        probs = jnp.exp(scores - log_total)
        probs_ref[head] = probs
        attended_ref[:, head_columns(head)] = jnp.dot(
            probs.astype(bf16), values, preferred_element_type=f32
        ).astype(bf16)

    for head in range(group_size):
        attend(head)
    cot.from_y(order[2])
    cot.from_z(order[3])
    gate_arrive(range(0, parts // 2))
    for head in range(group_size, HEADS):
        attend(head)
    cot.from_y(order[3])
    out.local.wait()
    for z in order:
        out.from_core(z)
    for part in range(parts):
        full_out_ref[pl.ds(part * depth, depth)] = all_out_ref[part, :depth]
    residual = tokens + jnp.dot(
        attended_ref[...], full_out_ref[...], preferred_element_type=f32
    )
    residual_ref[...] = residual
    normed_two, _ = rms_forward(residual)
    second_ref[...] = (normed_two * gains_ref[1:2]).astype(bf16)
    gate_arrive(range(parts // 2, parts))
    for z in order:
        cot.from_core(z)
    for step in range(parts):
        gate_x(lax.rem(at.me + parts - step, parts), 1 - at.c, step).wait_recv()
    for part in range(parts):
        rows = pl.ds(part * depth, depth)
        weight_ref[rows, :width] = gate_all[0, part]
        weight_ref[rows, width:] = gate_all[1, part]
    kv_copy.wait_send()
    for copy in gate_copies:
        copy.wait_send()
    cot.local.wait()
    for gather in (qkv, out, cot):
        gather.end()


def forward(qkv, out, cot, gate_up, tokens, tables, query_pos, key_pos, bias_count, collective_id):
    parts = lax.axis_size("seq")
    rows = qkv.shape[0]
    depth = gate_up.shape[0]
    hidden = gate_up.shape[1] // (2 * parts)
    width = padded(hidden)
    count, model = cot.shape
    f32, bf16 = jnp.float32, jnp.bfloat16
    query_width = HEADS * HEAD_DIM
    key_width = KV_HEADS * HEAD_DIM
    shape = jax.ShapeDtypeStruct
    vmem = pl.BlockSpec(memory_space=pltpu.VMEM)
    outs = (
        shape((parts * depth, qkv.shape[1]), bf16),
        shape((parts * depth, out.shape[1]), bf16),
        shape((parts * count, model), bf16),
        shape((parts * depth, 2 * width), bf16),
        shape((2, model), f32),
        shape((count, model), bf16),
        shape((count, query_width), bf16),
        shape((2, count, 2 * key_width), bf16),
        shape((HEADS, count, 2 * count), f32),
        shape((count, query_width), bf16),
        shape((count, model), f32),
        shape((count, model), bf16),
    )
    return pl.pallas_call(
        forward_kernel,
        out_shape=outs,
        in_specs=[vmem] * 9,
        out_specs=(vmem,) * len(outs),
        scratch_shapes=[
            pltpu.VMEM((parts, rows, qkv.shape[1]), bf16),
            pltpu.VMEM((parts, rows, out.shape[1]), bf16),
            pltpu.VMEM((1, parts * bias_count), f32),
            pltpu.VMEM((parts, depth, width), bf16),
            pltpu.VMEM((2, parts, depth, width), bf16),
            pltpu.SemaphoreType.DMA((4, 9)),
            pltpu.SemaphoreType.DMA((4, 8)),
            pltpu.SemaphoreType.DMA((4, 9)),
            pltpu.SemaphoreType.DMA((4, 8)),
            pltpu.SemaphoreType.DMA((4, 5)),
            pltpu.SemaphoreType.DMA((4, 4)),
            pltpu.SemaphoreType.DMA((3,)),
            pltpu.SemaphoreType.DMA((2, parts - 1)),
            pltpu.SemaphoreType.DMA((2, parts)),
            pltpu.SemaphoreType.DMA((2,)),
        ],
        compiler_params=pltpu.CompilerParams(
            collective_id=collective_id, has_side_effects=True, vmem_limit_bytes=48 * 2**20
        ),
    )(qkv, out, cot, gate_up, tokens, *tables, query_pos, key_pos)


class Flow:
    def __init__(self, at, source, out_ref, bufs, sems, x_first, halves):
        self.at, self.source, self.out = at, source, out_ref
        (self.core_recv, self.x_send, self.x_recv, self.y_send, self.y_recv,
         self.z_send, self.z_recv, self.last_send, self.last_recv) = bufs
        self.sems = sems
        self.x_first, self.halves = x_first, halves
        rows = source.shape[3]
        self.count = rows // 2 if halves else rows
        self.mine = self.half(at.c) if halves else pl.ds(0, rows)
        self.theirs = self.half(1 - at.c) if halves else pl.ds(0, rows)
        self.all_rows = pl.ds(0, rows)
        self.sent = []

    def half(self, ctx):
        return pl.ds(pl.multiple_of(ctx * self.count, self.count), self.count)

    def send(self, source, target, slot, device, recv_slot=None):
        copy = remote_copy(
            source,
            target,
            self.sems.at[0, slot],
            self.sems.at[1, slot if recv_slot is None else recv_slot],
            device,
        )
        copy.start()
        self.sent.append(copy)
        return copy

    def begin(self):
        at = self.at
        self.core = self.send(
            self.source.at[1 - at.k], self.core_recv, 0, at.seq(at.z, at.y, 1 - at.k)
        )

    def add_core(self):
        at = self.at
        self.core.wait_recv()
        for z in range(4):
            for y in range(2):
                self.source[at.k, z, y] += self.core_recv[z, y]
        if self.x_first:
            self.to_x_both()
        else:
            self.to_y()

    def to_x_both(self):
        at = self.at
        for z in range(4):
            for y in range(2):
                self.x_send[z, y] = self.source[at.k, z, y, self.theirs].astype(self.x_send.dtype)
        self.x = self.send(self.x_send, self.x_recv, 1, {"ctx": 1 - at.c})

    def to_y(self):
        at = self.at
        rows = self.mine if self.x_first else self.all_rows
        for z in range(4):
            self.y_send[z] = self.source[at.k, z, 1 - at.y, rows].astype(self.y_send.dtype)
        self.y = self.send(self.y_send, self.y_recv, 2, at.seq(at.z, 1 - at.y, at.k))

    def second(self):
        at = self.at
        if self.x_first:
            self.x.wait_recv()
            for z in range(4):
                for y in range(2):
                    self.source[at.k, z, y, self.mine] += self.x_recv[z, y].astype(jnp.float32)
            self.to_y()
        else:
            self.y.wait_recv()
            for z in range(4):
                self.source[at.k, z, at.y] += self.y_recv[z].astype(jnp.float32)
            for z in range(4):
                self.x_send[z] = self.source[at.k, z, at.y, self.theirs].astype(self.x_send.dtype)
            self.x = self.send(self.x_send, self.x_recv, 1, {"ctx": 1 - at.c})

    def to_z(self):
        at = self.at
        (self.y if self.x_first else self.x).wait_recv()
        arrived = self.y_recv if self.x_first else self.x_recv
        for z in range(4):
            total = self.source[at.k, z, at.y, self.mine] + arrived[z].astype(jnp.float32)
            self.source[at.k, z, at.y, self.mine] = total
            self.z_send[z] = total.astype(self.z_send.dtype)
        for index, z in enumerate(z_order(at.z)):
            self.send(
                self.z_send.at[z], self.z_recv.at[at.z], 3 + z, at.seq(z, at.y, at.k), 3 + at.z
            )

    def finish(self):
        at = self.at
        total = self.source[at.k, at.z, at.y, self.mine]
        for z in z_order(at.z):
            remote_copy(
                self.z_send.at[z],
                self.z_recv.at[z],
                self.sems.at[0, 3 + z],
                self.sems.at[1, 3 + z],
                at.seq(z, at.y, at.k),
            ).wait_recv()
            total += self.z_recv[z].astype(jnp.float32)
        self.out[self.mine] = total
        if self.halves:
            self.last_send[...] = total
            self.last = self.send(self.last_send, self.last_recv, 7, {"ctx": 1 - at.c})

    def end(self):
        if self.halves:
            self.last.wait_recv()
            self.out[self.theirs] = self.last_recv[...]
        for copy in self.sent:
            copy.wait_send()


def flow_scratch(rows, width, x_first, halves, dtype):
    f32 = jnp.float32
    count = rows // 2 if halves else rows
    x_shape = (4, 2, count, width) if x_first else (4, count, width)
    y_shape = (4, count if x_first else rows, width)
    z_shape = (4, count, width)
    last = (count, width) if halves else (8, LANES)
    return [
        pltpu.VMEM((2, 4, 2, rows, width), f32),
        pltpu.VMEM((4, 2, rows, width), f32),
        pltpu.VMEM(x_shape, dtype),
        pltpu.VMEM(x_shape, dtype),
        pltpu.VMEM(y_shape, dtype),
        pltpu.VMEM(y_shape, dtype),
        pltpu.VMEM(z_shape, dtype),
        pltpu.VMEM(z_shape, dtype),
        pltpu.VMEM(last, f32),
        pltpu.VMEM(last, f32),
        pltpu.SemaphoreType.DMA((2, 8)),
    ]


def grads_kernel(
    first_ref,
    grad_proj_ref,
    attended_ref,
    grad_res_ref,
    small_ref,
    gate_mine_ref,
    gate_other_ref,
    qkv_out_ref,
    out_out_ref,
    small_out_ref,
    gate_out_ref,
    *scratch,
):
    at = Place()
    flow_bufs = [scratch[11 * index : 11 * (index + 1)] for index in range(3)]
    flat_ref, out_flat_ref, gate_ref, gate_recv, gate_sems, half_sems = scratch[33:]
    parts, depth, width = gate_ref.shape
    hidden = gate_out_ref.shape[1] // (2 * parts)
    seq_peers = [lax.rem(at.me + step, parts) for step in range(1, parts)]
    greet([{"seq": peer} for peer in seq_peers] + [{"ctx": 1 - at.c}])
    qkv = Flow(at, flow_bufs[0][0], qkv_out_ref, flow_bufs[0][1:10], flow_bufs[0][10], True, True)
    out = Flow(at, flow_bufs[1][0], out_out_ref, flow_bufs[1][1:10], flow_bufs[1][10], False, True)
    small = Flow(
        at, flow_bufs[2][0], small_out_ref, flow_bufs[2][1:10], flow_bufs[2][10], True, False
    )

    def spread(flat, source):
        rows = source.shape[3]
        tail = jnp.zeros((rows - depth, source.shape[4]), jnp.float32)
        for part in range(parts):
            z, y, k = part // 4, (part // 2) % 2, part % 2
            source[k, z, y, :depth] = flat[part * depth : (part + 1) * depth]
            source[k, z, y, depth:] = tail

    for part in range(parts):
        total = gate_mine_ref[part].astype(jnp.float32) + gate_other_ref[part].astype(jnp.float32)
        gate_ref[part] = total.astype(gate_ref.dtype)
    gate_copies = []
    for step, peer in enumerate(seq_peers):
        copy = remote_copy(
            gate_ref.at[peer],
            gate_recv.at[at.c, at.me],
            gate_sems.at[0, step],
            gate_sems.at[1, step],
            {"seq": peer},
        )
        copy.start()
        gate_copies.append(copy)
    out_flat_ref[...] = dot_first(attended_ref[...], grad_res_ref[...])
    spread(out_flat_ref, out.source)
    out.begin()
    small.source[...] = small_ref[...]
    small.begin()
    flat_ref[...] = dot_first(first_ref[...], grad_proj_ref[...])
    spread(flat_ref, qkv.source)
    qkv.begin()
    out.add_core()
    small.add_core()
    qkv.add_core()
    out.second()
    small.second()
    qkv.second()
    out.to_z()
    small.to_z()
    gate_recv[at.c, at.me] = gate_ref[at.me]

    def gate_x(source, ctx, step):
        here = gate_recv.at[ctx, source]
        return remote_copy(
            here, here, half_sems.at[0, step], half_sems.at[1, step], {"ctx": 1 - at.c}
        )

    def gate_forward(step):
        copy = gate_x(lax.rem(at.me + parts - step, parts), at.c, step)
        copy.start()
        gate_copies.append(copy)

    def gate_arrive(steps):
        for step in steps:
            source = lax.rem(at.me + parts - step, parts)
            remote_copy(
                gate_ref.at[source],
                gate_recv.at[at.c, source],
                gate_sems.at[0, step - 1],
                gate_sems.at[1, step - 1],
                {"seq": source},
            ).wait_recv()
            gate_forward(step)

    gate_forward(0)
    gate_arrive(range(1, parts))
    qkv.to_z()
    out.finish()
    small.finish()
    qkv.finish()
    for step in range(parts):
        gate_x(lax.rem(at.me + parts - step, parts), 1 - at.c, step).wait_recv()
    for ctx in range(2):
        for part in range(parts):
            start = (ctx * parts + part) * hidden
            gate_out_ref[:, start : start + hidden] = gate_recv[ctx, part, :, :hidden].astype(
                jnp.float32
            )
    for copy in gate_copies:
        copy.wait_send()
    out.end()
    small.end()
    qkv.end()


def reduce_grads(
    first_in, grad_proj, attended, grad_res, small, gate_mine, gate_other, hidden, collective_id
):
    parts, depth, width = gate_mine.shape
    f32, bf16 = jnp.float32, jnp.bfloat16
    rows = (depth + 31) // 32 * 32
    model, qkv_columns = first_in.shape[1], grad_proj.shape[1]
    out_columns = grad_res.shape[1]
    out_rows = attended.shape[1]
    whole = parts * hidden
    vmem = pl.BlockSpec(memory_space=pltpu.VMEM)
    return pl.pallas_call(
        grads_kernel,
        out_shape=(
            jax.ShapeDtypeStruct((rows, qkv_columns), f32),
            jax.ShapeDtypeStruct((rows, out_columns), f32),
            jax.ShapeDtypeStruct(small.shape[3:], f32),
            jax.ShapeDtypeStruct((depth, 2 * whole), f32),
        ),
        in_specs=[vmem] * 7,
        out_specs=(vmem,) * 4,
        scratch_shapes=flow_scratch(rows, qkv_columns, True, True, bf16)
        + flow_scratch(rows, out_columns, False, True, bf16)
        + flow_scratch(small.shape[3], small.shape[4], True, False, f32)
        + [
            pltpu.VMEM((model, qkv_columns), f32),
            pltpu.VMEM((out_rows, out_columns), f32),
            pltpu.VMEM((parts, depth, width), bf16),
            pltpu.VMEM((2, parts, depth, width), bf16),
            pltpu.SemaphoreType.DMA((2, parts - 1)),
            pltpu.SemaphoreType.DMA((2, parts)),
        ],
        compiler_params=pltpu.CompilerParams(
            collective_id=collective_id, has_side_effects=True, vmem_limit_bytes=52 * 2**20
        ),
    )(first_in, grad_proj, attended, grad_res, small, gate_mine, gate_other)


def shards(
    tokens,
    positions,
    cotangent,
    qkv_weight,
    qkv_bias,
    out_weight,
    gate_up_weight,
    down_weight,
    attn_gain,
    ffn_gain,
):
    f32 = jnp.float32
    qkv_columns = qkv_weight.shape[1]
    depth = qkv_weight.shape[0]
    bias_count = qkv_bias.shape[0]
    packed_rows = packed_height(depth)
    pair = jnp.concatenate([qkv_weight, out_weight], 1)
    extra = jnp.concatenate([qkv_bias, attn_gain, ffn_gain])
    extra = jnp.pad(extra, (0, pair.shape[1] - extra.shape[0]))[None]
    packed = jnp.concatenate(
        [pair, extra, jnp.zeros((packed_rows - depth - 1, pair.shape[1]), pair.dtype)], 0
    )
    packed = lax.all_gather(packed, "seq", axis=0, tiled=True).reshape(-1, packed_rows, pair.shape[1])
    full_qkv = packed[:, :depth, :qkv_columns].reshape(-1, qkv_columns)
    full_out = packed[:, :depth, qkv_columns:].reshape(-1, out_weight.shape[1])
    full_bias = packed[:, depth, :bias_count].reshape(-1)
    gain_one = packed[:, depth, bias_count : bias_count + depth].reshape(-1)
    gain_two = packed[:, depth, bias_count + depth : bias_count + 2 * depth].reshape(-1)
    parts = lax.axis_size("seq")
    hidden = down_weight.shape[0]
    own_gate_up = columns_from_rows(gate_up_weight, parts)
    all_cot = gather_rows(cotangent[0], 0)
    own_gate_up, all_cot, full_qkv = lax.optimization_barrier((own_gate_up, all_cot, full_qkv))
    inputs_f = tokens[0].astype(f32)
    cot_row = cotangent[0]
    row_count = inputs_f.shape[0]
    group_size = HEADS // KV_HEADS
    query_width = HEADS * HEAD_DIM
    key_width = KV_HEADS * HEAD_DIM
    score_scale = HEAD_DIM ** (-0.5)
    all_positions = positions[0]
    position_row = lax.dynamic_slice_in_dim(
        all_positions, lax.axis_index("ctx") * row_count, row_count, 0
    )
    normed_one, scale_one = rms_forward(inputs_f)
    first_in = to_bf16(normed_one * gain_one.astype(f32))
    projected = jnp.dot(first_in, full_qkv, preferred_element_type=f32) + full_bias.astype(f32)
    cosine_table, sine_table = rope_tables(position_row)
    cos_query = cosine_table[:, None, None, :]
    sin_query = sine_table[:, None, None, :]
    cos_key = cosine_table[:, None, :]
    sin_key = sine_table[:, None, :]
    query = projected[:, :query_width].reshape(row_count, KV_HEADS, group_size, HEAD_DIM)
    keys = projected[:, query_width : query_width + key_width].reshape(
        row_count, KV_HEADS, HEAD_DIM
    )
    values = projected[:, query_width + key_width :]
    query_rot = to_bf16(query * cos_query + rotate_half(query) * sin_query)
    key_rot = to_bf16(keys * cos_key + rotate_half(keys) * sin_key).reshape(row_count, key_width)
    value_b = to_bf16(values)
    both = jnp.concatenate([key_rot, value_b], -1)
    if lax.axis_size("ctx") == 2:
        both = jnp.concatenate([both, other(both)], 0)
        other_row = lax.dynamic_slice_in_dim(
            all_positions, (1 - lax.axis_index("ctx")) * row_count, row_count, 0
        )
        all_positions = jnp.concatenate([position_row, other_row])
    else:
        both = lax.all_gather(both, "ctx", axis=0, tiled=True)
    all_keys, all_values = both[:, :key_width], both[:, key_width:]
    all_keys = all_keys.reshape(-1, KV_HEADS, HEAD_DIM)
    all_values = all_values.reshape(-1, KV_HEADS, HEAD_DIM)
    scores = (
        jnp.einsum("tkgd,skd->kgts", query_rot, all_keys, preferred_element_type=f32) * score_scale
    )
    allowed = all_positions[None, :] <= position_row[:, None]
    scores = jnp.where(allowed, scores, -1e30)
    row_top = jnp.max(scores, axis=-1, keepdims=True)
    log_total = row_top + jnp.log(jnp.sum(jnp.exp(scores - row_top), axis=-1, keepdims=True))
    probs = jnp.exp(scores - log_total)
    probs_b = to_bf16(probs)
    attended = to_bf16(
        jnp.einsum("kgts,skd->tkgd", probs_b, all_values, preferred_element_type=f32)
    )
    attended_flat = attended.reshape(row_count, query_width)
    residual = inputs_f + jnp.dot(attended_flat, full_out, preferred_element_type=f32)
    normed_two, scale_two = rms_forward(residual)
    second_in = to_bf16(normed_two * gain_two.astype(f32))
    all_second = gather_rows(second_in, 1)
    gate_up = jnp.dot(all_second, own_gate_up, preferred_element_type=f32)
    gate = gate_up[:, :hidden]
    upward = gate_up[:, hidden:]
    sigmoid_gate = jax.nn.sigmoid(gate)
    activated = to_bf16(gate * sigmoid_gate * upward)
    grad_act = contract_columns(all_cot, down_weight)
    grad_gate = grad_act * upward * sigmoid_gate * (1.0 + gate * (1.0 - sigmoid_gate))
    grad_upward = grad_act * (gate * sigmoid_gate)
    grad_gate_up = to_bf16(jnp.concatenate([grad_gate, grad_upward], -1))
    grad_second = scatter_tokens(contract_columns(grad_gate_up, own_gate_up))
    down_sum = scatter_tokens(jnp.dot(activated, down_weight, preferred_element_type=f32))
    output_row = (residual + down_sum).astype(jnp.bfloat16)
    result_down = sum_rounded(contract_rows(activated, all_cot))
    result_gate_up = rows_from_columns(
        to_bf16(sum_rounded(contract_rows(all_second, grad_gate_up))), parts
    ).astype(f32)
    grad_through, gain_two_grad = rms_backward(
        grad_second, normed_two, scale_two, gain_two.astype(f32)
    )
    grad_residual = cot_row.astype(f32) + grad_through
    grad_res_b = to_bf16(grad_residual)
    out_grad = weight_rows(attended_flat, grad_res_b)
    grad_attended = to_bf16(jnp.dot(grad_res_b, full_out.T, preferred_element_type=f32))
    grad_attended = grad_attended.reshape(row_count, KV_HEADS, group_size, HEAD_DIM)
    grad_probs = jnp.einsum("tkgd,skd->kgts", grad_attended, all_values, preferred_element_type=f32)
    delta = jnp.sum(grad_attended.astype(f32) * attended.astype(f32), axis=-1)
    delta = jnp.transpose(delta, (1, 2, 0))[..., None]
    grad_scores = to_bf16(probs * (grad_probs - delta) * score_scale)
    grad_query_rot = jnp.einsum("kgts,skd->tkgd", grad_scores, all_keys, preferred_element_type=f32)
    key_part = jnp.einsum("kgts,tkgd->skd", grad_scores, query_rot, preferred_element_type=f32)
    value_part = jnp.einsum("kgts,tkgd->skd", probs_b, grad_attended, preferred_element_type=f32)
    key_parts = jnp.concatenate(
        [
            key_part.reshape(row_count * lax.axis_size("ctx"), key_width),
            value_part.reshape(row_count * lax.axis_size("ctx"), key_width),
        ],
        -1,
    )
    if lax.axis_size("ctx") == 2:
        key_local = key_parts[:row_count] + other(key_parts[row_count:])
    else:
        key_local = lax.psum_scatter(key_parts, "ctx", scatter_dimension=0, tiled=True)
    grad_key_rot = key_local[:, :key_width].reshape(row_count, KV_HEADS, HEAD_DIM)
    grad_value = key_local[:, key_width:]
    grad_query = grad_query_rot * cos_query + rotate_back(grad_query_rot * sin_query)
    grad_key = grad_key_rot * cos_key + rotate_back(grad_key_rot * sin_key)
    grad_projected = jnp.concatenate(
        [
            grad_query.reshape(row_count, query_width),
            grad_key.reshape(row_count, key_width),
            grad_value,
        ],
        -1,
    )
    bias_grad = jnp.sum(grad_projected, axis=0)
    grad_proj_b = to_bf16(grad_projected)
    grad_first = jnp.dot(grad_proj_b, full_qkv.T, preferred_element_type=f32)
    grad_input_part, gain_one_grad = rms_backward(
        grad_first, normed_one, scale_one, gain_one.astype(f32)
    )
    input_row_grad = grad_residual + grad_input_part
    small = jnp.concatenate(
        [
            bias_grad.reshape(parts, -1),
            gain_one_grad.reshape(parts, -1),
            gain_two_grad.reshape(parts, -1),
        ],
        -1,
    )
    small = jnp.pad(small, ((0, 0), (0, qkv_columns - small.shape[1])))[:, None]
    grad_rows = (depth + 8) // 8 * 8
    packed_grad = jnp.concatenate(
        [
            contract_rows(first_in, grad_proj_b).reshape(parts, depth, qkv_columns),
            small,
            jnp.zeros((parts, grad_rows - depth - 1, qkv_columns), f32),
        ],
        1,
    ).reshape(parts * grad_rows, qkv_columns)
    packed_grad, output_row = lax.optimization_barrier((packed_grad, output_row))
    packed_sum = sum_ctx(lax.psum_scatter(packed_grad, "seq", scatter_dimension=0, tiled=True))
    result_qkv = packed_sum[:depth]
    result_bias = packed_sum[depth, :bias_count]
    result_gain_one = packed_sum[depth, bias_count : bias_count + depth]
    result_gain_two = packed_sum[depth, bias_count + depth : bias_count + 2 * depth]
    result_out = sum_ctx(out_grad)
    return (
        output_row[None],
        input_row_grad[None],
        result_qkv,
        result_bias,
        result_out,
        result_gate_up,
        result_down,
        result_gain_one,
        result_gain_two,
    )


def shards_fast(
    tokens,
    positions,
    cotangent,
    qkv_weight,
    qkv_bias,
    out_weight,
    gate_up_weight,
    down_weight,
    attn_gain,
    ffn_gain,
):
    f32 = jnp.float32
    qkv_columns = qkv_weight.shape[1]
    depth = qkv_weight.shape[0]
    bias_count = qkv_bias.shape[0]
    packed_rows = packed_height(depth)
    parts = lax.axis_size("seq")
    hidden = down_weight.shape[0]
    extra = jnp.concatenate([qkv_bias, attn_gain, ffn_gain])
    extra = jnp.pad(extra, (0, qkv_columns - extra.shape[0]))[None]
    qkv_packed = jnp.concatenate(
        [qkv_weight, extra, jnp.zeros((packed_rows - depth - 1, qkv_columns), extra.dtype)], 0
    )
    out_packed = jnp.pad(out_weight, ((0, packed_rows - depth), (0, 0)))
    inputs_f = tokens[0].astype(f32)
    cot_row = cotangent[0]
    row_count = inputs_f.shape[0]
    group_size = HEADS // KV_HEADS
    query_width = HEADS * HEAD_DIM
    key_width = KV_HEADS * HEAD_DIM
    score_scale = HEAD_DIM ** (-0.5)
    at_ctx = lax.axis_index("ctx")
    position_row = lax.dynamic_slice_in_dim(positions[0], at_ctx * row_count, row_count, 0)
    other_row = lax.dynamic_slice_in_dim(positions[0], (1 - at_ctx) * row_count, row_count, 0)
    cosine_table, sine_table = rope_tables(position_row)
    cos_query = cosine_table[:, None, None, :]
    sin_query = sine_table[:, None, None, :]
    cos_key = cosine_table[:, None, :]
    sin_key = sine_table[:, None, :]
    tables = [jnp.concatenate([table, table], -1) for table in (cosine_table, sine_table)]
    (
        full_qkv,
        full_out,
        all_cot,
        weight_wide,
        gains,
        first_in,
        query_flat,
        both,
        probs,
        attended_flat,
        residual,
        second_in,
    ) = forward(
        qkv_packed,
        out_packed,
        cot_row,
        gate_up_weight,
        tokens[0],
        tables,
        position_row[:, None],
        jnp.concatenate([position_row, other_row])[None],
        bias_count,
        0,
    )
    gain_one, gain_two = gains[0], gains[1]
    normed_one, scale_one = rms_forward(inputs_f)
    normed_two, scale_two = rms_forward(residual)
    query_rot = query_flat.reshape(row_count, KV_HEADS, group_size, HEAD_DIM)
    both = both.reshape(-1, 2 * key_width)
    all_keys = both[:, :key_width].reshape(-1, KV_HEADS, HEAD_DIM)
    all_values = both[:, key_width:].reshape(-1, KV_HEADS, HEAD_DIM)
    probs = probs.reshape(KV_HEADS, group_size, row_count, -1)
    probs_b = to_bf16(probs)
    attended = attended_flat.reshape(row_count, KV_HEADS, group_size, HEAD_DIM)
    down_sum_width = padded(hidden)
    extra_rows = down_sum_width - hidden
    down_wide = jnp.pad(down_weight, ((0, extra_rows), (0, 0)))
    grad_second, down_part, down_mine, gate_mine, gate_theirs = ffn(
        second_in, all_cot, weight_wide, down_wide, hidden, 1
    )
    down_total = lax.psum_scatter(down_part, "seq", scatter_dimension=0, tiled=True)
    output_row = (residual + down_total.astype(f32)).astype(jnp.bfloat16)
    gate_other = other(gate_theirs)
    result_down = down_mine.astype(f32) + other(down_mine).astype(f32)
    grad_through, gain_two_grad = rms_backward(
        grad_second, normed_two, scale_two, gain_two.astype(f32)
    )
    grad_residual = cot_row.astype(f32) + grad_through
    grad_res_b = to_bf16(grad_residual)
    grad_attended = to_bf16(jnp.dot(grad_res_b, full_out.T, preferred_element_type=f32))
    grad_attended = grad_attended.reshape(row_count, KV_HEADS, group_size, HEAD_DIM)
    grad_probs = jnp.einsum("tkgd,skd->kgts", grad_attended, all_values, preferred_element_type=f32)
    delta = jnp.sum(grad_attended.astype(f32) * attended.astype(f32), axis=-1)
    delta = jnp.transpose(delta, (1, 2, 0))[..., None]
    grad_scores = to_bf16(probs * (grad_probs - delta) * score_scale)
    grad_query_rot = jnp.einsum("kgts,skd->tkgd", grad_scores, all_keys, preferred_element_type=f32)
    key_part = jnp.einsum("kgts,tkgd->skd", grad_scores, query_rot, preferred_element_type=f32)
    value_part = jnp.einsum("kgts,tkgd->skd", probs_b, grad_attended, preferred_element_type=f32)
    key_parts = jnp.concatenate(
        [
            key_part.reshape(row_count * lax.axis_size("ctx"), key_width),
            value_part.reshape(row_count * lax.axis_size("ctx"), key_width),
        ],
        -1,
    )
    if lax.axis_size("ctx") == 2:
        key_local = key_parts[:row_count] + other(key_parts[row_count:])
    else:
        key_local = lax.psum_scatter(key_parts, "ctx", scatter_dimension=0, tiled=True)
    grad_key_rot = key_local[:, :key_width].reshape(row_count, KV_HEADS, HEAD_DIM)
    grad_value = key_local[:, key_width:]
    grad_query = grad_query_rot * cos_query + rotate_back(grad_query_rot * sin_query)
    grad_key = grad_key_rot * cos_key + rotate_back(grad_key_rot * sin_key)
    grad_projected = jnp.concatenate(
        [
            grad_query.reshape(row_count, query_width),
            grad_key.reshape(row_count, key_width),
            grad_value,
        ],
        -1,
    )
    bias_grad = jnp.sum(grad_projected, axis=0)
    grad_proj_b = to_bf16(grad_projected)
    grad_first = jnp.dot(grad_proj_b, full_qkv.T, preferred_element_type=f32)
    grad_input_part, gain_one_grad = rms_backward(
        grad_first, normed_one, scale_one, gain_one.astype(f32)
    )
    input_row_grad = grad_residual + grad_input_part
    small = jnp.concatenate(
        [
            bias_grad.reshape(parts, -1),
            gain_one_grad.reshape(parts, -1),
            gain_two_grad.reshape(parts, -1),
        ],
        -1,
    )
    small_width = padded(small.shape[1])
    small = jnp.pad(small, ((0, 0), (0, small_width - small.shape[1])))[:, None]
    small = jnp.pad(small, ((0, 0), (0, 7), (0, 0))).reshape(4, 2, 2, 8, small_width)
    small = jnp.transpose(small, (2, 0, 1, 3, 4))
    qkv_sum, out_sum, small_sum, result_gate_up = reduce_grads(
        first_in, grad_proj_b, attended_flat, grad_res_b, small, gate_mine, gate_other, hidden, 2
    )
    result_qkv = qkv_sum[:depth]
    result_out = out_sum[:depth]
    result_bias = small_sum[0, :bias_count]
    result_gain_one = small_sum[0, bias_count : bias_count + depth]
    result_gain_two = small_sum[0, bias_count + depth : bias_count + 2 * depth]
    return (
        output_row[None],
        input_row_grad[None],
        result_qkv,
        result_bias,
        result_out,
        result_gate_up,
        result_down,
        result_gain_one,
        result_gain_two,
    )


def solution(mesh):
    in_specs = (
        P("seq", "ctx", None),
        P("seq", None),
        P("seq", "ctx", None),
        P("seq", None),
        P("seq"),
        P("seq", None),
        P("seq", None),
        P("seq", None),
        P("seq"),
        P("seq"),
    )
    out_specs = (
        P("seq", "ctx", None),
        P("seq", "ctx", None),
        P("seq", None),
        P("seq"),
        P("seq", None),
        P("seq", None),
        P("seq", None),
        P("seq"),
        P("seq"),
    )
    fast = mesh.shape["ctx"] == 2 and mesh.shape["seq"] == 16
    return jax.shard_map(shards_fast if fast else shards, mesh=mesh, in_specs=in_specs, out_specs=out_specs, check_vma=False)
```

```python
import functools

import jax
import jax.numpy as jnp
from jax import lax
from jax.experimental import pallas as pl
from jax.experimental.pallas import tpu as pltpu
from jax.sharding import PartitionSpec as P

HEADS = 14
KV_HEADS = 2
HEAD_DIM = 64


EPS = 1e-06
ROPE_BASE = 1000000.0


def to_bf16(values):
    return lax.optimization_barrier(values.astype(jnp.bfloat16))


def rope_tables(position_row):
    half_dim = HEAD_DIM // 2
    exponent = jnp.arange(half_dim, dtype=jnp.float32) * (2.0 / HEAD_DIM)
    inverse = ROPE_BASE ** (-exponent)
    angles = position_row.astype(jnp.float32)[:, None] * inverse[None, :]
    cosine_table = jnp.cos(angles)
    sine_table = jnp.sin(angles)
    return (
        jnp.concatenate([cosine_table, cosine_table], -1),
        jnp.concatenate([sine_table, sine_table], -1),
    )


def rotate_half(values):
    half_dim = values.shape[-1] // 2
    return jnp.concatenate([-values[..., half_dim:], values[..., :half_dim]], -1)


def rotate_back(values):
    half_dim = values.shape[-1] // 2
    return jnp.concatenate([values[..., half_dim:], -values[..., :half_dim]], -1)


def rms_forward(values):
    scaling = lax.rsqrt(jnp.mean(values * values, axis=-1, keepdims=True) + EPS)
    return (values * scaling, scaling)


def rms_backward(grad_normed, normed, scaling, gain_float):
    gain_grad = jnp.sum(grad_normed * normed, axis=0)
    grad_scaled = grad_normed * gain_float
    inner = jnp.mean(grad_scaled * normed, axis=-1, keepdims=True)
    return (scaling * (grad_scaled - normed * inner), gain_grad)


def weight_rows(left_side, right_side):
    return lax.psum_scatter(
        lax.dot_general(
            left_side, right_side, (((0,), (0,)), ((), ())), preferred_element_type=jnp.float32
        ),
        "seq",
        scatter_dimension=0,
        tiled=True,
    )


def columns_from_rows(rows, parts):
    depth = rows.shape[0]
    hidden = rows.shape[1] // (2 * parts)
    split = jnp.transpose(rows.reshape(depth, 2, parts, hidden), (2, 0, 1, 3))
    split = split.reshape(parts, depth, 2 * hidden)
    moved = lax.all_to_all(split, "seq", split_axis=0, concat_axis=0, tiled=True)
    return moved.reshape(parts * depth, 2 * hidden)


def rows_from_columns(columns, parts):
    depth = columns.shape[0] // parts
    hidden = columns.shape[1] // 2
    split = columns.reshape(parts, depth, 2 * hidden)
    moved = lax.all_to_all(split, "seq", split_axis=0, concat_axis=0, tiled=True)
    moved = jnp.transpose(moved.reshape(parts, depth, 2, hidden), (1, 2, 0, 3))
    return moved.reshape(depth, 2 * parts * hidden)


def contract_rows(left_side, right_side):
    return lax.dot_general(
        left_side, right_side, (((0,), (0,)), ((), ())), preferred_element_type=jnp.float32
    )


def contract_columns(left_side, right_side):
    return lax.dot_general(
        left_side, right_side, (((1,), (1,)), ((), ())), preferred_element_type=jnp.float32
    )


def scatter_tokens(partial):
    total = lax.psum_scatter(to_bf16(partial), "seq", scatter_dimension=0, tiled=True)
    return total.astype(jnp.float32)


def gather_kernel(outer, own_ref, all_ref, local_sem, outer_sems, middle_sems, core_sems):
    me = lax.axis_index("seq")
    at_outer = me // 4
    middle = (me // 2) % 2
    core = me % 2
    rows = own_ref.shape[0]

    def place(outer_at, middle_at, core_at):
        index = outer_at * 4 + middle_at * 2 + core_at
        return all_ref.at[pl.ds(pl.multiple_of(index * rows, rows), rows)]

    def remote(source, target, sems, slot, device):
        return pltpu.make_async_remote_copy(
            src_ref=source,
            dst_ref=target,
            send_sem=sems.at[0, slot],
            recv_sem=sems.at[1, slot],
            device_id={"seq": device},
            device_id_type=pl.DeviceIdType.MESH,
        )

    middle_partner = at_outer * 4 + (1 - middle) * 2 + core
    core_partner = at_outer * 4 + middle * 2 + (1 - core)
    outer_partners = [
        ((at_outer + step) % outer) * 4 + middle * 2 + core for step in range(1, outer)
    ]
    barrier = pltpu.get_barrier_semaphore()
    for device in [middle_partner, core_partner] + outer_partners:
        pl.semaphore_signal(
            barrier, inc=1, device_id={"seq": device}, device_id_type=pl.DeviceIdType.MESH
        )
    pl.semaphore_wait(barrier, outer + 1)

    own_place = place(at_outer, middle, core)
    local = pltpu.make_async_copy(own_ref, own_place, local_sem)
    local.start()
    started = []
    outer_copies = []
    for step in range(1, outer):
        copy = remote(own_ref, own_place, outer_sems, step - 1, outer_partners[step - 1])
        copy.start()
        outer_copies.append(copy)
    middle_copies = []
    for step in range(outer):
        source_outer = (at_outer + outer - step) % outer
        here = place(source_outer, middle, core)
        if step == 0:
            source = own_ref
        else:
            outer_copies[step - 1].wait_recv()
            source = here
        copy = remote(source, here, middle_sems, step, middle_partner)
        copy.start()
        middle_copies.append(copy)
        copy = remote(source, here, core_sems, 2 * step, core_partner)
        copy.start()
        started.append(copy)
    for step in range(outer):
        source_outer = (at_outer + outer - step) % outer
        middle_copies[step].wait_recv()
        here = place(source_outer, 1 - middle, core)
        copy = remote(here, here, core_sems, 2 * step + 1, core_partner)
        copy.start()
        started.append(copy)
    for copy in started:
        copy.wait_recv()
    for copy in outer_copies + middle_copies + started:
        copy.wait_send()
    local.wait()


def gather_rows(rows, collective_id):
    parts = lax.axis_size("seq")
    if parts % 4:
        return lax.all_gather(rows, "seq", axis=0, tiled=True)
    outer = parts // 4
    return pl.pallas_call(
        functools.partial(gather_kernel, outer),
        out_shape=jax.ShapeDtypeStruct((parts * rows.shape[0], rows.shape[1]), rows.dtype),
        in_specs=[pl.BlockSpec(memory_space=pltpu.VMEM)],
        out_specs=pl.BlockSpec(memory_space=pltpu.VMEM),
        scratch_shapes=[
            pltpu.SemaphoreType.DMA,
            pltpu.SemaphoreType.DMA((2, max(outer - 1, 1))),
            pltpu.SemaphoreType.DMA((2, outer)),
            pltpu.SemaphoreType.DMA((2, 2 * outer)),
        ],
        compiler_params=pltpu.CompilerParams(
            collective_id=collective_id, has_side_effects=True, vmem_limit_bytes=24 * 2**20
        ),
    )(rows)


def packed_height(depth):
    return (depth + 16) // 16 * 16


def other(values):
    return lax.ppermute(values, "ctx", [(0, 1), (1, 0)])


def sum_rounded(values):
    if lax.axis_size("ctx") != 2:
        return lax.psum(values, "ctx")
    mine = to_bf16(values)
    return mine.astype(jnp.float32) + other(mine).astype(jnp.float32)


def sum_ctx(values):
    if lax.axis_size("ctx") != 2:
        return lax.psum(values, "ctx")
    return values + other(values)


MESH = pl.DeviceIdType.MESH
LANES = 128


def padded(width):
    return (width + LANES - 1) // LANES * LANES


def remote_copy(source, target, send_sem, recv_sem, device):
    return pltpu.make_async_remote_copy(
        src_ref=source,
        dst_ref=target,
        send_sem=send_sem,
        recv_sem=recv_sem,
        device_id=device,
        device_id_type=MESH,
    )


def greet(devices):
    barrier = pltpu.get_barrier_semaphore()
    for device in devices:
        pl.semaphore_signal(barrier, inc=1, device_id=device, device_id_type=MESH)
    pl.semaphore_wait(barrier, len(devices))


def dot_last(left, right):
    return lax.dot_general(
        left, right, (((1,), (1,)), ((), ())), preferred_element_type=jnp.float32
    )


def dot_first(left, right):
    return lax.dot_general(
        left, right, (((0,), (0,)), ((), ())), preferred_element_type=jnp.float32
    )


def z_order(z):
    return (z + 1 - 2 * (z % 2), 2 - z // 2, 3 - 3 * (z // 2))


class Place:
    def __init__(self):
        me = lax.axis_index("seq")
        self.z = me // 4
        self.y = (me // 2) % 2
        self.k = me % 2
        self.c = lax.axis_index("ctx")
        self.me = me

    def seq(self, z, y, k):
        return {"seq": z * 4 + y * 2 + k}

    def others(self):
        z, y, k = self.z, self.y, self.k
        return (
            [self.seq(z, 1 - y, k), self.seq(z, y, 1 - k)]
            + [self.seq(other, y, k) for other in z_order(z)]
        )


class Gather:
    def __init__(self, at, own_ref, all_ref, send_sems, recv_sems, local_sem):
        self.at, self.own, self.all = at, own_ref, all_ref
        self.send_sems, self.recv_sems, self.local_sem = send_sems, recv_sems, local_sem
        self.rows = own_ref.shape[0]
        self.sent = []
        self.hop_sent = []

    def block(self, z, y, k):
        start = pl.multiple_of((z * 4 + y * 2 + k) * self.rows, self.rows)
        return self.all.at[pl.ds(start, self.rows)]

    def copy(self, source, z, y, k, kind, device, slot=None):
        return remote_copy(
            source,
            self.block(z, y, k),
            self.send_sems.at[z, kind if slot is None else slot],
            self.recv_sems.at[z, kind],
            device,
        )

    def to_y_and_core(self, source, z):
        at = self.at
        copy = self.copy(source, z, at.y, at.k, 1, at.seq(at.z, 1 - at.y, at.k))
        copy.start()
        self.sent.append(copy)
        self.to_core(source, z, at.y)

    def to_core(self, source, z, y):
        at = self.at
        copy = self.copy(source, z, y, at.k, 2 + y, at.seq(at.z, at.y, 1 - at.k))
        copy.start()
        self.sent.append(copy)

    def hop(self, source, z, right):
        at = self.at
        target = at.z + 1 if right else at.z - 1
        copy = self.copy(
            source, z, at.y, at.k, 0, at.seq(target, at.y, at.k), slot=None if right else 4
        )
        ok = (target < 4) if right else (target >= 0)
        return ok, copy

    def begin(self):
        at = self.at
        for right in (True, False):
            ok, copy = self.hop(self.own, at.z, right)
            self.hop_sent.append((ok, copy))

            @pl.when(ok)
            def _():
                copy.start()

        self.to_y_and_core(self.own, at.z)
        self.local = pltpu.make_async_copy(
            self.own, self.block(at.z, at.y, at.k), self.local_sem
        )
        self.local.start()

    def from_z(self, z):
        at = self.at
        here = self.block(z, at.y, at.k)
        self.copy(here, z, at.y, at.k, 0, at.seq(at.z, 1 - at.y, at.k)).wait_recv()
        for right in (True, False):
            ok, copy = self.hop(here, z, right)
            ok = jnp.logical_and(ok, z < at.z if right else z > at.z)
            self.hop_sent.append((ok, copy))

            @pl.when(ok)
            def _():
                copy.start()

        self.to_y_and_core(here, z)

    def from_y(self, z):
        at = self.at
        here = self.block(z, 1 - at.y, at.k)
        self.copy(here, z, 1 - at.y, at.k, 1, at.seq(at.z, 1 - at.y, at.k)).wait_recv()
        self.to_core(here, z, 1 - at.y)

    def from_core(self, z):
        at = self.at
        for y in range(2):
            here = self.block(z, y, 1 - at.k)
            self.copy(here, z, y, 1 - at.k, 2 + y, at.seq(at.z, at.y, 1 - at.k)).wait_recv()

    def end(self):
        for copy in self.sent:
            copy.wait_send()
        for ok, copy in self.hop_sent:

            @pl.when(ok)
            def _():
                copy.wait_send()


class Scatter:
    def __init__(self, at, part, core_buf, y_buf, z_buf, out_ref, send_sems, recv_sems):
        self.at, self.part, self.out = at, part, out_ref
        self.core_buf, self.y_buf, self.z_buf = core_buf, y_buf, z_buf
        self.send_sems, self.recv_sems = send_sems, recv_sems
        self.rows = out_ref.shape[0]
        self.sent = []
        self.core_copies = {}

    def block(self, z, y, k):
        start = pl.multiple_of((z * 4 + y * 2 + k) * self.rows, self.rows)
        return self.part.at[pl.ds(start, self.rows)]

    def core_copy(self, z, y):
        at = self.at
        return remote_copy(
            self.block(z, y, 1 - at.k),
            self.core_buf.at[z, y],
            self.send_sems.at[z, y],
            self.recv_sems.at[z, y],
            at.seq(at.z, at.y, 1 - at.k),
        )

    def to_core(self, z):
        for y in range(2):
            copy = self.core_copy(z, y)
            copy.start()
            self.sent.append(copy)

    def y_copy(self, z):
        at = self.at
        return remote_copy(
            self.core_buf.at[z, 1 - at.y],
            self.y_buf.at[z],
            self.send_sems.at[z, 2],
            self.recv_sems.at[z, 2],
            at.seq(at.z, 1 - at.y, at.k),
        )

    def add_core(self, z, y):
        here = self.block(z, y, self.at.k)
        total = here[...].astype(jnp.float32) + self.core_buf[z, y].astype(jnp.float32)
        self.core_buf[z, y] = total.astype(jnp.bfloat16)

    def to_y(self, z):
        at = self.at
        for y in range(2):
            self.core_copy(z, y).wait_recv()
        self.add_core(z, 1 - at.y)
        copy = self.y_copy(z)
        copy.start()
        self.sent.append(copy)
        self.add_core(z, at.y)

    def z_copy(self, z, source_z):
        at = self.at
        return remote_copy(
            self.y_buf.at[z],
            self.z_buf.at[source_z],
            self.send_sems.at[z, 3],
            self.recv_sems.at[source_z, 3],
            at.seq(z, at.y, at.k),
        )

    def to_z(self, z, own):
        at = self.at
        self.y_copy(z).wait_recv()
        total = self.core_buf[z, at.y].astype(jnp.float32) + self.y_buf[z].astype(jnp.float32)
        if own:
            self.out[...] = total
        else:
            self.y_buf[z] = total.astype(jnp.bfloat16)
            copy = self.z_copy(z, at.z)
            copy.start()
            self.sent.append(copy)

    def finish(self):
        at = self.at
        total = self.out[...]
        for z in z_order(at.z):
            self.z_copy(z, z).wait_recv()
            total += self.z_buf[z].astype(jnp.float32)
        self.out[...] = total

    def end(self):
        for copy in self.sent:
            copy.wait_send()


def ffn_kernel(
    own_ref,
    cot_ref,
    weight_ref,
    down_ref,
    second_sum_ref,
    down_part_ref,
    down_grad_ref,
    gate_mine_ref,
    gate_theirs_ref,
    all_ref,
    act_ref,
    grad_ref,
    part_ref,
    core_buf,
    y_buf,
    z_buf,
    flat_ref,
    down_send,
    down_recv,
    gather_send,
    gather_recv,
    local_sem,
    scatter_send,
    scatter_recv,
    x_sems,
):
    at = Place()
    width = down_ref.shape[0]
    rows = own_ref.shape[0]
    parts = all_ref.shape[0] // rows
    depth = weight_ref.shape[0] // parts
    other_ctx = {"ctx": 1 - at.c}
    greet(at.others() + [other_ctx])
    gather = Gather(at, own_ref, all_ref, gather_send, gather_recv, local_sem)
    second = Scatter(
        at, part_ref, core_buf, y_buf, z_buf, second_sum_ref, scatter_send, scatter_recv
    )
    tile = 2 * rows

    def compute(z):
        def step(index, carry):
            start = pl.multiple_of(z * (4 * rows) + index * tile, tile)
            here = pl.ds(start, tile)
            gate_up = jnp.dot(
                all_ref[here], weight_ref[...], preferred_element_type=jnp.float32
            )
            grad_act = dot_last(cot_ref[here], down_ref[...])
            gate = gate_up[:, :width]
            upward = gate_up[:, width:]
            sigmoid_gate = jax.nn.sigmoid(gate)
            silu = gate * sigmoid_gate
            activated = (silu * upward).astype(jnp.bfloat16)
            act_ref[here] = activated
            grad_gate = grad_act * upward * sigmoid_gate * (1.0 + gate * (1.0 - sigmoid_gate))
            grad_ref[here, :width] = grad_gate.astype(jnp.bfloat16)
            grad_ref[here, width:] = (grad_act * silu).astype(jnp.bfloat16)
            part_ref[here] = dot_last(grad_ref[here], weight_ref[...]).astype(jnp.bfloat16)
            down_part_ref[here] = jnp.dot(
                activated, down_ref[...], preferred_element_type=jnp.float32
            ).astype(jnp.bfloat16)
            return carry

        lax.fori_loop(0, 2, step, 0)

    order = (at.z,) + z_order(at.z)
    gather.begin()
    for index, z in enumerate(order):
        if index + 1 < len(order):
            gather.from_z(order[index + 1])
        gather.from_y(z)
        if index == 0:
            gather.local.wait()
        gather.from_core(z)
        if index > 0:
            second.to_y(order[index - 1])
        compute(z)
        second.to_core(z)
        if index > 0:
            second.to_z(order[index - 1], index == 1)
    last = order[-1]

    def gate_tile(index, carry):
        columns = pl.ds(pl.multiple_of(index * LANES, LANES), LANES)
        flat_ref[columns] = dot_first(all_ref[:, columns], grad_ref[...])
        return carry

    def columns_of(ctx):
        return pl.ds(pl.multiple_of(ctx * width, LANES), width)

    down_grad = dot_first(act_ref[...], cot_ref[...])
    hidden = down_grad_ref.shape[0]
    down_send[...] = down_grad[:hidden].astype(jnp.bfloat16)
    down_copy = remote_copy(down_send, down_recv, x_sems.at[0], x_sems.at[1], other_ctx)
    down_copy.start()
    second.to_y(last)
    tiles = all_ref.shape[1] // LANES
    lax.fori_loop(0, tiles, gate_tile, 0)
    second.to_z(last, False)
    for part in range(parts):
        here = slice(part * depth, (part + 1) * depth)
        gate_mine_ref[part] = flat_ref[here, columns_of(at.c)].astype(jnp.bfloat16)
        gate_theirs_ref[part] = flat_ref[here, columns_of(1 - at.c)].astype(jnp.bfloat16)
    down_copy.wait_recv()
    down_grad_ref[...] = down_send[...].astype(jnp.float32) + down_recv[...].astype(jnp.float32)
    second.finish()
    down_copy.wait_send()
    gather.end()
    second.end()


def ffn(second_in, all_cot, weight, down, hidden, collective_id):
    rows, model = second_in.shape
    parts = all_cot.shape[0] // rows
    width = down.shape[0]
    depth = model // parts
    tokens = parts * rows
    f32, bf16 = jnp.float32, jnp.bfloat16
    vmem = pl.BlockSpec(memory_space=pltpu.VMEM)
    flops = 2 * tokens * model * width * 9
    return pl.pallas_call(
        ffn_kernel,
        out_shape=(
            jax.ShapeDtypeStruct((rows, model), f32),
            jax.ShapeDtypeStruct((tokens, model), bf16),
            jax.ShapeDtypeStruct((hidden, model), f32),
            jax.ShapeDtypeStruct((parts, depth, width), bf16),
            jax.ShapeDtypeStruct((parts, depth, width), bf16),
        ),
        in_specs=[vmem] * 4,
        out_specs=(vmem,) * 5,
        scratch_shapes=[
            pltpu.VMEM((tokens, model), bf16),
            pltpu.VMEM((tokens, width), bf16),
            pltpu.VMEM((tokens, 2 * width), bf16),
            pltpu.VMEM((tokens, model), bf16),
            pltpu.VMEM((4, 2, rows, model), bf16),
            pltpu.VMEM((4, rows, model), bf16),
            pltpu.VMEM((4, rows, model), bf16),
            pltpu.VMEM((model, 2 * width), f32),
            pltpu.VMEM((hidden, model), bf16),
            pltpu.VMEM((hidden, model), bf16),
            pltpu.SemaphoreType.DMA((4, 5)),
            pltpu.SemaphoreType.DMA((4, 4)),
            pltpu.SemaphoreType.DMA,
            pltpu.SemaphoreType.DMA((4, 4)),
            pltpu.SemaphoreType.DMA((4, 4)),
            pltpu.SemaphoreType.DMA((2,)),
        ],
        compiler_params=pltpu.CompilerParams(
            collective_id=collective_id, has_side_effects=True, vmem_limit_bytes=48 * 2**20
        ),
        cost_estimate=pl.CostEstimate(
            flops=flops, bytes_accessed=16 * 2**20, transcendentals=tokens * width
        ),
    )(second_in, all_cot, weight, down)


class SharedGather(Gather):
    def __init__(self, at, own_ref, all_ref, send_sems, recv_sems, local_sem):
        self.at, self.whole_all = at, all_ref
        self.count = own_ref.shape[0] // 2
        self.mine = self.half(at.c)
        self.theirs = self.half(1 - at.c)
        self.own = own_ref.at[self.mine]
        self.all = all_ref
        self.send_sems, self.recv_sems, self.local_sem = send_sems, recv_sems, local_sem
        self.sent = []
        self.hop_sent = []

    def half(self, ctx):
        return pl.ds(pl.multiple_of(ctx * self.count, self.count), self.count)

    def block(self, z, y, k, rows=None):
        return self.all.at[z * 4 + y * 2 + k, self.mine if rows is None else rows]

    def to_core(self, source, z, y):
        super().to_core(source, z, y)
        self.to_x(source, z, y)

    def x_copy(self, source, z, y, rows):
        at = self.at
        return remote_copy(
            source,
            self.block(z, y, at.k, rows),
            self.send_sems.at[z, 5 + y],
            self.recv_sems.at[z, 4 + y],
            {"ctx": 1 - at.c},
        )

    def to_x(self, source, z, y):
        copy = self.x_copy(source, z, y, self.mine)
        copy.start()
        self.sent.append(copy)

    def core_again(self, z, y, k):
        at = self.at
        here = self.block(z, y, k, self.theirs)
        return remote_copy(
            here,
            here,
            self.send_sems.at[z, 7 + y],
            self.recv_sems.at[z, 6 + y],
            at.seq(at.z, at.y, 1 - at.k),
        )

    def from_x(self, z, y):
        at = self.at
        here = self.block(z, y, at.k, self.theirs)
        self.x_copy(here, z, y, self.theirs).wait_recv()
        copy = self.core_again(z, y, at.k)
        copy.start()
        self.sent.append(copy)

    def from_core(self, z):
        super().from_core(z)
        for y in range(2):
            self.core_again(z, y, 1 - self.at.k).wait_recv()


def rotated(values):
    width = values.shape[1]
    half = HEAD_DIM // 2
    lane = lax.broadcasted_iota(jnp.int32, values.shape, 1) % HEAD_DIM
    ahead = pltpu.roll(values, width - half, 1)
    behind = pltpu.roll(values, half, 1)
    return jnp.where(lane < half, -ahead, behind)


def tiled(table, width):
    return jnp.concatenate([table] * (width // table.shape[1]), 1)


def head_columns(head):
    return slice(head * HEAD_DIM, (head + 1) * HEAD_DIM)


def forward_kernel(
    qkv_ref,
    out_ref,
    cot_ref,
    gate_up_ref,
    tokens_ref,
    cos_ref,
    sin_ref,
    query_pos_ref,
    key_pos_ref,
    full_qkv_ref,
    full_out_ref,
    all_cot_ref,
    weight_ref,
    gains_ref,
    first_ref,
    query_ref,
    kv_ref,
    probs_ref,
    attended_ref,
    residual_ref,
    second_ref,
    all_qkv_ref,
    all_out_ref,
    bias_ref,
    gate_send,
    gate_all,
    qkv_send,
    qkv_recv,
    out_send,
    out_recv,
    cot_send,
    cot_recv,
    local_sems,
    gate_sems,
    x_sems,
    kv_sems,
):
    f32, bf16 = jnp.float32, jnp.bfloat16
    at = Place()
    parts, depth, width = gate_send.shape
    half = gate_up_ref.shape[1] // 2
    hidden = half // parts
    bias_count = bias_ref.shape[1] // parts
    query_width = HEADS * HEAD_DIM
    key_width = KV_HEADS * HEAD_DIM
    seq_peers = [lax.rem(at.me + step, parts) for step in range(1, parts)]
    other_ctx = {"ctx": 1 - at.c}
    greet([{"seq": peer} for peer in seq_peers] + [other_ctx])
    qkv = SharedGather(at, qkv_ref, all_qkv_ref, qkv_send, qkv_recv, local_sems.at[0])
    out = SharedGather(at, out_ref, all_out_ref, out_send, out_recv, local_sems.at[1])
    cot = Gather(at, cot_ref, all_cot_ref, cot_send, cot_recv, local_sems.at[2])
    order = (at.z,) + z_order(at.z)
    qkv.begin()
    half_value = gate_up_ref[:, pl.ds(pl.multiple_of(at.c * half, LANES), half)]
    tail = jnp.zeros((depth, width - hidden), gate_send.dtype)
    for part in range(parts):
        gate_send[part, :, :hidden] = half_value[:, part * hidden : (part + 1) * hidden]
        gate_send[part, :, hidden:] = tail
    qkv.from_y(order[0])
    qkv.from_z(order[1])
    out.begin()
    qkv.from_y(order[1])
    qkv.from_z(order[2])
    gate_copies = []

    def gate_start(steps):
        for step in steps:
            peer = lax.rem(at.me + step, parts)
            copy = remote_copy(
                gate_send.at[peer],
                gate_all.at[at.c, at.me],
                gate_sems.at[0, step - 1],
                gate_sems.at[1, step - 1],
                {"seq": peer},
            )
            copy.start()
            gate_copies.append(copy)

    def gate_x(source, ctx, step):
        here = gate_all.at[ctx, source]
        return remote_copy(here, here, x_sems.at[0, step], x_sems.at[1, step], other_ctx)

    def gate_arrive(steps):
        for step in steps:
            source = lax.rem(at.me + parts - step, parts)
            if step > 0:
                remote_copy(
                    gate_send.at[source],
                    gate_all.at[at.c, source],
                    gate_sems.at[0, step - 1],
                    gate_sems.at[1, step - 1],
                    {"seq": source},
                ).wait_recv()
            copy = gate_x(source, at.c, step)
            copy.start()
            gate_copies.append(copy)

    gate_all[at.c, at.me] = gate_send[at.me]
    qkv.from_y(order[2])
    qkv.from_z(order[3])
    cot.begin()
    qkv.from_y(order[3])
    out.from_y(order[0])
    out.from_z(order[1])
    for z in order:
        for y in range(2):
            qkv.from_x(z, y)
    out.from_y(order[1])
    out.from_z(order[2])
    qkv.local.wait()
    for z in order:
        qkv.from_core(z)
    gate_start(range(1, parts))
    cot.from_y(order[0])
    cot.from_z(order[1])
    for part in range(parts):
        rows = pl.ds(part * depth, depth)
        full_qkv_ref[rows] = all_qkv_ref[part, :depth]
        extra = all_qkv_ref[part, depth : depth + 1, : bias_count + 2 * depth].astype(f32)
        bias_ref[:, part * bias_count : (part + 1) * bias_count] = extra[:, :bias_count]
        for index in range(2):
            start = bias_count + index * depth
            gains_ref[index : index + 1, part * depth : (part + 1) * depth] = extra[
                :, start : start + depth
            ]
    tokens = tokens_ref[...].astype(f32)
    normed_one, _ = rms_forward(tokens)
    first_ref[...] = (normed_one * gains_ref[0:1]).astype(bf16)
    projected = (
        jnp.dot(first_ref[...], full_qkv_ref[...], preferred_element_type=f32) + bias_ref[...]
    )
    rotary = projected[:, : query_width + key_width]
    turned = rotary * tiled(cos_ref[...], rotary.shape[1]) + rotated(rotary) * tiled(
        sin_ref[...], rotary.shape[1]
    )
    turned = turned.astype(bf16)
    query_ref[...] = turned[:, :query_width]
    kv_ref[0, :, :key_width] = turned[:, query_width:]
    kv_ref[0, :, key_width:] = projected[:, query_width + key_width :].astype(bf16)
    kv_copy = remote_copy(kv_ref.at[0], kv_ref.at[1], kv_sems.at[0], kv_sems.at[1], other_ctx)
    kv_copy.start()
    out.from_y(order[2])
    out.from_z(order[3])
    cot.from_y(order[1])
    cot.from_z(order[2])
    out.from_y(order[3])
    for z in order:
        for y in range(2):
            out.from_x(z, y)
    kv_copy.wait_recv()
    rows = tokens.shape[0]
    kv = kv_ref[...].reshape(2 * rows, 2 * key_width)
    allowed = key_pos_ref[...] <= query_pos_ref[...]
    group_size = HEADS // KV_HEADS

    def attend(head):
        keys = kv[:, head_columns(head // group_size)]
        values = kv[:, head_columns(KV_HEADS + head // group_size)]
        scores = dot_last(query_ref[:, head_columns(head)], keys) * (HEAD_DIM ** (-0.5))
        scores = jnp.where(allowed, scores, -1e30)
        row_top = jnp.max(scores, axis=-1, keepdims=True)
        log_total = row_top + jnp.log(
            jnp.sum(jnp.exp(scores - row_top), axis=-1, keepdims=True)
        )
        probs = jnp.exp(scores - log_total)
        probs_ref[head] = probs
        attended_ref[:, head_columns(head)] = jnp.dot(
            probs.astype(bf16), values, preferred_element_type=f32
        ).astype(bf16)

    for head in range(group_size):
        attend(head)
    cot.from_y(order[2])
    cot.from_z(order[3])
    gate_arrive(range(0, parts // 2))
    for head in range(group_size, HEADS):
        attend(head)
    cot.from_y(order[3])
    out.local.wait()
    for z in order:
        out.from_core(z)
    for part in range(parts):
        full_out_ref[pl.ds(part * depth, depth)] = all_out_ref[part, :depth]
    residual = tokens + jnp.dot(
        attended_ref[...], full_out_ref[...], preferred_element_type=f32
    )
    residual_ref[...] = residual
    normed_two, _ = rms_forward(residual)
    second_ref[...] = (normed_two * gains_ref[1:2]).astype(bf16)
    gate_arrive(range(parts // 2, parts))
    for z in order:
        cot.from_core(z)
    for step in range(parts):
        gate_x(lax.rem(at.me + parts - step, parts), 1 - at.c, step).wait_recv()
    for part in range(parts):
        rows = pl.ds(part * depth, depth)
        weight_ref[rows, :width] = gate_all[0, part]
        weight_ref[rows, width:] = gate_all[1, part]
    kv_copy.wait_send()
    for copy in gate_copies:
        copy.wait_send()
    cot.local.wait()
    for gather in (qkv, out, cot):
        gather.end()


def forward(qkv, out, cot, gate_up, tokens, tables, query_pos, key_pos, bias_count, collective_id):
    parts = lax.axis_size("seq")
    rows = qkv.shape[0]
    depth = gate_up.shape[0]
    hidden = gate_up.shape[1] // (2 * parts)
    width = padded(hidden)
    count, model = cot.shape
    f32, bf16 = jnp.float32, jnp.bfloat16
    query_width = HEADS * HEAD_DIM
    key_width = KV_HEADS * HEAD_DIM
    shape = jax.ShapeDtypeStruct
    vmem = pl.BlockSpec(memory_space=pltpu.VMEM)
    outs = (
        shape((parts * depth, qkv.shape[1]), bf16),
        shape((parts * depth, out.shape[1]), bf16),
        shape((parts * count, model), bf16),
        shape((parts * depth, 2 * width), bf16),
        shape((2, model), f32),
        shape((count, model), bf16),
        shape((count, query_width), bf16),
        shape((2, count, 2 * key_width), bf16),
        shape((HEADS, count, 2 * count), f32),
        shape((count, query_width), bf16),
        shape((count, model), f32),
        shape((count, model), bf16),
    )
    return pl.pallas_call(
        forward_kernel,
        out_shape=outs,
        in_specs=[vmem] * 9,
        out_specs=(vmem,) * len(outs),
        scratch_shapes=[
            pltpu.VMEM((parts, rows, qkv.shape[1]), bf16),
            pltpu.VMEM((parts, rows, out.shape[1]), bf16),
            pltpu.VMEM((1, parts * bias_count), f32),
            pltpu.VMEM((parts, depth, width), bf16),
            pltpu.VMEM((2, parts, depth, width), bf16),
            pltpu.SemaphoreType.DMA((4, 9)),
            pltpu.SemaphoreType.DMA((4, 8)),
            pltpu.SemaphoreType.DMA((4, 9)),
            pltpu.SemaphoreType.DMA((4, 8)),
            pltpu.SemaphoreType.DMA((4, 5)),
            pltpu.SemaphoreType.DMA((4, 4)),
            pltpu.SemaphoreType.DMA((3,)),
            pltpu.SemaphoreType.DMA((2, parts - 1)),
            pltpu.SemaphoreType.DMA((2, parts)),
            pltpu.SemaphoreType.DMA((2,)),
        ],
        compiler_params=pltpu.CompilerParams(
            collective_id=collective_id, has_side_effects=True, vmem_limit_bytes=48 * 2**20
        ),
    )(qkv, out, cot, gate_up, tokens, *tables, query_pos, key_pos)


class Flow:
    def __init__(self, at, source, out_ref, bufs, sems, x_first, halves):
        self.at, self.source, self.out = at, source, out_ref
        (self.core_recv, self.x_send, self.x_recv, self.y_send, self.y_recv,
         self.z_send, self.z_recv, self.last_send, self.last_recv) = bufs
        self.sems = sems
        self.x_first, self.halves = x_first, halves
        rows = source.shape[3]
        self.count = rows // 2 if halves else rows
        self.mine = self.half(at.c) if halves else pl.ds(0, rows)
        self.theirs = self.half(1 - at.c) if halves else pl.ds(0, rows)
        self.all_rows = pl.ds(0, rows)
        self.sent = []

    def half(self, ctx):
        return pl.ds(pl.multiple_of(ctx * self.count, self.count), self.count)

    def send(self, source, target, slot, device, recv_slot=None):
        copy = remote_copy(
            source,
            target,
            self.sems.at[0, slot],
            self.sems.at[1, slot if recv_slot is None else recv_slot],
            device,
        )
        copy.start()
        self.sent.append(copy)
        return copy

    def begin(self):
        at = self.at
        self.core = self.send(
            self.source.at[1 - at.k], self.core_recv, 0, at.seq(at.z, at.y, 1 - at.k)
        )

    def add_core(self):
        at = self.at
        self.core.wait_recv()
        for z in range(4):
            for y in range(2):
                self.source[at.k, z, y] += self.core_recv[z, y]
        if self.x_first:
            self.to_x_both()
        else:
            self.to_y()

    def to_x_both(self):
        at = self.at
        for z in range(4):
            for y in range(2):
                self.x_send[z, y] = self.source[at.k, z, y, self.theirs].astype(self.x_send.dtype)
        self.x = self.send(self.x_send, self.x_recv, 1, {"ctx": 1 - at.c})

    def to_y(self):
        at = self.at
        rows = self.mine if self.x_first else self.all_rows
        for z in range(4):
            self.y_send[z] = self.source[at.k, z, 1 - at.y, rows].astype(self.y_send.dtype)
        self.y = self.send(self.y_send, self.y_recv, 2, at.seq(at.z, 1 - at.y, at.k))

    def second(self):
        at = self.at
        if self.x_first:
            self.x.wait_recv()
            for z in range(4):
                for y in range(2):
                    self.source[at.k, z, y, self.mine] += self.x_recv[z, y].astype(jnp.float32)
            self.to_y()
        else:
            self.y.wait_recv()
            for z in range(4):
                self.source[at.k, z, at.y] += self.y_recv[z].astype(jnp.float32)
            for z in range(4):
                self.x_send[z] = self.source[at.k, z, at.y, self.theirs].astype(self.x_send.dtype)
            self.x = self.send(self.x_send, self.x_recv, 1, {"ctx": 1 - at.c})

    def to_z(self):
        at = self.at
        (self.y if self.x_first else self.x).wait_recv()
        arrived = self.y_recv if self.x_first else self.x_recv
        for z in range(4):
            total = self.source[at.k, z, at.y, self.mine] + arrived[z].astype(jnp.float32)
            self.source[at.k, z, at.y, self.mine] = total
            self.z_send[z] = total.astype(self.z_send.dtype)
        for index, z in enumerate(z_order(at.z)):
            self.send(
                self.z_send.at[z], self.z_recv.at[at.z], 3 + z, at.seq(z, at.y, at.k), 3 + at.z
            )

    def finish(self):
        at = self.at
        total = self.source[at.k, at.z, at.y, self.mine]
        for z in z_order(at.z):
            remote_copy(
                self.z_send.at[z],
                self.z_recv.at[z],
                self.sems.at[0, 3 + z],
                self.sems.at[1, 3 + z],
                at.seq(z, at.y, at.k),
            ).wait_recv()
            total += self.z_recv[z].astype(jnp.float32)
        self.out[self.mine] = total
        if self.halves:
            self.last_send[...] = total
            self.last = self.send(self.last_send, self.last_recv, 7, {"ctx": 1 - at.c})

    def end(self):
        if self.halves:
            self.last.wait_recv()
            self.out[self.theirs] = self.last_recv[...]
        for copy in self.sent:
            copy.wait_send()


def flow_scratch(rows, width, x_first, halves, dtype):
    f32 = jnp.float32
    count = rows // 2 if halves else rows
    x_shape = (4, 2, count, width) if x_first else (4, count, width)
    y_shape = (4, count if x_first else rows, width)
    z_shape = (4, count, width)
    last = (count, width) if halves else (8, LANES)
    return [
        pltpu.VMEM((2, 4, 2, rows, width), f32),
        pltpu.VMEM((4, 2, rows, width), f32),
        pltpu.VMEM(x_shape, dtype),
        pltpu.VMEM(x_shape, dtype),
        pltpu.VMEM(y_shape, dtype),
        pltpu.VMEM(y_shape, dtype),
        pltpu.VMEM(z_shape, dtype),
        pltpu.VMEM(z_shape, dtype),
        pltpu.VMEM(last, f32),
        pltpu.VMEM(last, f32),
        pltpu.SemaphoreType.DMA((2, 8)),
    ]


def backward_kernel(
    cot_ref,
    residual_ref,
    tokens_ref,
    gains_ref,
    second_sum_ref,
    down_part_ref,
    gate_mine_ref,
    gate_theirs_ref,
    query_ref,
    kv_ref,
    probs_ref,
    attended_ref,
    full_qkv_ref,
    full_out_ref,
    first_ref,
    cos_ref,
    sin_ref,
    output_ref,
    input_grad_ref,
    qkv_out_ref,
    out_out_ref,
    small_out_ref,
    gate_out_ref,
    *scratch,
):
    f32, bf16 = jnp.float32, jnp.bfloat16
    at = Place()
    flow_bufs = [scratch[11 * index : 11 * (index + 1)] for index in range(3)]
    (
        flat_ref,
        out_flat_ref,
        gate_other,
        gate_ref,
        gate_recv,
        core_buf,
        y_buf,
        z_buf,
        down_ref,
        grad_query_ref,
        grad_kv_ref,
        kv_other,
        grad_att_ref,
        grad_proj_ref,
        gate_sems,
        half_sems,
        x_sems,
        scatter_send,
        scatter_recv,
    ) = scratch[33:]
    parts, depth, width = gate_ref.shape
    hidden = gate_out_ref.shape[1] // (2 * parts)
    rows, model = tokens_ref.shape
    query_width = HEADS * HEAD_DIM
    key_width = KV_HEADS * HEAD_DIM
    group_size = HEADS // KV_HEADS
    seq_peers = [lax.rem(at.me + step, parts) for step in range(1, parts)]
    other_ctx = {"ctx": 1 - at.c}
    greet([{"seq": peer} for peer in seq_peers] + [other_ctx])
    qkv = Flow(at, flow_bufs[0][0], qkv_out_ref, flow_bufs[0][1:10], flow_bufs[0][10], False, True)
    out = Flow(at, flow_bufs[1][0], out_out_ref, flow_bufs[1][1:10], flow_bufs[1][10], False, True)
    small = Flow(
        at, flow_bufs[2][0], small_out_ref, flow_bufs[2][1:10], flow_bufs[2][10], True, False
    )
    down = Scatter(
        at, down_part_ref, core_buf, y_buf, z_buf, down_ref, scatter_send, scatter_recv
    )
    near = z_order(at.z)
    far = (near[2], near[1], near[0], at.z)

    def spread(flat, source):
        count = source.shape[3]
        tail = jnp.zeros((count - depth, source.shape[4]), f32)
        for part in range(parts):
            z, y, k = part // 4, (part // 2) % 2, part % 2
            source[k, z, y, :depth] = flat[part * depth : (part + 1) * depth]
            source[k, z, y, depth:] = tail

    gate_x_copy = remote_copy(gate_theirs_ref, gate_other, x_sems.at[0, 0], x_sems.at[1, 0], other_ctx)
    gate_x_copy.start()
    for z in far:
        down.to_core(z)
    normed_two, scale_two = rms_forward(residual_ref[...])
    grad_through, gain_two_grad = rms_backward(
        second_sum_ref[...], normed_two, scale_two, gains_ref[1:2]
    )
    grad_residual = cot_ref[...].astype(f32) + grad_through
    input_grad_ref[...] = grad_residual
    grad_res_b = grad_residual.astype(bf16)
    down.to_y(far[0])
    down.to_y(far[1])
    out_flat_ref[...] = dot_first(attended_ref[...], grad_res_b)
    spread(out_flat_ref, out.source)
    out.begin()
    down.to_y(far[2])
    down.to_y(far[3])
    grad_att_ref[...] = dot_last(grad_res_b, full_out_ref[...]).astype(bf16)
    kv = kv_ref[...].reshape(2 * rows, 2 * key_width)
    grad_kv_ref[...] = jnp.zeros_like(grad_kv_ref)

    def backward_head(head):
        group = head // group_size
        key_columns = head_columns(group)
        value_columns = head_columns(KV_HEADS + group)
        columns = head_columns(head)
        grad_att = grad_att_ref[:, columns]
        grad_probs = dot_last(grad_att, kv[:, value_columns])
        delta = jnp.sum(
            grad_att.astype(f32) * attended_ref[:, columns].astype(f32), axis=-1, keepdims=True
        )
        probs = probs_ref[head]
        grad_scores = (probs * (grad_probs - delta) * (HEAD_DIM ** (-0.5))).astype(bf16)
        grad_query_ref[:, columns] = jnp.dot(
            grad_scores, kv[:, key_columns], preferred_element_type=f32
        )
        return (
            dot_first(grad_scores, query_ref[:, columns]),
            dot_first(probs.astype(bf16), grad_att),
        )

    def backward_group(group):
        heads = range(group * group_size, (group + 1) * group_size)
        parts_of = [backward_head(head) for head in heads]
        grad_kv_ref[:, head_columns(group)] = sum(part[0] for part in parts_of[1:]) + parts_of[0][0]
        grad_kv_ref[:, head_columns(KV_HEADS + group)] = (
            sum(part[1] for part in parts_of[1:]) + parts_of[0][1]
        )

    backward_group(0)
    down.to_z(far[0], False)
    out.add_core()
    backward_group(1)
    kv_copy = remote_copy(
        grad_kv_ref.at[pl.ds(rows, rows)], kv_other, x_sems.at[0, 1], x_sems.at[1, 1], other_ctx
    )
    kv_copy.start()
    down.to_z(far[1], False)
    gate_x_copy.wait_recv()
    for part in range(parts):
        total = gate_mine_ref[part].astype(f32) + gate_other[part].astype(f32)
        gate_ref[part] = total.astype(bf16)
    gate_copies = []
    for step, peer in enumerate(seq_peers):
        copy = remote_copy(
            gate_ref.at[peer],
            gate_recv.at[at.c, at.me],
            gate_sems.at[0, step],
            gate_sems.at[1, step],
            {"seq": peer},
        )
        copy.start()
        gate_copies.append(copy)
    gate_recv[at.c, at.me] = gate_ref[at.me]
    kv_copy.wait_recv()
    grad_query = grad_query_ref[...]
    grad_kv = grad_kv_ref[:rows] + kv_other[...]
    rotary = jnp.concatenate([grad_query, grad_kv[:, :key_width]], 1)
    turned = rotary * tiled(cos_ref[...], rotary.shape[1]) - rotated(
        rotary * tiled(sin_ref[...], rotary.shape[1])
    )
    bias_row = jnp.concatenate(
        [
            jnp.sum(turned, axis=0, keepdims=True),
            jnp.sum(grad_kv[:, key_width:], axis=0, keepdims=True),
        ],
        1,
    )
    grad_proj_ref[:, : query_width + key_width] = turned.astype(bf16)
    grad_proj_ref[:, query_width + key_width :] = grad_kv[:, key_width:].astype(bf16)
    flat_ref[...] = dot_first(first_ref[...], grad_proj_ref[...])
    spread(flat_ref, qkv.source)
    qkv.begin()
    down.to_z(far[2], False)
    down.to_z(far[3], True)
    grad_first = dot_last(grad_proj_ref[...], full_qkv_ref[...])
    normed_one, scale_one = rms_forward(tokens_ref[...].astype(f32))
    grad_part, gain_one_grad = rms_backward(grad_first, normed_one, scale_one, gains_ref[0:1])
    input_grad_ref[...] += grad_part
    bias_count = bias_row.shape[1] // parts
    gain_one_row = gain_one_grad.reshape(1, model)
    gain_two_row = gain_two_grad.reshape(1, model)
    small.source[...] = jnp.zeros_like(small.source)
    for part in range(parts):
        z, y, k = part // 4, (part // 2) % 2, part % 2
        small.source[k, z, y, 0:1, :bias_count] = bias_row[
            :, part * bias_count : (part + 1) * bias_count
        ]
        for index, row in enumerate((gain_one_row, gain_two_row)):
            start = bias_count + index * depth
            small.source[k, z, y, 0:1, start : start + depth] = row[
                :, part * depth : (part + 1) * depth
            ]
    small.begin()
    out.second()
    qkv.add_core()
    small.add_core()
    out.to_z()
    small.second()

    def gate_x(source, ctx, step):
        here = gate_recv.at[ctx, source]
        return remote_copy(
            here, here, half_sems.at[0, step], half_sems.at[1, step], other_ctx
        )

    def gate_forward(step):
        copy = gate_x(lax.rem(at.me + parts - step, parts), at.c, step)
        copy.start()
        gate_copies.append(copy)

    def gate_arrive(steps):
        for step in steps:
            source = lax.rem(at.me + parts - step, parts)
            remote_copy(
                gate_ref.at[source],
                gate_recv.at[at.c, source],
                gate_sems.at[0, step - 1],
                gate_sems.at[1, step - 1],
                {"seq": source},
            ).wait_recv()
            gate_forward(step)

    gate_forward(0)
    gate_arrive(range(1, parts // 2))
    qkv.second()
    small.to_z()
    gate_arrive(range(parts // 2, parts))
    qkv.to_z()
    down.finish()
    output_ref[...] = (residual_ref[...] + down_ref[...]).astype(bf16)
    out.finish()
    small.finish()
    for step in range(parts):
        gate_x(lax.rem(at.me + parts - step, parts), 1 - at.c, step).wait_recv()
    for ctx in range(2):
        for part in range(parts):
            start = (ctx * parts + part) * hidden
            gate_out_ref[:, start : start + hidden] = gate_recv[ctx, part, :, :hidden].astype(f32)
    qkv.finish()
    gate_x_copy.wait_send()
    kv_copy.wait_send()
    for copy in gate_copies:
        copy.wait_send()
    down.end()
    out.end()
    small.end()
    qkv.end()


def backward(operands, hidden, bias_count, collective_id):
    cot, gate_mine, first_in = operands[0], operands[6], operands[14]
    parts, depth, width = gate_mine.shape
    f32, bf16 = jnp.float32, jnp.bfloat16
    rows = (depth + 31) // 32 * 32
    count, model = cot.shape
    qkv_columns = operands[12].shape[1]
    out_rows, out_columns = operands[13].shape
    kv_columns = operands[9].shape[2]
    small_width = padded(bias_count + 2 * depth)
    shape = jax.ShapeDtypeStruct
    vmem = pl.BlockSpec(memory_space=pltpu.VMEM)
    return pl.pallas_call(
        backward_kernel,
        out_shape=(
            shape((count, model), bf16),
            shape((count, model), f32),
            shape((rows, qkv_columns), f32),
            shape((rows, out_columns), f32),
            shape((8, small_width), f32),
            shape((depth, 2 * parts * hidden), f32),
        ),
        in_specs=[vmem] * len(operands),
        out_specs=(vmem,) * 6,
        scratch_shapes=flow_scratch(rows, qkv_columns, False, True, bf16)
        + flow_scratch(rows, out_columns, False, True, bf16)
        + flow_scratch(8, small_width, True, False, f32)
        + [
            pltpu.VMEM((model, qkv_columns), f32),
            pltpu.VMEM((out_rows, out_columns), f32),
            pltpu.VMEM((parts, depth, width), bf16),
            pltpu.VMEM((parts, depth, width), bf16),
            pltpu.VMEM((2, parts, depth, width), bf16),
            pltpu.VMEM((4, 2, count, model), bf16),
            pltpu.VMEM((4, count, model), bf16),
            pltpu.VMEM((4, count, model), bf16),
            pltpu.VMEM((count, model), f32),
            pltpu.VMEM((count, out_rows), f32),
            pltpu.VMEM((2 * count, kv_columns), f32),
            pltpu.VMEM((count, kv_columns), f32),
            pltpu.VMEM((count, out_rows), bf16),
            pltpu.VMEM((count, qkv_columns), bf16),
            pltpu.SemaphoreType.DMA((2, parts - 1)),
            pltpu.SemaphoreType.DMA((2, parts)),
            pltpu.SemaphoreType.DMA((2, 2)),
            pltpu.SemaphoreType.DMA((4, 4)),
            pltpu.SemaphoreType.DMA((4, 4)),
        ],
        compiler_params=pltpu.CompilerParams(
            collective_id=collective_id, has_side_effects=True, vmem_limit_bytes=58 * 2**20
        ),
    )(*operands)


def shards(
    tokens,
    positions,
    cotangent,
    qkv_weight,
    qkv_bias,
    out_weight,
    gate_up_weight,
    down_weight,
    attn_gain,
    ffn_gain,
):
    f32 = jnp.float32
    qkv_columns = qkv_weight.shape[1]
    depth = qkv_weight.shape[0]
    bias_count = qkv_bias.shape[0]
    packed_rows = packed_height(depth)
    pair = jnp.concatenate([qkv_weight, out_weight], 1)
    extra = jnp.concatenate([qkv_bias, attn_gain, ffn_gain])
    extra = jnp.pad(extra, (0, pair.shape[1] - extra.shape[0]))[None]
    packed = jnp.concatenate(
        [pair, extra, jnp.zeros((packed_rows - depth - 1, pair.shape[1]), pair.dtype)], 0
    )
    packed = lax.all_gather(packed, "seq", axis=0, tiled=True).reshape(-1, packed_rows, pair.shape[1])
    full_qkv = packed[:, :depth, :qkv_columns].reshape(-1, qkv_columns)
    full_out = packed[:, :depth, qkv_columns:].reshape(-1, out_weight.shape[1])
    full_bias = packed[:, depth, :bias_count].reshape(-1)
    gain_one = packed[:, depth, bias_count : bias_count + depth].reshape(-1)
    gain_two = packed[:, depth, bias_count + depth : bias_count + 2 * depth].reshape(-1)
    parts = lax.axis_size("seq")
    hidden = down_weight.shape[0]
    own_gate_up = columns_from_rows(gate_up_weight, parts)
    all_cot = gather_rows(cotangent[0], 0)
    own_gate_up, all_cot, full_qkv = lax.optimization_barrier((own_gate_up, all_cot, full_qkv))
    inputs_f = tokens[0].astype(f32)
    cot_row = cotangent[0]
    row_count = inputs_f.shape[0]
    group_size = HEADS // KV_HEADS
    query_width = HEADS * HEAD_DIM
    key_width = KV_HEADS * HEAD_DIM
    score_scale = HEAD_DIM ** (-0.5)
    all_positions = positions[0]
    position_row = lax.dynamic_slice_in_dim(
        all_positions, lax.axis_index("ctx") * row_count, row_count, 0
    )
    normed_one, scale_one = rms_forward(inputs_f)
    first_in = to_bf16(normed_one * gain_one.astype(f32))
    projected = jnp.dot(first_in, full_qkv, preferred_element_type=f32) + full_bias.astype(f32)
    cosine_table, sine_table = rope_tables(position_row)
    cos_query = cosine_table[:, None, None, :]
    sin_query = sine_table[:, None, None, :]
    cos_key = cosine_table[:, None, :]
    sin_key = sine_table[:, None, :]
    query = projected[:, :query_width].reshape(row_count, KV_HEADS, group_size, HEAD_DIM)
    keys = projected[:, query_width : query_width + key_width].reshape(
        row_count, KV_HEADS, HEAD_DIM
    )
    values = projected[:, query_width + key_width :]
    query_rot = to_bf16(query * cos_query + rotate_half(query) * sin_query)
    key_rot = to_bf16(keys * cos_key + rotate_half(keys) * sin_key).reshape(row_count, key_width)
    value_b = to_bf16(values)
    both = jnp.concatenate([key_rot, value_b], -1)
    if lax.axis_size("ctx") == 2:
        both = jnp.concatenate([both, other(both)], 0)
        other_row = lax.dynamic_slice_in_dim(
            all_positions, (1 - lax.axis_index("ctx")) * row_count, row_count, 0
        )
        all_positions = jnp.concatenate([position_row, other_row])
    else:
        both = lax.all_gather(both, "ctx", axis=0, tiled=True)
    all_keys, all_values = both[:, :key_width], both[:, key_width:]
    all_keys = all_keys.reshape(-1, KV_HEADS, HEAD_DIM)
    all_values = all_values.reshape(-1, KV_HEADS, HEAD_DIM)
    scores = (
        jnp.einsum("tkgd,skd->kgts", query_rot, all_keys, preferred_element_type=f32) * score_scale
    )
    allowed = all_positions[None, :] <= position_row[:, None]
    scores = jnp.where(allowed, scores, -1e30)
    row_top = jnp.max(scores, axis=-1, keepdims=True)
    log_total = row_top + jnp.log(jnp.sum(jnp.exp(scores - row_top), axis=-1, keepdims=True))
    probs = jnp.exp(scores - log_total)
    probs_b = to_bf16(probs)
    attended = to_bf16(
        jnp.einsum("kgts,skd->tkgd", probs_b, all_values, preferred_element_type=f32)
    )
    attended_flat = attended.reshape(row_count, query_width)
    residual = inputs_f + jnp.dot(attended_flat, full_out, preferred_element_type=f32)
    normed_two, scale_two = rms_forward(residual)
    second_in = to_bf16(normed_two * gain_two.astype(f32))
    all_second = gather_rows(second_in, 1)
    gate_up = jnp.dot(all_second, own_gate_up, preferred_element_type=f32)
    gate = gate_up[:, :hidden]
    upward = gate_up[:, hidden:]
    sigmoid_gate = jax.nn.sigmoid(gate)
    activated = to_bf16(gate * sigmoid_gate * upward)
    grad_act = contract_columns(all_cot, down_weight)
    grad_gate = grad_act * upward * sigmoid_gate * (1.0 + gate * (1.0 - sigmoid_gate))
    grad_upward = grad_act * (gate * sigmoid_gate)
    grad_gate_up = to_bf16(jnp.concatenate([grad_gate, grad_upward], -1))
    grad_second = scatter_tokens(contract_columns(grad_gate_up, own_gate_up))
    down_sum = scatter_tokens(jnp.dot(activated, down_weight, preferred_element_type=f32))
    output_row = (residual + down_sum).astype(jnp.bfloat16)
    result_down = sum_rounded(contract_rows(activated, all_cot))
    result_gate_up = rows_from_columns(
        to_bf16(sum_rounded(contract_rows(all_second, grad_gate_up))), parts
    ).astype(f32)
    grad_through, gain_two_grad = rms_backward(
        grad_second, normed_two, scale_two, gain_two.astype(f32)
    )
    grad_residual = cot_row.astype(f32) + grad_through
    grad_res_b = to_bf16(grad_residual)
    out_grad = weight_rows(attended_flat, grad_res_b)
    grad_attended = to_bf16(jnp.dot(grad_res_b, full_out.T, preferred_element_type=f32))
    grad_attended = grad_attended.reshape(row_count, KV_HEADS, group_size, HEAD_DIM)
    grad_probs = jnp.einsum("tkgd,skd->kgts", grad_attended, all_values, preferred_element_type=f32)
    delta = jnp.sum(grad_attended.astype(f32) * attended.astype(f32), axis=-1)
    delta = jnp.transpose(delta, (1, 2, 0))[..., None]
    grad_scores = to_bf16(probs * (grad_probs - delta) * score_scale)
    grad_query_rot = jnp.einsum("kgts,skd->tkgd", grad_scores, all_keys, preferred_element_type=f32)
    key_part = jnp.einsum("kgts,tkgd->skd", grad_scores, query_rot, preferred_element_type=f32)
    value_part = jnp.einsum("kgts,tkgd->skd", probs_b, grad_attended, preferred_element_type=f32)
    key_parts = jnp.concatenate(
        [
            key_part.reshape(row_count * lax.axis_size("ctx"), key_width),
            value_part.reshape(row_count * lax.axis_size("ctx"), key_width),
        ],
        -1,
    )
    if lax.axis_size("ctx") == 2:
        key_local = key_parts[:row_count] + other(key_parts[row_count:])
    else:
        key_local = lax.psum_scatter(key_parts, "ctx", scatter_dimension=0, tiled=True)
    grad_key_rot = key_local[:, :key_width].reshape(row_count, KV_HEADS, HEAD_DIM)
    grad_value = key_local[:, key_width:]
    grad_query = grad_query_rot * cos_query + rotate_back(grad_query_rot * sin_query)
    grad_key = grad_key_rot * cos_key + rotate_back(grad_key_rot * sin_key)
    grad_projected = jnp.concatenate(
        [
            grad_query.reshape(row_count, query_width),
            grad_key.reshape(row_count, key_width),
            grad_value,
        ],
        -1,
    )
    bias_grad = jnp.sum(grad_projected, axis=0)
    grad_proj_b = to_bf16(grad_projected)
    grad_first = jnp.dot(grad_proj_b, full_qkv.T, preferred_element_type=f32)
    grad_input_part, gain_one_grad = rms_backward(
        grad_first, normed_one, scale_one, gain_one.astype(f32)
    )
    input_row_grad = grad_residual + grad_input_part
    small = jnp.concatenate(
        [
            bias_grad.reshape(parts, -1),
            gain_one_grad.reshape(parts, -1),
            gain_two_grad.reshape(parts, -1),
        ],
        -1,
    )
    small = jnp.pad(small, ((0, 0), (0, qkv_columns - small.shape[1])))[:, None]
    grad_rows = (depth + 8) // 8 * 8
    packed_grad = jnp.concatenate(
        [
            contract_rows(first_in, grad_proj_b).reshape(parts, depth, qkv_columns),
            small,
            jnp.zeros((parts, grad_rows - depth - 1, qkv_columns), f32),
        ],
        1,
    ).reshape(parts * grad_rows, qkv_columns)
    packed_grad, output_row = lax.optimization_barrier((packed_grad, output_row))
    packed_sum = sum_ctx(lax.psum_scatter(packed_grad, "seq", scatter_dimension=0, tiled=True))
    result_qkv = packed_sum[:depth]
    result_bias = packed_sum[depth, :bias_count]
    result_gain_one = packed_sum[depth, bias_count : bias_count + depth]
    result_gain_two = packed_sum[depth, bias_count + depth : bias_count + 2 * depth]
    result_out = sum_ctx(out_grad)
    return (
        output_row[None],
        input_row_grad[None],
        result_qkv,
        result_bias,
        result_out,
        result_gate_up,
        result_down,
        result_gain_one,
        result_gain_two,
    )


def shards_fast(
    tokens,
    positions,
    cotangent,
    qkv_weight,
    qkv_bias,
    out_weight,
    gate_up_weight,
    down_weight,
    attn_gain,
    ffn_gain,
):
    qkv_columns = qkv_weight.shape[1]
    depth = qkv_weight.shape[0]
    bias_count = qkv_bias.shape[0]
    packed_rows = packed_height(depth)
    parts = lax.axis_size("seq")
    hidden = down_weight.shape[0]
    extra = jnp.concatenate([qkv_bias, attn_gain, ffn_gain])
    extra = jnp.pad(extra, (0, qkv_columns - extra.shape[0]))[None]
    qkv_packed = jnp.concatenate(
        [qkv_weight, extra, jnp.zeros((packed_rows - depth - 1, qkv_columns), extra.dtype)], 0
    )
    out_packed = jnp.pad(out_weight, ((0, packed_rows - depth), (0, 0)))
    cot_row = cotangent[0]
    row_count = cot_row.shape[0]
    at_ctx = lax.axis_index("ctx")
    position_row = lax.dynamic_slice_in_dim(positions[0], at_ctx * row_count, row_count, 0)
    other_row = lax.dynamic_slice_in_dim(positions[0], (1 - at_ctx) * row_count, row_count, 0)
    cosine_table, sine_table = rope_tables(position_row)
    tables = [jnp.concatenate([table, table], -1) for table in (cosine_table, sine_table)]
    (
        full_qkv,
        full_out,
        all_cot,
        weight_wide,
        gains,
        first_in,
        query_flat,
        both,
        probs,
        attended_flat,
        residual,
        second_in,
    ) = forward(
        qkv_packed,
        out_packed,
        cot_row,
        gate_up_weight,
        tokens[0],
        tables,
        position_row[:, None],
        jnp.concatenate([position_row, other_row])[None],
        bias_count,
        0,
    )
    down_sum_width = padded(hidden)
    extra_rows = down_sum_width - hidden
    down_wide = jnp.pad(down_weight, ((0, extra_rows), (0, 0)))
    grad_second, down_part, result_down, gate_mine, gate_theirs = ffn(
        second_in, all_cot, weight_wide, down_wide, hidden, 1
    )
    output_row, input_row_grad, qkv_sum, out_sum, small_sum, result_gate_up = backward(
        (
            cot_row,
            residual,
            tokens[0],
            gains,
            grad_second,
            down_part,
            gate_mine,
            gate_theirs,
            query_flat,
            both,
            probs,
            attended_flat,
            full_qkv,
            full_out,
            first_in,
            *tables,
        ),
        hidden,
        bias_count,
        2,
    )
    result_qkv = qkv_sum[:depth]
    result_out = out_sum[:depth]
    result_bias = small_sum[0, :bias_count]
    result_gain_one = small_sum[0, bias_count : bias_count + depth]
    result_gain_two = small_sum[0, bias_count + depth : bias_count + 2 * depth]
    return (
        output_row[None],
        input_row_grad[None],
        result_qkv,
        result_bias,
        result_out,
        result_gate_up,
        result_down,
        result_gain_one,
        result_gain_two,
    )


def solution(mesh):
    in_specs = (
        P("seq", "ctx", None),
        P("seq", None),
        P("seq", "ctx", None),
        P("seq", None),
        P("seq"),
        P("seq", None),
        P("seq", None),
        P("seq", None),
        P("seq"),
        P("seq"),
    )
    out_specs = (
        P("seq", "ctx", None),
        P("seq", "ctx", None),
        P("seq", None),
        P("seq"),
        P("seq", None),
        P("seq", None),
        P("seq", None),
        P("seq"),
        P("seq"),
    )
    fast = mesh.shape["ctx"] == 2 and mesh.shape["seq"] == 16
    return jax.shard_map(shards_fast if fast else shards, mesh=mesh, in_specs=in_specs, out_specs=out_specs, check_vma=False)
```

```python
import functools

import jax
import jax.numpy as jnp
from jax import lax
from jax.experimental import pallas as pl
from jax.experimental.pallas import tpu as pltpu
from jax.sharding import PartitionSpec as P

HEADS = 14
KV_HEADS = 2
HEAD_DIM = 64


EPS = 1e-06
ROPE_BASE = 1000000.0


def to_bf16(values):
    return lax.optimization_barrier(values.astype(jnp.bfloat16))


def rope_tables(position_row):
    half_dim = HEAD_DIM // 2
    exponent = jnp.arange(half_dim, dtype=jnp.float32) * (2.0 / HEAD_DIM)
    inverse = ROPE_BASE ** (-exponent)
    angles = position_row.astype(jnp.float32)[:, None] * inverse[None, :]
    cosine_table = jnp.cos(angles)
    sine_table = jnp.sin(angles)
    return (
        jnp.concatenate([cosine_table, cosine_table], -1),
        jnp.concatenate([sine_table, sine_table], -1),
    )


def rotate_half(values):
    half_dim = values.shape[-1] // 2
    return jnp.concatenate([-values[..., half_dim:], values[..., :half_dim]], -1)


def rotate_back(values):
    half_dim = values.shape[-1] // 2
    return jnp.concatenate([values[..., half_dim:], -values[..., :half_dim]], -1)


def rms_forward(values):
    scaling = lax.rsqrt(jnp.mean(values * values, axis=-1, keepdims=True) + EPS)
    return (values * scaling, scaling)


def rms_backward(grad_normed, normed, scaling, gain_float):
    gain_grad = jnp.sum(grad_normed * normed, axis=0)
    grad_scaled = grad_normed * gain_float
    inner = jnp.mean(grad_scaled * normed, axis=-1, keepdims=True)
    return (scaling * (grad_scaled - normed * inner), gain_grad)


def weight_rows(left_side, right_side):
    return lax.psum_scatter(
        lax.dot_general(
            left_side, right_side, (((0,), (0,)), ((), ())), preferred_element_type=jnp.float32
        ),
        "seq",
        scatter_dimension=0,
        tiled=True,
    )


def columns_from_rows(rows, parts):
    depth = rows.shape[0]
    hidden = rows.shape[1] // (2 * parts)
    split = jnp.transpose(rows.reshape(depth, 2, parts, hidden), (2, 0, 1, 3))
    split = split.reshape(parts, depth, 2 * hidden)
    moved = lax.all_to_all(split, "seq", split_axis=0, concat_axis=0, tiled=True)
    return moved.reshape(parts * depth, 2 * hidden)


def rows_from_columns(columns, parts):
    depth = columns.shape[0] // parts
    hidden = columns.shape[1] // 2
    split = columns.reshape(parts, depth, 2 * hidden)
    moved = lax.all_to_all(split, "seq", split_axis=0, concat_axis=0, tiled=True)
    moved = jnp.transpose(moved.reshape(parts, depth, 2, hidden), (1, 2, 0, 3))
    return moved.reshape(depth, 2 * parts * hidden)


def contract_rows(left_side, right_side):
    return lax.dot_general(
        left_side, right_side, (((0,), (0,)), ((), ())), preferred_element_type=jnp.float32
    )


def contract_columns(left_side, right_side):
    return lax.dot_general(
        left_side, right_side, (((1,), (1,)), ((), ())), preferred_element_type=jnp.float32
    )


def scatter_tokens(partial):
    total = lax.psum_scatter(to_bf16(partial), "seq", scatter_dimension=0, tiled=True)
    return total.astype(jnp.float32)


def gather_kernel(outer, own_ref, all_ref, local_sem, outer_sems, middle_sems, core_sems):
    me = lax.axis_index("seq")
    at_outer = me // 4
    middle = (me // 2) % 2
    core = me % 2
    rows = own_ref.shape[0]

    def place(outer_at, middle_at, core_at):
        index = outer_at * 4 + middle_at * 2 + core_at
        return all_ref.at[pl.ds(pl.multiple_of(index * rows, rows), rows)]

    def remote(source, target, sems, slot, device):
        return pltpu.make_async_remote_copy(
            src_ref=source,
            dst_ref=target,
            send_sem=sems.at[0, slot],
            recv_sem=sems.at[1, slot],
            device_id={"seq": device},
            device_id_type=pl.DeviceIdType.MESH,
        )

    middle_partner = at_outer * 4 + (1 - middle) * 2 + core
    core_partner = at_outer * 4 + middle * 2 + (1 - core)
    outer_partners = [
        ((at_outer + step) % outer) * 4 + middle * 2 + core for step in range(1, outer)
    ]
    barrier = pltpu.get_barrier_semaphore()
    for device in [middle_partner, core_partner] + outer_partners:
        pl.semaphore_signal(
            barrier, inc=1, device_id={"seq": device}, device_id_type=pl.DeviceIdType.MESH
        )
    pl.semaphore_wait(barrier, outer + 1)

    own_place = place(at_outer, middle, core)
    local = pltpu.make_async_copy(own_ref, own_place, local_sem)
    local.start()
    started = []
    outer_copies = []
    for step in range(1, outer):
        copy = remote(own_ref, own_place, outer_sems, step - 1, outer_partners[step - 1])
        copy.start()
        outer_copies.append(copy)
    middle_copies = []
    for step in range(outer):
        source_outer = (at_outer + outer - step) % outer
        here = place(source_outer, middle, core)
        if step == 0:
            source = own_ref
        else:
            outer_copies[step - 1].wait_recv()
            source = here
        copy = remote(source, here, middle_sems, step, middle_partner)
        copy.start()
        middle_copies.append(copy)
        copy = remote(source, here, core_sems, 2 * step, core_partner)
        copy.start()
        started.append(copy)
    for step in range(outer):
        source_outer = (at_outer + outer - step) % outer
        middle_copies[step].wait_recv()
        here = place(source_outer, 1 - middle, core)
        copy = remote(here, here, core_sems, 2 * step + 1, core_partner)
        copy.start()
        started.append(copy)
    for copy in started:
        copy.wait_recv()
    for copy in outer_copies + middle_copies + started:
        copy.wait_send()
    local.wait()


def gather_rows(rows, collective_id):
    parts = lax.axis_size("seq")
    if parts % 4:
        return lax.all_gather(rows, "seq", axis=0, tiled=True)
    outer = parts // 4
    return pl.pallas_call(
        functools.partial(gather_kernel, outer),
        out_shape=jax.ShapeDtypeStruct((parts * rows.shape[0], rows.shape[1]), rows.dtype),
        in_specs=[pl.BlockSpec(memory_space=pltpu.VMEM)],
        out_specs=pl.BlockSpec(memory_space=pltpu.VMEM),
        scratch_shapes=[
            pltpu.SemaphoreType.DMA,
            pltpu.SemaphoreType.DMA((2, max(outer - 1, 1))),
            pltpu.SemaphoreType.DMA((2, outer)),
            pltpu.SemaphoreType.DMA((2, 2 * outer)),
        ],
        compiler_params=pltpu.CompilerParams(
            collective_id=collective_id, has_side_effects=True, vmem_limit_bytes=24 * 2**20
        ),
    )(rows)


def packed_height(depth):
    return (depth + 16) // 16 * 16


def other(values):
    return lax.ppermute(values, "ctx", [(0, 1), (1, 0)])


def sum_rounded(values):
    if lax.axis_size("ctx") != 2:
        return lax.psum(values, "ctx")
    mine = to_bf16(values)
    return mine.astype(jnp.float32) + other(mine).astype(jnp.float32)


def sum_ctx(values):
    if lax.axis_size("ctx") != 2:
        return lax.psum(values, "ctx")
    return values + other(values)


MESH = pl.DeviceIdType.MESH
LANES = 128


def padded(width):
    return (width + LANES - 1) // LANES * LANES


def remote_copy(source, target, send_sem, recv_sem, device):
    return pltpu.make_async_remote_copy(
        src_ref=source,
        dst_ref=target,
        send_sem=send_sem,
        recv_sem=recv_sem,
        device_id=device,
        device_id_type=MESH,
    )


def greet(devices):
    barrier = pltpu.get_barrier_semaphore()
    for device in devices:
        pl.semaphore_signal(barrier, inc=1, device_id=device, device_id_type=MESH)
    pl.semaphore_wait(barrier, len(devices))


def dot_last(left, right):
    return lax.dot_general(
        left, right, (((1,), (1,)), ((), ())), preferred_element_type=jnp.float32
    )


def dot_first(left, right):
    return lax.dot_general(
        left, right, (((0,), (0,)), ((), ())), preferred_element_type=jnp.float32
    )


def z_order(z):
    return (z + 1 - 2 * (z % 2), 2 - z // 2, 3 - 3 * (z // 2))


class Place:
    def __init__(self):
        me = lax.axis_index("seq")
        self.z = me // 4
        self.y = (me // 2) % 2
        self.k = me % 2
        self.c = lax.axis_index("ctx")
        self.me = me

    def seq(self, z, y, k):
        return {"seq": z * 4 + y * 2 + k}

    def others(self):
        z, y, k = self.z, self.y, self.k
        return (
            [self.seq(z, 1 - y, k), self.seq(z, y, 1 - k)]
            + [self.seq(other, y, k) for other in z_order(z)]
        )


class Gather:
    def __init__(self, at, own_ref, all_ref, send_sems, recv_sems, local_sem):
        self.at, self.own, self.all = at, own_ref, all_ref
        self.send_sems, self.recv_sems, self.local_sem = send_sems, recv_sems, local_sem
        self.rows = own_ref.shape[0]
        self.sent = []
        self.hop_sent = []

    def block(self, z, y, k):
        start = pl.multiple_of((z * 4 + y * 2 + k) * self.rows, self.rows)
        return self.all.at[pl.ds(start, self.rows)]

    def copy(self, source, z, y, k, kind, device, slot=None):
        return remote_copy(
            source,
            self.block(z, y, k),
            self.send_sems.at[z, kind if slot is None else slot],
            self.recv_sems.at[z, kind],
            device,
        )

    def to_y_and_core(self, source, z):
        at = self.at
        copy = self.copy(source, z, at.y, at.k, 1, at.seq(at.z, 1 - at.y, at.k))
        copy.start()
        self.sent.append(copy)
        self.to_core(source, z, at.y)

    def to_core(self, source, z, y):
        at = self.at
        copy = self.copy(source, z, y, at.k, 2 + y, at.seq(at.z, at.y, 1 - at.k))
        copy.start()
        self.sent.append(copy)

    def hop(self, source, z, right):
        at = self.at
        target = at.z + 1 if right else at.z - 1
        copy = self.copy(
            source, z, at.y, at.k, 0, at.seq(target, at.y, at.k), slot=None if right else 4
        )
        ok = (target < 4) if right else (target >= 0)
        return ok, copy

    def begin(self):
        at = self.at
        for right in (True, False):
            ok, copy = self.hop(self.own, at.z, right)
            self.hop_sent.append((ok, copy))

            @pl.when(ok)
            def _():
                copy.start()

        self.to_y_and_core(self.own, at.z)
        self.local = pltpu.make_async_copy(
            self.own, self.block(at.z, at.y, at.k), self.local_sem
        )
        self.local.start()

    def from_z(self, z):
        at = self.at
        here = self.block(z, at.y, at.k)
        self.copy(here, z, at.y, at.k, 0, at.seq(at.z, 1 - at.y, at.k)).wait_recv()
        for right in (True, False):
            ok, copy = self.hop(here, z, right)
            ok = jnp.logical_and(ok, z < at.z if right else z > at.z)
            self.hop_sent.append((ok, copy))

            @pl.when(ok)
            def _():
                copy.start()

        self.to_y_and_core(here, z)

    def from_y(self, z):
        at = self.at
        here = self.block(z, 1 - at.y, at.k)
        self.copy(here, z, 1 - at.y, at.k, 1, at.seq(at.z, 1 - at.y, at.k)).wait_recv()
        self.to_core(here, z, 1 - at.y)

    def from_core(self, z):
        at = self.at
        for y in range(2):
            here = self.block(z, y, 1 - at.k)
            self.copy(here, z, y, 1 - at.k, 2 + y, at.seq(at.z, at.y, 1 - at.k)).wait_recv()

    def end(self):
        for copy in self.sent:
            copy.wait_send()
        for ok, copy in self.hop_sent:

            @pl.when(ok)
            def _():
                copy.wait_send()


class Scatter:
    def __init__(self, at, part, core_buf, y_buf, z_buf, out_ref, send_sems, recv_sems):
        self.at, self.part, self.out = at, part, out_ref
        self.core_buf, self.y_buf, self.z_buf = core_buf, y_buf, z_buf
        self.send_sems, self.recv_sems = send_sems, recv_sems
        self.rows = out_ref.shape[0]
        self.sent = []
        self.core_copies = {}

    def block(self, z, y, k):
        start = pl.multiple_of((z * 4 + y * 2 + k) * self.rows, self.rows)
        return self.part.at[pl.ds(start, self.rows)]

    def core_copy(self, z, y):
        at = self.at
        return remote_copy(
            self.block(z, y, 1 - at.k),
            self.core_buf.at[z, y],
            self.send_sems.at[z, y],
            self.recv_sems.at[z, y],
            at.seq(at.z, at.y, 1 - at.k),
        )

    def to_core(self, z):
        for y in range(2):
            copy = self.core_copy(z, y)
            copy.start()
            self.sent.append(copy)

    def y_copy(self, z):
        at = self.at
        return remote_copy(
            self.core_buf.at[z, 1 - at.y],
            self.y_buf.at[z],
            self.send_sems.at[z, 2],
            self.recv_sems.at[z, 2],
            at.seq(at.z, 1 - at.y, at.k),
        )

    def add_core(self, z, y):
        here = self.block(z, y, self.at.k)
        total = here[...].astype(jnp.float32) + self.core_buf[z, y].astype(jnp.float32)
        self.core_buf[z, y] = total.astype(jnp.bfloat16)

    def to_y(self, z):
        at = self.at
        for y in range(2):
            self.core_copy(z, y).wait_recv()
        self.add_core(z, 1 - at.y)
        copy = self.y_copy(z)
        copy.start()
        self.sent.append(copy)
        self.add_core(z, at.y)

    def z_copy(self, z, source_z):
        at = self.at
        return remote_copy(
            self.y_buf.at[z],
            self.z_buf.at[source_z],
            self.send_sems.at[z, 3],
            self.recv_sems.at[source_z, 3],
            at.seq(z, at.y, at.k),
        )

    def to_z(self, z, own):
        at = self.at
        self.y_copy(z).wait_recv()
        total = self.core_buf[z, at.y].astype(jnp.float32) + self.y_buf[z].astype(jnp.float32)
        if own:
            self.out[...] = total
        else:
            self.y_buf[z] = total.astype(jnp.bfloat16)
            copy = self.z_copy(z, at.z)
            copy.start()
            self.sent.append(copy)

    def finish(self):
        at = self.at
        total = self.out[...]
        for z in z_order(at.z):
            self.z_copy(z, z).wait_recv()
            total += self.z_buf[z].astype(jnp.float32)
        self.out[...] = total

    def end(self):
        for copy in self.sent:
            copy.wait_send()


def ffn_kernel(
    own_ref,
    cot_ref,
    weight_ref,
    down_ref,
    second_sum_ref,
    down_part_ref,
    down_grad_ref,
    gate_sum_ref,
    all_ref,
    act_ref,
    grad_ref,
    part_ref,
    core_buf,
    y_buf,
    z_buf,
    flat_ref,
    gate_send,
    gate_recv,
    gather_send,
    gather_recv,
    local_sem,
    scatter_send,
    scatter_recv,
    x_sems,
):
    at = Place()
    width = down_ref.shape[0]
    rows = own_ref.shape[0]
    parts = all_ref.shape[0] // rows
    depth = weight_ref.shape[0] // parts
    other_ctx = {"ctx": 1 - at.c}
    greet(at.others() + [other_ctx])
    gather = Gather(at, own_ref, all_ref, gather_send, gather_recv, local_sem)
    second = Scatter(
        at, part_ref, core_buf, y_buf, z_buf, second_sum_ref, scatter_send, scatter_recv
    )
    tile = 2 * rows

    def compute(z):
        def step(index, carry):
            start = pl.multiple_of(z * (4 * rows) + index * tile, tile)
            here = pl.ds(start, tile)
            gate_up = jnp.dot(
                all_ref[here], weight_ref[...], preferred_element_type=jnp.float32
            )
            grad_act = dot_last(cot_ref[here], down_ref[...])
            gate = gate_up[:, :width]
            upward = gate_up[:, width:]
            sigmoid_gate = jax.nn.sigmoid(gate)
            silu = gate * sigmoid_gate
            activated = (silu * upward).astype(jnp.bfloat16)
            act_ref[here] = activated
            grad_gate = grad_act * upward * sigmoid_gate * (1.0 + gate * (1.0 - sigmoid_gate))
            grad_ref[here, :width] = grad_gate.astype(jnp.bfloat16)
            grad_ref[here, width:] = (grad_act * silu).astype(jnp.bfloat16)
            part_ref[here] = dot_last(grad_ref[here], weight_ref[...]).astype(jnp.bfloat16)
            down_part_ref[here] = jnp.dot(
                activated, down_ref[...], preferred_element_type=jnp.float32
            ).astype(jnp.bfloat16)
            return carry

        lax.fori_loop(0, 2, step, 0)

    order = (at.z,) + z_order(at.z)
    gather.begin()
    for index, z in enumerate(order):
        if index + 1 < len(order):
            gather.from_z(order[index + 1])
        gather.from_y(z)
        if index == 0:
            gather.local.wait()
        gather.from_core(z)
        compute(z)
        second.to_core(z)
        if index == 2:
            second.to_y(order[1])
        if index == 3:
            second.to_y(order[2])
    own, near, middle, last = order

    def gate_tile(index, carry):
        columns = pl.ds(pl.multiple_of(index * LANES, LANES), LANES)
        flat_ref[columns] = dot_first(all_ref[:, columns], grad_ref[...])
        return carry

    def columns_of(ctx):
        return pl.ds(pl.multiple_of(ctx * width, LANES), width)

    second.to_y(last)
    second.to_y(own)
    tiles = all_ref.shape[1] // LANES
    lax.fori_loop(0, tiles, gate_tile, 0)
    for part in range(parts):
        here = slice(part * depth, (part + 1) * depth)
        gate_send[part] = flat_ref[here, columns_of(1 - at.c)].astype(jnp.bfloat16)
    gate_copy = remote_copy(gate_send, gate_recv, x_sems.at[0], x_sems.at[1], other_ctx)
    gate_copy.start()
    second.to_z(middle, False)
    second.to_z(last, False)
    hidden = down_grad_ref.shape[0]
    down_grad_ref[...] = dot_first(act_ref[...], cot_ref[...])[:hidden].astype(jnp.bfloat16)
    second.to_z(near, False)
    second.to_z(own, True)
    second.finish()
    gate_copy.wait_recv()
    for part in range(parts):
        here = slice(part * depth, (part + 1) * depth)
        mine = flat_ref[here, columns_of(at.c)].astype(jnp.bfloat16).astype(jnp.float32)
        gate_sum_ref[part] = (mine + gate_recv[part].astype(jnp.float32)).astype(jnp.bfloat16)
    gate_copy.wait_send()
    gather.end()
    second.end()


def ffn(second_in, all_cot, weight, down, hidden, collective_id):
    rows, model = second_in.shape
    parts = all_cot.shape[0] // rows
    width = down.shape[0]
    depth = model // parts
    tokens = parts * rows
    f32, bf16 = jnp.float32, jnp.bfloat16
    vmem = pl.BlockSpec(memory_space=pltpu.VMEM)
    flops = 2 * tokens * model * width * 9
    return pl.pallas_call(
        ffn_kernel,
        out_shape=(
            jax.ShapeDtypeStruct((rows, model), f32),
            jax.ShapeDtypeStruct((tokens, model), bf16),
            jax.ShapeDtypeStruct((hidden, model), bf16),
            jax.ShapeDtypeStruct((parts, depth, width), bf16),
        ),
        in_specs=[vmem] * 4,
        out_specs=(vmem,) * 4,
        scratch_shapes=[
            pltpu.VMEM((tokens, model), bf16),
            pltpu.VMEM((tokens, width), bf16),
            pltpu.VMEM((tokens, 2 * width), bf16),
            pltpu.VMEM((tokens, model), bf16),
            pltpu.VMEM((4, 2, rows, model), bf16),
            pltpu.VMEM((4, rows, model), bf16),
            pltpu.VMEM((4, rows, model), bf16),
            pltpu.VMEM((model, 2 * width), f32),
            pltpu.VMEM((parts, depth, width), bf16),
            pltpu.VMEM((parts, depth, width), bf16),
            pltpu.SemaphoreType.DMA((4, 5)),
            pltpu.SemaphoreType.DMA((4, 4)),
            pltpu.SemaphoreType.DMA,
            pltpu.SemaphoreType.DMA((4, 4)),
            pltpu.SemaphoreType.DMA((4, 4)),
            pltpu.SemaphoreType.DMA((2,)),
        ],
        compiler_params=pltpu.CompilerParams(
            collective_id=collective_id, has_side_effects=True, vmem_limit_bytes=38 * 2**20
        ),
        cost_estimate=pl.CostEstimate(
            flops=flops, bytes_accessed=16 * 2**20, transcendentals=tokens * width
        ),
    )(second_in, all_cot, weight, down)


class SharedGather(Gather):
    def __init__(self, at, own_ref, all_ref, send_sems, recv_sems, local_sem):
        self.at, self.whole_all = at, all_ref
        self.count = own_ref.shape[0] // 2
        self.mine = self.half(at.c)
        self.theirs = self.half(1 - at.c)
        self.own = own_ref.at[self.mine]
        self.all = all_ref
        self.send_sems, self.recv_sems, self.local_sem = send_sems, recv_sems, local_sem
        self.sent = []
        self.hop_sent = []

    def half(self, ctx):
        return pl.ds(pl.multiple_of(ctx * self.count, self.count), self.count)

    def block(self, z, y, k, rows=None):
        return self.all.at[z * 4 + y * 2 + k, self.mine if rows is None else rows]

    def to_core(self, source, z, y):
        super().to_core(source, z, y)
        self.to_x(source, z, y)

    def x_copy(self, source, z, y, rows):
        at = self.at
        return remote_copy(
            source,
            self.block(z, y, at.k, rows),
            self.send_sems.at[z, 5 + y],
            self.recv_sems.at[z, 4 + y],
            {"ctx": 1 - at.c},
        )

    def to_x(self, source, z, y):
        copy = self.x_copy(source, z, y, self.mine)
        copy.start()
        self.sent.append(copy)

    def core_again(self, z, y, k):
        at = self.at
        here = self.block(z, y, k, self.theirs)
        return remote_copy(
            here,
            here,
            self.send_sems.at[z, 7 + y],
            self.recv_sems.at[z, 6 + y],
            at.seq(at.z, at.y, 1 - at.k),
        )

    def from_x(self, z, y):
        at = self.at
        here = self.block(z, y, at.k, self.theirs)
        self.x_copy(here, z, y, self.theirs).wait_recv()
        copy = self.core_again(z, y, at.k)
        copy.start()
        self.sent.append(copy)

    def from_core(self, z):
        super().from_core(z)
        for y in range(2):
            self.core_again(z, y, 1 - self.at.k).wait_recv()


def rotated(values):
    width = values.shape[1]
    half = HEAD_DIM // 2
    lane = lax.broadcasted_iota(jnp.int32, values.shape, 1) % HEAD_DIM
    ahead = pltpu.roll(values, width - half, 1)
    behind = pltpu.roll(values, half, 1)
    return jnp.where(lane < half, -ahead, behind)


def tiled(table, width):
    return jnp.concatenate([table] * (width // table.shape[1]), 1)


def head_columns(head):
    return slice(head * HEAD_DIM, (head + 1) * HEAD_DIM)


def forward_kernel(
    qkv_ref,
    out_ref,
    cot_ref,
    gate_up_ref,
    tokens_ref,
    cos_ref,
    sin_ref,
    query_pos_ref,
    key_pos_ref,
    full_qkv_ref,
    full_out_ref,
    all_cot_ref,
    weight_ref,
    gains_ref,
    first_ref,
    query_ref,
    kv_ref,
    probs_ref,
    attended_ref,
    residual_ref,
    second_ref,
    all_qkv_ref,
    all_out_ref,
    bias_ref,
    gate_send,
    gate_all,
    qkv_send,
    qkv_recv,
    out_send,
    out_recv,
    cot_send,
    cot_recv,
    local_sems,
    gate_sems,
    x_sems,
    kv_sems,
):
    f32, bf16 = jnp.float32, jnp.bfloat16
    at = Place()
    parts, depth, width = gate_send.shape
    half = gate_up_ref.shape[1] // 2
    hidden = half // parts
    bias_count = bias_ref.shape[1] // parts
    query_width = HEADS * HEAD_DIM
    key_width = KV_HEADS * HEAD_DIM
    seq_peers = [lax.rem(at.me + step, parts) for step in range(1, parts)]
    other_ctx = {"ctx": 1 - at.c}
    greet([{"seq": peer} for peer in seq_peers] + [other_ctx])
    qkv = SharedGather(at, qkv_ref, all_qkv_ref, qkv_send, qkv_recv, local_sems.at[0])
    out = SharedGather(at, out_ref, all_out_ref, out_send, out_recv, local_sems.at[1])
    cot = Gather(at, cot_ref, all_cot_ref, cot_send, cot_recv, local_sems.at[2])
    order = (at.z,) + z_order(at.z)
    qkv.begin()
    half_value = gate_up_ref[:, pl.ds(pl.multiple_of(at.c * half, LANES), half)]
    tail = jnp.zeros((depth, width - hidden), gate_send.dtype)
    for part in range(parts):
        gate_send[part, :, :hidden] = half_value[:, part * hidden : (part + 1) * hidden]
        gate_send[part, :, hidden:] = tail
    qkv.from_y(order[0])
    qkv.from_z(order[1])
    out.begin()
    qkv.from_y(order[1])
    qkv.from_z(order[2])
    gate_copies = []

    def gate_start(steps):
        for step in steps:
            peer = lax.rem(at.me + step, parts)
            copy = remote_copy(
                gate_send.at[peer],
                gate_all.at[at.c, at.me],
                gate_sems.at[0, step - 1],
                gate_sems.at[1, step - 1],
                {"seq": peer},
            )
            copy.start()
            gate_copies.append(copy)

    def gate_x(source, ctx, step):
        here = gate_all.at[ctx, source]
        return remote_copy(here, here, x_sems.at[0, step], x_sems.at[1, step], other_ctx)

    def gate_arrive(steps):
        for step in steps:
            source = lax.rem(at.me + parts - step, parts)
            if step > 0:
                remote_copy(
                    gate_send.at[source],
                    gate_all.at[at.c, source],
                    gate_sems.at[0, step - 1],
                    gate_sems.at[1, step - 1],
                    {"seq": source},
                ).wait_recv()
            copy = gate_x(source, at.c, step)
            copy.start()
            gate_copies.append(copy)

    gate_all[at.c, at.me] = gate_send[at.me]
    qkv.from_y(order[2])
    qkv.from_z(order[3])
    cot.begin()
    qkv.from_y(order[3])
    out.from_y(order[0])
    out.from_z(order[1])
    for z in order:
        for y in range(2):
            qkv.from_x(z, y)
    out.from_y(order[1])
    out.from_z(order[2])
    qkv.local.wait()
    for z in order:
        qkv.from_core(z)
    gate_start(range(1, parts))
    cot.from_y(order[0])
    cot.from_z(order[1])
    for part in range(parts):
        rows = pl.ds(part * depth, depth)
        full_qkv_ref[rows] = all_qkv_ref[part, :depth]
        extra = all_qkv_ref[part, depth : depth + 1, : bias_count + 2 * depth].astype(f32)
        bias_ref[:, part * bias_count : (part + 1) * bias_count] = extra[:, :bias_count]
        for index in range(2):
            start = bias_count + index * depth
            gains_ref[index : index + 1, part * depth : (part + 1) * depth] = extra[
                :, start : start + depth
            ]
    tokens = tokens_ref[...].astype(f32)
    normed_one, _ = rms_forward(tokens)
    first_ref[...] = (normed_one * gains_ref[0:1]).astype(bf16)
    projected = (
        jnp.dot(first_ref[...], full_qkv_ref[...], preferred_element_type=f32) + bias_ref[...]
    )
    rotary = projected[:, : query_width + key_width]
    turned = rotary * tiled(cos_ref[...], rotary.shape[1]) + rotated(rotary) * tiled(
        sin_ref[...], rotary.shape[1]
    )
    turned = turned.astype(bf16)
    query_ref[...] = turned[:, :query_width]
    kv_ref[0, :, :key_width] = turned[:, query_width:]
    kv_ref[0, :, key_width:] = projected[:, query_width + key_width :].astype(bf16)
    kv_copy = remote_copy(kv_ref.at[0], kv_ref.at[1], kv_sems.at[0], kv_sems.at[1], other_ctx)
    kv_copy.start()
    out.from_y(order[2])
    out.from_z(order[3])
    cot.from_y(order[1])
    cot.from_z(order[2])
    out.from_y(order[3])
    for z in order:
        for y in range(2):
            out.from_x(z, y)
    kv_copy.wait_recv()
    rows = tokens.shape[0]
    kv = kv_ref[...].reshape(2 * rows, 2 * key_width)
    allowed = key_pos_ref[...] <= query_pos_ref[...]
    group_size = HEADS // KV_HEADS

    def attend(head):
        keys = kv[:, head_columns(head // group_size)]
        values = kv[:, head_columns(KV_HEADS + head // group_size)]
        scores = dot_last(query_ref[:, head_columns(head)], keys) * (HEAD_DIM ** (-0.5))
        scores = jnp.where(allowed, scores, -1e30)
        row_top = jnp.max(scores, axis=-1, keepdims=True)
        log_total = row_top + jnp.log(
            jnp.sum(jnp.exp(scores - row_top), axis=-1, keepdims=True)
        )
        probs = jnp.exp(scores - log_total)
        probs_ref[head] = probs
        attended_ref[:, head_columns(head)] = jnp.dot(
            probs.astype(bf16), values, preferred_element_type=f32
        ).astype(bf16)

    for head in range(group_size):
        attend(head)
    cot.from_y(order[2])
    cot.from_z(order[3])
    gate_arrive(range(0, parts // 2))
    for head in range(group_size, HEADS):
        attend(head)
    cot.from_y(order[3])
    out.local.wait()
    for z in order:
        out.from_core(z)
    for part in range(parts):
        full_out_ref[pl.ds(part * depth, depth)] = all_out_ref[part, :depth]
    residual = tokens + jnp.dot(
        attended_ref[...], full_out_ref[...], preferred_element_type=f32
    )
    residual_ref[...] = residual
    normed_two, _ = rms_forward(residual)
    second_ref[...] = (normed_two * gains_ref[1:2]).astype(bf16)
    gate_arrive(range(parts // 2, parts))
    for z in order:
        cot.from_core(z)
    for step in range(parts):
        gate_x(lax.rem(at.me + parts - step, parts), 1 - at.c, step).wait_recv()
    for part in range(parts):
        rows = pl.ds(part * depth, depth)
        weight_ref[rows, :width] = gate_all[0, part]
        weight_ref[rows, width:] = gate_all[1, part]
    kv_copy.wait_send()
    for copy in gate_copies:
        copy.wait_send()
    cot.local.wait()
    for gather in (qkv, out, cot):
        gather.end()


def forward(qkv, out, cot, gate_up, tokens, tables, query_pos, key_pos, bias_count, collective_id):
    parts = lax.axis_size("seq")
    rows = qkv.shape[0]
    depth = gate_up.shape[0]
    hidden = gate_up.shape[1] // (2 * parts)
    width = padded(hidden)
    count, model = cot.shape
    f32, bf16 = jnp.float32, jnp.bfloat16
    query_width = HEADS * HEAD_DIM
    key_width = KV_HEADS * HEAD_DIM
    shape = jax.ShapeDtypeStruct
    vmem = pl.BlockSpec(memory_space=pltpu.VMEM)
    outs = (
        shape((parts * depth, qkv.shape[1]), bf16),
        shape((parts * depth, out.shape[1]), bf16),
        shape((parts * count, model), bf16),
        shape((parts * depth, 2 * width), bf16),
        shape((2, model), f32),
        shape((count, model), bf16),
        shape((count, query_width), bf16),
        shape((2, count, 2 * key_width), bf16),
        shape((HEADS, count, 2 * count), f32),
        shape((count, query_width), bf16),
        shape((count, model), f32),
        shape((count, model), bf16),
    )
    return pl.pallas_call(
        forward_kernel,
        out_shape=outs,
        in_specs=[vmem] * 9,
        out_specs=(vmem,) * len(outs),
        scratch_shapes=[
            pltpu.VMEM((parts, rows, qkv.shape[1]), bf16),
            pltpu.VMEM((parts, rows, out.shape[1]), bf16),
            pltpu.VMEM((1, parts * bias_count), f32),
            pltpu.VMEM((parts, depth, width), bf16),
            pltpu.VMEM((2, parts, depth, width), bf16),
            pltpu.SemaphoreType.DMA((4, 9)),
            pltpu.SemaphoreType.DMA((4, 8)),
            pltpu.SemaphoreType.DMA((4, 9)),
            pltpu.SemaphoreType.DMA((4, 8)),
            pltpu.SemaphoreType.DMA((4, 5)),
            pltpu.SemaphoreType.DMA((4, 4)),
            pltpu.SemaphoreType.DMA((3,)),
            pltpu.SemaphoreType.DMA((2, parts - 1)),
            pltpu.SemaphoreType.DMA((2, parts)),
            pltpu.SemaphoreType.DMA((2,)),
        ],
        compiler_params=pltpu.CompilerParams(
            collective_id=collective_id, has_side_effects=True, vmem_limit_bytes=28 * 2**20
        ),
    )(qkv, out, cot, gate_up, tokens, *tables, query_pos, key_pos)


class Flow:
    def __init__(self, at, source, out_ref, bufs, sems, x_first, halves):
        self.at, self.source, self.out = at, source, out_ref
        (self.core_recv, self.x_send, self.x_recv, self.y_send, self.y_recv,
         self.z_send, self.z_recv, self.last_send, self.last_recv) = bufs
        self.sems = sems
        self.x_first, self.halves = x_first, halves
        rows = source.shape[3]
        self.count = rows // 2 if halves else rows
        self.mine = self.half(at.c) if halves else pl.ds(0, rows)
        self.theirs = self.half(1 - at.c) if halves else pl.ds(0, rows)
        self.all_rows = pl.ds(0, rows)
        self.sent = []
        near = z_order(at.z)
        self.order = (near[2], near[1], near[0], at.z)

    def half(self, ctx):
        return pl.ds(pl.multiple_of(ctx * self.count, self.count), self.count)

    def start(self, copy):
        copy.start()
        self.sent.append(copy)

    def copy(self, source, target, slot, device):
        return remote_copy(source, target, self.sems.at[0, slot], self.sems.at[1, slot], device)

    def core_copy(self, z):
        at = self.at
        return self.copy(
            self.source.at[1 - at.k, z], self.core_recv.at[z], z, at.seq(at.z, at.y, 1 - at.k)
        )

    def x_copy(self, z):
        return self.copy(self.x_send.at[z], self.x_recv.at[z], 4 + z, {"ctx": 1 - self.at.c})

    def y_copy(self, z):
        at = self.at
        return self.copy(
            self.y_send.at[z], self.y_recv.at[z], 8 + z, at.seq(at.z, 1 - at.y, at.k)
        )

    def last_copy(self):
        return self.copy(self.last_send, self.last_recv, 16, {"ctx": 1 - self.at.c})

    def begin(self):
        for z in self.order:
            self.start(self.core_copy(z))

    def add_core(self):
        at = self.at
        for z in self.order:
            self.core_copy(z).wait_recv()
            for y in range(2):
                self.source[at.k, z, y] += self.core_recv[z, y]
            if self.x_first:
                for y in range(2):
                    self.x_send[z, y] = self.source[at.k, z, y, self.theirs].astype(
                        self.x_send.dtype
                    )
                self.start(self.x_copy(z))
            else:
                self.to_y(z, self.all_rows)

    def to_y(self, z, rows):
        at = self.at
        self.y_send[z] = self.source[at.k, z, 1 - at.y, rows].astype(self.y_send.dtype)
        self.start(self.y_copy(z))

    def second(self, steps=range(4)):
        at = self.at
        for step in steps:
            z = self.order[step]
            if self.x_first:
                self.x_copy(z).wait_recv()
                for y in range(2):
                    self.source[at.k, z, y, self.mine] += self.x_recv[z, y].astype(jnp.float32)
                self.to_y(z, self.mine)
            else:
                self.y_copy(z).wait_recv()
                self.source[at.k, z, at.y] += self.y_recv[z].astype(jnp.float32)
                self.x_send[z] = self.source[at.k, z, at.y, self.theirs].astype(
                    self.x_send.dtype
                )
                self.start(self.x_copy(z))

    def z_copy(self, z, source_z):
        at = self.at
        return remote_copy(
            self.z_send.at[z],
            self.z_recv.at[source_z],
            self.sems.at[0, 12 + z],
            self.sems.at[1, 12 + source_z],
            at.seq(z, at.y, at.k),
        )

    def to_z(self, steps=range(4)):
        at = self.at
        arrived = self.y_recv if self.x_first else self.x_recv
        for step in steps:
            z = self.order[step]
            (self.y_copy(z) if self.x_first else self.x_copy(z)).wait_recv()
            total = self.source[at.k, z, at.y, self.mine] + arrived[z].astype(jnp.float32)
            if step == 3:
                self.source[at.k, z, at.y, self.mine] = total
            else:
                self.z_send[z] = total.astype(self.z_send.dtype)
                self.start(self.z_copy(z, at.z))

    def finish(self):
        at = self.at
        total = self.source[at.k, at.z, at.y, self.mine]
        for z in z_order(at.z):
            self.z_copy(z, z).wait_recv()
            total += self.z_recv[z].astype(jnp.float32)
        self.out[self.mine] = total
        if self.halves:
            self.last_send[...] = total
            self.start(self.last_copy())

    def end(self):
        if self.halves:
            self.last_copy().wait_recv()
            self.out[self.theirs] = self.last_recv[...]
        for copy in self.sent:
            copy.wait_send()


def flow_scratch(rows, width, x_first, halves, dtype):
    f32 = jnp.float32
    count = rows // 2 if halves else rows
    x_shape = (4, 2, count, width) if x_first else (4, count, width)
    y_shape = (4, count if x_first else rows, width)
    z_shape = (4, count, width)
    last = (count, width) if halves else (8, LANES)
    return [
        pltpu.VMEM((2, 4, 2, rows, width), f32),
        pltpu.VMEM((4, 2, rows, width), f32),
        pltpu.VMEM(x_shape, dtype),
        pltpu.VMEM(x_shape, dtype),
        pltpu.VMEM(y_shape, dtype),
        pltpu.VMEM(y_shape, dtype),
        pltpu.VMEM(z_shape, dtype),
        pltpu.VMEM(z_shape, dtype),
        pltpu.VMEM(last, f32),
        pltpu.VMEM(last, f32),
        pltpu.SemaphoreType.DMA((2, 17)),
    ]


def backward_kernel(
    cot_ref,
    residual_ref,
    tokens_ref,
    gains_ref,
    second_sum_ref,
    down_part_ref,
    gate_ref,
    down_mine_ref,
    query_ref,
    kv_ref,
    probs_ref,
    attended_ref,
    full_qkv_ref,
    full_out_ref,
    first_ref,
    cos_ref,
    sin_ref,
    output_ref,
    input_grad_ref,
    qkv_out_ref,
    out_out_ref,
    small_out_ref,
    gate_out_ref,
    down_grad_ref,
    *scratch,
):
    f32, bf16 = jnp.float32, jnp.bfloat16
    at = Place()
    flow_bufs = [scratch[11 * index : 11 * (index + 1)] for index in range(3)]
    (
        flat_ref,
        down_other,
        gate_recv,
        core_buf,
        y_buf,
        z_buf,
        down_ref,
        grad_query_ref,
        grad_kv_ref,
        kv_other,
        grad_att_ref,
        grad_proj_ref,
        gate_sems,
        half_sems,
        x_sems,
        scatter_send,
        scatter_recv,
    ) = scratch[33:]
    parts, depth, width = gate_ref.shape
    hidden = gate_out_ref.shape[1] // (2 * parts)
    rows, model = tokens_ref.shape
    query_width = HEADS * HEAD_DIM
    key_width = KV_HEADS * HEAD_DIM
    group_size = HEADS // KV_HEADS
    seq_peers = [lax.rem(at.me + step, parts) for step in range(1, parts)]
    other_ctx = {"ctx": 1 - at.c}
    greet([{"seq": peer} for peer in seq_peers] + [other_ctx])
    qkv = Flow(at, flow_bufs[0][0], qkv_out_ref, flow_bufs[0][1:10], flow_bufs[0][10], False, True)
    out = Flow(at, flow_bufs[1][0], out_out_ref, flow_bufs[1][1:10], flow_bufs[1][10], False, True)
    small = Flow(
        at, flow_bufs[2][0], small_out_ref, flow_bufs[2][1:10], flow_bufs[2][10], True, False
    )
    down = Scatter(
        at, down_part_ref, core_buf, y_buf, z_buf, down_ref, scatter_send, scatter_recv
    )
    near = z_order(at.z)
    far = (near[2], near[1], near[0], at.z)

    def spread(flat, source):
        count = source.shape[3]
        tail = jnp.zeros((count - depth, source.shape[4]), f32)
        for part in range(parts):
            z, y, k = part // 4, (part // 2) % 2, part % 2
            source[k, z, y, :depth] = flat[
                part * depth : (part + 1) * depth, : source.shape[4]
            ]
            source[k, z, y, depth:] = tail

    for z in far:
        down.to_core(z)
    gate_copies = []
    for step, peer in enumerate(seq_peers):
        copy = remote_copy(
            gate_ref.at[peer],
            gate_recv.at[at.c, at.me],
            gate_sems.at[0, step],
            gate_sems.at[1, step],
            {"seq": peer},
        )
        copy.start()
        gate_copies.append(copy)
    down_copy = remote_copy(
        down_mine_ref, down_other, x_sems.at[0, 0], x_sems.at[1, 0], other_ctx
    )
    down_copy.start()
    gate_recv[at.c, at.me] = gate_ref[at.me]
    normed_two, scale_two = rms_forward(residual_ref[...])
    grad_through, gain_two_grad = rms_backward(
        second_sum_ref[...], normed_two, scale_two, gains_ref[1:2]
    )
    grad_residual = cot_ref[...].astype(f32) + grad_through
    input_grad_ref[...] = grad_residual
    grad_res_b = grad_residual.astype(bf16)
    down.to_y(far[0])
    down.to_y(far[1])
    out_columns = out.source.shape[4]
    flat_ref[:, :out_columns] = dot_first(attended_ref[...], grad_res_b)
    spread(flat_ref, out.source)
    out.begin()
    down.to_y(far[2])
    down.to_y(far[3])
    grad_att_ref[...] = dot_last(grad_res_b, full_out_ref[...]).astype(bf16)
    kv = kv_ref[...].reshape(2 * rows, 2 * key_width)
    grad_kv_ref[...] = jnp.zeros_like(grad_kv_ref)

    def backward_head(head):
        group = head // group_size
        key_columns = head_columns(group)
        value_columns = head_columns(KV_HEADS + group)
        columns = head_columns(head)
        grad_att = grad_att_ref[:, columns]
        grad_probs = dot_last(grad_att, kv[:, value_columns])
        delta = jnp.sum(
            grad_att.astype(f32) * attended_ref[:, columns].astype(f32), axis=-1, keepdims=True
        )
        probs = probs_ref[head]
        grad_scores = (probs * (grad_probs - delta) * (HEAD_DIM ** (-0.5))).astype(bf16)
        grad_query_ref[:, columns] = jnp.dot(
            grad_scores, kv[:, key_columns], preferred_element_type=f32
        )
        return (
            dot_first(grad_scores, query_ref[:, columns]),
            dot_first(probs.astype(bf16), grad_att),
        )

    def backward_group(group):
        heads = range(group * group_size, (group + 1) * group_size)
        parts_of = [backward_head(head) for head in heads]
        grad_kv_ref[:, head_columns(group)] = sum(part[0] for part in parts_of[1:]) + parts_of[0][0]
        grad_kv_ref[:, head_columns(KV_HEADS + group)] = (
            sum(part[1] for part in parts_of[1:]) + parts_of[0][1]
        )

    backward_group(0)
    down.to_z(far[0], False)
    out.add_core()
    backward_group(1)
    kv_copy = remote_copy(
        grad_kv_ref.at[pl.ds(rows, rows)], kv_other, x_sems.at[0, 1], x_sems.at[1, 1], other_ctx
    )
    kv_copy.start()
    down.to_z(far[1], False)
    kv_copy.wait_recv()
    grad_query = grad_query_ref[...]
    grad_kv = grad_kv_ref[:rows] + kv_other[...]
    rotary = jnp.concatenate([grad_query, grad_kv[:, :key_width]], 1)
    turned = rotary * tiled(cos_ref[...], rotary.shape[1]) - rotated(
        rotary * tiled(sin_ref[...], rotary.shape[1])
    )
    bias_row = jnp.concatenate(
        [
            jnp.sum(turned, axis=0, keepdims=True),
            jnp.sum(grad_kv[:, key_width:], axis=0, keepdims=True),
        ],
        1,
    )
    grad_proj_ref[:, : query_width + key_width] = turned.astype(bf16)
    grad_proj_ref[:, query_width + key_width :] = grad_kv[:, key_width:].astype(bf16)
    flat_ref[...] = dot_first(first_ref[...], grad_proj_ref[...])
    spread(flat_ref, qkv.source)
    qkv.begin()
    down.to_z(far[2], False)
    down.to_z(far[3], True)
    grad_first = dot_last(grad_proj_ref[...], full_qkv_ref[...])
    normed_one, scale_one = rms_forward(tokens_ref[...].astype(f32))
    grad_part, gain_one_grad = rms_backward(grad_first, normed_one, scale_one, gains_ref[0:1])
    input_grad_ref[...] += grad_part
    bias_count = bias_row.shape[1] // parts
    gain_one_row = gain_one_grad.reshape(1, model)
    gain_two_row = gain_two_grad.reshape(1, model)
    small.source[...] = jnp.zeros_like(small.source)
    for part in range(parts):
        z, y, k = part // 4, (part // 2) % 2, part % 2
        small.source[k, z, y, 0:1, :bias_count] = bias_row[
            :, part * bias_count : (part + 1) * bias_count
        ]
        for index, row in enumerate((gain_one_row, gain_two_row)):
            start = bias_count + index * depth
            small.source[k, z, y, 0:1, start : start + depth] = row[
                :, part * depth : (part + 1) * depth
            ]
    small.begin()
    out.second()
    qkv.add_core()
    small.add_core()
    out.to_z()
    small.second()

    def gate_x(source, ctx, step):
        here = gate_recv.at[ctx, source]
        return remote_copy(
            here, here, half_sems.at[0, step], half_sems.at[1, step], other_ctx
        )

    def gate_forward(step):
        copy = gate_x(lax.rem(at.me + parts - step, parts), at.c, step)
        copy.start()
        gate_copies.append(copy)

    def gate_arrive(steps):
        for step in steps:
            source = lax.rem(at.me + parts - step, parts)
            remote_copy(
                gate_ref.at[source],
                gate_recv.at[at.c, source],
                gate_sems.at[0, step - 1],
                gate_sems.at[1, step - 1],
                {"seq": source},
            ).wait_recv()
            gate_forward(step)

    gate_forward(0)
    gate_arrive(range(1, parts // 2))
    qkv.second()
    small.to_z()
    gate_arrive(range(parts // 2, parts))
    qkv.to_z()
    down.finish()
    output_ref[...] = (residual_ref[...] + down_ref[...]).astype(bf16)
    down_copy.wait_recv()
    down_grad_ref[...] = down_mine_ref[...].astype(f32) + down_other[...].astype(f32)
    out.finish()
    small.finish()
    for step in range(parts):
        gate_x(lax.rem(at.me + parts - step, parts), 1 - at.c, step).wait_recv()
    for ctx in range(2):
        for part in range(parts):
            start = (ctx * parts + part) * hidden
            gate_out_ref[:, start : start + hidden] = gate_recv[ctx, part, :, :hidden].astype(f32)
    qkv.finish()
    down_copy.wait_send()
    kv_copy.wait_send()
    for copy in gate_copies:
        copy.wait_send()
    down.end()
    out.end()
    small.end()
    qkv.end()


def backward(operands, hidden, bias_count, collective_id):
    cot, gate_sum, first_in = operands[0], operands[6], operands[14]
    parts, depth, width = gate_sum.shape
    f32, bf16 = jnp.float32, jnp.bfloat16
    rows = (depth + 31) // 32 * 32
    count, model = cot.shape
    qkv_columns = operands[12].shape[1]
    out_rows, out_columns = operands[13].shape
    kv_columns = operands[9].shape[2]
    small_width = padded(bias_count + 2 * depth)
    shape = jax.ShapeDtypeStruct
    vmem = pl.BlockSpec(memory_space=pltpu.VMEM)
    return pl.pallas_call(
        backward_kernel,
        out_shape=(
            shape((count, model), bf16),
            shape((count, model), f32),
            shape((rows, qkv_columns), f32),
            shape((rows, out_columns), f32),
            shape((8, small_width), f32),
            shape((depth, 2 * parts * hidden), f32),
            shape((hidden, model), f32),
        ),
        in_specs=[vmem] * len(operands),
        out_specs=(vmem,) * 7,
        scratch_shapes=flow_scratch(rows, qkv_columns, False, True, bf16)
        + flow_scratch(rows, out_columns, False, True, bf16)
        + flow_scratch(8, small_width, True, False, f32)
        + [
            pltpu.VMEM((model, qkv_columns), f32),
            pltpu.VMEM((hidden, model), bf16),
            pltpu.VMEM((2, parts, depth, width), bf16),
            pltpu.VMEM((4, 2, count, model), bf16),
            pltpu.VMEM((4, count, model), bf16),
            pltpu.VMEM((4, count, model), bf16),
            pltpu.VMEM((count, model), f32),
            pltpu.VMEM((count, out_rows), f32),
            pltpu.VMEM((2 * count, kv_columns), f32),
            pltpu.VMEM((count, kv_columns), f32),
            pltpu.VMEM((count, out_rows), bf16),
            pltpu.VMEM((count, qkv_columns), bf16),
            pltpu.SemaphoreType.DMA((2, parts - 1)),
            pltpu.SemaphoreType.DMA((2, parts)),
            pltpu.SemaphoreType.DMA((2, 2)),
            pltpu.SemaphoreType.DMA((4, 4)),
            pltpu.SemaphoreType.DMA((4, 4)),
        ],
        compiler_params=pltpu.CompilerParams(
            collective_id=collective_id, has_side_effects=True, vmem_limit_bytes=40 * 2**20
        ),
    )(*operands)


def finish_kernel(*refs):
    count = len(refs) // 2
    for index in range(count):
        source, target = refs[index], refs[count + index]
        if len(target.shape) == 3:
            target[0] = source[...]
        else:
            target[...] = source[: target.shape[0], : target.shape[1]]


def finish(values, shapes):
    vmem = pl.BlockSpec(memory_space=pltpu.VMEM)
    return pl.pallas_call(
        finish_kernel,
        out_shape=tuple(
            jax.ShapeDtypeStruct(shape, value.dtype) for value, shape in zip(values, shapes)
        ),
        in_specs=[vmem] * len(values),
        out_specs=(vmem,) * len(values),
        compiler_params=pltpu.CompilerParams(vmem_limit_bytes=24 * 2**20),
    )(*values)


def shards(
    tokens,
    positions,
    cotangent,
    qkv_weight,
    qkv_bias,
    out_weight,
    gate_up_weight,
    down_weight,
    attn_gain,
    ffn_gain,
):
    f32 = jnp.float32
    qkv_columns = qkv_weight.shape[1]
    depth = qkv_weight.shape[0]
    bias_count = qkv_bias.shape[0]
    packed_rows = packed_height(depth)
    pair = jnp.concatenate([qkv_weight, out_weight], 1)
    extra = jnp.concatenate([qkv_bias, attn_gain, ffn_gain])
    extra = jnp.pad(extra, (0, pair.shape[1] - extra.shape[0]))[None]
    packed = jnp.concatenate(
        [pair, extra, jnp.zeros((packed_rows - depth - 1, pair.shape[1]), pair.dtype)], 0
    )
    packed = lax.all_gather(packed, "seq", axis=0, tiled=True).reshape(-1, packed_rows, pair.shape[1])
    full_qkv = packed[:, :depth, :qkv_columns].reshape(-1, qkv_columns)
    full_out = packed[:, :depth, qkv_columns:].reshape(-1, out_weight.shape[1])
    full_bias = packed[:, depth, :bias_count].reshape(-1)
    gain_one = packed[:, depth, bias_count : bias_count + depth].reshape(-1)
    gain_two = packed[:, depth, bias_count + depth : bias_count + 2 * depth].reshape(-1)
    parts = lax.axis_size("seq")
    hidden = down_weight.shape[0]
    own_gate_up = columns_from_rows(gate_up_weight, parts)
    all_cot = gather_rows(cotangent[0], 0)
    own_gate_up, all_cot, full_qkv = lax.optimization_barrier((own_gate_up, all_cot, full_qkv))
    inputs_f = tokens[0].astype(f32)
    cot_row = cotangent[0]
    row_count = inputs_f.shape[0]
    group_size = HEADS // KV_HEADS
    query_width = HEADS * HEAD_DIM
    key_width = KV_HEADS * HEAD_DIM
    score_scale = HEAD_DIM ** (-0.5)
    all_positions = positions[0]
    position_row = lax.dynamic_slice_in_dim(
        all_positions, lax.axis_index("ctx") * row_count, row_count, 0
    )
    normed_one, scale_one = rms_forward(inputs_f)
    first_in = to_bf16(normed_one * gain_one.astype(f32))
    projected = jnp.dot(first_in, full_qkv, preferred_element_type=f32) + full_bias.astype(f32)
    cosine_table, sine_table = rope_tables(position_row)
    cos_query = cosine_table[:, None, None, :]
    sin_query = sine_table[:, None, None, :]
    cos_key = cosine_table[:, None, :]
    sin_key = sine_table[:, None, :]
    query = projected[:, :query_width].reshape(row_count, KV_HEADS, group_size, HEAD_DIM)
    keys = projected[:, query_width : query_width + key_width].reshape(
        row_count, KV_HEADS, HEAD_DIM
    )
    values = projected[:, query_width + key_width :]
    query_rot = to_bf16(query * cos_query + rotate_half(query) * sin_query)
    key_rot = to_bf16(keys * cos_key + rotate_half(keys) * sin_key).reshape(row_count, key_width)
    value_b = to_bf16(values)
    both = jnp.concatenate([key_rot, value_b], -1)
    if lax.axis_size("ctx") == 2:
        both = jnp.concatenate([both, other(both)], 0)
        other_row = lax.dynamic_slice_in_dim(
            all_positions, (1 - lax.axis_index("ctx")) * row_count, row_count, 0
        )
        all_positions = jnp.concatenate([position_row, other_row])
    else:
        both = lax.all_gather(both, "ctx", axis=0, tiled=True)
    all_keys, all_values = both[:, :key_width], both[:, key_width:]
    all_keys = all_keys.reshape(-1, KV_HEADS, HEAD_DIM)
    all_values = all_values.reshape(-1, KV_HEADS, HEAD_DIM)
    scores = (
        jnp.einsum("tkgd,skd->kgts", query_rot, all_keys, preferred_element_type=f32) * score_scale
    )
    allowed = all_positions[None, :] <= position_row[:, None]
    scores = jnp.where(allowed, scores, -1e30)
    row_top = jnp.max(scores, axis=-1, keepdims=True)
    log_total = row_top + jnp.log(jnp.sum(jnp.exp(scores - row_top), axis=-1, keepdims=True))
    probs = jnp.exp(scores - log_total)
    probs_b = to_bf16(probs)
    attended = to_bf16(
        jnp.einsum("kgts,skd->tkgd", probs_b, all_values, preferred_element_type=f32)
    )
    attended_flat = attended.reshape(row_count, query_width)
    residual = inputs_f + jnp.dot(attended_flat, full_out, preferred_element_type=f32)
    normed_two, scale_two = rms_forward(residual)
    second_in = to_bf16(normed_two * gain_two.astype(f32))
    all_second = gather_rows(second_in, 1)
    gate_up = jnp.dot(all_second, own_gate_up, preferred_element_type=f32)
    gate = gate_up[:, :hidden]
    upward = gate_up[:, hidden:]
    sigmoid_gate = jax.nn.sigmoid(gate)
    activated = to_bf16(gate * sigmoid_gate * upward)
    grad_act = contract_columns(all_cot, down_weight)
    grad_gate = grad_act * upward * sigmoid_gate * (1.0 + gate * (1.0 - sigmoid_gate))
    grad_upward = grad_act * (gate * sigmoid_gate)
    grad_gate_up = to_bf16(jnp.concatenate([grad_gate, grad_upward], -1))
    grad_second = scatter_tokens(contract_columns(grad_gate_up, own_gate_up))
    down_sum = scatter_tokens(jnp.dot(activated, down_weight, preferred_element_type=f32))
    output_row = (residual + down_sum).astype(jnp.bfloat16)
    result_down = sum_rounded(contract_rows(activated, all_cot))
    result_gate_up = rows_from_columns(
        to_bf16(sum_rounded(contract_rows(all_second, grad_gate_up))), parts
    ).astype(f32)
    grad_through, gain_two_grad = rms_backward(
        grad_second, normed_two, scale_two, gain_two.astype(f32)
    )
    grad_residual = cot_row.astype(f32) + grad_through
    grad_res_b = to_bf16(grad_residual)
    out_grad = weight_rows(attended_flat, grad_res_b)
    grad_attended = to_bf16(jnp.dot(grad_res_b, full_out.T, preferred_element_type=f32))
    grad_attended = grad_attended.reshape(row_count, KV_HEADS, group_size, HEAD_DIM)
    grad_probs = jnp.einsum("tkgd,skd->kgts", grad_attended, all_values, preferred_element_type=f32)
    delta = jnp.sum(grad_attended.astype(f32) * attended.astype(f32), axis=-1)
    delta = jnp.transpose(delta, (1, 2, 0))[..., None]
    grad_scores = to_bf16(probs * (grad_probs - delta) * score_scale)
    grad_query_rot = jnp.einsum("kgts,skd->tkgd", grad_scores, all_keys, preferred_element_type=f32)
    key_part = jnp.einsum("kgts,tkgd->skd", grad_scores, query_rot, preferred_element_type=f32)
    value_part = jnp.einsum("kgts,tkgd->skd", probs_b, grad_attended, preferred_element_type=f32)
    key_parts = jnp.concatenate(
        [
            key_part.reshape(row_count * lax.axis_size("ctx"), key_width),
            value_part.reshape(row_count * lax.axis_size("ctx"), key_width),
        ],
        -1,
    )
    if lax.axis_size("ctx") == 2:
        key_local = key_parts[:row_count] + other(key_parts[row_count:])
    else:
        key_local = lax.psum_scatter(key_parts, "ctx", scatter_dimension=0, tiled=True)
    grad_key_rot = key_local[:, :key_width].reshape(row_count, KV_HEADS, HEAD_DIM)
    grad_value = key_local[:, key_width:]
    grad_query = grad_query_rot * cos_query + rotate_back(grad_query_rot * sin_query)
    grad_key = grad_key_rot * cos_key + rotate_back(grad_key_rot * sin_key)
    grad_projected = jnp.concatenate(
        [
            grad_query.reshape(row_count, query_width),
            grad_key.reshape(row_count, key_width),
            grad_value,
        ],
        -1,
    )
    bias_grad = jnp.sum(grad_projected, axis=0)
    grad_proj_b = to_bf16(grad_projected)
    grad_first = jnp.dot(grad_proj_b, full_qkv.T, preferred_element_type=f32)
    grad_input_part, gain_one_grad = rms_backward(
        grad_first, normed_one, scale_one, gain_one.astype(f32)
    )
    input_row_grad = grad_residual + grad_input_part
    small = jnp.concatenate(
        [
            bias_grad.reshape(parts, -1),
            gain_one_grad.reshape(parts, -1),
            gain_two_grad.reshape(parts, -1),
        ],
        -1,
    )
    small = jnp.pad(small, ((0, 0), (0, qkv_columns - small.shape[1])))[:, None]
    grad_rows = (depth + 8) // 8 * 8
    packed_grad = jnp.concatenate(
        [
            contract_rows(first_in, grad_proj_b).reshape(parts, depth, qkv_columns),
            small,
            jnp.zeros((parts, grad_rows - depth - 1, qkv_columns), f32),
        ],
        1,
    ).reshape(parts * grad_rows, qkv_columns)
    packed_grad, output_row = lax.optimization_barrier((packed_grad, output_row))
    packed_sum = sum_ctx(lax.psum_scatter(packed_grad, "seq", scatter_dimension=0, tiled=True))
    result_qkv = packed_sum[:depth]
    result_bias = packed_sum[depth, :bias_count]
    result_gain_one = packed_sum[depth, bias_count : bias_count + depth]
    result_gain_two = packed_sum[depth, bias_count + depth : bias_count + 2 * depth]
    result_out = sum_ctx(out_grad)
    return (
        output_row[None],
        input_row_grad[None],
        result_qkv,
        result_bias,
        result_out,
        result_gate_up,
        result_down,
        result_gain_one,
        result_gain_two,
    )


def shards_fast(
    tokens,
    positions,
    cotangent,
    qkv_weight,
    qkv_bias,
    out_weight,
    gate_up_weight,
    down_weight,
    attn_gain,
    ffn_gain,
):
    qkv_columns = qkv_weight.shape[1]
    depth = qkv_weight.shape[0]
    bias_count = qkv_bias.shape[0]
    packed_rows = packed_height(depth)
    parts = lax.axis_size("seq")
    hidden = down_weight.shape[0]
    extra = jnp.concatenate([qkv_bias, attn_gain, ffn_gain])
    extra = jnp.pad(extra, (0, qkv_columns - extra.shape[0]))[None]
    qkv_packed = jnp.concatenate(
        [qkv_weight, extra, jnp.zeros((packed_rows - depth - 1, qkv_columns), extra.dtype)], 0
    )
    out_packed = jnp.pad(out_weight, ((0, packed_rows - depth), (0, 0)))
    cot_row = cotangent[0]
    row_count = cot_row.shape[0]
    at_ctx = lax.axis_index("ctx")
    position_row = lax.dynamic_slice_in_dim(positions[0], at_ctx * row_count, row_count, 0)
    other_row = lax.dynamic_slice_in_dim(positions[0], (1 - at_ctx) * row_count, row_count, 0)
    cosine_table, sine_table = rope_tables(position_row)
    tables = [jnp.concatenate([table, table], -1) for table in (cosine_table, sine_table)]
    (
        full_qkv,
        full_out,
        all_cot,
        weight_wide,
        gains,
        first_in,
        query_flat,
        both,
        probs,
        attended_flat,
        residual,
        second_in,
    ) = forward(
        qkv_packed,
        out_packed,
        cot_row,
        gate_up_weight,
        tokens[0],
        tables,
        position_row[:, None],
        jnp.concatenate([position_row, other_row])[None],
        bias_count,
        0,
    )
    down_sum_width = padded(hidden)
    extra_rows = down_sum_width - hidden
    down_wide = jnp.pad(down_weight, ((0, extra_rows), (0, 0)))
    grad_second, down_part, down_mine, gate_sum = ffn(
        second_in, all_cot, weight_wide, down_wide, hidden, 1
    )
    output_row, input_row_grad, qkv_sum, out_sum, small_sum, gate_grad, down_grad = backward(
        (
            cot_row,
            residual,
            tokens[0],
            gains,
            grad_second,
            down_part,
            gate_sum,
            down_mine,
            query_flat,
            both,
            probs,
            attended_flat,
            full_qkv,
            full_out,
            first_in,
            *tables,
        ),
        hidden,
        bias_count,
        2,
    )
    output_row, input_row_grad, result_qkv, result_out, result_gate_up, result_down = finish(
        (output_row, input_row_grad, qkv_sum, out_sum, gate_grad, down_grad),
        (
            (1,) + output_row.shape,
            (1,) + input_row_grad.shape,
            (depth, qkv_columns),
            (depth, out_weight.shape[1]),
            gate_grad.shape,
            down_grad.shape,
        ),
    )
    result_bias = small_sum[0, :bias_count]
    result_gain_one = small_sum[0, bias_count : bias_count + depth]
    result_gain_two = small_sum[0, bias_count + depth : bias_count + 2 * depth]
    return (
        output_row,
        input_row_grad,
        result_qkv,
        result_bias,
        result_out,
        result_gate_up,
        result_down,
        result_gain_one,
        result_gain_two,
    )


def solution(mesh):
    in_specs = (
        P("seq", "ctx", None),
        P("seq", None),
        P("seq", "ctx", None),
        P("seq", None),
        P("seq"),
        P("seq", None),
        P("seq", None),
        P("seq", None),
        P("seq"),
        P("seq"),
    )
    out_specs = (
        P("seq", "ctx", None),
        P("seq", "ctx", None),
        P("seq", None),
        P("seq"),
        P("seq", None),
        P("seq", None),
        P("seq", None),
        P("seq"),
        P("seq"),
    )
    fast = mesh.shape["ctx"] == 2 and mesh.shape["seq"] == 16
    return jax.shard_map(shards_fast if fast else shards, mesh=mesh, in_specs=in_specs, out_specs=out_specs, check_vma=False)
```

```python
import functools

import jax
import jax.numpy as jnp
from jax import lax
from jax.experimental import pallas as pl
from jax.experimental.pallas import tpu as pltpu
from jax.sharding import PartitionSpec as P

HEADS = 14
KV_HEADS = 2
HEAD_DIM = 64


EPS = 1e-06
ROPE_BASE = 1000000.0


def to_bf16(values):
    return lax.optimization_barrier(values.astype(jnp.bfloat16))


def rope_tables(position_row):
    half_dim = HEAD_DIM // 2
    exponent = jnp.arange(half_dim, dtype=jnp.float32) * (2.0 / HEAD_DIM)
    inverse = ROPE_BASE ** (-exponent)
    angles = position_row.astype(jnp.float32)[:, None] * inverse[None, :]
    cosine_table = jnp.cos(angles)
    sine_table = jnp.sin(angles)
    return (
        jnp.concatenate([cosine_table, cosine_table], -1),
        jnp.concatenate([sine_table, sine_table], -1),
    )


def rotate_half(values):
    half_dim = values.shape[-1] // 2
    return jnp.concatenate([-values[..., half_dim:], values[..., :half_dim]], -1)


def rotate_back(values):
    half_dim = values.shape[-1] // 2
    return jnp.concatenate([values[..., half_dim:], -values[..., :half_dim]], -1)


def rms_forward(values):
    scaling = lax.rsqrt(jnp.mean(values * values, axis=-1, keepdims=True) + EPS)
    return (values * scaling, scaling)


def rms_backward(grad_normed, normed, scaling, gain_float):
    gain_grad = jnp.sum(grad_normed * normed, axis=0)
    grad_scaled = grad_normed * gain_float
    inner = jnp.mean(grad_scaled * normed, axis=-1, keepdims=True)
    return (scaling * (grad_scaled - normed * inner), gain_grad)


def weight_rows(left_side, right_side):
    return lax.psum_scatter(
        lax.dot_general(
            left_side, right_side, (((0,), (0,)), ((), ())), preferred_element_type=jnp.float32
        ),
        "seq",
        scatter_dimension=0,
        tiled=True,
    )


def columns_from_rows(rows, parts):
    depth = rows.shape[0]
    hidden = rows.shape[1] // (2 * parts)
    split = jnp.transpose(rows.reshape(depth, 2, parts, hidden), (2, 0, 1, 3))
    split = split.reshape(parts, depth, 2 * hidden)
    moved = lax.all_to_all(split, "seq", split_axis=0, concat_axis=0, tiled=True)
    return moved.reshape(parts * depth, 2 * hidden)


def rows_from_columns(columns, parts):
    depth = columns.shape[0] // parts
    hidden = columns.shape[1] // 2
    split = columns.reshape(parts, depth, 2 * hidden)
    moved = lax.all_to_all(split, "seq", split_axis=0, concat_axis=0, tiled=True)
    moved = jnp.transpose(moved.reshape(parts, depth, 2, hidden), (1, 2, 0, 3))
    return moved.reshape(depth, 2 * parts * hidden)


def contract_rows(left_side, right_side):
    return lax.dot_general(
        left_side, right_side, (((0,), (0,)), ((), ())), preferred_element_type=jnp.float32
    )


def contract_columns(left_side, right_side):
    return lax.dot_general(
        left_side, right_side, (((1,), (1,)), ((), ())), preferred_element_type=jnp.float32
    )


def scatter_tokens(partial):
    total = lax.psum_scatter(to_bf16(partial), "seq", scatter_dimension=0, tiled=True)
    return total.astype(jnp.float32)


def gather_kernel(outer, own_ref, all_ref, local_sem, outer_sems, middle_sems, core_sems):
    me = lax.axis_index("seq")
    at_outer = me // 4
    middle = (me // 2) % 2
    core = me % 2
    rows = own_ref.shape[0]

    def place(outer_at, middle_at, core_at):
        index = outer_at * 4 + middle_at * 2 + core_at
        return all_ref.at[pl.ds(pl.multiple_of(index * rows, rows), rows)]

    def remote(source, target, sems, slot, device):
        return pltpu.make_async_remote_copy(
            src_ref=source,
            dst_ref=target,
            send_sem=sems.at[0, slot],
            recv_sem=sems.at[1, slot],
            device_id={"seq": device},
            device_id_type=pl.DeviceIdType.MESH,
        )

    middle_partner = at_outer * 4 + (1 - middle) * 2 + core
    core_partner = at_outer * 4 + middle * 2 + (1 - core)
    outer_partners = [
        ((at_outer + step) % outer) * 4 + middle * 2 + core for step in range(1, outer)
    ]
    barrier = pltpu.get_barrier_semaphore()
    for device in [middle_partner, core_partner] + outer_partners:
        pl.semaphore_signal(
            barrier, inc=1, device_id={"seq": device}, device_id_type=pl.DeviceIdType.MESH
        )
    pl.semaphore_wait(barrier, outer + 1)

    own_place = place(at_outer, middle, core)
    local = pltpu.make_async_copy(own_ref, own_place, local_sem)
    local.start()
    started = []
    outer_copies = []
    for step in range(1, outer):
        copy = remote(own_ref, own_place, outer_sems, step - 1, outer_partners[step - 1])
        copy.start()
        outer_copies.append(copy)
    middle_copies = []
    for step in range(outer):
        source_outer = (at_outer + outer - step) % outer
        here = place(source_outer, middle, core)
        if step == 0:
            source = own_ref
        else:
            outer_copies[step - 1].wait_recv()
            source = here
        copy = remote(source, here, middle_sems, step, middle_partner)
        copy.start()
        middle_copies.append(copy)
        copy = remote(source, here, core_sems, 2 * step, core_partner)
        copy.start()
        started.append(copy)
    for step in range(outer):
        source_outer = (at_outer + outer - step) % outer
        middle_copies[step].wait_recv()
        here = place(source_outer, 1 - middle, core)
        copy = remote(here, here, core_sems, 2 * step + 1, core_partner)
        copy.start()
        started.append(copy)
    for copy in started:
        copy.wait_recv()
    for copy in outer_copies + middle_copies + started:
        copy.wait_send()
    local.wait()


def gather_rows(rows, collective_id):
    parts = lax.axis_size("seq")
    if parts % 4:
        return lax.all_gather(rows, "seq", axis=0, tiled=True)
    outer = parts // 4
    return pl.pallas_call(
        functools.partial(gather_kernel, outer),
        out_shape=jax.ShapeDtypeStruct((parts * rows.shape[0], rows.shape[1]), rows.dtype),
        in_specs=[pl.BlockSpec(memory_space=pltpu.VMEM)],
        out_specs=pl.BlockSpec(memory_space=pltpu.VMEM),
        scratch_shapes=[
            pltpu.SemaphoreType.DMA,
            pltpu.SemaphoreType.DMA((2, max(outer - 1, 1))),
            pltpu.SemaphoreType.DMA((2, outer)),
            pltpu.SemaphoreType.DMA((2, 2 * outer)),
        ],
        compiler_params=pltpu.CompilerParams(
            collective_id=collective_id, has_side_effects=True, vmem_limit_bytes=24 * 2**20
        ),
    )(rows)


def packed_height(depth):
    return (depth + 16) // 16 * 16


def other(values):
    return lax.ppermute(values, "ctx", [(0, 1), (1, 0)])


def sum_rounded(values):
    if lax.axis_size("ctx") != 2:
        return lax.psum(values, "ctx")
    mine = to_bf16(values)
    return mine.astype(jnp.float32) + other(mine).astype(jnp.float32)


def sum_ctx(values):
    if lax.axis_size("ctx") != 2:
        return lax.psum(values, "ctx")
    return values + other(values)


MESH = pl.DeviceIdType.MESH
LANES = 128


def padded(width):
    return (width + LANES - 1) // LANES * LANES


def remote_copy(source, target, send_sem, recv_sem, device):
    return pltpu.make_async_remote_copy(
        src_ref=source,
        dst_ref=target,
        send_sem=send_sem,
        recv_sem=recv_sem,
        device_id=device,
        device_id_type=MESH,
    )


def greet(devices):
    barrier = pltpu.get_barrier_semaphore()
    for device in devices:
        pl.semaphore_signal(barrier, inc=1, device_id=device, device_id_type=MESH)
    pl.semaphore_wait(barrier, len(devices))


def dot_last(left, right):
    return lax.dot_general(
        left, right, (((1,), (1,)), ((), ())), preferred_element_type=jnp.float32
    )


def dot_first(left, right):
    return lax.dot_general(
        left, right, (((0,), (0,)), ((), ())), preferred_element_type=jnp.float32
    )


def z_order(z):
    return (z + 1 - 2 * (z % 2), 2 - z // 2, 3 - 3 * (z // 2))


class Place:
    def __init__(self):
        me = lax.axis_index("seq")
        self.z = me // 4
        self.y = (me // 2) % 2
        self.k = me % 2
        self.c = lax.axis_index("ctx")
        self.me = me

    def seq(self, z, y, k):
        return {"seq": z * 4 + y * 2 + k}

    def others(self):
        z, y, k = self.z, self.y, self.k
        return (
            [self.seq(z, 1 - y, k), self.seq(z, y, 1 - k)]
            + [self.seq(other, y, k) for other in z_order(z)]
        )


class Gather:
    def __init__(self, at, own_ref, all_ref, send_sems, recv_sems, local_sem):
        self.at, self.own, self.all = at, own_ref, all_ref
        self.send_sems, self.recv_sems, self.local_sem = send_sems, recv_sems, local_sem
        self.rows = own_ref.shape[0]
        self.sent = []
        self.hop_sent = []

    def block(self, z, y, k):
        start = pl.multiple_of((z * 4 + y * 2 + k) * self.rows, self.rows)
        return self.all.at[pl.ds(start, self.rows)]

    def copy(self, source, z, y, k, kind, device, slot=None):
        return remote_copy(
            source,
            self.block(z, y, k),
            self.send_sems.at[z, kind if slot is None else slot],
            self.recv_sems.at[z, kind],
            device,
        )

    def to_y_and_core(self, source, z):
        at = self.at
        copy = self.copy(source, z, at.y, at.k, 1, at.seq(at.z, 1 - at.y, at.k))
        copy.start()
        self.sent.append(copy)
        self.to_core(source, z, at.y)

    def to_core(self, source, z, y):
        at = self.at
        copy = self.copy(source, z, y, at.k, 2 + y, at.seq(at.z, at.y, 1 - at.k))
        copy.start()
        self.sent.append(copy)

    def hop(self, source, z, right):
        at = self.at
        target = at.z + 1 if right else at.z - 1
        copy = self.copy(
            source, z, at.y, at.k, 0, at.seq(target, at.y, at.k), slot=None if right else 4
        )
        ok = (target < 4) if right else (target >= 0)
        return ok, copy

    def begin(self):
        at = self.at
        for right in (True, False):
            ok, copy = self.hop(self.own, at.z, right)
            self.hop_sent.append((ok, copy))

            @pl.when(ok)
            def _():
                copy.start()

        self.to_y_and_core(self.own, at.z)
        self.local = pltpu.make_async_copy(
            self.own, self.block(at.z, at.y, at.k), self.local_sem
        )
        self.local.start()

    def from_z(self, z):
        at = self.at
        here = self.block(z, at.y, at.k)
        self.copy(here, z, at.y, at.k, 0, at.seq(at.z, 1 - at.y, at.k)).wait_recv()
        for right in (True, False):
            ok, copy = self.hop(here, z, right)
            ok = jnp.logical_and(ok, z < at.z if right else z > at.z)
            self.hop_sent.append((ok, copy))

            @pl.when(ok)
            def _():
                copy.start()

        self.to_y_and_core(here, z)

    def from_y(self, z):
        at = self.at
        here = self.block(z, 1 - at.y, at.k)
        self.copy(here, z, 1 - at.y, at.k, 1, at.seq(at.z, 1 - at.y, at.k)).wait_recv()
        self.to_core(here, z, 1 - at.y)

    def from_core(self, z):
        at = self.at
        for y in range(2):
            here = self.block(z, y, 1 - at.k)
            self.copy(here, z, y, 1 - at.k, 2 + y, at.seq(at.z, at.y, 1 - at.k)).wait_recv()

    def end(self):
        for copy in self.sent:
            copy.wait_send()
        for ok, copy in self.hop_sent:

            @pl.when(ok)
            def _():
                copy.wait_send()


class Scatter:
    def __init__(self, at, part, core_buf, y_buf, z_buf, out_ref, send_sems, recv_sems):
        self.at, self.part, self.out = at, part, out_ref
        self.core_buf, self.y_buf, self.z_buf = core_buf, y_buf, z_buf
        self.send_sems, self.recv_sems = send_sems, recv_sems
        self.rows = out_ref.shape[0]
        self.sent = []
        self.core_copies = {}

    def block(self, z, y, k):
        start = pl.multiple_of((z * 4 + y * 2 + k) * self.rows, self.rows)
        return self.part.at[pl.ds(start, self.rows)]

    def core_copy(self, z, y):
        at = self.at
        return remote_copy(
            self.block(z, y, 1 - at.k),
            self.core_buf.at[z, y],
            self.send_sems.at[z, y],
            self.recv_sems.at[z, y],
            at.seq(at.z, at.y, 1 - at.k),
        )

    def to_core(self, z):
        for y in range(2):
            copy = self.core_copy(z, y)
            copy.start()
            self.sent.append(copy)

    def y_copy(self, z):
        at = self.at
        return remote_copy(
            self.core_buf.at[z, 1 - at.y],
            self.y_buf.at[z],
            self.send_sems.at[z, 2],
            self.recv_sems.at[z, 2],
            at.seq(at.z, 1 - at.y, at.k),
        )

    def add_core(self, z, y):
        here = self.block(z, y, self.at.k)
        total = here[...].astype(jnp.float32) + self.core_buf[z, y].astype(jnp.float32)
        self.core_buf[z, y] = total.astype(jnp.bfloat16)

    def to_y(self, z):
        at = self.at
        for y in range(2):
            self.core_copy(z, y).wait_recv()
        self.add_core(z, 1 - at.y)
        copy = self.y_copy(z)
        copy.start()
        self.sent.append(copy)
        self.add_core(z, at.y)

    def z_copy(self, z, source_z):
        at = self.at
        return remote_copy(
            self.y_buf.at[z],
            self.z_buf.at[source_z],
            self.send_sems.at[z, 3],
            self.recv_sems.at[source_z, 3],
            at.seq(z, at.y, at.k),
        )

    def to_z(self, z, own):
        at = self.at
        self.y_copy(z).wait_recv()
        total = self.core_buf[z, at.y].astype(jnp.float32) + self.y_buf[z].astype(jnp.float32)
        if own:
            self.out[...] = total
        else:
            self.y_buf[z] = total.astype(jnp.bfloat16)
            copy = self.z_copy(z, at.z)
            copy.start()
            self.sent.append(copy)

    def finish(self):
        at = self.at
        total = self.out[...]
        for z in z_order(at.z):
            self.z_copy(z, z).wait_recv()
            total += self.z_buf[z].astype(jnp.float32)
        self.out[...] = total

    def end(self):
        for copy in self.sent:
            copy.wait_send()


def ffn_kernel(
    own_ref,
    cot_ref,
    weight_ref,
    down_ref,
    second_sum_ref,
    down_part_ref,
    down_grad_ref,
    gate_sum_ref,
    all_ref,
    act_ref,
    grad_ref,
    part_ref,
    core_buf,
    y_buf,
    z_buf,
    flat_ref,
    gate_send,
    gate_recv,
    gather_send,
    gather_recv,
    local_sem,
    scatter_send,
    scatter_recv,
    x_sems,
):
    at = Place()
    width = down_ref.shape[0]
    rows = own_ref.shape[0]
    parts = all_ref.shape[0] // rows
    depth = weight_ref.shape[0] // parts
    other_ctx = {"ctx": 1 - at.c}
    greet(at.others() + [other_ctx])
    gather = Gather(at, own_ref, all_ref, gather_send, gather_recv, local_sem)
    second = Scatter(
        at, part_ref, core_buf, y_buf, z_buf, second_sum_ref, scatter_send, scatter_recv
    )
    tile = 2 * rows

    def compute(z):
        def step(index, carry):
            start = pl.multiple_of(z * (4 * rows) + index * tile, tile)
            here = pl.ds(start, tile)
            gate_up = jnp.dot(
                all_ref[here], weight_ref[...], preferred_element_type=jnp.float32
            )
            grad_act = dot_last(cot_ref[here], down_ref[...])
            gate = gate_up[:, :width]
            upward = gate_up[:, width:]
            sigmoid_gate = jax.nn.sigmoid(gate)
            silu = gate * sigmoid_gate
            activated = (silu * upward).astype(jnp.bfloat16)
            act_ref[here] = activated
            grad_gate = grad_act * upward * sigmoid_gate * (1.0 + gate * (1.0 - sigmoid_gate))
            grad_ref[here, :width] = grad_gate.astype(jnp.bfloat16)
            grad_ref[here, width:] = (grad_act * silu).astype(jnp.bfloat16)
            part_ref[here] = dot_last(grad_ref[here], weight_ref[...]).astype(jnp.bfloat16)
            down_part_ref[here] = jnp.dot(
                activated, down_ref[...], preferred_element_type=jnp.float32
            ).astype(jnp.bfloat16)
            return carry

        lax.fori_loop(0, 2, step, 0)

    order = (at.z,) + z_order(at.z)
    gather.begin()
    for index, z in enumerate(order):
        if index + 1 < len(order):
            gather.from_z(order[index + 1])
        gather.from_y(z)
        if index == 0:
            gather.local.wait()
        gather.from_core(z)
        compute(z)
        second.to_core(z)
        if index == 2:
            second.to_y(order[1])
        if index == 3:
            second.to_y(order[2])
    own, near, middle, last = order

    def gate_tile(index, carry):
        columns = pl.ds(pl.multiple_of(index * LANES, LANES), LANES)
        flat_ref[columns] = dot_first(all_ref[:, columns], grad_ref[...])
        return carry

    def columns_of(ctx):
        return pl.ds(pl.multiple_of(ctx * width, LANES), width)

    second.to_y(last)
    second.to_y(own)
    tiles = all_ref.shape[1] // LANES
    lax.fori_loop(0, tiles, gate_tile, 0)
    for part in range(parts):
        here = slice(part * depth, (part + 1) * depth)
        gate_send[part] = flat_ref[here, columns_of(1 - at.c)].astype(jnp.bfloat16)
    gate_copy = remote_copy(gate_send, gate_recv, x_sems.at[0], x_sems.at[1], other_ctx)
    gate_copy.start()
    second.to_z(middle, False)
    second.to_z(last, False)
    hidden = down_grad_ref.shape[0]
    down_grad_ref[...] = dot_first(act_ref[...], cot_ref[...])[:hidden].astype(jnp.bfloat16)
    second.to_z(near, False)
    second.to_z(own, True)
    second.finish()
    gate_copy.wait_recv()
    for part in range(parts):
        here = slice(part * depth, (part + 1) * depth)
        mine = flat_ref[here, columns_of(at.c)].astype(jnp.bfloat16).astype(jnp.float32)
        gate_sum_ref[part] = (mine + gate_recv[part].astype(jnp.float32)).astype(jnp.bfloat16)
    gate_copy.wait_send()
    gather.end()
    second.end()


def ffn(second_in, all_cot, weight, down, hidden, collective_id):
    rows, model = second_in.shape
    parts = all_cot.shape[0] // rows
    width = down.shape[0]
    depth = model // parts
    tokens = parts * rows
    f32, bf16 = jnp.float32, jnp.bfloat16
    vmem = pl.BlockSpec(memory_space=pltpu.VMEM)
    flops = 2 * tokens * model * width * 9
    return pl.pallas_call(
        ffn_kernel,
        out_shape=(
            jax.ShapeDtypeStruct((rows, model), f32),
            jax.ShapeDtypeStruct((tokens, model), bf16),
            jax.ShapeDtypeStruct((hidden, model), bf16),
            jax.ShapeDtypeStruct((parts, depth, width), bf16),
        ),
        in_specs=[vmem] * 4,
        out_specs=(vmem,) * 4,
        scratch_shapes=[
            pltpu.VMEM((tokens, model), bf16),
            pltpu.VMEM((tokens, width), bf16),
            pltpu.VMEM((tokens, 2 * width), bf16),
            pltpu.VMEM((tokens, model), bf16),
            pltpu.VMEM((4, 2, rows, model), bf16),
            pltpu.VMEM((4, rows, model), bf16),
            pltpu.VMEM((4, rows, model), bf16),
            pltpu.VMEM((model, 2 * width), f32),
            pltpu.VMEM((parts, depth, width), bf16),
            pltpu.VMEM((parts, depth, width), bf16),
            pltpu.SemaphoreType.DMA((4, 5)),
            pltpu.SemaphoreType.DMA((4, 4)),
            pltpu.SemaphoreType.DMA,
            pltpu.SemaphoreType.DMA((4, 4)),
            pltpu.SemaphoreType.DMA((4, 4)),
            pltpu.SemaphoreType.DMA((2,)),
        ],
        compiler_params=pltpu.CompilerParams(
            collective_id=collective_id, has_side_effects=True, vmem_limit_bytes=38 * 2**20
        ),
        cost_estimate=pl.CostEstimate(
            flops=flops, bytes_accessed=16 * 2**20, transcendentals=tokens * width
        ),
    )(second_in, all_cot, weight, down)


class SharedGather(Gather):
    def __init__(self, at, own_ref, all_ref, send_sems, recv_sems, local_sem):
        self.at, self.whole_all = at, all_ref
        self.count = own_ref.shape[0] // 2
        self.mine = self.half(at.c)
        self.theirs = self.half(1 - at.c)
        self.own = own_ref.at[self.mine]
        self.all = all_ref
        self.send_sems, self.recv_sems, self.local_sem = send_sems, recv_sems, local_sem
        self.sent = []
        self.hop_sent = []

    def half(self, ctx):
        return pl.ds(pl.multiple_of(ctx * self.count, self.count), self.count)

    def block(self, z, y, k, rows=None):
        return self.all.at[z * 4 + y * 2 + k, self.mine if rows is None else rows]

    def to_core(self, source, z, y):
        super().to_core(source, z, y)
        self.to_x(source, z, y)

    def x_copy(self, source, z, y, rows):
        at = self.at
        return remote_copy(
            source,
            self.block(z, y, at.k, rows),
            self.send_sems.at[z, 5 + y],
            self.recv_sems.at[z, 4 + y],
            {"ctx": 1 - at.c},
        )

    def to_x(self, source, z, y):
        copy = self.x_copy(source, z, y, self.mine)
        copy.start()
        self.sent.append(copy)

    def core_again(self, z, y, k):
        at = self.at
        here = self.block(z, y, k, self.theirs)
        return remote_copy(
            here,
            here,
            self.send_sems.at[z, 7 + y],
            self.recv_sems.at[z, 6 + y],
            at.seq(at.z, at.y, 1 - at.k),
        )

    def from_x(self, z, y):
        at = self.at
        here = self.block(z, y, at.k, self.theirs)
        self.x_copy(here, z, y, self.theirs).wait_recv()
        copy = self.core_again(z, y, at.k)
        copy.start()
        self.sent.append(copy)

    def from_core(self, z):
        super().from_core(z)
        for y in range(2):
            self.core_again(z, y, 1 - self.at.k).wait_recv()


def rotated(values):
    width = values.shape[1]
    half = HEAD_DIM // 2
    lane = lax.broadcasted_iota(jnp.int32, values.shape, 1) % HEAD_DIM
    ahead = pltpu.roll(values, width - half, 1)
    behind = pltpu.roll(values, half, 1)
    return jnp.where(lane < half, -ahead, behind)


def tiled(table, width):
    return jnp.concatenate([table] * (width // table.shape[1]), 1)


def head_columns(head):
    return slice(head * HEAD_DIM, (head + 1) * HEAD_DIM)


def forward_kernel(
    qkv_ref,
    out_ref,
    cot_ref,
    gate_up_ref,
    tokens_ref,
    cos_ref,
    sin_ref,
    query_pos_ref,
    key_pos_ref,
    full_qkv_ref,
    full_out_ref,
    all_cot_ref,
    weight_ref,
    gains_ref,
    first_ref,
    query_ref,
    kv_ref,
    probs_ref,
    attended_ref,
    residual_ref,
    second_ref,
    all_qkv_ref,
    all_out_ref,
    bias_ref,
    gate_send,
    gate_all,
    qkv_send,
    qkv_recv,
    out_send,
    out_recv,
    cot_send,
    cot_recv,
    local_sems,
    gate_sems,
    x_sems,
    kv_sems,
):
    f32, bf16 = jnp.float32, jnp.bfloat16
    at = Place()
    parts, depth, width = gate_send.shape
    half = gate_up_ref.shape[1] // 2
    hidden = half // parts
    bias_count = bias_ref.shape[1] // parts
    query_width = HEADS * HEAD_DIM
    key_width = KV_HEADS * HEAD_DIM
    seq_peers = [lax.rem(at.me + step, parts) for step in range(1, parts)]
    other_ctx = {"ctx": 1 - at.c}
    greet([{"seq": peer} for peer in seq_peers] + [other_ctx])
    qkv = SharedGather(at, qkv_ref, all_qkv_ref, qkv_send, qkv_recv, local_sems.at[0])
    out = SharedGather(at, out_ref, all_out_ref, out_send, out_recv, local_sems.at[1])
    cot = Gather(at, cot_ref, all_cot_ref, cot_send, cot_recv, local_sems.at[2])
    order = (at.z,) + z_order(at.z)
    qkv.begin()
    half_value = gate_up_ref[:, pl.ds(pl.multiple_of(at.c * half, LANES), half)]
    tail = jnp.zeros((depth, width - hidden), gate_send.dtype)
    for part in range(parts):
        gate_send[part, :, :hidden] = half_value[:, part * hidden : (part + 1) * hidden]
        gate_send[part, :, hidden:] = tail
    gate_copies = []

    def gate_start(steps):
        for step in steps:
            peer = lax.rem(at.me + step, parts)
            copy = remote_copy(
                gate_send.at[peer],
                gate_all.at[at.c, at.me],
                gate_sems.at[0, step - 1],
                gate_sems.at[1, step - 1],
                {"seq": peer},
            )
            copy.start()
            gate_copies.append(copy)

    def gate_x(source, ctx, step):
        here = gate_all.at[ctx, source]
        return remote_copy(here, here, x_sems.at[0, step], x_sems.at[1, step], other_ctx)

    def gate_arrive(steps):
        for step in steps:
            source = lax.rem(at.me + parts - step, parts)
            if step > 0:
                remote_copy(
                    gate_send.at[source],
                    gate_all.at[at.c, source],
                    gate_sems.at[0, step - 1],
                    gate_sems.at[1, step - 1],
                    {"seq": source},
                ).wait_recv()
            copy = gate_x(source, at.c, step)
            copy.start()
            gate_copies.append(copy)

    gate_start(range(1, parts))
    qkv.from_y(order[0])
    qkv.from_z(order[1])
    out.begin()
    qkv.from_y(order[1])
    qkv.from_z(order[2])
    gate_all[at.c, at.me] = gate_send[at.me]
    qkv.from_y(order[2])
    qkv.from_z(order[3])
    cot.begin()
    qkv.from_y(order[3])
    out.from_y(order[0])
    out.from_z(order[1])
    for z in order:
        for y in range(2):
            qkv.from_x(z, y)
    out.from_y(order[1])
    out.from_z(order[2])
    qkv.local.wait()
    for z in order:
        qkv.from_core(z)
    cot.from_y(order[0])
    cot.from_z(order[1])
    for part in range(parts):
        rows = pl.ds(part * depth, depth)
        full_qkv_ref[rows] = all_qkv_ref[part, :depth]
        extra = all_qkv_ref[part, depth : depth + 1, : bias_count + 2 * depth].astype(f32)
        bias_ref[:, part * bias_count : (part + 1) * bias_count] = extra[:, :bias_count]
        for index in range(2):
            start = bias_count + index * depth
            gains_ref[index : index + 1, part * depth : (part + 1) * depth] = extra[
                :, start : start + depth
            ]
    tokens = tokens_ref[...].astype(f32)
    normed_one, _ = rms_forward(tokens)
    first_ref[...] = (normed_one * gains_ref[0:1]).astype(bf16)
    projected = (
        jnp.dot(first_ref[...], full_qkv_ref[...], preferred_element_type=f32) + bias_ref[...]
    )
    rotary = projected[:, : query_width + key_width]
    turned = rotary * tiled(cos_ref[...], rotary.shape[1]) + rotated(rotary) * tiled(
        sin_ref[...], rotary.shape[1]
    )
    turned = turned.astype(bf16)
    query_ref[...] = turned[:, :query_width]
    kv_ref[0, :, :key_width] = turned[:, query_width:]
    kv_ref[0, :, key_width:] = projected[:, query_width + key_width :].astype(bf16)
    kv_copy = remote_copy(kv_ref.at[0], kv_ref.at[1], kv_sems.at[0], kv_sems.at[1], other_ctx)
    kv_copy.start()
    out.from_y(order[2])
    out.from_z(order[3])
    cot.from_y(order[1])
    cot.from_z(order[2])
    out.from_y(order[3])
    for z in order:
        for y in range(2):
            out.from_x(z, y)
    kv_copy.wait_recv()
    rows = tokens.shape[0]
    kv = kv_ref[...].reshape(2 * rows, 2 * key_width)
    allowed = key_pos_ref[...] <= query_pos_ref[...]
    group_size = HEADS // KV_HEADS

    def attend(head):
        keys = kv[:, head_columns(head // group_size)]
        values = kv[:, head_columns(KV_HEADS + head // group_size)]
        scores = dot_last(query_ref[:, head_columns(head)], keys) * (HEAD_DIM ** (-0.5))
        scores = jnp.where(allowed, scores, -1e30)
        row_top = jnp.max(scores, axis=-1, keepdims=True)
        log_total = row_top + jnp.log(
            jnp.sum(jnp.exp(scores - row_top), axis=-1, keepdims=True)
        )
        probs = jnp.exp(scores - log_total)
        probs_ref[head] = probs
        attended_ref[:, head_columns(head)] = jnp.dot(
            probs.astype(bf16), values, preferred_element_type=f32
        ).astype(bf16)

    for head in range(group_size):
        attend(head)
    cot.from_y(order[2])
    cot.from_z(order[3])
    gate_arrive(range(0, parts // 2))
    for head in range(group_size, HEADS):
        attend(head)
    cot.from_y(order[3])
    out.local.wait()
    for z in order:
        out.from_core(z)
    for part in range(parts):
        full_out_ref[pl.ds(part * depth, depth)] = all_out_ref[part, :depth]
    residual = tokens + jnp.dot(
        attended_ref[...], full_out_ref[...], preferred_element_type=f32
    )
    residual_ref[...] = residual
    normed_two, _ = rms_forward(residual)
    second_ref[...] = (normed_two * gains_ref[1:2]).astype(bf16)
    gate_arrive(range(parts // 2, parts))
    for z in order:
        cot.from_core(z)
    for step in range(parts):
        gate_x(lax.rem(at.me + parts - step, parts), 1 - at.c, step).wait_recv()
    for part in range(parts):
        rows = pl.ds(part * depth, depth)
        weight_ref[rows, :width] = gate_all[0, part]
        weight_ref[rows, width:] = gate_all[1, part]
    kv_copy.wait_send()
    for copy in gate_copies:
        copy.wait_send()
    cot.local.wait()
    for gather in (qkv, out, cot):
        gather.end()


def forward(qkv, out, cot, gate_up, tokens, tables, query_pos, key_pos, bias_count, collective_id):
    parts = lax.axis_size("seq")
    rows = qkv.shape[0]
    depth = gate_up.shape[0]
    hidden = gate_up.shape[1] // (2 * parts)
    width = padded(hidden)
    count, model = cot.shape
    f32, bf16 = jnp.float32, jnp.bfloat16
    query_width = HEADS * HEAD_DIM
    key_width = KV_HEADS * HEAD_DIM
    shape = jax.ShapeDtypeStruct
    vmem = pl.BlockSpec(memory_space=pltpu.VMEM)
    outs = (
        shape((parts * depth, qkv.shape[1]), bf16),
        shape((parts * depth, out.shape[1]), bf16),
        shape((parts * count, model), bf16),
        shape((parts * depth, 2 * width), bf16),
        shape((2, model), f32),
        shape((count, model), bf16),
        shape((count, query_width), bf16),
        shape((2, count, 2 * key_width), bf16),
        shape((HEADS, count, 2 * count), f32),
        shape((count, query_width), bf16),
        shape((count, model), f32),
        shape((count, model), bf16),
    )
    return pl.pallas_call(
        forward_kernel,
        out_shape=outs,
        in_specs=[vmem] * 9,
        out_specs=(vmem,) * len(outs),
        scratch_shapes=[
            pltpu.VMEM((parts, rows, qkv.shape[1]), bf16),
            pltpu.VMEM((parts, rows, out.shape[1]), bf16),
            pltpu.VMEM((1, parts * bias_count), f32),
            pltpu.VMEM((parts, depth, width), bf16),
            pltpu.VMEM((2, parts, depth, width), bf16),
            pltpu.SemaphoreType.DMA((4, 9)),
            pltpu.SemaphoreType.DMA((4, 8)),
            pltpu.SemaphoreType.DMA((4, 9)),
            pltpu.SemaphoreType.DMA((4, 8)),
            pltpu.SemaphoreType.DMA((4, 5)),
            pltpu.SemaphoreType.DMA((4, 4)),
            pltpu.SemaphoreType.DMA((3,)),
            pltpu.SemaphoreType.DMA((2, parts - 1)),
            pltpu.SemaphoreType.DMA((2, parts)),
            pltpu.SemaphoreType.DMA((2,)),
        ],
        compiler_params=pltpu.CompilerParams(
            collective_id=collective_id, has_side_effects=True, vmem_limit_bytes=28 * 2**20
        ),
    )(qkv, out, cot, gate_up, tokens, *tables, query_pos, key_pos)


class Flow:
    def __init__(self, at, source, out_ref, bufs, sems, x_first, halves):
        self.at, self.source, self.out = at, source, out_ref
        (self.core_recv, self.x_send, self.x_recv, self.y_send, self.y_recv,
         self.z_send, self.z_recv, self.last_send, self.last_recv) = bufs
        self.sems = sems
        self.x_first, self.halves = x_first, halves
        rows = source.shape[3]
        self.count = rows // 2 if halves else rows
        self.mine = self.half(at.c) if halves else pl.ds(0, rows)
        self.theirs = self.half(1 - at.c) if halves else pl.ds(0, rows)
        self.all_rows = pl.ds(0, rows)
        self.sent = []
        near = z_order(at.z)
        self.order = (near[2], near[1], near[0], at.z)

    def half(self, ctx):
        return pl.ds(pl.multiple_of(ctx * self.count, self.count), self.count)

    def start(self, copy):
        copy.start()
        self.sent.append(copy)

    def copy(self, source, target, slot, device):
        return remote_copy(source, target, self.sems.at[0, slot], self.sems.at[1, slot], device)

    def core_copy(self, z):
        at = self.at
        return self.copy(
            self.source.at[1 - at.k, z], self.core_recv.at[z], z, at.seq(at.z, at.y, 1 - at.k)
        )

    def x_copy(self, z):
        return self.copy(self.x_send.at[z], self.x_recv.at[z], 4 + z, {"ctx": 1 - self.at.c})

    def y_copy(self, z):
        at = self.at
        return self.copy(
            self.y_send.at[z], self.y_recv.at[z], 8 + z, at.seq(at.z, 1 - at.y, at.k)
        )

    def last_copy(self):
        return self.copy(self.last_send, self.last_recv, 16, {"ctx": 1 - self.at.c})

    def begin(self):
        for z in self.order:
            self.start(self.core_copy(z))

    def add_core(self):
        at = self.at
        for z in self.order:
            self.core_copy(z).wait_recv()
            for y in range(2):
                self.source[at.k, z, y] += self.core_recv[z, y]
            if self.x_first:
                for y in range(2):
                    self.x_send[z, y] = self.source[at.k, z, y, self.theirs].astype(
                        self.x_send.dtype
                    )
                self.start(self.x_copy(z))
            else:
                self.to_y(z, self.all_rows)

    def to_y(self, z, rows):
        at = self.at
        self.y_send[z] = self.source[at.k, z, 1 - at.y, rows].astype(self.y_send.dtype)
        self.start(self.y_copy(z))

    def second(self, steps=range(4)):
        at = self.at
        for step in steps:
            z = self.order[step]
            if self.x_first:
                self.x_copy(z).wait_recv()
                for y in range(2):
                    self.source[at.k, z, y, self.mine] += self.x_recv[z, y].astype(jnp.float32)
                self.to_y(z, self.mine)
            else:
                self.y_copy(z).wait_recv()
                self.source[at.k, z, at.y] += self.y_recv[z].astype(jnp.float32)
                self.x_send[z] = self.source[at.k, z, at.y, self.theirs].astype(
                    self.x_send.dtype
                )
                self.start(self.x_copy(z))

    def z_copy(self, z, source_z):
        at = self.at
        return remote_copy(
            self.z_send.at[z],
            self.z_recv.at[source_z],
            self.sems.at[0, 12 + z],
            self.sems.at[1, 12 + source_z],
            at.seq(z, at.y, at.k),
        )

    def to_z(self, steps=range(4)):
        at = self.at
        arrived = self.y_recv if self.x_first else self.x_recv
        for step in steps:
            z = self.order[step]
            (self.y_copy(z) if self.x_first else self.x_copy(z)).wait_recv()
            total = self.source[at.k, z, at.y, self.mine] + arrived[z].astype(jnp.float32)
            if step == 3:
                self.source[at.k, z, at.y, self.mine] = total
            else:
                self.z_send[z] = total.astype(self.z_send.dtype)
                self.start(self.z_copy(z, at.z))

    def finish(self):
        at = self.at
        total = self.source[at.k, at.z, at.y, self.mine]
        for z in z_order(at.z):
            self.z_copy(z, z).wait_recv()
            total += self.z_recv[z].astype(jnp.float32)
        self.out[self.mine] = total
        if self.halves:
            self.last_send[...] = total
            self.start(self.last_copy())

    def end(self):
        if self.halves:
            self.last_copy().wait_recv()
            self.out[self.theirs] = self.last_recv[...]
        for copy in self.sent:
            copy.wait_send()


def flow_scratch(rows, width, x_first, halves, dtype):
    f32 = jnp.float32
    count = rows // 2 if halves else rows
    x_shape = (4, 2, count, width) if x_first else (4, count, width)
    y_shape = (4, count if x_first else rows, width)
    z_shape = (4, count, width)
    last = (count, width) if halves else (8, LANES)
    return [
        pltpu.VMEM((2, 4, 2, rows, width), f32),
        pltpu.VMEM((4, 2, rows, width), f32),
        pltpu.VMEM(x_shape, dtype),
        pltpu.VMEM(x_shape, dtype),
        pltpu.VMEM(y_shape, dtype),
        pltpu.VMEM(y_shape, dtype),
        pltpu.VMEM(z_shape, dtype),
        pltpu.VMEM(z_shape, dtype),
        pltpu.VMEM(last, f32),
        pltpu.VMEM(last, f32),
        pltpu.SemaphoreType.DMA((2, 17)),
    ]


def backward_kernel(
    cot_ref,
    residual_ref,
    tokens_ref,
    gains_ref,
    second_sum_ref,
    down_part_ref,
    gate_ref,
    down_mine_ref,
    query_ref,
    kv_ref,
    probs_ref,
    attended_ref,
    full_qkv_ref,
    full_out_ref,
    first_ref,
    cos_ref,
    sin_ref,
    output_ref,
    input_grad_ref,
    qkv_out_ref,
    out_out_ref,
    small_out_ref,
    gate_out_ref,
    down_grad_ref,
    *scratch,
):
    f32, bf16 = jnp.float32, jnp.bfloat16
    at = Place()
    flow_bufs = [scratch[11 * index : 11 * (index + 1)] for index in range(3)]
    (
        flat_ref,
        down_other,
        gate_recv,
        core_buf,
        y_buf,
        z_buf,
        down_ref,
        grad_query_ref,
        grad_kv_ref,
        kv_other,
        grad_att_ref,
        grad_proj_ref,
        gate_sems,
        half_sems,
        x_sems,
        scatter_send,
        scatter_recv,
    ) = scratch[33:]
    parts, depth, width = gate_ref.shape
    hidden = gate_out_ref.shape[1] // (2 * parts)
    rows, model = tokens_ref.shape
    query_width = HEADS * HEAD_DIM
    key_width = KV_HEADS * HEAD_DIM
    group_size = HEADS // KV_HEADS
    seq_peers = [lax.rem(at.me + step, parts) for step in range(1, parts)]
    other_ctx = {"ctx": 1 - at.c}
    greet([{"seq": peer} for peer in seq_peers] + [other_ctx])
    qkv = Flow(at, flow_bufs[0][0], qkv_out_ref, flow_bufs[0][1:10], flow_bufs[0][10], False, True)
    out = Flow(at, flow_bufs[1][0], out_out_ref, flow_bufs[1][1:10], flow_bufs[1][10], False, True)
    small = Flow(
        at, flow_bufs[2][0], small_out_ref, flow_bufs[2][1:10], flow_bufs[2][10], True, False
    )
    down = Scatter(
        at, down_part_ref, core_buf, y_buf, z_buf, down_ref, scatter_send, scatter_recv
    )
    near = z_order(at.z)
    far = (near[2], near[1], near[0], at.z)

    def spread(flat, source):
        count = source.shape[3]
        tail = jnp.zeros((count - depth, source.shape[4]), f32)
        for part in range(parts):
            z, y, k = part // 4, (part // 2) % 2, part % 2
            source[k, z, y, :depth] = flat[
                part * depth : (part + 1) * depth, : source.shape[4]
            ]
            source[k, z, y, depth:] = tail

    for z in far:
        down.to_core(z)
    gate_copies = []
    for step, peer in enumerate(seq_peers):
        copy = remote_copy(
            gate_ref.at[peer],
            gate_recv.at[at.c, at.me],
            gate_sems.at[0, step],
            gate_sems.at[1, step],
            {"seq": peer},
        )
        copy.start()
        gate_copies.append(copy)
    down_copy = remote_copy(
        down_mine_ref, down_other, x_sems.at[0, 0], x_sems.at[1, 0], other_ctx
    )
    down_copy.start()
    gate_recv[at.c, at.me] = gate_ref[at.me]
    normed_two, scale_two = rms_forward(residual_ref[...])
    grad_through, gain_two_grad = rms_backward(
        second_sum_ref[...], normed_two, scale_two, gains_ref[1:2]
    )
    grad_residual = cot_ref[...].astype(f32) + grad_through
    input_grad_ref[...] = grad_residual
    grad_res_b = grad_residual.astype(bf16)
    down.to_y(far[0])
    down.to_y(far[1])
    out_columns = out.source.shape[4]
    flat_ref[:, :out_columns] = dot_first(attended_ref[...], grad_res_b)
    spread(flat_ref, out.source)
    out.begin()
    down.to_y(far[2])
    down.to_y(far[3])
    def gate_x(source, ctx, step):
        here = gate_recv.at[ctx, source]
        return remote_copy(
            here, here, half_sems.at[0, step], half_sems.at[1, step], other_ctx
        )

    def gate_forward(step):
        copy = gate_x(lax.rem(at.me + parts - step, parts), at.c, step)
        copy.start()
        gate_copies.append(copy)

    def gate_arrive(steps):
        for step in steps:
            source = lax.rem(at.me + parts - step, parts)
            remote_copy(
                gate_ref.at[source],
                gate_recv.at[at.c, source],
                gate_sems.at[0, step - 1],
                gate_sems.at[1, step - 1],
                {"seq": source},
            ).wait_recv()
            gate_forward(step)

    grad_att_ref[...] = dot_last(grad_res_b, full_out_ref[...]).astype(bf16)
    kv = kv_ref[...].reshape(2 * rows, 2 * key_width)
    grad_kv_ref[...] = jnp.zeros_like(grad_kv_ref)

    def backward_head(head):
        group = head // group_size
        key_columns = head_columns(group)
        value_columns = head_columns(KV_HEADS + group)
        columns = head_columns(head)
        grad_att = grad_att_ref[:, columns]
        grad_probs = dot_last(grad_att, kv[:, value_columns])
        delta = jnp.sum(
            grad_att.astype(f32) * attended_ref[:, columns].astype(f32), axis=-1, keepdims=True
        )
        probs = probs_ref[head]
        grad_scores = (probs * (grad_probs - delta) * (HEAD_DIM ** (-0.5))).astype(bf16)
        grad_query_ref[:, columns] = jnp.dot(
            grad_scores, kv[:, key_columns], preferred_element_type=f32
        )
        return (
            dot_first(grad_scores, query_ref[:, columns]),
            dot_first(probs.astype(bf16), grad_att),
        )

    def backward_group(group):
        heads = range(group * group_size, (group + 1) * group_size)
        parts_of = [backward_head(head) for head in heads]
        grad_kv_ref[:, head_columns(group)] = sum(part[0] for part in parts_of[1:]) + parts_of[0][0]
        grad_kv_ref[:, head_columns(KV_HEADS + group)] = (
            sum(part[1] for part in parts_of[1:]) + parts_of[0][1]
        )

    backward_group(0)
    down.to_z(far[0], False)
    out.add_core()
    backward_group(1)
    kv_copy = remote_copy(
        grad_kv_ref.at[pl.ds(rows, rows)], kv_other, x_sems.at[0, 1], x_sems.at[1, 1], other_ctx
    )
    kv_copy.start()
    down.to_z(far[1], False)
    gate_forward(0)
    gate_arrive(range(1, parts // 2))
    kv_copy.wait_recv()
    grad_query = grad_query_ref[...]
    grad_kv = grad_kv_ref[:rows] + kv_other[...]
    rotary = jnp.concatenate([grad_query, grad_kv[:, :key_width]], 1)
    turned = rotary * tiled(cos_ref[...], rotary.shape[1]) - rotated(
        rotary * tiled(sin_ref[...], rotary.shape[1])
    )
    bias_row = jnp.concatenate(
        [
            jnp.sum(turned, axis=0, keepdims=True),
            jnp.sum(grad_kv[:, key_width:], axis=0, keepdims=True),
        ],
        1,
    )
    grad_proj_ref[:, : query_width + key_width] = turned.astype(bf16)
    grad_proj_ref[:, query_width + key_width :] = grad_kv[:, key_width:].astype(bf16)
    flat_ref[...] = dot_first(first_ref[...], grad_proj_ref[...])
    spread(flat_ref, qkv.source)
    qkv.begin()
    gate_arrive(range(parts // 2, parts))
    down.to_z(far[2], False)
    down.to_z(far[3], True)
    grad_first = dot_last(grad_proj_ref[...], full_qkv_ref[...])
    normed_one, scale_one = rms_forward(tokens_ref[...].astype(f32))
    grad_part, gain_one_grad = rms_backward(grad_first, normed_one, scale_one, gains_ref[0:1])
    input_grad_ref[...] += grad_part
    bias_count = bias_row.shape[1] // parts
    gain_one_row = gain_one_grad.reshape(1, model)
    gain_two_row = gain_two_grad.reshape(1, model)
    small.source[...] = jnp.zeros_like(small.source)
    for part in range(parts):
        z, y, k = part // 4, (part // 2) % 2, part % 2
        small.source[k, z, y, 0:1, :bias_count] = bias_row[
            :, part * bias_count : (part + 1) * bias_count
        ]
        for index, row in enumerate((gain_one_row, gain_two_row)):
            start = bias_count + index * depth
            small.source[k, z, y, 0:1, start : start + depth] = row[
                :, part * depth : (part + 1) * depth
            ]
    small.begin()
    out.second()
    qkv.add_core()
    small.add_core()
    out.to_z()
    small.second()

    qkv.second()
    small.to_z()
    qkv.to_z()
    down.finish()
    output_ref[...] = (residual_ref[...] + down_ref[...]).astype(bf16)
    down_copy.wait_recv()
    down_grad_ref[...] = down_mine_ref[...].astype(f32) + down_other[...].astype(f32)
    out.finish()
    small.finish()
    for step in range(parts):
        gate_x(lax.rem(at.me + parts - step, parts), 1 - at.c, step).wait_recv()
    for ctx in range(2):
        for part in range(parts):
            start = (ctx * parts + part) * hidden
            gate_out_ref[:, start : start + hidden] = gate_recv[ctx, part, :, :hidden].astype(f32)
    qkv.finish()
    down_copy.wait_send()
    kv_copy.wait_send()
    for copy in gate_copies:
        copy.wait_send()
    down.end()
    out.end()
    small.end()
    qkv.end()


def backward(operands, hidden, bias_count, collective_id):
    cot, gate_sum, first_in = operands[0], operands[6], operands[14]
    parts, depth, width = gate_sum.shape
    f32, bf16 = jnp.float32, jnp.bfloat16
    rows = (depth + 31) // 32 * 32
    count, model = cot.shape
    qkv_columns = operands[12].shape[1]
    out_rows, out_columns = operands[13].shape
    kv_columns = operands[9].shape[2]
    small_width = padded(bias_count + 2 * depth)
    shape = jax.ShapeDtypeStruct
    vmem = pl.BlockSpec(memory_space=pltpu.VMEM)
    return pl.pallas_call(
        backward_kernel,
        out_shape=(
            shape((count, model), bf16),
            shape((count, model), f32),
            shape((rows, qkv_columns), f32),
            shape((rows, out_columns), f32),
            shape((8, small_width), f32),
            shape((depth, 2 * parts * hidden), f32),
            shape((hidden, model), f32),
        ),
        in_specs=[vmem] * len(operands),
        out_specs=(vmem,) * 7,
        scratch_shapes=flow_scratch(rows, qkv_columns, False, True, bf16)
        + flow_scratch(rows, out_columns, False, True, bf16)
        + flow_scratch(8, small_width, True, False, f32)
        + [
            pltpu.VMEM((model, qkv_columns), f32),
            pltpu.VMEM((hidden, model), bf16),
            pltpu.VMEM((2, parts, depth, width), bf16),
            pltpu.VMEM((4, 2, count, model), bf16),
            pltpu.VMEM((4, count, model), bf16),
            pltpu.VMEM((4, count, model), bf16),
            pltpu.VMEM((count, model), f32),
            pltpu.VMEM((count, out_rows), f32),
            pltpu.VMEM((2 * count, kv_columns), f32),
            pltpu.VMEM((count, kv_columns), f32),
            pltpu.VMEM((count, out_rows), bf16),
            pltpu.VMEM((count, qkv_columns), bf16),
            pltpu.SemaphoreType.DMA((2, parts - 1)),
            pltpu.SemaphoreType.DMA((2, parts)),
            pltpu.SemaphoreType.DMA((2, 2)),
            pltpu.SemaphoreType.DMA((4, 4)),
            pltpu.SemaphoreType.DMA((4, 4)),
        ],
        compiler_params=pltpu.CompilerParams(
            collective_id=collective_id, has_side_effects=True, vmem_limit_bytes=40 * 2**20
        ),
    )(*operands)


def finish_kernel(*refs):
    count = len(refs) // 2
    for index in range(count):
        source, target = refs[index], refs[count + index]
        if len(target.shape) == 3:
            target[0] = source[...]
        else:
            target[...] = source[: target.shape[0], : target.shape[1]]


def finish(values, shapes):
    vmem = pl.BlockSpec(memory_space=pltpu.VMEM)
    return pl.pallas_call(
        finish_kernel,
        out_shape=tuple(
            jax.ShapeDtypeStruct(shape, value.dtype) for value, shape in zip(values, shapes)
        ),
        in_specs=[vmem] * len(values),
        out_specs=(vmem,) * len(values),
        compiler_params=pltpu.CompilerParams(vmem_limit_bytes=24 * 2**20),
    )(*values)


def shards(
    tokens,
    positions,
    cotangent,
    qkv_weight,
    qkv_bias,
    out_weight,
    gate_up_weight,
    down_weight,
    attn_gain,
    ffn_gain,
):
    f32 = jnp.float32
    qkv_columns = qkv_weight.shape[1]
    depth = qkv_weight.shape[0]
    bias_count = qkv_bias.shape[0]
    packed_rows = packed_height(depth)
    pair = jnp.concatenate([qkv_weight, out_weight], 1)
    extra = jnp.concatenate([qkv_bias, attn_gain, ffn_gain])
    extra = jnp.pad(extra, (0, pair.shape[1] - extra.shape[0]))[None]
    packed = jnp.concatenate(
        [pair, extra, jnp.zeros((packed_rows - depth - 1, pair.shape[1]), pair.dtype)], 0
    )
    packed = lax.all_gather(packed, "seq", axis=0, tiled=True).reshape(-1, packed_rows, pair.shape[1])
    full_qkv = packed[:, :depth, :qkv_columns].reshape(-1, qkv_columns)
    full_out = packed[:, :depth, qkv_columns:].reshape(-1, out_weight.shape[1])
    full_bias = packed[:, depth, :bias_count].reshape(-1)
    gain_one = packed[:, depth, bias_count : bias_count + depth].reshape(-1)
    gain_two = packed[:, depth, bias_count + depth : bias_count + 2 * depth].reshape(-1)
    parts = lax.axis_size("seq")
    hidden = down_weight.shape[0]
    own_gate_up = columns_from_rows(gate_up_weight, parts)
    all_cot = gather_rows(cotangent[0], 0)
    own_gate_up, all_cot, full_qkv = lax.optimization_barrier((own_gate_up, all_cot, full_qkv))
    inputs_f = tokens[0].astype(f32)
    cot_row = cotangent[0]
    row_count = inputs_f.shape[0]
    group_size = HEADS // KV_HEADS
    query_width = HEADS * HEAD_DIM
    key_width = KV_HEADS * HEAD_DIM
    score_scale = HEAD_DIM ** (-0.5)
    all_positions = positions[0]
    position_row = lax.dynamic_slice_in_dim(
        all_positions, lax.axis_index("ctx") * row_count, row_count, 0
    )
    normed_one, scale_one = rms_forward(inputs_f)
    first_in = to_bf16(normed_one * gain_one.astype(f32))
    projected = jnp.dot(first_in, full_qkv, preferred_element_type=f32) + full_bias.astype(f32)
    cosine_table, sine_table = rope_tables(position_row)
    cos_query = cosine_table[:, None, None, :]
    sin_query = sine_table[:, None, None, :]
    cos_key = cosine_table[:, None, :]
    sin_key = sine_table[:, None, :]
    query = projected[:, :query_width].reshape(row_count, KV_HEADS, group_size, HEAD_DIM)
    keys = projected[:, query_width : query_width + key_width].reshape(
        row_count, KV_HEADS, HEAD_DIM
    )
    values = projected[:, query_width + key_width :]
    query_rot = to_bf16(query * cos_query + rotate_half(query) * sin_query)
    key_rot = to_bf16(keys * cos_key + rotate_half(keys) * sin_key).reshape(row_count, key_width)
    value_b = to_bf16(values)
    both = jnp.concatenate([key_rot, value_b], -1)
    if lax.axis_size("ctx") == 2:
        both = jnp.concatenate([both, other(both)], 0)
        other_row = lax.dynamic_slice_in_dim(
            all_positions, (1 - lax.axis_index("ctx")) * row_count, row_count, 0
        )
        all_positions = jnp.concatenate([position_row, other_row])
    else:
        both = lax.all_gather(both, "ctx", axis=0, tiled=True)
    all_keys, all_values = both[:, :key_width], both[:, key_width:]
    all_keys = all_keys.reshape(-1, KV_HEADS, HEAD_DIM)
    all_values = all_values.reshape(-1, KV_HEADS, HEAD_DIM)
    scores = (
        jnp.einsum("tkgd,skd->kgts", query_rot, all_keys, preferred_element_type=f32) * score_scale
    )
    allowed = all_positions[None, :] <= position_row[:, None]
    scores = jnp.where(allowed, scores, -1e30)
    row_top = jnp.max(scores, axis=-1, keepdims=True)
    log_total = row_top + jnp.log(jnp.sum(jnp.exp(scores - row_top), axis=-1, keepdims=True))
    probs = jnp.exp(scores - log_total)
    probs_b = to_bf16(probs)
    attended = to_bf16(
        jnp.einsum("kgts,skd->tkgd", probs_b, all_values, preferred_element_type=f32)
    )
    attended_flat = attended.reshape(row_count, query_width)
    residual = inputs_f + jnp.dot(attended_flat, full_out, preferred_element_type=f32)
    normed_two, scale_two = rms_forward(residual)
    second_in = to_bf16(normed_two * gain_two.astype(f32))
    all_second = gather_rows(second_in, 1)
    gate_up = jnp.dot(all_second, own_gate_up, preferred_element_type=f32)
    gate = gate_up[:, :hidden]
    upward = gate_up[:, hidden:]
    sigmoid_gate = jax.nn.sigmoid(gate)
    activated = to_bf16(gate * sigmoid_gate * upward)
    grad_act = contract_columns(all_cot, down_weight)
    grad_gate = grad_act * upward * sigmoid_gate * (1.0 + gate * (1.0 - sigmoid_gate))
    grad_upward = grad_act * (gate * sigmoid_gate)
    grad_gate_up = to_bf16(jnp.concatenate([grad_gate, grad_upward], -1))
    grad_second = scatter_tokens(contract_columns(grad_gate_up, own_gate_up))
    down_sum = scatter_tokens(jnp.dot(activated, down_weight, preferred_element_type=f32))
    output_row = (residual + down_sum).astype(jnp.bfloat16)
    result_down = sum_rounded(contract_rows(activated, all_cot))
    result_gate_up = rows_from_columns(
        to_bf16(sum_rounded(contract_rows(all_second, grad_gate_up))), parts
    ).astype(f32)
    grad_through, gain_two_grad = rms_backward(
        grad_second, normed_two, scale_two, gain_two.astype(f32)
    )
    grad_residual = cot_row.astype(f32) + grad_through
    grad_res_b = to_bf16(grad_residual)
    out_grad = weight_rows(attended_flat, grad_res_b)
    grad_attended = to_bf16(jnp.dot(grad_res_b, full_out.T, preferred_element_type=f32))
    grad_attended = grad_attended.reshape(row_count, KV_HEADS, group_size, HEAD_DIM)
    grad_probs = jnp.einsum("tkgd,skd->kgts", grad_attended, all_values, preferred_element_type=f32)
    delta = jnp.sum(grad_attended.astype(f32) * attended.astype(f32), axis=-1)
    delta = jnp.transpose(delta, (1, 2, 0))[..., None]
    grad_scores = to_bf16(probs * (grad_probs - delta) * score_scale)
    grad_query_rot = jnp.einsum("kgts,skd->tkgd", grad_scores, all_keys, preferred_element_type=f32)
    key_part = jnp.einsum("kgts,tkgd->skd", grad_scores, query_rot, preferred_element_type=f32)
    value_part = jnp.einsum("kgts,tkgd->skd", probs_b, grad_attended, preferred_element_type=f32)
    key_parts = jnp.concatenate(
        [
            key_part.reshape(row_count * lax.axis_size("ctx"), key_width),
            value_part.reshape(row_count * lax.axis_size("ctx"), key_width),
        ],
        -1,
    )
    if lax.axis_size("ctx") == 2:
        key_local = key_parts[:row_count] + other(key_parts[row_count:])
    else:
        key_local = lax.psum_scatter(key_parts, "ctx", scatter_dimension=0, tiled=True)
    grad_key_rot = key_local[:, :key_width].reshape(row_count, KV_HEADS, HEAD_DIM)
    grad_value = key_local[:, key_width:]
    grad_query = grad_query_rot * cos_query + rotate_back(grad_query_rot * sin_query)
    grad_key = grad_key_rot * cos_key + rotate_back(grad_key_rot * sin_key)
    grad_projected = jnp.concatenate(
        [
            grad_query.reshape(row_count, query_width),
            grad_key.reshape(row_count, key_width),
            grad_value,
        ],
        -1,
    )
    bias_grad = jnp.sum(grad_projected, axis=0)
    grad_proj_b = to_bf16(grad_projected)
    grad_first = jnp.dot(grad_proj_b, full_qkv.T, preferred_element_type=f32)
    grad_input_part, gain_one_grad = rms_backward(
        grad_first, normed_one, scale_one, gain_one.astype(f32)
    )
    input_row_grad = grad_residual + grad_input_part
    small = jnp.concatenate(
        [
            bias_grad.reshape(parts, -1),
            gain_one_grad.reshape(parts, -1),
            gain_two_grad.reshape(parts, -1),
        ],
        -1,
    )
    small = jnp.pad(small, ((0, 0), (0, qkv_columns - small.shape[1])))[:, None]
    grad_rows = (depth + 8) // 8 * 8
    packed_grad = jnp.concatenate(
        [
            contract_rows(first_in, grad_proj_b).reshape(parts, depth, qkv_columns),
            small,
            jnp.zeros((parts, grad_rows - depth - 1, qkv_columns), f32),
        ],
        1,
    ).reshape(parts * grad_rows, qkv_columns)
    packed_grad, output_row = lax.optimization_barrier((packed_grad, output_row))
    packed_sum = sum_ctx(lax.psum_scatter(packed_grad, "seq", scatter_dimension=0, tiled=True))
    result_qkv = packed_sum[:depth]
    result_bias = packed_sum[depth, :bias_count]
    result_gain_one = packed_sum[depth, bias_count : bias_count + depth]
    result_gain_two = packed_sum[depth, bias_count + depth : bias_count + 2 * depth]
    result_out = sum_ctx(out_grad)
    return (
        output_row[None],
        input_row_grad[None],
        result_qkv,
        result_bias,
        result_out,
        result_gate_up,
        result_down,
        result_gain_one,
        result_gain_two,
    )


def shards_fast(
    tokens,
    positions,
    cotangent,
    qkv_weight,
    qkv_bias,
    out_weight,
    gate_up_weight,
    down_weight,
    attn_gain,
    ffn_gain,
):
    qkv_columns = qkv_weight.shape[1]
    depth = qkv_weight.shape[0]
    bias_count = qkv_bias.shape[0]
    packed_rows = packed_height(depth)
    parts = lax.axis_size("seq")
    hidden = down_weight.shape[0]
    extra = jnp.concatenate([qkv_bias, attn_gain, ffn_gain])
    extra = jnp.pad(extra, (0, qkv_columns - extra.shape[0]))[None]
    qkv_packed = jnp.concatenate(
        [qkv_weight, extra, jnp.zeros((packed_rows - depth - 1, qkv_columns), extra.dtype)], 0
    )
    out_packed = jnp.pad(out_weight, ((0, packed_rows - depth), (0, 0)))
    cot_row = cotangent[0]
    row_count = cot_row.shape[0]
    at_ctx = lax.axis_index("ctx")
    position_row = lax.dynamic_slice_in_dim(positions[0], at_ctx * row_count, row_count, 0)
    other_row = lax.dynamic_slice_in_dim(positions[0], (1 - at_ctx) * row_count, row_count, 0)
    cosine_table, sine_table = rope_tables(position_row)
    tables = [jnp.concatenate([table, table], -1) for table in (cosine_table, sine_table)]
    (
        full_qkv,
        full_out,
        all_cot,
        weight_wide,
        gains,
        first_in,
        query_flat,
        both,
        probs,
        attended_flat,
        residual,
        second_in,
    ) = forward(
        qkv_packed,
        out_packed,
        cot_row,
        gate_up_weight,
        tokens[0],
        tables,
        position_row[:, None],
        jnp.concatenate([position_row, other_row])[None],
        bias_count,
        0,
    )
    down_sum_width = padded(hidden)
    extra_rows = down_sum_width - hidden
    down_wide = jnp.pad(down_weight, ((0, extra_rows), (0, 0)))
    grad_second, down_part, down_mine, gate_sum = ffn(
        second_in, all_cot, weight_wide, down_wide, hidden, 1
    )
    output_row, input_row_grad, qkv_sum, out_sum, small_sum, gate_grad, down_grad = backward(
        (
            cot_row,
            residual,
            tokens[0],
            gains,
            grad_second,
            down_part,
            gate_sum,
            down_mine,
            query_flat,
            both,
            probs,
            attended_flat,
            full_qkv,
            full_out,
            first_in,
            *tables,
        ),
        hidden,
        bias_count,
        2,
    )
    output_row, input_row_grad, result_qkv, result_out, result_gate_up, result_down = finish(
        (output_row, input_row_grad, qkv_sum, out_sum, gate_grad, down_grad),
        (
            (1,) + output_row.shape,
            (1,) + input_row_grad.shape,
            (depth, qkv_columns),
            (depth, out_weight.shape[1]),
            gate_grad.shape,
            down_grad.shape,
        ),
    )
    result_bias = small_sum[0, :bias_count]
    result_gain_one = small_sum[0, bias_count : bias_count + depth]
    result_gain_two = small_sum[0, bias_count + depth : bias_count + 2 * depth]
    return (
        output_row,
        input_row_grad,
        result_qkv,
        result_bias,
        result_out,
        result_gate_up,
        result_down,
        result_gain_one,
        result_gain_two,
    )


def solution(mesh):
    in_specs = (
        P("seq", "ctx", None),
        P("seq", None),
        P("seq", "ctx", None),
        P("seq", None),
        P("seq"),
        P("seq", None),
        P("seq", None),
        P("seq", None),
        P("seq"),
        P("seq"),
    )
    out_specs = (
        P("seq", "ctx", None),
        P("seq", "ctx", None),
        P("seq", None),
        P("seq"),
        P("seq", None),
        P("seq", None),
        P("seq", None),
        P("seq"),
        P("seq"),
    )
    fast = mesh.shape["ctx"] == 2 and mesh.shape["seq"] == 16
    return jax.shard_map(shards_fast if fast else shards, mesh=mesh, in_specs=in_specs, out_specs=out_specs, check_vma=False)
```

```python
import functools

import jax
import jax.numpy as jnp
from jax import lax
from jax.experimental import pallas as pl
from jax.experimental.pallas import tpu as pltpu
from jax.sharding import PartitionSpec as P

HEADS = 14
KV_HEADS = 2
HEAD_DIM = 64


EPS = 1e-06
ROPE_BASE = 1000000.0


def to_bf16(values):
    return lax.optimization_barrier(values.astype(jnp.bfloat16))


def rope_tables(position_row):
    half_dim = HEAD_DIM // 2
    exponent = jnp.arange(half_dim, dtype=jnp.float32) * (2.0 / HEAD_DIM)
    inverse = ROPE_BASE ** (-exponent)
    angles = position_row.astype(jnp.float32)[:, None] * inverse[None, :]
    cosine_table = jnp.cos(angles)
    sine_table = jnp.sin(angles)
    return (
        jnp.concatenate([cosine_table, cosine_table], -1),
        jnp.concatenate([sine_table, sine_table], -1),
    )


def rotate_half(values):
    half_dim = values.shape[-1] // 2
    return jnp.concatenate([-values[..., half_dim:], values[..., :half_dim]], -1)


def rotate_back(values):
    half_dim = values.shape[-1] // 2
    return jnp.concatenate([values[..., half_dim:], -values[..., :half_dim]], -1)


def rms_forward(values):
    scaling = lax.rsqrt(jnp.mean(values * values, axis=-1, keepdims=True) + EPS)
    return (values * scaling, scaling)


def rms_backward(grad_normed, normed, scaling, gain_float):
    gain_grad = jnp.sum(grad_normed * normed, axis=0)
    grad_scaled = grad_normed * gain_float
    inner = jnp.mean(grad_scaled * normed, axis=-1, keepdims=True)
    return (scaling * (grad_scaled - normed * inner), gain_grad)


def weight_rows(left_side, right_side):
    return lax.psum_scatter(
        lax.dot_general(
            left_side, right_side, (((0,), (0,)), ((), ())), preferred_element_type=jnp.float32
        ),
        "seq",
        scatter_dimension=0,
        tiled=True,
    )


def columns_from_rows(rows, parts):
    depth = rows.shape[0]
    hidden = rows.shape[1] // (2 * parts)
    split = jnp.transpose(rows.reshape(depth, 2, parts, hidden), (2, 0, 1, 3))
    split = split.reshape(parts, depth, 2 * hidden)
    moved = lax.all_to_all(split, "seq", split_axis=0, concat_axis=0, tiled=True)
    return moved.reshape(parts * depth, 2 * hidden)


def rows_from_columns(columns, parts):
    depth = columns.shape[0] // parts
    hidden = columns.shape[1] // 2
    split = columns.reshape(parts, depth, 2 * hidden)
    moved = lax.all_to_all(split, "seq", split_axis=0, concat_axis=0, tiled=True)
    moved = jnp.transpose(moved.reshape(parts, depth, 2, hidden), (1, 2, 0, 3))
    return moved.reshape(depth, 2 * parts * hidden)


def contract_rows(left_side, right_side):
    return lax.dot_general(
        left_side, right_side, (((0,), (0,)), ((), ())), preferred_element_type=jnp.float32
    )


def contract_columns(left_side, right_side):
    return lax.dot_general(
        left_side, right_side, (((1,), (1,)), ((), ())), preferred_element_type=jnp.float32
    )


def scatter_tokens(partial):
    total = lax.psum_scatter(to_bf16(partial), "seq", scatter_dimension=0, tiled=True)
    return total.astype(jnp.float32)


def gather_kernel(outer, own_ref, all_ref, local_sem, outer_sems, middle_sems, core_sems):
    me = lax.axis_index("seq")
    at_outer = me // 4
    middle = (me // 2) % 2
    core = me % 2
    rows = own_ref.shape[0]

    def place(outer_at, middle_at, core_at):
        index = outer_at * 4 + middle_at * 2 + core_at
        return all_ref.at[pl.ds(pl.multiple_of(index * rows, rows), rows)]

    def remote(source, target, sems, slot, device):
        return pltpu.make_async_remote_copy(
            src_ref=source,
            dst_ref=target,
            send_sem=sems.at[0, slot],
            recv_sem=sems.at[1, slot],
            device_id={"seq": device},
            device_id_type=pl.DeviceIdType.MESH,
        )

    middle_partner = at_outer * 4 + (1 - middle) * 2 + core
    core_partner = at_outer * 4 + middle * 2 + (1 - core)
    outer_partners = [
        ((at_outer + step) % outer) * 4 + middle * 2 + core for step in range(1, outer)
    ]
    barrier = pltpu.get_barrier_semaphore()
    for device in [middle_partner, core_partner] + outer_partners:
        pl.semaphore_signal(
            barrier, inc=1, device_id={"seq": device}, device_id_type=pl.DeviceIdType.MESH
        )
    pl.semaphore_wait(barrier, outer + 1)

    own_place = place(at_outer, middle, core)
    local = pltpu.make_async_copy(own_ref, own_place, local_sem)
    local.start()
    started = []
    outer_copies = []
    for step in range(1, outer):
        copy = remote(own_ref, own_place, outer_sems, step - 1, outer_partners[step - 1])
        copy.start()
        outer_copies.append(copy)
    middle_copies = []
    for step in range(outer):
        source_outer = (at_outer + outer - step) % outer
        here = place(source_outer, middle, core)
        if step == 0:
            source = own_ref
        else:
            outer_copies[step - 1].wait_recv()
            source = here
        copy = remote(source, here, middle_sems, step, middle_partner)
        copy.start()
        middle_copies.append(copy)
        copy = remote(source, here, core_sems, 2 * step, core_partner)
        copy.start()
        started.append(copy)
    for step in range(outer):
        source_outer = (at_outer + outer - step) % outer
        middle_copies[step].wait_recv()
        here = place(source_outer, 1 - middle, core)
        copy = remote(here, here, core_sems, 2 * step + 1, core_partner)
        copy.start()
        started.append(copy)
    for copy in started:
        copy.wait_recv()
    for copy in outer_copies + middle_copies + started:
        copy.wait_send()
    local.wait()


def gather_rows(rows, collective_id):
    parts = lax.axis_size("seq")
    if parts % 4:
        return lax.all_gather(rows, "seq", axis=0, tiled=True)
    outer = parts // 4
    return pl.pallas_call(
        functools.partial(gather_kernel, outer),
        out_shape=jax.ShapeDtypeStruct((parts * rows.shape[0], rows.shape[1]), rows.dtype),
        in_specs=[pl.BlockSpec(memory_space=pltpu.VMEM)],
        out_specs=pl.BlockSpec(memory_space=pltpu.VMEM),
        scratch_shapes=[
            pltpu.SemaphoreType.DMA,
            pltpu.SemaphoreType.DMA((2, max(outer - 1, 1))),
            pltpu.SemaphoreType.DMA((2, outer)),
            pltpu.SemaphoreType.DMA((2, 2 * outer)),
        ],
        compiler_params=pltpu.CompilerParams(
            collective_id=collective_id, has_side_effects=True, vmem_limit_bytes=24 * 2**20
        ),
    )(rows)


def packed_height(depth):
    return (depth + 16) // 16 * 16


def other(values):
    return lax.ppermute(values, "ctx", [(0, 1), (1, 0)])


def sum_rounded(values):
    if lax.axis_size("ctx") != 2:
        return lax.psum(values, "ctx")
    mine = to_bf16(values)
    return mine.astype(jnp.float32) + other(mine).astype(jnp.float32)


def sum_ctx(values):
    if lax.axis_size("ctx") != 2:
        return lax.psum(values, "ctx")
    return values + other(values)


MESH = pl.DeviceIdType.MESH
LANES = 128


def padded(width):
    return (width + LANES - 1) // LANES * LANES


def remote_copy(source, target, send_sem, recv_sem, device):
    return pltpu.make_async_remote_copy(
        src_ref=source,
        dst_ref=target,
        send_sem=send_sem,
        recv_sem=recv_sem,
        device_id=device,
        device_id_type=MESH,
    )


def greet(devices):
    barrier = pltpu.get_barrier_semaphore()
    for device in devices:
        pl.semaphore_signal(barrier, inc=1, device_id=device, device_id_type=MESH)
    pl.semaphore_wait(barrier, len(devices))


def dot_last(left, right):
    return lax.dot_general(
        left, right, (((1,), (1,)), ((), ())), preferred_element_type=jnp.float32
    )


def dot_first(left, right):
    return lax.dot_general(
        left, right, (((0,), (0,)), ((), ())), preferred_element_type=jnp.float32
    )


def z_order(z):
    return (z + 1 - 2 * (z % 2), 2 - z // 2, 3 - 3 * (z // 2))


class Place:
    def __init__(self):
        me = lax.axis_index("seq")
        self.z = me // 4
        self.y = (me // 2) % 2
        self.k = me % 2
        self.c = lax.axis_index("ctx")
        self.me = me

    def seq(self, z, y, k):
        return {"seq": z * 4 + y * 2 + k}

    def others(self):
        z, y, k = self.z, self.y, self.k
        return (
            [self.seq(z, 1 - y, k), self.seq(z, y, 1 - k)]
            + [self.seq(other, y, k) for other in z_order(z)]
        )


class Gather:
    def __init__(self, at, own_ref, all_ref, send_sems, recv_sems, local_sem):
        self.at, self.own, self.all = at, own_ref, all_ref
        self.send_sems, self.recv_sems, self.local_sem = send_sems, recv_sems, local_sem
        self.rows = own_ref.shape[0]
        self.sent = []
        self.hop_sent = []

    def block(self, z, y, k):
        start = pl.multiple_of((z * 4 + y * 2 + k) * self.rows, self.rows)
        return self.all.at[pl.ds(start, self.rows)]

    def copy(self, source, z, y, k, kind, device, slot=None):
        return remote_copy(
            source,
            self.block(z, y, k),
            self.send_sems.at[z, kind if slot is None else slot],
            self.recv_sems.at[z, kind],
            device,
        )

    def to_y_and_core(self, source, z):
        at = self.at
        copy = self.copy(source, z, at.y, at.k, 1, at.seq(at.z, 1 - at.y, at.k))
        copy.start()
        self.sent.append(copy)
        self.to_core(source, z, at.y)

    def to_core(self, source, z, y):
        at = self.at
        copy = self.copy(source, z, y, at.k, 2 + y, at.seq(at.z, at.y, 1 - at.k))
        copy.start()
        self.sent.append(copy)

    def hop(self, source, z, right):
        at = self.at
        target = at.z + 1 if right else at.z - 1
        copy = self.copy(
            source, z, at.y, at.k, 0, at.seq(target, at.y, at.k), slot=None if right else 4
        )
        ok = (target < 4) if right else (target >= 0)
        return ok, copy

    def begin(self):
        at = self.at
        for right in (True, False):
            ok, copy = self.hop(self.own, at.z, right)
            self.hop_sent.append((ok, copy))

            @pl.when(ok)
            def _():
                copy.start()

        self.to_y_and_core(self.own, at.z)
        self.local = pltpu.make_async_copy(
            self.own, self.block(at.z, at.y, at.k), self.local_sem
        )
        self.local.start()

    def from_z(self, z):
        at = self.at
        here = self.block(z, at.y, at.k)
        self.copy(here, z, at.y, at.k, 0, at.seq(at.z, 1 - at.y, at.k)).wait_recv()
        for right in (True, False):
            ok, copy = self.hop(here, z, right)
            ok = jnp.logical_and(ok, z < at.z if right else z > at.z)
            self.hop_sent.append((ok, copy))

            @pl.when(ok)
            def _():
                copy.start()

        self.to_y_and_core(here, z)

    def from_y(self, z):
        at = self.at
        here = self.block(z, 1 - at.y, at.k)
        self.copy(here, z, 1 - at.y, at.k, 1, at.seq(at.z, 1 - at.y, at.k)).wait_recv()
        self.to_core(here, z, 1 - at.y)

    def from_core(self, z):
        at = self.at
        for y in range(2):
            here = self.block(z, y, 1 - at.k)
            self.copy(here, z, y, 1 - at.k, 2 + y, at.seq(at.z, at.y, 1 - at.k)).wait_recv()

    def end(self):
        for copy in self.sent:
            copy.wait_send()
        for ok, copy in self.hop_sent:

            @pl.when(ok)
            def _():
                copy.wait_send()


class Scatter:
    def __init__(self, at, part, core_buf, y_buf, z_buf, out_ref, send_sems, recv_sems):
        self.at, self.part, self.out = at, part, out_ref
        self.core_buf, self.y_buf, self.z_buf = core_buf, y_buf, z_buf
        self.send_sems, self.recv_sems = send_sems, recv_sems
        self.rows = out_ref.shape[0]
        self.sent = []
        self.core_copies = {}

    def block(self, z, y, k):
        start = pl.multiple_of((z * 4 + y * 2 + k) * self.rows, self.rows)
        return self.part.at[pl.ds(start, self.rows)]

    def core_copy(self, z, y):
        at = self.at
        return remote_copy(
            self.block(z, y, 1 - at.k),
            self.core_buf.at[z, y],
            self.send_sems.at[z, y],
            self.recv_sems.at[z, y],
            at.seq(at.z, at.y, 1 - at.k),
        )

    def to_core(self, z):
        for y in range(2):
            copy = self.core_copy(z, y)
            copy.start()
            self.sent.append(copy)

    def y_copy(self, z):
        at = self.at
        return remote_copy(
            self.core_buf.at[z, 1 - at.y],
            self.y_buf.at[z],
            self.send_sems.at[z, 2],
            self.recv_sems.at[z, 2],
            at.seq(at.z, 1 - at.y, at.k),
        )

    def add_core(self, z, y):
        here = self.block(z, y, self.at.k)
        total = here[...].astype(jnp.float32) + self.core_buf[z, y].astype(jnp.float32)
        self.core_buf[z, y] = total.astype(jnp.bfloat16)

    def to_y(self, z):
        at = self.at
        for y in range(2):
            self.core_copy(z, y).wait_recv()
        self.add_core(z, 1 - at.y)
        copy = self.y_copy(z)
        copy.start()
        self.sent.append(copy)
        self.add_core(z, at.y)

    def z_copy(self, z, source_z):
        at = self.at
        return remote_copy(
            self.y_buf.at[z],
            self.z_buf.at[source_z],
            self.send_sems.at[z, 3],
            self.recv_sems.at[source_z, 3],
            at.seq(z, at.y, at.k),
        )

    def to_z(self, z, own):
        at = self.at
        self.y_copy(z).wait_recv()
        total = self.core_buf[z, at.y].astype(jnp.float32) + self.y_buf[z].astype(jnp.float32)
        if own:
            self.out[...] = total
        else:
            self.y_buf[z] = total.astype(jnp.bfloat16)
            copy = self.z_copy(z, at.z)
            copy.start()
            self.sent.append(copy)

    def finish(self):
        at = self.at
        total = self.out[...]
        for z in z_order(at.z):
            self.z_copy(z, z).wait_recv()
            total += self.z_buf[z].astype(jnp.float32)
        self.out[...] = total

    def end(self):
        for copy in self.sent:
            copy.wait_send()


def ffn_kernel(
    own_ref,
    cot_ref,
    weight_ref,
    down_ref,
    second_sum_ref,
    down_part_ref,
    down_grad_ref,
    gate_sum_ref,
    all_ref,
    act_ref,
    grad_ref,
    part_ref,
    core_buf,
    y_buf,
    z_buf,
    flat_ref,
    gate_send,
    gate_recv,
    gather_send,
    gather_recv,
    local_sem,
    scatter_send,
    scatter_recv,
    x_sems,
):
    at = Place()
    width = down_ref.shape[0]
    rows = own_ref.shape[0]
    parts = all_ref.shape[0] // rows
    depth = weight_ref.shape[0] // parts
    other_ctx = {"ctx": 1 - at.c}
    greet(at.others() + [other_ctx])
    gather = Gather(at, own_ref, all_ref, gather_send, gather_recv, local_sem)
    second = Scatter(
        at, part_ref, core_buf, y_buf, z_buf, second_sum_ref, scatter_send, scatter_recv
    )
    tile = 2 * rows

    def compute(z):
        def step(index, carry):
            start = pl.multiple_of(z * (4 * rows) + index * tile, tile)
            here = pl.ds(start, tile)
            gate_up = jnp.dot(
                all_ref[here], weight_ref[...], preferred_element_type=jnp.float32
            )
            grad_act = dot_last(cot_ref[here], down_ref[...])
            gate = gate_up[:, :width]
            upward = gate_up[:, width:]
            sigmoid_gate = jax.nn.sigmoid(gate)
            silu = gate * sigmoid_gate
            activated = (silu * upward).astype(jnp.bfloat16)
            act_ref[here] = activated
            grad_gate = grad_act * upward * sigmoid_gate * (1.0 + gate * (1.0 - sigmoid_gate))
            grad_ref[here, :width] = grad_gate.astype(jnp.bfloat16)
            grad_ref[here, width:] = (grad_act * silu).astype(jnp.bfloat16)
            part_ref[here] = dot_last(grad_ref[here], weight_ref[...]).astype(jnp.bfloat16)
            down_part_ref[here] = jnp.dot(
                activated, down_ref[...], preferred_element_type=jnp.float32
            ).astype(jnp.bfloat16)
            return carry

        lax.fori_loop(0, 2, step, 0)

    order = (at.z,) + z_order(at.z)
    gather.begin()
    for index, z in enumerate(order):
        if index + 1 < len(order):
            gather.from_z(order[index + 1])
        gather.from_y(z)
        if index == 0:
            gather.local.wait()
        gather.from_core(z)
        compute(z)
        second.to_core(z)
        if index == 2:
            second.to_y(order[1])
        if index == 3:
            second.to_y(order[2])
    own, near, middle, last = order

    def gate_tile(index, carry):
        columns = pl.ds(pl.multiple_of(index * LANES, LANES), LANES)
        flat_ref[columns] = dot_first(all_ref[:, columns], grad_ref[...])
        return carry

    def columns_of(ctx):
        return pl.ds(pl.multiple_of(ctx * width, LANES), width)

    second.to_y(last)
    second.to_y(own)
    tiles = all_ref.shape[1] // LANES
    lax.fori_loop(0, tiles, gate_tile, 0)
    for part in range(parts):
        here = slice(part * depth, (part + 1) * depth)
        gate_send[part] = flat_ref[here, columns_of(1 - at.c)].astype(jnp.bfloat16)
    gate_copy = remote_copy(gate_send, gate_recv, x_sems.at[0], x_sems.at[1], other_ctx)
    gate_copy.start()
    second.to_z(middle, False)
    second.to_z(last, False)
    hidden = down_grad_ref.shape[0]
    down_grad_ref[...] = dot_first(act_ref[...], cot_ref[...])[:hidden].astype(jnp.bfloat16)
    second.to_z(near, False)
    second.to_z(own, True)
    second.finish()
    gate_copy.wait_recv()
    for part in range(parts):
        here = slice(part * depth, (part + 1) * depth)
        mine = flat_ref[here, columns_of(at.c)].astype(jnp.bfloat16).astype(jnp.float32)
        gate_sum_ref[part] = (mine + gate_recv[part].astype(jnp.float32)).astype(jnp.bfloat16)
    gate_copy.wait_send()
    gather.end()
    second.end()


def ffn(second_in, all_cot, weight, down, hidden, collective_id):
    rows, model = second_in.shape
    parts = all_cot.shape[0] // rows
    width = down.shape[0]
    depth = model // parts
    tokens = parts * rows
    f32, bf16 = jnp.float32, jnp.bfloat16
    vmem = pl.BlockSpec(memory_space=pltpu.VMEM)
    flops = 2 * tokens * model * width * 9
    return pl.pallas_call(
        ffn_kernel,
        out_shape=(
            jax.ShapeDtypeStruct((rows, model), f32),
            jax.ShapeDtypeStruct((tokens, model), bf16),
            jax.ShapeDtypeStruct((hidden, model), bf16),
            jax.ShapeDtypeStruct((parts, depth, width), bf16),
        ),
        in_specs=[vmem] * 4,
        out_specs=(vmem,) * 4,
        scratch_shapes=[
            pltpu.VMEM((tokens, model), bf16),
            pltpu.VMEM((tokens, width), bf16),
            pltpu.VMEM((tokens, 2 * width), bf16),
            pltpu.VMEM((tokens, model), bf16),
            pltpu.VMEM((4, 2, rows, model), bf16),
            pltpu.VMEM((4, rows, model), bf16),
            pltpu.VMEM((4, rows, model), bf16),
            pltpu.VMEM((model, 2 * width), f32),
            pltpu.VMEM((parts, depth, width), bf16),
            pltpu.VMEM((parts, depth, width), bf16),
            pltpu.SemaphoreType.DMA((4, 5)),
            pltpu.SemaphoreType.DMA((4, 4)),
            pltpu.SemaphoreType.DMA,
            pltpu.SemaphoreType.DMA((4, 4)),
            pltpu.SemaphoreType.DMA((4, 4)),
            pltpu.SemaphoreType.DMA((2,)),
        ],
        compiler_params=pltpu.CompilerParams(
            collective_id=collective_id, has_side_effects=True, vmem_limit_bytes=38 * 2**20
        ),
        cost_estimate=pl.CostEstimate(
            flops=flops, bytes_accessed=16 * 2**20, transcendentals=tokens * width
        ),
    )(second_in, all_cot, weight, down)


class SharedGather(Gather):
    def __init__(self, at, own_ref, all_ref, send_sems, recv_sems, local_sem):
        self.at, self.whole_all = at, all_ref
        self.count = own_ref.shape[0] // 2
        self.mine = self.half(at.c)
        self.theirs = self.half(1 - at.c)
        self.own = own_ref.at[self.mine]
        self.all = all_ref
        self.send_sems, self.recv_sems, self.local_sem = send_sems, recv_sems, local_sem
        self.sent = []
        self.hop_sent = []

    def half(self, ctx):
        return pl.ds(pl.multiple_of(ctx * self.count, self.count), self.count)

    def block(self, z, y, k, rows=None):
        return self.all.at[z * 4 + y * 2 + k, self.mine if rows is None else rows]

    def to_core(self, source, z, y):
        super().to_core(source, z, y)
        self.to_x(source, z, y)

    def x_copy(self, source, z, y, rows):
        at = self.at
        return remote_copy(
            source,
            self.block(z, y, at.k, rows),
            self.send_sems.at[z, 5 + y],
            self.recv_sems.at[z, 4 + y],
            {"ctx": 1 - at.c},
        )

    def to_x(self, source, z, y):
        copy = self.x_copy(source, z, y, self.mine)
        copy.start()
        self.sent.append(copy)

    def core_again(self, z, y, k):
        at = self.at
        here = self.block(z, y, k, self.theirs)
        return remote_copy(
            here,
            here,
            self.send_sems.at[z, 7 + y],
            self.recv_sems.at[z, 6 + y],
            at.seq(at.z, at.y, 1 - at.k),
        )

    def from_x(self, z, y):
        at = self.at
        here = self.block(z, y, at.k, self.theirs)
        self.x_copy(here, z, y, self.theirs).wait_recv()
        copy = self.core_again(z, y, at.k)
        copy.start()
        self.sent.append(copy)

    def from_core(self, z):
        super().from_core(z)
        for y in range(2):
            self.core_again(z, y, 1 - self.at.k).wait_recv()


def rotated(values):
    width = values.shape[1]
    half = HEAD_DIM // 2
    lane = lax.broadcasted_iota(jnp.int32, values.shape, 1) % HEAD_DIM
    ahead = pltpu.roll(values, width - half, 1)
    behind = pltpu.roll(values, half, 1)
    return jnp.where(lane < half, -ahead, behind)


def tiled(table, width):
    return jnp.concatenate([table] * (width // table.shape[1]), 1)


def head_columns(head):
    return slice(head * HEAD_DIM, (head + 1) * HEAD_DIM)


def forward_kernel(
    qkv_ref,
    out_ref,
    cot_ref,
    gate_up_ref,
    tokens_ref,
    cos_ref,
    sin_ref,
    query_pos_ref,
    key_pos_ref,
    full_qkv_ref,
    full_out_ref,
    all_cot_ref,
    weight_ref,
    gains_ref,
    first_ref,
    query_ref,
    kv_ref,
    probs_ref,
    attended_ref,
    residual_ref,
    second_ref,
    all_qkv_ref,
    all_out_ref,
    bias_ref,
    gate_send,
    gate_all,
    qkv_send,
    qkv_recv,
    out_send,
    out_recv,
    cot_send,
    cot_recv,
    local_sems,
    gate_sems,
    x_sems,
    kv_sems,
):
    f32, bf16 = jnp.float32, jnp.bfloat16
    at = Place()
    parts, depth, width = gate_send.shape
    half = gate_up_ref.shape[1] // 2
    hidden = half // parts
    bias_count = bias_ref.shape[1] // parts
    query_width = HEADS * HEAD_DIM
    key_width = KV_HEADS * HEAD_DIM
    seq_peers = [lax.rem(at.me + step, parts) for step in range(1, parts)]
    other_ctx = {"ctx": 1 - at.c}
    greet([{"seq": peer} for peer in seq_peers] + [other_ctx])
    qkv = SharedGather(at, qkv_ref, all_qkv_ref, qkv_send, qkv_recv, local_sems.at[0])
    out = SharedGather(at, out_ref, all_out_ref, out_send, out_recv, local_sems.at[1])
    cot = Gather(at, cot_ref, all_cot_ref, cot_send, cot_recv, local_sems.at[2])
    order = (at.z,) + z_order(at.z)
    qkv.begin()
    half_value = gate_up_ref[:, pl.ds(pl.multiple_of(at.c * half, LANES), half)]
    tail = jnp.zeros((depth, width - hidden), gate_send.dtype)
    for part in range(parts):
        gate_send[part, :, :hidden] = half_value[:, part * hidden : (part + 1) * hidden]
        gate_send[part, :, hidden:] = tail
    gate_copies = []

    def gate_start(steps):
        for step in steps:
            peer = lax.rem(at.me + step, parts)
            copy = remote_copy(
                gate_send.at[peer],
                gate_all.at[at.c, at.me],
                gate_sems.at[0, step - 1],
                gate_sems.at[1, step - 1],
                {"seq": peer},
            )
            copy.start()
            gate_copies.append(copy)

    def gate_x(source, ctx, step):
        here = gate_all.at[ctx, source]
        return remote_copy(here, here, x_sems.at[0, step], x_sems.at[1, step], other_ctx)

    def gate_arrive(steps):
        for step in steps:
            source = lax.rem(at.me + parts - step, parts)
            if step > 0:
                remote_copy(
                    gate_send.at[source],
                    gate_all.at[at.c, source],
                    gate_sems.at[0, step - 1],
                    gate_sems.at[1, step - 1],
                    {"seq": source},
                ).wait_recv()
            copy = gate_x(source, at.c, step)
            copy.start()
            gate_copies.append(copy)

    gate_start(range(1, parts))
    qkv.from_y(order[0])
    qkv.from_z(order[1])
    out.begin()
    qkv.from_y(order[1])
    qkv.from_z(order[2])
    gate_all[at.c, at.me] = gate_send[at.me]
    qkv.from_y(order[2])
    qkv.from_z(order[3])
    cot.begin()
    qkv.from_y(order[3])
    out.from_y(order[0])
    out.from_z(order[1])
    for z in order:
        for y in range(2):
            qkv.from_x(z, y)
    out.from_y(order[1])
    out.from_z(order[2])
    qkv.local.wait()
    for z in order:
        qkv.from_core(z)
    cot.from_y(order[0])
    cot.from_z(order[1])
    for part in range(parts):
        rows = pl.ds(part * depth, depth)
        full_qkv_ref[rows] = all_qkv_ref[part, :depth]
        extra = all_qkv_ref[part, depth : depth + 1, : bias_count + 2 * depth].astype(f32)
        bias_ref[:, part * bias_count : (part + 1) * bias_count] = extra[:, :bias_count]
        for index in range(2):
            start = bias_count + index * depth
            gains_ref[index : index + 1, part * depth : (part + 1) * depth] = extra[
                :, start : start + depth
            ]
    tokens = tokens_ref[...].astype(f32)
    normed_one, _ = rms_forward(tokens)
    first_ref[...] = (normed_one * gains_ref[0:1]).astype(bf16)
    projected = (
        jnp.dot(first_ref[...], full_qkv_ref[...], preferred_element_type=f32) + bias_ref[...]
    )
    rotary = projected[:, : query_width + key_width]
    turned = rotary * tiled(cos_ref[...], rotary.shape[1]) + rotated(rotary) * tiled(
        sin_ref[...], rotary.shape[1]
    )
    turned = turned.astype(bf16)
    query_ref[...] = turned[:, :query_width]
    kv_ref[0, :, :key_width] = turned[:, query_width:]
    kv_ref[0, :, key_width:] = projected[:, query_width + key_width :].astype(bf16)
    kv_copy = remote_copy(kv_ref.at[0], kv_ref.at[1], kv_sems.at[0], kv_sems.at[1], other_ctx)
    kv_copy.start()
    out.from_y(order[2])
    out.from_z(order[3])
    cot.from_y(order[1])
    cot.from_z(order[2])
    out.from_y(order[3])
    for z in order:
        for y in range(2):
            out.from_x(z, y)
    gate_arrive(range(0, parts // 2))
    kv_copy.wait_recv()
    rows = tokens.shape[0]
    kv = kv_ref[...].reshape(2 * rows, 2 * key_width)
    allowed = key_pos_ref[...] <= query_pos_ref[...]
    group_size = HEADS // KV_HEADS

    def attend(head):
        keys = kv[:, head_columns(head // group_size)]
        values = kv[:, head_columns(KV_HEADS + head // group_size)]
        scores = dot_last(query_ref[:, head_columns(head)], keys) * (HEAD_DIM ** (-0.5))
        scores = jnp.where(allowed, scores, -1e30)
        row_top = jnp.max(scores, axis=-1, keepdims=True)
        log_total = row_top + jnp.log(
            jnp.sum(jnp.exp(scores - row_top), axis=-1, keepdims=True)
        )
        probs = jnp.exp(scores - log_total)
        probs_ref[head] = probs
        attended_ref[:, head_columns(head)] = jnp.dot(
            probs.astype(bf16), values, preferred_element_type=f32
        ).astype(bf16)

    for head in range(group_size):
        attend(head)
    cot.from_y(order[2])
    cot.from_z(order[3])
    gate_arrive(range(parts // 2, parts))
    for head in range(group_size, HEADS):
        attend(head)
    cot.from_y(order[3])
    out.local.wait()
    for z in order:
        out.from_core(z)
    for part in range(parts):
        full_out_ref[pl.ds(part * depth, depth)] = all_out_ref[part, :depth]
    residual = tokens + jnp.dot(
        attended_ref[...], full_out_ref[...], preferred_element_type=f32
    )
    residual_ref[...] = residual
    normed_two, _ = rms_forward(residual)
    second_ref[...] = (normed_two * gains_ref[1:2]).astype(bf16)
    for z in order:
        cot.from_core(z)
    for step in range(parts):
        gate_x(lax.rem(at.me + parts - step, parts), 1 - at.c, step).wait_recv()
    for part in range(parts):
        rows = pl.ds(part * depth, depth)
        weight_ref[rows, :width] = gate_all[0, part]
        weight_ref[rows, width:] = gate_all[1, part]
    kv_copy.wait_send()
    for copy in gate_copies:
        copy.wait_send()
    cot.local.wait()
    for gather in (qkv, out, cot):
        gather.end()


def forward(qkv, out, cot, gate_up, tokens, tables, query_pos, key_pos, bias_count, collective_id):
    parts = lax.axis_size("seq")
    rows = qkv.shape[0]
    depth = gate_up.shape[0]
    hidden = gate_up.shape[1] // (2 * parts)
    width = padded(hidden)
    count, model = cot.shape
    f32, bf16 = jnp.float32, jnp.bfloat16
    query_width = HEADS * HEAD_DIM
    key_width = KV_HEADS * HEAD_DIM
    shape = jax.ShapeDtypeStruct
    vmem = pl.BlockSpec(memory_space=pltpu.VMEM)
    outs = (
        shape((parts * depth, qkv.shape[1]), bf16),
        shape((parts * depth, out.shape[1]), bf16),
        shape((parts * count, model), bf16),
        shape((parts * depth, 2 * width), bf16),
        shape((2, model), f32),
        shape((count, model), bf16),
        shape((count, query_width), bf16),
        shape((2, count, 2 * key_width), bf16),
        shape((HEADS, count, 2 * count), f32),
        shape((count, query_width), bf16),
        shape((count, model), f32),
        shape((count, model), bf16),
    )
    return pl.pallas_call(
        forward_kernel,
        out_shape=outs,
        in_specs=[vmem] * 9,
        out_specs=(vmem,) * len(outs),
        scratch_shapes=[
            pltpu.VMEM((parts, rows, qkv.shape[1]), bf16),
            pltpu.VMEM((parts, rows, out.shape[1]), bf16),
            pltpu.VMEM((1, parts * bias_count), f32),
            pltpu.VMEM((parts, depth, width), bf16),
            pltpu.VMEM((2, parts, depth, width), bf16),
            pltpu.SemaphoreType.DMA((4, 9)),
            pltpu.SemaphoreType.DMA((4, 8)),
            pltpu.SemaphoreType.DMA((4, 9)),
            pltpu.SemaphoreType.DMA((4, 8)),
            pltpu.SemaphoreType.DMA((4, 5)),
            pltpu.SemaphoreType.DMA((4, 4)),
            pltpu.SemaphoreType.DMA((3,)),
            pltpu.SemaphoreType.DMA((2, parts - 1)),
            pltpu.SemaphoreType.DMA((2, parts)),
            pltpu.SemaphoreType.DMA((2,)),
        ],
        compiler_params=pltpu.CompilerParams(
            collective_id=collective_id, has_side_effects=True, vmem_limit_bytes=28 * 2**20
        ),
    )(qkv, out, cot, gate_up, tokens, *tables, query_pos, key_pos)


class Flow:
    def __init__(self, at, source, out_ref, bufs, sems, x_first, halves):
        self.at, self.source, self.out = at, source, out_ref
        (self.core_recv, self.x_send, self.x_recv, self.y_send, self.y_recv,
         self.z_send, self.z_recv, self.last_send, self.last_recv) = bufs
        self.sems = sems
        self.x_first, self.halves = x_first, halves
        rows = source.shape[3]
        self.count = rows // 2 if halves else rows
        self.mine = self.half(at.c) if halves else pl.ds(0, rows)
        self.theirs = self.half(1 - at.c) if halves else pl.ds(0, rows)
        self.all_rows = pl.ds(0, rows)
        self.sent = []
        near = z_order(at.z)
        self.order = (near[2], near[1], near[0], at.z)

    def half(self, ctx):
        return pl.ds(pl.multiple_of(ctx * self.count, self.count), self.count)

    def start(self, copy):
        copy.start()
        self.sent.append(copy)

    def copy(self, source, target, slot, device):
        return remote_copy(source, target, self.sems.at[0, slot], self.sems.at[1, slot], device)

    def core_copy(self, z):
        at = self.at
        return self.copy(
            self.source.at[1 - at.k, z], self.core_recv.at[z], z, at.seq(at.z, at.y, 1 - at.k)
        )

    def x_copy(self, z):
        return self.copy(self.x_send.at[z], self.x_recv.at[z], 4 + z, {"ctx": 1 - self.at.c})

    def y_copy(self, z):
        at = self.at
        return self.copy(
            self.y_send.at[z], self.y_recv.at[z], 8 + z, at.seq(at.z, 1 - at.y, at.k)
        )

    def last_copy(self):
        return self.copy(self.last_send, self.last_recv, 16, {"ctx": 1 - self.at.c})

    def begin(self):
        for z in self.order:
            self.start(self.core_copy(z))

    def add_core(self):
        at = self.at
        for z in self.order:
            self.core_copy(z).wait_recv()
            for y in range(2):
                self.source[at.k, z, y] += self.core_recv[z, y]
            if self.x_first:
                for y in range(2):
                    self.x_send[z, y] = self.source[at.k, z, y, self.theirs].astype(
                        self.x_send.dtype
                    )
                self.start(self.x_copy(z))
            else:
                self.to_y(z, self.all_rows)

    def to_y(self, z, rows):
        at = self.at
        self.y_send[z] = self.source[at.k, z, 1 - at.y, rows].astype(self.y_send.dtype)
        self.start(self.y_copy(z))

    def second(self, steps=range(4)):
        at = self.at
        for step in steps:
            z = self.order[step]
            if self.x_first:
                self.x_copy(z).wait_recv()
                for y in range(2):
                    self.source[at.k, z, y, self.mine] += self.x_recv[z, y].astype(jnp.float32)
                self.to_y(z, self.mine)
            else:
                self.y_copy(z).wait_recv()
                self.source[at.k, z, at.y] += self.y_recv[z].astype(jnp.float32)
                self.x_send[z] = self.source[at.k, z, at.y, self.theirs].astype(
                    self.x_send.dtype
                )
                self.start(self.x_copy(z))

    def z_copy(self, z, source_z):
        at = self.at
        return remote_copy(
            self.z_send.at[z],
            self.z_recv.at[source_z],
            self.sems.at[0, 12 + z],
            self.sems.at[1, 12 + source_z],
            at.seq(z, at.y, at.k),
        )

    def to_z(self, steps=range(4)):
        at = self.at
        arrived = self.y_recv if self.x_first else self.x_recv
        for step in steps:
            z = self.order[step]
            (self.y_copy(z) if self.x_first else self.x_copy(z)).wait_recv()
            total = self.source[at.k, z, at.y, self.mine] + arrived[z].astype(jnp.float32)
            if step == 3:
                self.source[at.k, z, at.y, self.mine] = total
            else:
                self.z_send[z] = total.astype(self.z_send.dtype)
                self.start(self.z_copy(z, at.z))

    def finish(self):
        at = self.at
        total = self.source[at.k, at.z, at.y, self.mine]
        for z in z_order(at.z):
            self.z_copy(z, z).wait_recv()
            total += self.z_recv[z].astype(jnp.float32)
        self.out[self.mine] = total
        if self.halves:
            self.last_send[...] = total
            self.start(self.last_copy())

    def end(self):
        if self.halves:
            self.last_copy().wait_recv()
            self.out[self.theirs] = self.last_recv[...]
        for copy in self.sent:
            copy.wait_send()


def flow_scratch(rows, width, x_first, halves, dtype):
    f32 = jnp.float32
    count = rows // 2 if halves else rows
    x_shape = (4, 2, count, width) if x_first else (4, count, width)
    y_shape = (4, count if x_first else rows, width)
    z_shape = (4, count, width)
    last = (count, width) if halves else (8, LANES)
    return [
        pltpu.VMEM((2, 4, 2, rows, width), f32),
        pltpu.VMEM((4, 2, rows, width), f32),
        pltpu.VMEM(x_shape, dtype),
        pltpu.VMEM(x_shape, dtype),
        pltpu.VMEM(y_shape, dtype),
        pltpu.VMEM(y_shape, dtype),
        pltpu.VMEM(z_shape, dtype),
        pltpu.VMEM(z_shape, dtype),
        pltpu.VMEM(last, f32),
        pltpu.VMEM(last, f32),
        pltpu.SemaphoreType.DMA((2, 17)),
    ]


def backward_kernel(
    cot_ref,
    residual_ref,
    tokens_ref,
    gains_ref,
    second_sum_ref,
    down_part_ref,
    gate_ref,
    down_mine_ref,
    query_ref,
    kv_ref,
    probs_ref,
    attended_ref,
    full_qkv_ref,
    full_out_ref,
    first_ref,
    cos_ref,
    sin_ref,
    output_ref,
    input_grad_ref,
    qkv_out_ref,
    out_out_ref,
    small_out_ref,
    gate_out_ref,
    down_grad_ref,
    *scratch,
):
    f32, bf16 = jnp.float32, jnp.bfloat16
    at = Place()
    flow_bufs = [scratch[11 * index : 11 * (index + 1)] for index in range(3)]
    (
        flat_ref,
        down_other,
        gate_recv,
        core_buf,
        y_buf,
        z_buf,
        down_ref,
        grad_query_ref,
        grad_kv_ref,
        kv_other,
        grad_att_ref,
        grad_proj_ref,
        gate_sems,
        half_sems,
        x_sems,
        scatter_send,
        scatter_recv,
    ) = scratch[33:]
    parts, depth, width = gate_ref.shape
    hidden = gate_out_ref.shape[1] // (2 * parts)
    rows, model = tokens_ref.shape
    query_width = HEADS * HEAD_DIM
    key_width = KV_HEADS * HEAD_DIM
    group_size = HEADS // KV_HEADS
    seq_peers = [lax.rem(at.me + step, parts) for step in range(1, parts)]
    other_ctx = {"ctx": 1 - at.c}
    greet([{"seq": peer} for peer in seq_peers] + [other_ctx])
    qkv = Flow(at, flow_bufs[0][0], qkv_out_ref, flow_bufs[0][1:10], flow_bufs[0][10], False, True)
    out = Flow(at, flow_bufs[1][0], out_out_ref, flow_bufs[1][1:10], flow_bufs[1][10], False, True)
    small = Flow(
        at, flow_bufs[2][0], small_out_ref, flow_bufs[2][1:10], flow_bufs[2][10], True, False
    )
    down = Scatter(
        at, down_part_ref, core_buf, y_buf, z_buf, down_ref, scatter_send, scatter_recv
    )
    near = z_order(at.z)
    far = (near[2], near[1], near[0], at.z)

    def spread(flat, source):
        count = source.shape[3]
        tail = jnp.zeros((count - depth, source.shape[4]), f32)
        for part in range(parts):
            z, y, k = part // 4, (part // 2) % 2, part % 2
            source[k, z, y, :depth] = flat[
                part * depth : (part + 1) * depth, : source.shape[4]
            ]
            source[k, z, y, depth:] = tail

    for z in far:
        down.to_core(z)
    gate_copies = []
    for step, peer in enumerate(seq_peers):
        copy = remote_copy(
            gate_ref.at[peer],
            gate_recv.at[at.c, at.me],
            gate_sems.at[0, step],
            gate_sems.at[1, step],
            {"seq": peer},
        )
        copy.start()
        gate_copies.append(copy)
    down_copy = remote_copy(
        down_mine_ref, down_other, x_sems.at[0, 0], x_sems.at[1, 0], other_ctx
    )
    down_copy.start()
    gate_recv[at.c, at.me] = gate_ref[at.me]
    normed_two, scale_two = rms_forward(residual_ref[...])
    grad_through, gain_two_grad = rms_backward(
        second_sum_ref[...], normed_two, scale_two, gains_ref[1:2]
    )
    grad_residual = cot_ref[...].astype(f32) + grad_through
    input_grad_ref[...] = grad_residual
    grad_res_b = grad_residual.astype(bf16)
    down.to_y(far[0])
    down.to_y(far[1])
    out_columns = out.source.shape[4]
    flat_ref[:, :out_columns] = dot_first(attended_ref[...], grad_res_b)
    spread(flat_ref, out.source)
    out.begin()
    down.to_y(far[2])
    down.to_y(far[3])
    def gate_x(source, ctx, step):
        here = gate_recv.at[ctx, source]
        return remote_copy(
            here, here, half_sems.at[0, step], half_sems.at[1, step], other_ctx
        )

    def gate_forward(step):
        copy = gate_x(lax.rem(at.me + parts - step, parts), at.c, step)
        copy.start()
        gate_copies.append(copy)

    def gate_arrive(steps):
        for step in steps:
            source = lax.rem(at.me + parts - step, parts)
            remote_copy(
                gate_ref.at[source],
                gate_recv.at[at.c, source],
                gate_sems.at[0, step - 1],
                gate_sems.at[1, step - 1],
                {"seq": source},
            ).wait_recv()
            gate_forward(step)

    grad_att_ref[...] = dot_last(grad_res_b, full_out_ref[...]).astype(bf16)
    kv = kv_ref[...].reshape(2 * rows, 2 * key_width)
    grad_kv_ref[...] = jnp.zeros_like(grad_kv_ref)

    def backward_head(head):
        group = head // group_size
        key_columns = head_columns(group)
        value_columns = head_columns(KV_HEADS + group)
        columns = head_columns(head)
        grad_att = grad_att_ref[:, columns]
        grad_probs = dot_last(grad_att, kv[:, value_columns])
        delta = jnp.sum(
            grad_att.astype(f32) * attended_ref[:, columns].astype(f32), axis=-1, keepdims=True
        )
        probs = probs_ref[head]
        grad_scores = (probs * (grad_probs - delta) * (HEAD_DIM ** (-0.5))).astype(bf16)
        grad_query_ref[:, columns] = jnp.dot(
            grad_scores, kv[:, key_columns], preferred_element_type=f32
        )
        return (
            dot_first(grad_scores, query_ref[:, columns]),
            dot_first(probs.astype(bf16), grad_att),
        )

    def backward_group(group):
        heads = range(group * group_size, (group + 1) * group_size)
        parts_of = [backward_head(head) for head in heads]
        grad_kv_ref[:, head_columns(group)] = sum(part[0] for part in parts_of[1:]) + parts_of[0][0]
        grad_kv_ref[:, head_columns(KV_HEADS + group)] = (
            sum(part[1] for part in parts_of[1:]) + parts_of[0][1]
        )

    backward_group(0)
    down.to_z(far[0], False)
    out.add_core()
    backward_group(1)
    kv_copy = remote_copy(
        grad_kv_ref.at[pl.ds(rows, rows)], kv_other, x_sems.at[0, 1], x_sems.at[1, 1], other_ctx
    )
    kv_copy.start()
    down.to_z(far[1], False)
    gate_forward(0)
    gate_arrive(range(1, parts // 2))
    kv_copy.wait_recv()
    grad_query = grad_query_ref[...]
    grad_kv = grad_kv_ref[:rows] + kv_other[...]
    rotary = jnp.concatenate([grad_query, grad_kv[:, :key_width]], 1)
    turned = rotary * tiled(cos_ref[...], rotary.shape[1]) - rotated(
        rotary * tiled(sin_ref[...], rotary.shape[1])
    )
    bias_row = jnp.concatenate(
        [
            jnp.sum(turned, axis=0, keepdims=True),
            jnp.sum(grad_kv[:, key_width:], axis=0, keepdims=True),
        ],
        1,
    )
    grad_proj_ref[:, : query_width + key_width] = turned.astype(bf16)
    grad_proj_ref[:, query_width + key_width :] = grad_kv[:, key_width:].astype(bf16)
    flat_ref[...] = dot_first(first_ref[...], grad_proj_ref[...])
    spread(flat_ref, qkv.source)
    qkv.begin()
    gate_arrive(range(parts // 2, parts))
    down.to_z(far[2], False)
    down.to_z(far[3], True)
    grad_first = dot_last(grad_proj_ref[...], full_qkv_ref[...])
    normed_one, scale_one = rms_forward(tokens_ref[...].astype(f32))
    grad_part, gain_one_grad = rms_backward(grad_first, normed_one, scale_one, gains_ref[0:1])
    input_grad_ref[...] += grad_part
    bias_count = bias_row.shape[1] // parts
    gain_one_row = gain_one_grad.reshape(1, model)
    gain_two_row = gain_two_grad.reshape(1, model)
    small.source[...] = jnp.zeros_like(small.source)
    for part in range(parts):
        z, y, k = part // 4, (part // 2) % 2, part % 2
        small.source[k, z, y, 0:1, :bias_count] = bias_row[
            :, part * bias_count : (part + 1) * bias_count
        ]
        for index, row in enumerate((gain_one_row, gain_two_row)):
            start = bias_count + index * depth
            small.source[k, z, y, 0:1, start : start + depth] = row[
                :, part * depth : (part + 1) * depth
            ]
    small.begin()
    out.second()
    qkv.add_core()
    small.add_core()
    out.to_z()
    small.second()

    qkv.second()
    small.to_z()
    qkv.to_z()
    down.finish()
    output_ref[...] = (residual_ref[...] + down_ref[...]).astype(bf16)
    down_copy.wait_recv()
    down_grad_ref[...] = down_mine_ref[...].astype(f32) + down_other[...].astype(f32)
    out.finish()
    small.finish()
    for step in range(parts):
        gate_x(lax.rem(at.me + parts - step, parts), 1 - at.c, step).wait_recv()
    for ctx in range(2):
        for part in range(parts):
            start = (ctx * parts + part) * hidden
            gate_out_ref[:, start : start + hidden] = gate_recv[ctx, part, :, :hidden].astype(f32)
    qkv.finish()
    down_copy.wait_send()
    kv_copy.wait_send()
    for copy in gate_copies:
        copy.wait_send()
    down.end()
    out.end()
    small.end()
    qkv.end()


def backward(operands, hidden, bias_count, collective_id):
    cot, gate_sum, first_in = operands[0], operands[6], operands[14]
    parts, depth, width = gate_sum.shape
    f32, bf16 = jnp.float32, jnp.bfloat16
    rows = (depth + 31) // 32 * 32
    count, model = cot.shape
    qkv_columns = operands[12].shape[1]
    out_rows, out_columns = operands[13].shape
    kv_columns = operands[9].shape[2]
    small_width = padded(bias_count + 2 * depth)
    shape = jax.ShapeDtypeStruct
    vmem = pl.BlockSpec(memory_space=pltpu.VMEM)
    return pl.pallas_call(
        backward_kernel,
        out_shape=(
            shape((count, model), bf16),
            shape((count, model), f32),
            shape((rows, qkv_columns), f32),
            shape((rows, out_columns), f32),
            shape((8, small_width), f32),
            shape((depth, 2 * parts * hidden), f32),
            shape((hidden, model), f32),
        ),
        in_specs=[vmem] * len(operands),
        out_specs=(vmem,) * 7,
        scratch_shapes=flow_scratch(rows, qkv_columns, False, True, bf16)
        + flow_scratch(rows, out_columns, False, True, bf16)
        + flow_scratch(8, small_width, True, False, f32)
        + [
            pltpu.VMEM((model, qkv_columns), f32),
            pltpu.VMEM((hidden, model), bf16),
            pltpu.VMEM((2, parts, depth, width), bf16),
            pltpu.VMEM((4, 2, count, model), bf16),
            pltpu.VMEM((4, count, model), bf16),
            pltpu.VMEM((4, count, model), bf16),
            pltpu.VMEM((count, model), f32),
            pltpu.VMEM((count, out_rows), f32),
            pltpu.VMEM((2 * count, kv_columns), f32),
            pltpu.VMEM((count, kv_columns), f32),
            pltpu.VMEM((count, out_rows), bf16),
            pltpu.VMEM((count, qkv_columns), bf16),
            pltpu.SemaphoreType.DMA((2, parts - 1)),
            pltpu.SemaphoreType.DMA((2, parts)),
            pltpu.SemaphoreType.DMA((2, 2)),
            pltpu.SemaphoreType.DMA((4, 4)),
            pltpu.SemaphoreType.DMA((4, 4)),
        ],
        compiler_params=pltpu.CompilerParams(
            collective_id=collective_id, has_side_effects=True, vmem_limit_bytes=40 * 2**20
        ),
    )(*operands)


def finish_kernel(*refs):
    count = len(refs) // 2
    for index in range(count):
        source, target = refs[index], refs[count + index]
        if len(target.shape) == 3:
            target[0] = source[...]
        else:
            target[...] = source[: target.shape[0], : target.shape[1]]


def finish(values, shapes):
    vmem = pl.BlockSpec(memory_space=pltpu.VMEM)
    return pl.pallas_call(
        finish_kernel,
        out_shape=tuple(
            jax.ShapeDtypeStruct(shape, value.dtype) for value, shape in zip(values, shapes)
        ),
        in_specs=[vmem] * len(values),
        out_specs=(vmem,) * len(values),
        compiler_params=pltpu.CompilerParams(vmem_limit_bytes=24 * 2**20),
    )(*values)


def shards(
    tokens,
    positions,
    cotangent,
    qkv_weight,
    qkv_bias,
    out_weight,
    gate_up_weight,
    down_weight,
    attn_gain,
    ffn_gain,
):
    f32 = jnp.float32
    qkv_columns = qkv_weight.shape[1]
    depth = qkv_weight.shape[0]
    bias_count = qkv_bias.shape[0]
    packed_rows = packed_height(depth)
    pair = jnp.concatenate([qkv_weight, out_weight], 1)
    extra = jnp.concatenate([qkv_bias, attn_gain, ffn_gain])
    extra = jnp.pad(extra, (0, pair.shape[1] - extra.shape[0]))[None]
    packed = jnp.concatenate(
        [pair, extra, jnp.zeros((packed_rows - depth - 1, pair.shape[1]), pair.dtype)], 0
    )
    packed = lax.all_gather(packed, "seq", axis=0, tiled=True).reshape(-1, packed_rows, pair.shape[1])
    full_qkv = packed[:, :depth, :qkv_columns].reshape(-1, qkv_columns)
    full_out = packed[:, :depth, qkv_columns:].reshape(-1, out_weight.shape[1])
    full_bias = packed[:, depth, :bias_count].reshape(-1)
    gain_one = packed[:, depth, bias_count : bias_count + depth].reshape(-1)
    gain_two = packed[:, depth, bias_count + depth : bias_count + 2 * depth].reshape(-1)
    parts = lax.axis_size("seq")
    hidden = down_weight.shape[0]
    own_gate_up = columns_from_rows(gate_up_weight, parts)
    all_cot = gather_rows(cotangent[0], 0)
    own_gate_up, all_cot, full_qkv = lax.optimization_barrier((own_gate_up, all_cot, full_qkv))
    inputs_f = tokens[0].astype(f32)
    cot_row = cotangent[0]
    row_count = inputs_f.shape[0]
    group_size = HEADS // KV_HEADS
    query_width = HEADS * HEAD_DIM
    key_width = KV_HEADS * HEAD_DIM
    score_scale = HEAD_DIM ** (-0.5)
    all_positions = positions[0]
    position_row = lax.dynamic_slice_in_dim(
        all_positions, lax.axis_index("ctx") * row_count, row_count, 0
    )
    normed_one, scale_one = rms_forward(inputs_f)
    first_in = to_bf16(normed_one * gain_one.astype(f32))
    projected = jnp.dot(first_in, full_qkv, preferred_element_type=f32) + full_bias.astype(f32)
    cosine_table, sine_table = rope_tables(position_row)
    cos_query = cosine_table[:, None, None, :]
    sin_query = sine_table[:, None, None, :]
    cos_key = cosine_table[:, None, :]
    sin_key = sine_table[:, None, :]
    query = projected[:, :query_width].reshape(row_count, KV_HEADS, group_size, HEAD_DIM)
    keys = projected[:, query_width : query_width + key_width].reshape(
        row_count, KV_HEADS, HEAD_DIM
    )
    values = projected[:, query_width + key_width :]
    query_rot = to_bf16(query * cos_query + rotate_half(query) * sin_query)
    key_rot = to_bf16(keys * cos_key + rotate_half(keys) * sin_key).reshape(row_count, key_width)
    value_b = to_bf16(values)
    both = jnp.concatenate([key_rot, value_b], -1)
    if lax.axis_size("ctx") == 2:
        both = jnp.concatenate([both, other(both)], 0)
        other_row = lax.dynamic_slice_in_dim(
            all_positions, (1 - lax.axis_index("ctx")) * row_count, row_count, 0
        )
        all_positions = jnp.concatenate([position_row, other_row])
    else:
        both = lax.all_gather(both, "ctx", axis=0, tiled=True)
    all_keys, all_values = both[:, :key_width], both[:, key_width:]
    all_keys = all_keys.reshape(-1, KV_HEADS, HEAD_DIM)
    all_values = all_values.reshape(-1, KV_HEADS, HEAD_DIM)
    scores = (
        jnp.einsum("tkgd,skd->kgts", query_rot, all_keys, preferred_element_type=f32) * score_scale
    )
    allowed = all_positions[None, :] <= position_row[:, None]
    scores = jnp.where(allowed, scores, -1e30)
    row_top = jnp.max(scores, axis=-1, keepdims=True)
    log_total = row_top + jnp.log(jnp.sum(jnp.exp(scores - row_top), axis=-1, keepdims=True))
    probs = jnp.exp(scores - log_total)
    probs_b = to_bf16(probs)
    attended = to_bf16(
        jnp.einsum("kgts,skd->tkgd", probs_b, all_values, preferred_element_type=f32)
    )
    attended_flat = attended.reshape(row_count, query_width)
    residual = inputs_f + jnp.dot(attended_flat, full_out, preferred_element_type=f32)
    normed_two, scale_two = rms_forward(residual)
    second_in = to_bf16(normed_two * gain_two.astype(f32))
    all_second = gather_rows(second_in, 1)
    gate_up = jnp.dot(all_second, own_gate_up, preferred_element_type=f32)
    gate = gate_up[:, :hidden]
    upward = gate_up[:, hidden:]
    sigmoid_gate = jax.nn.sigmoid(gate)
    activated = to_bf16(gate * sigmoid_gate * upward)
    grad_act = contract_columns(all_cot, down_weight)
    grad_gate = grad_act * upward * sigmoid_gate * (1.0 + gate * (1.0 - sigmoid_gate))
    grad_upward = grad_act * (gate * sigmoid_gate)
    grad_gate_up = to_bf16(jnp.concatenate([grad_gate, grad_upward], -1))
    grad_second = scatter_tokens(contract_columns(grad_gate_up, own_gate_up))
    down_sum = scatter_tokens(jnp.dot(activated, down_weight, preferred_element_type=f32))
    output_row = (residual + down_sum).astype(jnp.bfloat16)
    result_down = sum_rounded(contract_rows(activated, all_cot))
    result_gate_up = rows_from_columns(
        to_bf16(sum_rounded(contract_rows(all_second, grad_gate_up))), parts
    ).astype(f32)
    grad_through, gain_two_grad = rms_backward(
        grad_second, normed_two, scale_two, gain_two.astype(f32)
    )
    grad_residual = cot_row.astype(f32) + grad_through
    grad_res_b = to_bf16(grad_residual)
    out_grad = weight_rows(attended_flat, grad_res_b)
    grad_attended = to_bf16(jnp.dot(grad_res_b, full_out.T, preferred_element_type=f32))
    grad_attended = grad_attended.reshape(row_count, KV_HEADS, group_size, HEAD_DIM)
    grad_probs = jnp.einsum("tkgd,skd->kgts", grad_attended, all_values, preferred_element_type=f32)
    delta = jnp.sum(grad_attended.astype(f32) * attended.astype(f32), axis=-1)
    delta = jnp.transpose(delta, (1, 2, 0))[..., None]
    grad_scores = to_bf16(probs * (grad_probs - delta) * score_scale)
    grad_query_rot = jnp.einsum("kgts,skd->tkgd", grad_scores, all_keys, preferred_element_type=f32)
    key_part = jnp.einsum("kgts,tkgd->skd", grad_scores, query_rot, preferred_element_type=f32)
    value_part = jnp.einsum("kgts,tkgd->skd", probs_b, grad_attended, preferred_element_type=f32)
    key_parts = jnp.concatenate(
        [
            key_part.reshape(row_count * lax.axis_size("ctx"), key_width),
            value_part.reshape(row_count * lax.axis_size("ctx"), key_width),
        ],
        -1,
    )
    if lax.axis_size("ctx") == 2:
        key_local = key_parts[:row_count] + other(key_parts[row_count:])
    else:
        key_local = lax.psum_scatter(key_parts, "ctx", scatter_dimension=0, tiled=True)
    grad_key_rot = key_local[:, :key_width].reshape(row_count, KV_HEADS, HEAD_DIM)
    grad_value = key_local[:, key_width:]
    grad_query = grad_query_rot * cos_query + rotate_back(grad_query_rot * sin_query)
    grad_key = grad_key_rot * cos_key + rotate_back(grad_key_rot * sin_key)
    grad_projected = jnp.concatenate(
        [
            grad_query.reshape(row_count, query_width),
            grad_key.reshape(row_count, key_width),
            grad_value,
        ],
        -1,
    )
    bias_grad = jnp.sum(grad_projected, axis=0)
    grad_proj_b = to_bf16(grad_projected)
    grad_first = jnp.dot(grad_proj_b, full_qkv.T, preferred_element_type=f32)
    grad_input_part, gain_one_grad = rms_backward(
        grad_first, normed_one, scale_one, gain_one.astype(f32)
    )
    input_row_grad = grad_residual + grad_input_part
    small = jnp.concatenate(
        [
            bias_grad.reshape(parts, -1),
            gain_one_grad.reshape(parts, -1),
            gain_two_grad.reshape(parts, -1),
        ],
        -1,
    )
    small = jnp.pad(small, ((0, 0), (0, qkv_columns - small.shape[1])))[:, None]
    grad_rows = (depth + 8) // 8 * 8
    packed_grad = jnp.concatenate(
        [
            contract_rows(first_in, grad_proj_b).reshape(parts, depth, qkv_columns),
            small,
            jnp.zeros((parts, grad_rows - depth - 1, qkv_columns), f32),
        ],
        1,
    ).reshape(parts * grad_rows, qkv_columns)
    packed_grad, output_row = lax.optimization_barrier((packed_grad, output_row))
    packed_sum = sum_ctx(lax.psum_scatter(packed_grad, "seq", scatter_dimension=0, tiled=True))
    result_qkv = packed_sum[:depth]
    result_bias = packed_sum[depth, :bias_count]
    result_gain_one = packed_sum[depth, bias_count : bias_count + depth]
    result_gain_two = packed_sum[depth, bias_count + depth : bias_count + 2 * depth]
    result_out = sum_ctx(out_grad)
    return (
        output_row[None],
        input_row_grad[None],
        result_qkv,
        result_bias,
        result_out,
        result_gate_up,
        result_down,
        result_gain_one,
        result_gain_two,
    )


def shards_fast(
    tokens,
    positions,
    cotangent,
    qkv_weight,
    qkv_bias,
    out_weight,
    gate_up_weight,
    down_weight,
    attn_gain,
    ffn_gain,
):
    qkv_columns = qkv_weight.shape[1]
    depth = qkv_weight.shape[0]
    bias_count = qkv_bias.shape[0]
    packed_rows = packed_height(depth)
    parts = lax.axis_size("seq")
    hidden = down_weight.shape[0]
    extra = jnp.concatenate([qkv_bias, attn_gain, ffn_gain])
    extra = jnp.pad(extra, (0, qkv_columns - extra.shape[0]))[None]
    qkv_packed = jnp.concatenate(
        [qkv_weight, extra, jnp.zeros((packed_rows - depth - 1, qkv_columns), extra.dtype)], 0
    )
    out_packed = jnp.pad(out_weight, ((0, packed_rows - depth), (0, 0)))
    cot_row = cotangent[0]
    row_count = cot_row.shape[0]
    at_ctx = lax.axis_index("ctx")
    position_row = lax.dynamic_slice_in_dim(positions[0], at_ctx * row_count, row_count, 0)
    other_row = lax.dynamic_slice_in_dim(positions[0], (1 - at_ctx) * row_count, row_count, 0)
    cosine_table, sine_table = rope_tables(position_row)
    tables = [jnp.concatenate([table, table], -1) for table in (cosine_table, sine_table)]
    (
        full_qkv,
        full_out,
        all_cot,
        weight_wide,
        gains,
        first_in,
        query_flat,
        both,
        probs,
        attended_flat,
        residual,
        second_in,
    ) = forward(
        qkv_packed,
        out_packed,
        cot_row,
        gate_up_weight,
        tokens[0],
        tables,
        position_row[:, None],
        jnp.concatenate([position_row, other_row])[None],
        bias_count,
        0,
    )
    down_sum_width = padded(hidden)
    extra_rows = down_sum_width - hidden
    down_wide = jnp.pad(down_weight, ((0, extra_rows), (0, 0)))
    grad_second, down_part, down_mine, gate_sum = ffn(
        second_in, all_cot, weight_wide, down_wide, hidden, 1
    )
    output_row, input_row_grad, qkv_sum, out_sum, small_sum, gate_grad, down_grad = backward(
        (
            cot_row,
            residual,
            tokens[0],
            gains,
            grad_second,
            down_part,
            gate_sum,
            down_mine,
            query_flat,
            both,
            probs,
            attended_flat,
            full_qkv,
            full_out,
            first_in,
            *tables,
        ),
        hidden,
        bias_count,
        2,
    )
    output_row, input_row_grad, result_qkv, result_out, result_gate_up, result_down = finish(
        (output_row, input_row_grad, qkv_sum, out_sum, gate_grad, down_grad),
        (
            (1,) + output_row.shape,
            (1,) + input_row_grad.shape,
            (depth, qkv_columns),
            (depth, out_weight.shape[1]),
            gate_grad.shape,
            down_grad.shape,
        ),
    )
    result_bias = small_sum[0, :bias_count]
    result_gain_one = small_sum[0, bias_count : bias_count + depth]
    result_gain_two = small_sum[0, bias_count + depth : bias_count + 2 * depth]
    return (
        output_row,
        input_row_grad,
        result_qkv,
        result_bias,
        result_out,
        result_gate_up,
        result_down,
        result_gain_one,
        result_gain_two,
    )


def solution(mesh):
    in_specs = (
        P("seq", "ctx", None),
        P("seq", None),
        P("seq", "ctx", None),
        P("seq", None),
        P("seq"),
        P("seq", None),
        P("seq", None),
        P("seq", None),
        P("seq"),
        P("seq"),
    )
    out_specs = (
        P("seq", "ctx", None),
        P("seq", "ctx", None),
        P("seq", None),
        P("seq"),
        P("seq", None),
        P("seq", None),
        P("seq", None),
        P("seq"),
        P("seq"),
    )
    fast = mesh.shape["ctx"] == 2 and mesh.shape["seq"] == 16
    return jax.shard_map(shards_fast if fast else shards, mesh=mesh, in_specs=in_specs, out_specs=out_specs, check_vma=False)
```
